32 devices in a mesh: dp: 8 (over z, x), space: 4 (over y, core).
Axes of the slice: x: 2, y: 2, z: 4, core: 2. Of those that a mesh axis runs over, the one named last changes fastest.
Arguments:
- scenes: bfloat16 [16, 64, 64, 320], P('dp', 'space'), may hold values from -6 to 6
- params: bfloat16 [1658880], P(('dp', 'space')), may hold values from -3 to 3
- cotangent: bfloat16 [16, 64, 64, 320], P('dp', 'space'), may hold values from -6 to 6
Outputs:
- block_out: bfloat16 [16, 64, 64, 320], P('dp', 'space')
- input_grad: float32 [16, 64, 64, 320], P('dp', 'space')
- param_grad: float32 [1658880], P(('dp', 'space'))
The draws below stay inside these ranges and needn't reach their ends.
All inputs are finite; a program needn't handle non-finite values.
Results may differ from the reference program's by a relative error of at most 0.013.
Values may be sent and summed in bfloat16 or wider, within the bound.
A program may use at most 192 MiB of HBM per device.

```python
import math
import jax
import jax.numpy as jnp
from jax import lax

C = 320
HEADS = 5
HD = 64
FF = 1280
W = 64
SCENES = 16
H = 64
P_SIZE = 1658880


def param_table_drawn(width, hidden):
    return [('query_weight', width * width, 2.0 / math.sqrt(width), 0.0), ('query_bias', width, 0.5, 0.0), ('reduce_weight', 4 * width * width, 1.0 / math.sqrt(4 * width), 0.0), ('reduce_bias', width, 0.5, 0.0), ('reduce_gain', width, 0.2, 1.0), ('reduce_shift', width, 0.2, 0.0), ('keyval_weight', 2 * width * width, 1.0 / math.sqrt(width), 0.0), ('value_bias', width, 0.5, 0.0), ('output_weight', width * width, 4.0 / math.sqrt(width), 0.0), ('output_bias', width, 0.3, 0.0), ('first_gain', width, 0.2, 1.0), ('first_shift', width, 0.2, 0.0), ('second_gain', width, 0.2, 1.0), ('second_shift', width, 0.2, 0.0), ('expand_weight', width * hidden, 1.0 / math.sqrt(width), 0.0), ('expand_bias', hidden, 0.3, 0.0), ('depth_weight', 9 * hidden, 1.0 / 3.0, 0.0), ('depth_bias', hidden, 0.3, 0.0), ('shrink_weight', hidden * width, 1.0 / math.sqrt(hidden), 0.0), ('shrink_bias', width, 0.3, 0.0)]


def draw_params(key, part):
    pieces = []
    total = 0
    for index, entry in enumerate(param_table_drawn(C, FF)):
        count, scale, offset = (entry[1], entry[2], entry[3])
        sub_key = jax.random.fold_in(key, index + 11)
        unit = jnp.clip(jax.random.normal(sub_key, (count,), jnp.float32), -4.0, 4.0)
        pieces.append(offset + scale * unit)
        total += count
    spare = jax.random.uniform(jax.random.fold_in(key, 7), (P_SIZE - total,), jnp.float32, -0.01, 0.01)
    pieces.append(spare)
    return jnp.concatenate(pieces).astype(jnp.bfloat16)


def steps_of(stream_key, dims, shards, low, high):
    factor_of, own = 1.0, jax.random.fold_in(stream_key, 6)
    for axis_at, shards_of in shards:
        steps = jnp.exp(jax.random.uniform(jax.random.fold_in(own, axis_at), (shards_of,), jnp.float32, low / len(shards), high / len(shards)))
        factor_of = factor_of * jnp.repeat(steps, dims[axis_at] // shards_of).reshape([-1 if axis == axis_at else 1 for axis in range(len(dims))])
    return factor_of


def bell_draw(key, extent, scale, limit, cuts=(), kind=jnp.bfloat16):
    factor_of = steps_of(key, extent, cuts, -0.22, 0.18) if cuts else 1.0
    array = jax.random.normal(key, extent, jnp.float32) * scale * factor_of
    return jnp.minimum(jnp.maximum(array, -limit), limit).astype(kind)


def setup_inputs(seed: int = 0) -> dict:
    seeds = jax.random.split(jax.random.key(seed), 4)
    scenes = bell_draw(seeds[0], (SCENES, H, W, C), 1.0, 6.0, ((0, 8), (1, 4)))
    params = draw_params(jax.random.fold_in(seeds[3], 71), 0)
    cotangent = bell_draw(seeds[2], (SCENES, H, W, C), 1.0, 6.0, ((0, 8), (1, 4)))
    return {"scenes": scenes, "params": params, "cotangent": cotangent}


@jax.custom_vjp
def low(v):
    return lax.optimization_barrier(v.astype(jnp.bfloat16)).astype(jnp.float32)

@jax.custom_vjp
def low_back(v):
    return v

def low_keep(v):
    return (low(v), None)

def low_pass(kept, grad):
    return (grad,)

def back_keep(v):
    return (v, None)

def back_low(kept, grad):
    return (low(grad),)
low.defvjp(low_keep, low_pass)
low_back.defvjp(back_keep, back_low)
EPSILON = 1e-06

def param_table(width, hidden):
    return [('query_weight', (width, width)), ('query_bias', (width,)), ('reduce_weight', (4 * width, width)), ('reduce_bias', (width,)), ('reduce_gain', (width,)), ('reduce_shift', (width,)), ('keyval_weight', (width, 2 * width)), ('value_bias', (width,)), ('output_weight', (width, width)), ('output_bias', (width,)), ('first_gain', (width,)), ('first_shift', (width,)), ('second_gain', (width,)), ('second_shift', (width,)), ('expand_weight', (width, hidden)), ('expand_bias', (hidden,)), ('depth_weight', (9, hidden)), ('depth_bias', (hidden,)), ('shrink_weight', (hidden, width)), ('shrink_bias', (width,))]

def unpack(flat):
    pieces = {}
    start = 0
    for name, shape in param_table(C, FF):
        count = math.prod(shape)
        pieces[name] = flat[start:start + count].reshape(shape)
        start += count
    return pieces

def matmul(left, right):
    return jnp.dot(left, right, precision=lax.Precision.HIGHEST, preferred_element_type=jnp.float32)

def layer_norm(values, gain, shift):
    center = values - lax.optimization_barrier(jnp.mean(values, axis=-1, keepdims=True))
    spread = lax.optimization_barrier(jnp.mean(center * center, axis=-1, keepdims=True))
    return center * lax.rsqrt(spread + EPSILON) * gain + shift

def scene_forward(scene, weights):
    height, breadth = (scene.shape[0], scene.shape[1])
    flat_in = scene.reshape(-1, C)
    normed = low(layer_norm(flat_in, weights['first_gain'], weights['first_shift']))
    queries = low(low_back(matmul(normed, weights['query_weight']) + weights['query_bias']))
    patches = normed.reshape(height // 2, 2, breadth // 2, 2, C).transpose(0, 2, 1, 3, 4).reshape(-1, 4 * C)
    reduced = low_back(matmul(patches, weights['reduce_weight']) + weights['reduce_bias'])
    reduced_norm = low(layer_norm(reduced, weights['reduce_gain'], weights['reduce_shift']))
    kv_bias = jnp.concatenate([jnp.zeros((C,), jnp.float32), weights['value_bias']])
    keys_vals = low(matmul(reduced_norm, weights['keyval_weight']) + kv_bias)
    query_heads = queries.reshape(-1, HEADS, HD)
    key_heads = keys_vals[:, :C].reshape(-1, HEADS, HD)
    value_heads = keys_vals[:, C:].reshape(-1, HEADS, HD)
    scores = jnp.einsum('qhd,khd->hqk', query_heads, key_heads, precision=lax.Precision.HIGHEST)
    scores = low_back(scores * (1.0 / math.sqrt(HD)))
    probs = low(jax.nn.softmax(scores, axis=-1))
    mixed = jnp.einsum('hqk,khd->qhd', probs, value_heads, precision=lax.Precision.HIGHEST).reshape(-1, C)
    mixed = low(low_back(mixed))
    attended = low_back(matmul(mixed, weights['output_weight']) + weights['output_bias'])
    middle = flat_in + attended
    normed2 = low(layer_norm(middle, weights['second_gain'], weights['second_shift']))
    expanded = low(low_back(matmul(normed2, weights['expand_weight']) + weights['expand_bias']))
    expanded = expanded.reshape(height, breadth, FF)
    padded = jnp.pad(expanded, ((1, 1), (1, 1), (0, 0)))
    conv = jnp.zeros((height, breadth, FF), jnp.float32) + weights['depth_bias']
    for row in range(3):
        for col in range(3):
            conv = conv + padded[row:row + height, col:col + breadth] * weights['depth_weight'][row * 3 + col]
    conv = low_back(conv)
    activ = low(jax.nn.gelu(conv, approximate=False))
    branch = low_back(matmul(activ.reshape(-1, FF), weights['shrink_weight']) + weights['shrink_bias'])
    return (middle + branch).reshape(height, breadth, C)

def reference(scenes, params, cotangent):
    inputs = scenes.astype(jnp.float32)
    flat = params.astype(jnp.float32)

    def whole(inputs, flat):
        weights = unpack(flat)
        return lax.map(jax.checkpoint(lambda scene: scene_forward(scene, weights)), inputs)
    output, pull = jax.vjp(whole, inputs, flat)
    grad_inputs, grad_params = pull(cotangent.astype(jnp.float32))
    return (output.astype(jnp.bfloat16), grad_inputs, grad_params)
```

```python
import functools
import math

import jax
import jax.numpy as jnp
from jax import lax
from jax.experimental import pallas as pl
from jax.experimental.pallas import tpu as pltpu
from jax.sharding import PartitionSpec as P

C = 320
HEADS = 5
HD = 64
FF = 1280
W = 64
EPSILON = 1e-06
F32 = jnp.float32
BF16 = jnp.bfloat16

ROWS = 5184
USED_ROWS = 5175
BLOCKS = 32
BLOCK_ROWS = ROWS // BLOCKS
R_QUERY = 0
R_REDUCE = 321
R_KEYVAL = 1604
R_OUTPUT = 2245
R_EXPAND = 2570
R_HIDDEN = 3850
R_SHRINK = 3894
VECTOR_ROWS = (320, 1601, 1602, 1603, 2244, 2565, 2566, 2567, 2568, 2569, 5174)
(
    V_QUERY,
    V_REDUCE,
    V_RGAIN,
    V_RSHIFT,
    V_VALUE,
    V_OUTPUT,
    V_GAIN1,
    V_SHIFT1,
    V_GAIN2,
    V_SHIFT2,
    V_SHRINK,
) = range(11)
HIDDEN_ROWS = 11

PARAMS = pltpu.CompilerParams(vmem_limit_bytes=60 * 1024 * 1024)


def shape_of(dims, kind):
    return jax.ShapeDtypeStruct(dims, kind)


def mm(left, right):
    return jnp.dot(left, right, preferred_element_type=F32)


def mm_tn(left, right):
    return lax.dot_general(left, right, (((0,), (0,)), ((), ())), preferred_element_type=F32)


def mm_nt(left, right):
    return lax.dot_general(left, right, (((1,), (1,)), ((), ())), preferred_element_type=F32)


def mm_tt(left, right):
    return lax.dot_general(left, right, (((0,), (1,)), ((), ())), preferred_element_type=F32)


def norm_parts(values):
    center = values - jnp.mean(values, axis=-1, keepdims=True)
    rstd = lax.rsqrt(jnp.mean(center * center, axis=-1, keepdims=True) + EPSILON)
    return center * rstd, rstd


def norm_back(grad, unit, rstd, gain):
    scaled = grad * gain
    first = jnp.mean(scaled, axis=-1, keepdims=True)
    second = jnp.mean(scaled * unit, axis=-1, keepdims=True)
    return rstd * (scaled - first - unit * second)


def row_sum(values):
    return jnp.sum(values, axis=0, keepdims=True)


def full(dims):
    return pl.BlockSpec(dims, lambda *_: (0,) * len(dims))


def unpack_kernel(g_ref, wq, wr, wk, wv, wo, we, ws, vec, hid, rows, tiles):
    for i in range(BLOCKS):
        at = i * BLOCK_ROWS
        block = g_ref[i].astype(F32)
        rows[at : at + BLOCK_ROWS, :] = block
        tiles[0, at : at + BLOCK_ROWS, :] = block[:, 0:128]
        tiles[1, at : at + BLOCK_ROWS, :] = block[:, 128:256]
        tiles[2, at : at + BLOCK_ROWS, 0:64] = block[:, 256:320]

    def strided(start, count, step):
        parts = [tiles[t, pl.ds(start, count, stride=step), :] for t in range(3)]
        return jnp.concatenate([parts[0], parts[1], parts[2][:, 0:64]], axis=1)

    wq[...] = rows[R_QUERY : R_QUERY + C, :].astype(BF16)
    wr[...] = rows[R_REDUCE : R_REDUCE + 4 * C, :].astype(BF16)
    wk[...] = strided(R_KEYVAL, C, 2).astype(BF16)
    wv[...] = strided(R_KEYVAL + 1, C, 2).astype(BF16)
    wo[...] = rows[R_OUTPUT : R_OUTPUT + C, :].astype(BF16)
    ws[...] = rows[R_SHRINK : R_SHRINK + FF, :].astype(BF16)
    we[...] = jnp.concatenate([strided(R_EXPAND + j, C, 4) for j in range(4)], axis=1).astype(BF16)
    hid[0:HIDDEN_ROWS, :] = jnp.concatenate(
        [strided(R_HIDDEN + j, HIDDEN_ROWS, 4) for j in range(4)], axis=1
    )
    for i, row in enumerate(VECTOR_ROWS):
        vec[i : i + 1, :] = rows[row : row + 1, :]


def unpack(blocks):
    return pl.pallas_call(
        unpack_kernel,
        name="unpack",
        out_shape=(
            shape_of((C, C), BF16),
            shape_of((4 * C, C), BF16),
            shape_of((C, C), BF16),
            shape_of((C, C), BF16),
            shape_of((C, C), BF16),
            shape_of((C, FF), BF16),
            shape_of((FF, C), BF16),
            shape_of((16, C), F32),
            shape_of((16, FF), F32),
        ),
        scratch_shapes=[pltpu.VMEM((ROWS, C), F32), pltpu.VMEM((3, ROWS, 128), F32)],
        compiler_params=PARAMS,
    )(blocks)


def pack_kernel(gwq, gwr, gwk, gwv, gwo, gwe, gws, gvec0, gvec1, gvec2, ghid, out, tiles):
    def put(start, value):
        count = value.shape[0]
        tiles[0, start : start + count, :] = value[:, 0:128]
        tiles[1, start : start + count, :] = value[:, 128:256]
        tiles[2, start : start + count, 0:64] = value[:, 256:320]

    def put_strided(start, step, value):
        count = value.shape[0]
        tiles[0, pl.ds(start, count, stride=step), :] = value[:, 0:128]
        tiles[1, pl.ds(start, count, stride=step), :] = value[:, 128:256]
        tail = jnp.concatenate([value[:, 256:320], jnp.zeros((count, 64), F32)], axis=1)
        tiles[2, pl.ds(start, count, stride=step), :] = tail

    put(R_QUERY, gwq[...])
    put(R_REDUCE, gwr[...])
    put_strided(R_KEYVAL, 2, gwk[...])
    put_strided(R_KEYVAL + 1, 2, gwv[...])
    put(R_OUTPUT, gwo[...])
    put(R_SHRINK, gws[...])
    for j in range(4):
        put_strided(R_EXPAND + j, 4, gwe[:, C * j : C * j + C])
        put_strided(R_HIDDEN + j, 4, ghid[0:HIDDEN_ROWS, C * j : C * j + C])
    for source, names in (
        (gvec0, (V_QUERY, V_REDUCE, V_RGAIN, V_RSHIFT, V_GAIN1, V_SHIFT1)),
        (gvec1, (V_VALUE, V_OUTPUT)),
        (gvec2, (V_GAIN2, V_SHIFT2, V_SHRINK)),
    ):
        for i, name in enumerate(names):
            put(VECTOR_ROWS[name], source[i : i + 1, :])
    put(USED_ROWS, jnp.zeros((ROWS - USED_ROWS, C), F32))
    for i in range(BLOCKS):
        at = i * BLOCK_ROWS
        out[i, :, 0:128] = tiles[0, at : at + BLOCK_ROWS, :].astype(BF16)
        out[i, :, 128:256] = tiles[1, at : at + BLOCK_ROWS, :].astype(BF16)
        out[i, :, 256:320] = tiles[2, at : at + BLOCK_ROWS, 0:64].astype(BF16)


def pack(*pieces):
    return pl.pallas_call(
        pack_kernel,
        name="pack",
        out_shape=shape_of((BLOCKS, BLOCK_ROWS, C), BF16),
        scratch_shapes=[pltpu.VMEM((3, ROWS, 128), F32)],
        compiler_params=PARAMS,
    )(*pieces)


TILE = 8 * W
RTILE = TILE // 4


def split_tiles(scr, value):
    scr[0, :, :] = value[:, 0:128]
    scr[1, :, :] = value[:, 128:256]
    scr[2, :, 0:64] = value[:, 256:320]


def patch_pieces(scr):
    pieces = {}
    for b in range(2):
        parts = [scr[t, pl.ds(b, TILE // 2, stride=2), :] for t in range(3)]
        cols = jnp.concatenate([parts[0], parts[1], parts[2][:, 0:64]], axis=1)
        cols = cols.reshape(TILE // (2 * W), 2, W // 2, C)
        for a in range(2):
            pieces[2 * a + b] = cols[:, a].reshape(RTILE, C)
    return pieces


def front_kernel(x_ref, vec, wq, wr, q_out, red_out, rn_out, scr):
    unit, _ = norm_parts(x_ref[...].astype(F32))
    normed = (unit * vec[V_GAIN1 : V_GAIN1 + 1, :] + vec[V_SHIFT1 : V_SHIFT1 + 1, :]).astype(BF16)
    queries = (mm(normed, wq[...]) + vec[V_QUERY : V_QUERY + 1, :]).astype(BF16)
    q_out[...] = queries * jnp.asarray(1.0 / math.sqrt(HD), BF16)
    split_tiles(scr, normed.astype(F32))
    pieces = patch_pieces(scr)
    reduced = vec[V_REDUCE : V_REDUCE + 1, :]
    for k in range(4):
        reduced = reduced + mm(pieces[k].astype(BF16), wr[k * C : (k + 1) * C, :])
    red_out[...] = reduced
    unit, _ = norm_parts(reduced)
    rn_out[...] = (unit * vec[V_RGAIN : V_RGAIN + 1, :] + vec[V_RSHIFT : V_RSHIFT + 1, :]).astype(
        BF16
    )


def front(x, vec, wq, wr):
    tokens = x.shape[0]
    return pl.pallas_call(
        front_kernel,
        name="front",
        grid=(tokens // TILE,),
        in_specs=[
            pl.BlockSpec((TILE, C), lambda i: (i, 0)),
            full((16, C)),
            full((C, C)),
            full((4 * C, C)),
        ],
        out_specs=[
            pl.BlockSpec((TILE, C), lambda i: (i, 0)),
            pl.BlockSpec((RTILE, C), lambda i: (i, 0)),
            pl.BlockSpec((RTILE, C), lambda i: (i, 0)),
        ],
        out_shape=(
            shape_of((tokens, C), BF16),
            shape_of((tokens // 4, C), F32),
            shape_of((tokens // 4, C), BF16),
        ),
        scratch_shapes=[pltpu.VMEM((3, TILE, 128), F32)],
        compiler_params=PARAMS,
    )(x, vec, wq, wr)


QT = 256


def attend_kernel(
    x_ref, q_ref, rn_ref, vec, wk, wv, wo, mixed_out, lse_out, mid_out, n2_out, kt, vones
):
    keys = rn_ref.shape[0] * rn_ref.shape[2]

    @pl.when(pl.program_id(1) == 0)
    def _():
        rn = rn_ref[:, 0].reshape(keys, C)
        key = mm(rn, wk[...]).astype(BF16)
        value = (mm(rn, wv[...]) + vec[V_VALUE : V_VALUE + 1, :]).astype(BF16)
        kt[...] = key.T
        for h in range(HEADS):
            vones[h, :, 0:HD] = value[:, h * HD : (h + 1) * HD]
            vones[h, :, HD:] = jnp.ones((keys, HD), BF16)

    lane = lax.broadcasted_iota(jnp.int32, (QT, 128), 1)
    lses = jnp.zeros((QT, 128), F32)
    outs = []
    for h in range(HEADS):
        scores = mm(q_ref[:, h * HD : (h + 1) * HD], kt[h * HD : (h + 1) * HD, :])
        top = jnp.max(scores, axis=-1, keepdims=True)
        probs = jnp.exp(scores - top).astype(BF16)
        both = mm(probs, vones[h])
        outs.append(both[:, 0:HD] / both[:, HD:])
        lses = jnp.where(lane == h, top + jnp.log(both[:, HD : HD + 1]), lses)
    mixed = jnp.concatenate(outs, axis=1).astype(BF16)
    mixed_out[...] = mixed
    lse_out[...] = lses
    middle = x_ref[...].astype(F32) + mm(mixed, wo[...]) + vec[V_OUTPUT : V_OUTPUT + 1, :]
    mid_out[...] = middle
    unit, _ = norm_parts(middle)
    n2_out[...] = (unit * vec[V_GAIN2 : V_GAIN2 + 1, :] + vec[V_SHIFT2 : V_SHIFT2 + 1, :]).astype(
        BF16
    )


def attend(x, q, rn_all, vec, wk, wv, wo):
    tokens = x.shape[0]
    bands, scenes, per_band, _ = rn_all.shape
    keys = bands * per_band
    steps = tokens // scenes // QT
    tile = lambda s, i: (s * steps + i, 0)
    return pl.pallas_call(
        attend_kernel,
        name="attend",
        grid=(scenes, steps),
        in_specs=[
            pl.BlockSpec((QT, C), tile),
            pl.BlockSpec((QT, C), tile),
            pl.BlockSpec((bands, 1, per_band, C), lambda s, i: (0, s, 0, 0)),
            full((16, C)),
            full((C, C)),
            full((C, C)),
            full((C, C)),
        ],
        out_specs=[
            pl.BlockSpec((QT, C), tile),
            pl.BlockSpec((QT, 128), tile),
            pl.BlockSpec((QT, C), tile),
            pl.BlockSpec((QT, C), tile),
        ],
        out_shape=(
            shape_of((tokens, C), BF16),
            shape_of((tokens, 128), F32),
            shape_of((tokens, C), F32),
            shape_of((tokens, C), BF16),
        ),
        scratch_shapes=[pltpu.VMEM((C, keys), BF16), pltpu.VMEM((HEADS, keys, 2 * HD), BF16)],
        compiler_params=PARAMS,
    )(x, q, rn_all, vec, wk, wv, wo)


CH = 256


def gelu_parts(x):
    size = jnp.abs(x)
    t = 1.0 / (1.0 + (0.3275911 * math.sqrt(0.5)) * size)
    poly = t * (
        0.5 * 0.254829592
        + t
        * (
            0.5 * -0.284496736
            + t * (0.5 * 1.421413741 + t * (0.5 * -1.453152027 + t * (0.5 * 1.061405429)))
        )
    )
    bell = jnp.exp(-0.5 * (x * x))
    tail = poly * bell
    return jnp.where(x >= 0, 1.0 - tail, tail), bell * (1.0 / math.sqrt(2.0 * math.pi))


def mix_kernel(
    n2, n2_top, n2_low, cot, cot_top, cot_low, mid, edge, vec, hid, we, ws,
    y_out, gmid_out, gwe_out, gws_out, ghid_out, gvec_out,
    e_scr, ga_scr, gc_scr, act_scr, ge_scr, branch, gn2,
):
    step = pl.program_id(0)
    scenes, rows = n2.shape[0], n2.shape[1]
    ext = (rows + 4) * W
    gext = (rows + 2) * W
    own = rows * W
    wcol = we[...]
    wrow = ws[...]
    bias = hid[0:1, :]
    top, low = edge[0], edge[1]
    for s in range(scenes):
        body = mm(n2[s].reshape(own, C), wcol) + bias
        e_scr[s * ext + 2 * W : s * ext + 2 * W + own, :] = body.astype(BF16).astype(F32)
        part = mm(n2_top[s].reshape(2 * W, C), wcol) + bias
        e_scr[s * ext : s * ext + 2 * W, :] = part.astype(BF16).astype(F32) * top
        part = mm(n2_low[s].reshape(2 * W, C), wcol) + bias
        e_scr[s * ext + 2 * W + own : (s + 1) * ext, :] = part.astype(BF16).astype(F32) * low
        ga_scr[s * gext + W : s * gext + W + own, :] = mm_nt(cot[s].reshape(own, C), wrow)
        ga_scr[s * gext : s * gext + W, :] = mm_nt(cot_top[s].reshape(W, C), wrow) * top
        ga_scr[s * gext + W + own : (s + 1) * gext, :] = (
            mm_nt(cot_low[s].reshape(W, C), wrow) * low
        )
    col = lax.broadcasted_iota(jnp.int32, (W, 128), 0)
    first, last = col == 0, col == W - 1

    def right(value):
        return jnp.where(first, 0.0, pltpu.roll(value, 1, axis=0))

    def left(value):
        return jnp.where(last, 0.0, pltpu.roll(value, W - 1, axis=0))

    def fold(value):
        return jnp.sum(value.reshape(W // 8, 8, 128), axis=0)

    for half in range(CH // 128):
        lanes = slice(half * 128, half * 128 + 128)
        taps = [hid[1 + k : 2 + k, lanes] for k in range(9)]
        conv_bias = hid[10:11, lanes]

        for s in range(scenes):

            def forward(r, carry):
                at = pl.multiple_of(s * ext + r * W, W)
                lines = [e_scr[pl.ds(at + a * W, W), lanes] for a in range(3)]
                sums = [
                    lines[0] * taps[b] + lines[1] * taps[3 + b] + lines[2] * taps[6 + b]
                    for b in range(3)
                ]
                conv = conv_bias + right(sums[0]) + sums[1] + left(sums[2])
                cdf, density = gelu_parts(conv)
                gat = pl.multiple_of(s * gext + r * W, W)
                gc = ga_scr[pl.ds(gat, W), lanes] * (cdf + conv * density)
                gc = gc.astype(BF16).astype(F32)
                act_scr[pl.ds(gat, W), lanes] = (conv * cdf).astype(BF16)
                gc_scr[0, pl.ds(gat, W), lanes] = left(gc)
                gc_scr[1, pl.ds(gat, W), lanes] = gc
                gc_scr[2, pl.ds(gat, W), lanes] = right(gc)
                return carry

            lax.fori_loop(0, rows + 2, forward, 0)

        def backward(s, r, carry):
            line = e_scr[pl.ds(pl.multiple_of(s * ext + (r + 2) * W, W), W), lanes]
            grads = list(carry)
            total = None
            for a in range(3):
                gat = pl.multiple_of(s * gext + (r + 2 - a) * W, W)
                for b in range(3):
                    g = gc_scr[b, pl.ds(gat, W), lanes]
                    term = g * taps[3 * a + b]
                    total = term if total is None else total + term
                    grads[3 * a + b] = grads[3 * a + b] + fold(g * line)
                    if a == 1 and b == 1:
                        grads[9] = grads[9] + fold(g)
            total = total.astype(BF16)
            ge_scr[pl.ds(pl.multiple_of(s * own + r * W, W), W), lanes] = total
            grads[10] = grads[10] + fold(total.astype(F32))
            return tuple(grads)

        sums = tuple(jnp.zeros((8, 128), F32) for _ in range(11))
        for s in range(scenes):
            sums = lax.fori_loop(0, rows, functools.partial(backward, s), sums)
        ghid_out[0:1, lanes] = row_sum(sums[10])
        for k in range(10):
            ghid_out[1 + k : 2 + k, lanes] = row_sum(sums[k])

    gwe = gws = None
    for s in range(scenes):
        act = act_scr[s * gext + W : s * gext + W + own, :]
        ge = ge_scr[s * own : (s + 1) * own, :]
        term = mm_tn(act, cot[s].reshape(own, C))
        gws = term if gws is None else gws + term
        term = mm_tn(n2[s].reshape(own, C), ge)
        gwe = term if gwe is None else gwe + term
        out_part = mm(act, wrow)
        in_part = mm_nt(ge, wcol)
        at = slice(s * own, (s + 1) * own)

        @pl.when(step == 0)
        def _():
            branch[at, :] = out_part
            gn2[at, :] = in_part

        @pl.when(step > 0)
        def _():
            branch[at, :] += out_part
            gn2[at, :] += in_part

    gws_out[...] = gws
    gwe_out[...] = gwe

    @pl.when(step == pl.num_programs(0) - 1)
    def _():
        size = 4 * W
        per = own // size
        gain = vec[V_GAIN2 : V_GAIN2 + 1, :]

        def finish(i, carry):
            at = pl.multiple_of(i * size, size)
            s = i // per
            line = (i % per) * 4
            middle = mid[pl.ds(at, size), :]
            y_out[pl.ds(at, size), :] = (
                middle + branch[pl.ds(at, size), :] + vec[V_SHRINK : V_SHRINK + 1, :]
            ).astype(BF16)
            grad = gn2[pl.ds(at, size), :]
            unit, rstd = norm_parts(middle)
            direct = cot[s, pl.ds(line, 4)].reshape(size, C).astype(F32)
            gmid_out[pl.ds(at, size), :] = direct + norm_back(grad, unit, rstd, gain)
            return (
                carry[0] + row_sum(grad * unit),
                carry[1] + row_sum(grad),
                carry[2] + row_sum(direct),
            )

        zero = jnp.zeros((1, C), F32)
        sums = lax.fori_loop(0, scenes * per, finish, (zero, zero, zero))
        for i in range(3):
            gvec_out[i : i + 1, :] = sums[i]


def mix(n2, n2_top, n2_low, cot, cot_top, cot_low, mid, edge, vec, hid, we, ws):
    scenes, rows = n2.shape[0], n2.shape[1]
    tokens = scenes * rows * W
    ext = scenes * (rows + 4) * W
    gext = scenes * (rows + 2) * W
    once = dict(pipeline_mode=pl.Buffered(1))
    whole = lambda a: pl.BlockSpec(a.shape, lambda j: (0,) * a.ndim, **once)
    return pl.pallas_call(
        mix_kernel,
        name="mix",
        grid=(FF // CH,),
        in_specs=[
            whole(n2),
            whole(n2_top),
            whole(n2_low),
            whole(cot),
            whole(cot_top),
            whole(cot_low),
            whole(mid),
            pl.BlockSpec(memory_space=pltpu.SMEM),
            whole(vec),
            pl.BlockSpec((16, CH), lambda j: (0, j)),
            pl.BlockSpec((C, CH), lambda j: (0, j)),
            pl.BlockSpec((CH, C), lambda j: (j, 0)),
        ],
        out_specs=[
            full((tokens, C)),
            full((tokens, C)),
            pl.BlockSpec((C, CH), lambda j: (0, j)),
            pl.BlockSpec((CH, C), lambda j: (j, 0)),
            pl.BlockSpec((16, CH), lambda j: (0, j)),
            full((8, C)),
        ],
        out_shape=(
            shape_of((tokens, C), BF16),
            shape_of((tokens, C), F32),
            shape_of((C, FF), F32),
            shape_of((FF, C), F32),
            shape_of((16, FF), F32),
            shape_of((8, C), F32),
        ),
        scratch_shapes=[
            pltpu.VMEM((ext, CH), F32),
            pltpu.VMEM((gext, CH), F32),
            pltpu.VMEM((3, gext, CH), F32),
            pltpu.VMEM((gext, CH), BF16),
            pltpu.VMEM((tokens, CH), BF16),
            pltpu.VMEM((tokens, C), F32),
            pltpu.VMEM((tokens, C), F32),
        ],
        compiler_params=PARAMS,
    )(n2, n2_top, n2_low, cot, cot_top, cot_low, mid, edge, vec, hid, we, ws)


def attend_back_kernel(
    q_ref, lse_ref, mixed_ref, gmid_ref, rn_ref, vec, wk, wv, wo,
    dq_out, grn_out, gwk_out, gwv_out, gwo_out, gvec_out,
    kt, vt, kh, dkt, dvt,
):
    scene, step = pl.program_id(0), pl.program_id(1)
    keys = rn_ref.shape[0] * rn_ref.shape[2]
    start = jnp.logical_and(scene == 0, step == 0)

    @pl.when(start)
    def _():
        for ref in (gwk_out, gwv_out, gwo_out, gvec_out):
            ref[...] = jnp.zeros_like(ref)

    @pl.when(step == 0)
    def _():
        rn = rn_ref[:, 0].reshape(keys, C)
        key = mm(rn, wk[...]).astype(BF16)
        value = (mm(rn, wv[...]) + vec[V_VALUE : V_VALUE + 1, :]).astype(BF16)
        kt[...] = key.T
        vt[...] = value.T
        for h in range(HEADS):
            kh[h] = key[:, h * HD : (h + 1) * HD]
        dkt[...] = jnp.zeros_like(dkt)
        dvt[...] = jnp.zeros_like(dvt)

    gmid = gmid_ref[...]
    gatt = gmid.astype(BF16)
    gvec_out[1:2, :] += row_sum(gatt.astype(F32))
    mixed = mixed_ref[...]
    gwo_out[...] += mm_tn(mixed, gatt)
    gmixed = mm_nt(gatt, wo[...]).astype(BF16)
    prod = gmixed.astype(F32) * mixed.astype(F32)
    q = q_ref[...]
    q_t = q.T
    g_t = gmixed.T
    dqs = []
    for h in range(HEADS):
        cols = slice(h * HD, (h + 1) * HD)
        inner = jnp.sum(prod[:, cols], axis=-1, keepdims=True)
        probs = jnp.exp(mm(q[:, cols], kt[cols, :]) - lse_ref[:, h : h + 1])
        gprobs = mm(gmixed[:, cols], vt[cols, :])
        gscores = (probs * (gprobs - inner)).astype(BF16)
        dqs.append(mm(gscores, kh[h]))
        dkt[cols, :] += mm(q_t[cols, :], gscores)
        dvt[cols, :] += mm(g_t[cols, :], probs.astype(BF16))
    dq_out[...] = (jnp.concatenate(dqs, axis=1) * (1.0 / math.sqrt(HD))).astype(BF16)

    @pl.when(step == pl.num_programs(1) - 1)
    def _():
        rn = rn_ref[:, 0].reshape(keys, C)
        dk = dkt[...].T.astype(BF16)
        dv = dvt[...].T
        gvec_out[0:1, :] += row_sum(dv)
        dv = dv.astype(BF16)
        gwk_out[...] += mm_tn(rn, dk)
        gwv_out[...] += mm_tn(rn, dv)
        grn = mm_nt(dk, wk[...]) + mm_nt(dv, wv[...])
        grn_out[...] = grn.astype(BF16).reshape(grn_out.shape)


def attend_back(q, lse, mixed, gmid, rn_all, vec, wk, wv, wo):
    tokens = q.shape[0]
    bands, scenes, per_band, _ = rn_all.shape
    keys = bands * per_band
    steps = tokens // scenes // QT
    tile = lambda s, i: (s * steps + i, 0)
    return pl.pallas_call(
        attend_back_kernel,
        name="attend_back",
        grid=(scenes, steps),
        in_specs=[
            pl.BlockSpec((QT, C), tile),
            pl.BlockSpec((QT, 128), tile),
            pl.BlockSpec((QT, C), tile),
            pl.BlockSpec((QT, C), tile),
            pl.BlockSpec((bands, 1, per_band, C), lambda s, i: (0, s, 0, 0)),
            full((16, C)),
            full((C, C)),
            full((C, C)),
            full((C, C)),
        ],
        out_specs=[
            pl.BlockSpec((QT, C), tile),
            pl.BlockSpec((bands, 1, per_band, C), lambda s, i: (0, s, 0, 0)),
            full((C, C)),
            full((C, C)),
            full((C, C)),
            full((8, C)),
        ],
        out_shape=(
            shape_of((tokens, C), BF16),
            shape_of(rn_all.shape, BF16),
            shape_of((C, C), F32),
            shape_of((C, C), F32),
            shape_of((C, C), F32),
            shape_of((8, C), F32),
        ),
        scratch_shapes=[
            pltpu.VMEM((C, keys), BF16),
            pltpu.VMEM((C, keys), BF16),
            pltpu.VMEM((HEADS, keys, HD), BF16),
            pltpu.VMEM((C, keys), F32),
            pltpu.VMEM((C, keys), F32),
        ],
        compiler_params=PARAMS,
    )(q, lse, mixed, gmid, rn_all, vec, wk, wv, wo)


def tail_kernel(
    x_ref, gmid_ref, dq_ref, grn_ref, red_ref, vec, wq, wr,
    gx_out, gwq_out, gwr_out, gvec_out, scr, gscr,
):
    @pl.when(pl.program_id(0) == 0)
    def _():
        for ref in (gwq_out, gwr_out, gvec_out):
            ref[...] = jnp.zeros_like(ref)

    runit, rrstd = norm_parts(red_ref[...])
    grn = grn_ref[...].astype(F32)
    gred = norm_back(grn, runit, rrstd, vec[V_RGAIN : V_RGAIN + 1, :]).astype(BF16)
    unit, rstd = norm_parts(x_ref[...].astype(F32))
    gain = vec[V_GAIN1 : V_GAIN1 + 1, :]
    normed = (unit * gain + vec[V_SHIFT1 : V_SHIFT1 + 1, :]).astype(BF16)
    split_tiles(scr, normed.astype(F32))
    pieces = patch_pieces(scr)
    back = {}
    for k in range(4):
        at = slice(k * C, (k + 1) * C)
        gwr_out[at, :] += mm_tn(pieces[k].astype(BF16), gred)
        back[k] = mm_nt(gred, wr[at, :]).reshape(TILE // (2 * W), 1, W // 2, C)
    for b in range(2):
        cols = jnp.concatenate([back[b], back[2 + b]], axis=1).reshape(TILE // 2, C)
        spot = pl.ds(b, TILE // 2, stride=2)
        gscr[0, spot, :] = cols[:, 0:128]
        gscr[1, spot, :] = cols[:, 128:256]
        gscr[2, spot, :] = jnp.concatenate(
            [cols[:, 256:320], jnp.zeros((TILE // 2, 64), F32)], axis=1
        )
    dq = dq_ref[...]
    gwq_out[...] += mm_tn(normed, dq)
    placed = jnp.concatenate([gscr[0], gscr[1], gscr[2][:, 0:64]], axis=1)
    gnormed = mm_nt(dq, wq[...]) + placed
    gx_out[...] = gmid_ref[...] + norm_back(gnormed, unit, rstd, gain)
    gvec_out[0:1, :] += row_sum(dq.astype(F32))
    gvec_out[1:2, :] += row_sum(gred.astype(F32))
    gvec_out[2:3, :] += row_sum(grn * runit)
    gvec_out[3:4, :] += row_sum(grn)
    gvec_out[4:5, :] += row_sum(gnormed * unit)
    gvec_out[5:6, :] += row_sum(gnormed)


def tail(x, gmid, dq, grn, red, vec, wq, wr):
    tokens = x.shape[0]
    tile = pl.BlockSpec((TILE, C), lambda i: (i, 0))
    rtile = pl.BlockSpec((RTILE, C), lambda i: (i, 0))
    return pl.pallas_call(
        tail_kernel,
        name="tail",
        grid=(tokens // TILE,),
        in_specs=[
            tile, tile, tile, rtile, rtile, full((16, C)), full((C, C)), full((4 * C, C))
        ],
        out_specs=[tile, full((C, C)), full((4 * C, C)), full((8, C))],
        out_shape=(
            shape_of((tokens, C), F32),
            shape_of((C, C), F32),
            shape_of((4 * C, C), F32),
            shape_of((8, C), F32),
        ),
        scratch_shapes=[pltpu.VMEM((3, TILE, 128), F32), pltpu.VMEM((3, TILE, 128), F32)],
        compiler_params=PARAMS,
    )(x, gmid, dq, grn, red, vec, wq, wr)


def gather_params(params):
    size = params.shape[0]
    devices = lax.axis_size("dp") * lax.axis_size("space")
    if devices == BLOCKS and size == BLOCK_ROWS * C:
        return lax.all_gather(params.reshape(BLOCK_ROWS, C), ("dp", "space"), axis=0, tiled=False)
    flat = lax.all_gather(params, ("dp", "space"), axis=0, tiled=True)
    want = ROWS * C
    flat = flat[:want] if flat.shape[0] >= want else jnp.pad(flat, (0, want - flat.shape[0]))
    return flat.reshape(BLOCKS, BLOCK_ROWS, C)


def scatter_grads(blocks, size):
    devices = lax.axis_size("dp") * lax.axis_size("space")
    if devices == BLOCKS and size == BLOCK_ROWS * C:
        own = lax.psum_scatter(blocks, ("dp", "space"), scatter_dimension=0, tiled=False)
        return own.astype(F32).reshape(size)
    flat = blocks.reshape(-1)
    want = size * devices
    flat = flat[:want] if flat.shape[0] >= want else jnp.pad(flat, (0, want - flat.shape[0]))
    own = lax.psum_scatter(flat, ("dp", "space"), scatter_dimension=0, tiled=True)
    return own.astype(F32)


def edges(value, width):
    count = lax.axis_size("space")
    rows = value.shape[1]
    above = lax.ppermute(
        value[:, rows - width :], "space", [(i, i + 1) for i in range(count - 1)]
    )
    below = lax.ppermute(value[:, :width], "space", [(i + 1, i) for i in range(count - 1)])
    return above, below


def on_device(scenes, params, cotangent):
    count, rows, breadth = scenes.shape[0], scenes.shape[1], scenes.shape[2]
    tokens = count * rows * breadth
    bands = lax.axis_size("space")
    per_band = rows * breadth // 4
    band = lax.axis_index("space")
    edge = jnp.stack([band > 0, band < bands - 1]).astype(F32)
    wq, wr, wk, wv, wo, we, ws, vec, hid = unpack(gather_params(params))
    x = scenes.reshape(tokens, C)
    q, red, rn = front(x, vec, wq, wr)
    rn_all = lax.all_gather(rn, "space", axis=0, tiled=False)
    rn_all = rn_all.reshape(bands, count, per_band, C)
    cot_top, cot_low = edges(cotangent, 1)
    mixed, lse, mid, n2 = attend(x, q, rn_all, vec, wk, wv, wo)
    n2 = n2.reshape(scenes.shape)
    n2_top, n2_low = edges(n2, 2)
    y, gmid, gwe, gws, ghid, gvec2 = mix(
        n2, n2_top, n2_low, cotangent, cot_top, cot_low, mid, edge, vec, hid, we, ws
    )
    dq, grn_all, gwk, gwv, gwo, gvec1 = attend_back(
        q, lse, mixed, gmid, rn_all, vec, wk, wv, wo
    )
    grn = lax.psum_scatter(grn_all, "space", scatter_dimension=0, tiled=False)
    gx, gwq, gwr, gvec0 = tail(x, gmid, dq, grn.reshape(-1, C), red, vec, wq, wr)
    blocks = pack(gwq, gwr, gwk, gwv, gwo, gwe, gws, gvec0, gvec1, gvec2, ghid)
    shard = scatter_grads(blocks, params.shape[0])
    return y.reshape(scenes.shape), gx.reshape(scenes.shape), shard


def solution(mesh):
    band = P("dp", "space", None, None)
    flat = P(("dp", "space"))
    return jax.shard_map(
        on_device,
        mesh=mesh,
        in_specs=(band, flat, band),
        out_specs=(band, band, flat),
        check_vma=False,
    )
```

```python
import functools
import math

import jax
import jax.numpy as jnp
from jax import lax
from jax.experimental import pallas as pl
from jax.experimental.pallas import tpu as pltpu
from jax.sharding import PartitionSpec as P

C = 320
HEADS = 5
HD = 64
FF = 1280
W = 64
EPSILON = 1e-06
F32 = jnp.float32
BF16 = jnp.bfloat16

ROWS = 5184
USED_ROWS = 5175
BLOCKS = 32
BLOCK_ROWS = ROWS // BLOCKS
R_QUERY = 0
R_REDUCE = 321
R_KEYVAL = 1604
R_OUTPUT = 2245
R_EXPAND = 2570
R_HIDDEN = 3850
R_SHRINK = 3894
VECTOR_ROWS = (320, 1601, 1602, 1603, 2244, 2565, 2566, 2567, 2568, 2569, 5174)
(
    V_QUERY,
    V_REDUCE,
    V_RGAIN,
    V_RSHIFT,
    V_VALUE,
    V_OUTPUT,
    V_GAIN1,
    V_SHIFT1,
    V_GAIN2,
    V_SHIFT2,
    V_SHRINK,
) = range(11)
HIDDEN_ROWS = 11

PARAMS = pltpu.CompilerParams(vmem_limit_bytes=60 * 1024 * 1024)


def shape_of(dims, kind):
    return jax.ShapeDtypeStruct(dims, kind)


def mm(left, right):
    return jnp.dot(left, right, preferred_element_type=F32)


def mm_tn(left, right):
    return lax.dot_general(left, right, (((0,), (0,)), ((), ())), preferred_element_type=F32)


def mm_nt(left, right):
    return lax.dot_general(left, right, (((1,), (1,)), ((), ())), preferred_element_type=F32)


def mm_tt(left, right):
    return lax.dot_general(left, right, (((0,), (1,)), ((), ())), preferred_element_type=F32)


def norm_parts(values):
    center = values - jnp.mean(values, axis=-1, keepdims=True)
    rstd = lax.rsqrt(jnp.mean(center * center, axis=-1, keepdims=True) + EPSILON)
    return center * rstd, rstd


def norm_back(grad, unit, rstd, gain):
    scaled = grad * gain
    first = jnp.mean(scaled, axis=-1, keepdims=True)
    second = jnp.mean(scaled * unit, axis=-1, keepdims=True)
    return rstd * (scaled - first - unit * second)


def row_sum(values):
    return jnp.sum(values, axis=0, keepdims=True)


def full(dims):
    return pl.BlockSpec(dims, lambda *_: (0,) * len(dims))


def unpack_kernel(g_ref, wq, wr, wk, wv, wo, we, ws, vec, hid, rows, tiles):
    for i in range(BLOCKS):
        at = i * BLOCK_ROWS
        block = g_ref[i].astype(F32)
        rows[at : at + BLOCK_ROWS, :] = block
        tiles[0, at : at + BLOCK_ROWS, :] = block[:, 0:128]
        tiles[1, at : at + BLOCK_ROWS, :] = block[:, 128:256]
        tiles[2, at : at + BLOCK_ROWS, 0:64] = block[:, 256:320]

    def strided(start, count, step):
        parts = [tiles[t, pl.ds(start, count, stride=step), :] for t in range(3)]
        return jnp.concatenate([parts[0], parts[1], parts[2][:, 0:64]], axis=1)

    wq[...] = rows[R_QUERY : R_QUERY + C, :].astype(BF16)
    wr[...] = rows[R_REDUCE : R_REDUCE + 4 * C, :].astype(BF16)
    wk[...] = strided(R_KEYVAL, C, 2).astype(BF16)
    wv[...] = strided(R_KEYVAL + 1, C, 2).astype(BF16)
    wo[...] = rows[R_OUTPUT : R_OUTPUT + C, :].astype(BF16)
    ws[...] = rows[R_SHRINK : R_SHRINK + FF, :].astype(BF16)
    we[...] = jnp.concatenate([strided(R_EXPAND + j, C, 4) for j in range(4)], axis=1).astype(BF16)
    hid[0:HIDDEN_ROWS, :] = jnp.concatenate(
        [strided(R_HIDDEN + j, HIDDEN_ROWS, 4) for j in range(4)], axis=1
    )
    for i, row in enumerate(VECTOR_ROWS):
        vec[i : i + 1, :] = rows[row : row + 1, :]


def unpack(blocks):
    return pl.pallas_call(
        unpack_kernel,
        name="unpack",
        out_shape=(
            shape_of((C, C), BF16),
            shape_of((4 * C, C), BF16),
            shape_of((C, C), BF16),
            shape_of((C, C), BF16),
            shape_of((C, C), BF16),
            shape_of((C, FF), BF16),
            shape_of((FF, C), BF16),
            shape_of((16, C), F32),
            shape_of((16, FF), F32),
        ),
        scratch_shapes=[pltpu.VMEM((ROWS, C), F32), pltpu.VMEM((3, ROWS, 128), F32)],
        compiler_params=PARAMS,
    )(blocks)


def pack_kernel(gwq, gwr, gwk, gwv, gwo, gwe, gws, gvec0, gvec1, gvec2, ghid, out, tiles):
    def put(start, value):
        count = value.shape[0]
        tiles[0, start : start + count, :] = value[:, 0:128]
        tiles[1, start : start + count, :] = value[:, 128:256]
        tiles[2, start : start + count, 0:64] = value[:, 256:320]

    def put_strided(start, step, value):
        count = value.shape[0]
        tiles[0, pl.ds(start, count, stride=step), :] = value[:, 0:128]
        tiles[1, pl.ds(start, count, stride=step), :] = value[:, 128:256]
        tail = jnp.concatenate([value[:, 256:320], jnp.zeros((count, 64), F32)], axis=1)
        tiles[2, pl.ds(start, count, stride=step), :] = tail

    put(R_QUERY, gwq[...])
    put(R_REDUCE, gwr[...])
    put_strided(R_KEYVAL, 2, gwk[...])
    put_strided(R_KEYVAL + 1, 2, gwv[...])
    put(R_OUTPUT, gwo[...])
    put(R_SHRINK, gws[...])
    for j in range(4):
        put_strided(R_EXPAND + j, 4, gwe[:, C * j : C * j + C])
        put_strided(R_HIDDEN + j, 4, ghid[0:HIDDEN_ROWS, C * j : C * j + C])
    for source, names in (
        (gvec0, (V_QUERY, V_REDUCE, V_RGAIN, V_RSHIFT, V_GAIN1, V_SHIFT1)),
        (gvec1, (V_VALUE, V_OUTPUT)),
        (gvec2, (V_GAIN2, V_SHIFT2, V_SHRINK)),
    ):
        for i, name in enumerate(names):
            put(VECTOR_ROWS[name], source[i : i + 1, :])
    put(USED_ROWS, jnp.zeros((ROWS - USED_ROWS, C), F32))
    for i in range(BLOCKS):
        at = i * BLOCK_ROWS
        out[i, :, 0:128] = tiles[0, at : at + BLOCK_ROWS, :].astype(BF16)
        out[i, :, 128:256] = tiles[1, at : at + BLOCK_ROWS, :].astype(BF16)
        out[i, :, 256:320] = tiles[2, at : at + BLOCK_ROWS, 0:64].astype(BF16)


def pack(*pieces):
    return pl.pallas_call(
        pack_kernel,
        name="pack",
        out_shape=shape_of((BLOCKS, BLOCK_ROWS, C), BF16),
        scratch_shapes=[pltpu.VMEM((3, ROWS, 128), F32)],
        compiler_params=PARAMS,
    )(*pieces)


TILE = 8 * W
RTILE = TILE // 4


def split_tiles(scr, value):
    scr[0, :, :] = value[:, 0:128]
    scr[1, :, :] = value[:, 128:256]
    scr[2, :, 0:64] = value[:, 256:320]


def patch_pieces(scr):
    pieces = {}
    for b in range(2):
        parts = [scr[t, pl.ds(b, TILE // 2, stride=2), :] for t in range(3)]
        cols = jnp.concatenate([parts[0], parts[1], parts[2][:, 0:64]], axis=1)
        cols = cols.reshape(TILE // (2 * W), 2, W // 2, C)
        for a in range(2):
            pieces[2 * a + b] = cols[:, a].reshape(RTILE, C)
    return pieces


def front_kernel(x_ref, vec, wq, wr, q_out, red_out, rn_out, scr):
    unit, _ = norm_parts(x_ref[...].astype(F32))
    normed = (unit * vec[V_GAIN1 : V_GAIN1 + 1, :] + vec[V_SHIFT1 : V_SHIFT1 + 1, :]).astype(BF16)
    queries = (mm(normed, wq[...]) + vec[V_QUERY : V_QUERY + 1, :]).astype(BF16)
    q_out[...] = queries * jnp.asarray(1.0 / math.sqrt(HD), BF16)
    split_tiles(scr, normed.astype(F32))
    pieces = patch_pieces(scr)
    reduced = vec[V_REDUCE : V_REDUCE + 1, :]
    for k in range(4):
        reduced = reduced + mm(pieces[k].astype(BF16), wr[k * C : (k + 1) * C, :])
    red_out[...] = reduced
    unit, _ = norm_parts(reduced)
    rn_out[...] = (unit * vec[V_RGAIN : V_RGAIN + 1, :] + vec[V_RSHIFT : V_RSHIFT + 1, :]).astype(
        BF16
    )


def front(x, vec, wq, wr):
    tokens = x.shape[0]
    return pl.pallas_call(
        front_kernel,
        name="front",
        grid=(tokens // TILE,),
        in_specs=[
            pl.BlockSpec((TILE, C), lambda i: (i, 0)),
            full((16, C)),
            full((C, C)),
            full((4 * C, C)),
        ],
        out_specs=[
            pl.BlockSpec((TILE, C), lambda i: (i, 0)),
            pl.BlockSpec((RTILE, C), lambda i: (i, 0)),
            pl.BlockSpec((RTILE, C), lambda i: (i, 0)),
        ],
        out_shape=(
            shape_of((tokens, C), BF16),
            shape_of((tokens // 4, C), F32),
            shape_of((tokens // 4, C), BF16),
        ),
        scratch_shapes=[pltpu.VMEM((3, TILE, 128), F32)],
        compiler_params=PARAMS,
    )(x, vec, wq, wr)


QT = 256


def attend_kernel(
    x_ref, q_ref, rn_ref, vec, wk, wv, wo, mixed_out, lse_out, mid_out, n2_out, kt, vones
):
    keys = rn_ref.shape[0] * rn_ref.shape[2]

    @pl.when(pl.program_id(1) == 0)
    def _():
        rn = rn_ref[:, 0].reshape(keys, C)
        key = mm(rn, wk[...]).astype(BF16)
        value = (mm(rn, wv[...]) + vec[V_VALUE : V_VALUE + 1, :]).astype(BF16)
        kt[...] = key.T
        for h in range(HEADS):
            vones[h, :, 0:HD] = value[:, h * HD : (h + 1) * HD]
            vones[h, :, HD:] = jnp.ones((keys, HD), BF16)

    lane = lax.broadcasted_iota(jnp.int32, (QT, 128), 1)
    lses = jnp.zeros((QT, 128), F32)
    outs = []
    for h in range(HEADS):
        scores = mm(q_ref[:, h * HD : (h + 1) * HD], kt[h * HD : (h + 1) * HD, :])
        top = jnp.max(scores, axis=-1, keepdims=True)
        probs = jnp.exp(scores - top).astype(BF16)
        both = mm(probs, vones[h])
        outs.append(both[:, 0:HD] / both[:, HD:])
        lses = jnp.where(lane == h, top + jnp.log(both[:, HD : HD + 1]), lses)
    mixed = jnp.concatenate(outs, axis=1).astype(BF16)
    mixed_out[...] = mixed
    lse_out[...] = lses
    middle = x_ref[...].astype(F32) + mm(mixed, wo[...]) + vec[V_OUTPUT : V_OUTPUT + 1, :]
    mid_out[...] = middle
    unit, _ = norm_parts(middle)
    n2_out[...] = (unit * vec[V_GAIN2 : V_GAIN2 + 1, :] + vec[V_SHIFT2 : V_SHIFT2 + 1, :]).astype(
        BF16
    )


def attend(x, q, rn_all, vec, wk, wv, wo):
    tokens = x.shape[0]
    bands, scenes, per_band, _ = rn_all.shape
    keys = bands * per_band
    steps = tokens // scenes // QT
    tile = lambda s, i: (s * steps + i, 0)
    return pl.pallas_call(
        attend_kernel,
        name="attend",
        grid=(scenes, steps),
        in_specs=[
            pl.BlockSpec((QT, C), tile),
            pl.BlockSpec((QT, C), tile),
            pl.BlockSpec((bands, 1, per_band, C), lambda s, i: (0, s, 0, 0)),
            full((16, C)),
            full((C, C)),
            full((C, C)),
            full((C, C)),
        ],
        out_specs=[
            pl.BlockSpec((QT, C), tile),
            pl.BlockSpec((QT, 128), tile),
            pl.BlockSpec((QT, C), tile),
            pl.BlockSpec((QT, C), tile),
        ],
        out_shape=(
            shape_of((tokens, C), BF16),
            shape_of((tokens, 128), F32),
            shape_of((tokens, C), F32),
            shape_of((tokens, C), BF16),
        ),
        scratch_shapes=[pltpu.VMEM((C, keys), BF16), pltpu.VMEM((HEADS, keys, 2 * HD), BF16)],
        compiler_params=PARAMS,
    )(x, q, rn_all, vec, wk, wv, wo)


CH = 256


def gelu_parts(x):
    size = jnp.abs(x)
    t = 1.0 / (1.0 + (0.3275911 * math.sqrt(0.5)) * size)
    poly = t * (
        0.5 * 0.254829592
        + t
        * (
            0.5 * -0.284496736
            + t * (0.5 * 1.421413741 + t * (0.5 * -1.453152027 + t * (0.5 * 1.061405429)))
        )
    )
    bell = jnp.exp(-0.5 * (x * x))
    tail = poly * bell
    return jnp.where(x >= 0, 1.0 - tail, tail), bell * (1.0 / math.sqrt(2.0 * math.pi))


def mix_kernel(
    n2, n2_top, n2_low, cot, cot_top, cot_low, mid, edge, vec, hid, we, ws,
    y_out, gmid_out, gwe_out, gws_out, ghid_out, gvec_out,
    e_scr, ga_scr, gc_scr, act_scr, ge_scr, branch, gn2,
):
    step = pl.program_id(0)
    scenes, rows = n2.shape[0], n2.shape[1]
    ext = (rows + 4) * W
    gext = (rows + 2) * W
    own = rows * W
    wcol = we[...]
    wrow = ws[...]
    bias = hid[0:1, :]
    top, low = edge[0], edge[1]

    def inside(value, there):
        return jnp.where(there > 0, value, 0.0)

    for s in range(scenes):
        body = mm(n2[s].reshape(own, C), wcol) + bias
        e_scr[s * ext + 2 * W : s * ext + 2 * W + own, :] = body.astype(BF16).astype(F32)
        part = mm(n2_top[s].reshape(2 * W, C), wcol) + bias
        e_scr[s * ext : s * ext + 2 * W, :] = inside(part.astype(BF16).astype(F32), top)
        part = mm(n2_low[s].reshape(2 * W, C), wcol) + bias
        e_scr[s * ext + 2 * W + own : (s + 1) * ext, :] = inside(
            part.astype(BF16).astype(F32), low
        )
        ga_scr[s * gext + W : s * gext + W + own, :] = mm_nt(cot[s].reshape(own, C), wrow)
        ga_scr[s * gext : s * gext + W, :] = inside(mm_nt(cot_top[s].reshape(W, C), wrow), top)
        ga_scr[s * gext + W + own : (s + 1) * gext, :] = inside(
            mm_nt(cot_low[s].reshape(W, C), wrow), low
        )
    col = lax.broadcasted_iota(jnp.int32, (W, 128), 0)
    first, last = col == 0, col == W - 1

    def right(value):
        return jnp.where(first, 0.0, pltpu.roll(value, 1, axis=0))

    def left(value):
        return jnp.where(last, 0.0, pltpu.roll(value, W - 1, axis=0))

    def fold(value):
        return jnp.sum(value.reshape(W // 8, 8, 128), axis=0)

    for half in range(CH // 128):
        lanes = slice(half * 128, half * 128 + 128)
        taps = [hid[1 + k : 2 + k, lanes] for k in range(9)]
        conv_bias = hid[10:11, lanes]

        for s in range(scenes):

            def forward(r, carry):
                at = pl.multiple_of(s * ext + r * W, W)
                lines = [e_scr[pl.ds(at + a * W, W), lanes] for a in range(3)]
                sums = [
                    lines[0] * taps[b] + lines[1] * taps[3 + b] + lines[2] * taps[6 + b]
                    for b in range(3)
                ]
                conv = conv_bias + right(sums[0]) + sums[1] + left(sums[2])
                cdf, density = gelu_parts(conv)
                gat = pl.multiple_of(s * gext + r * W, W)
                gc = ga_scr[pl.ds(gat, W), lanes] * (cdf + conv * density)
                gc = gc.astype(BF16).astype(F32)
                act_scr[pl.ds(gat, W), lanes] = (conv * cdf).astype(BF16)
                gc_scr[0, pl.ds(gat, W), lanes] = left(gc)
                gc_scr[1, pl.ds(gat, W), lanes] = gc
                gc_scr[2, pl.ds(gat, W), lanes] = right(gc)
                return carry

            lax.fori_loop(0, rows + 2, forward, 0)

        def backward(s, r, carry):
            line = e_scr[pl.ds(pl.multiple_of(s * ext + (r + 2) * W, W), W), lanes]
            grads = list(carry)
            total = None
            for a in range(3):
                gat = pl.multiple_of(s * gext + (r + 2 - a) * W, W)
                for b in range(3):
                    g = gc_scr[b, pl.ds(gat, W), lanes]
                    term = g * taps[3 * a + b]
                    total = term if total is None else total + term
                    grads[3 * a + b] = grads[3 * a + b] + fold(g * line)
                    if a == 1 and b == 1:
                        grads[9] = grads[9] + fold(g)
            total = total.astype(BF16)
            ge_scr[pl.ds(pl.multiple_of(s * own + r * W, W), W), lanes] = total
            grads[10] = grads[10] + fold(total.astype(F32))
            return tuple(grads)

        sums = tuple(jnp.zeros((8, 128), F32) for _ in range(11))
        for s in range(scenes):
            sums = lax.fori_loop(0, rows, functools.partial(backward, s), sums)
        ghid_out[0:1, lanes] = row_sum(sums[10])
        for k in range(10):
            ghid_out[1 + k : 2 + k, lanes] = row_sum(sums[k])

    gwe = gws = None
    for s in range(scenes):
        act = act_scr[s * gext + W : s * gext + W + own, :]
        ge = ge_scr[s * own : (s + 1) * own, :]
        term = mm_tn(act, cot[s].reshape(own, C))
        gws = term if gws is None else gws + term
        term = mm_tn(n2[s].reshape(own, C), ge)
        gwe = term if gwe is None else gwe + term
        out_part = mm(act, wrow)
        in_part = mm_nt(ge, wcol)
        at = slice(s * own, (s + 1) * own)

        @pl.when(step == 0)
        def _():
            branch[at, :] = out_part
            gn2[at, :] = in_part

        @pl.when(step > 0)
        def _():
            branch[at, :] += out_part
            gn2[at, :] += in_part

    gws_out[...] = gws
    gwe_out[...] = gwe

    @pl.when(step == pl.num_programs(0) - 1)
    def _():
        size = 4 * W
        per = own // size
        gain = vec[V_GAIN2 : V_GAIN2 + 1, :]

        def finish(i, carry):
            at = pl.multiple_of(i * size, size)
            s = i // per
            line = (i % per) * 4
            middle = mid[pl.ds(at, size), :]
            y_out[pl.ds(at, size), :] = (
                middle + branch[pl.ds(at, size), :] + vec[V_SHRINK : V_SHRINK + 1, :]
            ).astype(BF16)
            grad = gn2[pl.ds(at, size), :]
            unit, rstd = norm_parts(middle)
            direct = cot[s, pl.ds(line, 4)].reshape(size, C).astype(F32)
            gmid_out[pl.ds(at, size), :] = direct + norm_back(grad, unit, rstd, gain)
            return (
                carry[0] + row_sum(grad * unit),
                carry[1] + row_sum(grad),
                carry[2] + row_sum(direct),
            )

        zero = jnp.zeros((1, C), F32)
        sums = lax.fori_loop(0, scenes * per, finish, (zero, zero, zero))
        for i in range(3):
            gvec_out[i : i + 1, :] = sums[i]


def mix(n2, n2_top, n2_low, cot, cot_top, cot_low, mid, edge, vec, hid, we, ws):
    scenes, rows = n2.shape[0], n2.shape[1]
    tokens = scenes * rows * W
    ext = scenes * (rows + 4) * W
    gext = scenes * (rows + 2) * W
    once = dict(pipeline_mode=pl.Buffered(1))
    whole = lambda a: pl.BlockSpec(a.shape, lambda j: (0,) * a.ndim, **once)
    return pl.pallas_call(
        mix_kernel,
        name="mix",
        grid=(FF // CH,),
        in_specs=[
            whole(n2),
            whole(n2_top),
            whole(n2_low),
            whole(cot),
            whole(cot_top),
            whole(cot_low),
            whole(mid),
            pl.BlockSpec(memory_space=pltpu.SMEM),
            whole(vec),
            pl.BlockSpec((16, CH), lambda j: (0, j)),
            pl.BlockSpec((C, CH), lambda j: (0, j)),
            pl.BlockSpec((CH, C), lambda j: (j, 0)),
        ],
        out_specs=[
            full((tokens, C)),
            full((tokens, C)),
            pl.BlockSpec((C, CH), lambda j: (0, j)),
            pl.BlockSpec((CH, C), lambda j: (j, 0)),
            pl.BlockSpec((16, CH), lambda j: (0, j)),
            full((8, C)),
        ],
        out_shape=(
            shape_of((tokens, C), BF16),
            shape_of((tokens, C), F32),
            shape_of((C, FF), F32),
            shape_of((FF, C), F32),
            shape_of((16, FF), F32),
            shape_of((8, C), F32),
        ),
        scratch_shapes=[
            pltpu.VMEM((ext, CH), F32),
            pltpu.VMEM((gext, CH), F32),
            pltpu.VMEM((3, gext, CH), F32),
            pltpu.VMEM((gext, CH), BF16),
            pltpu.VMEM((tokens, CH), BF16),
            pltpu.VMEM((tokens, C), F32),
            pltpu.VMEM((tokens, C), F32),
        ],
        compiler_params=PARAMS,
    )(n2, n2_top, n2_low, cot, cot_top, cot_low, mid, edge, vec, hid, we, ws)


def attend_back_kernel(
    q_ref, lse_ref, mixed_ref, gmid_ref, rn_ref, vec, wk, wv, wo,
    dq_out, grn_out, gwk_out, gwv_out, gwo_out, gvec_out,
    kt, vt, kh, dkt, dvt,
):
    scene, step = pl.program_id(0), pl.program_id(1)
    keys = rn_ref.shape[0] * rn_ref.shape[2]
    start = jnp.logical_and(scene == 0, step == 0)

    @pl.when(start)
    def _():
        for ref in (gwk_out, gwv_out, gwo_out, gvec_out):
            ref[...] = jnp.zeros_like(ref)

    @pl.when(step == 0)
    def _():
        rn = rn_ref[:, 0].reshape(keys, C)
        key = mm(rn, wk[...]).astype(BF16)
        value = (mm(rn, wv[...]) + vec[V_VALUE : V_VALUE + 1, :]).astype(BF16)
        kt[...] = key.T
        vt[...] = value.T
        for h in range(HEADS):
            kh[h] = key[:, h * HD : (h + 1) * HD]
        dkt[...] = jnp.zeros_like(dkt)
        dvt[...] = jnp.zeros_like(dvt)

    gmid = gmid_ref[...]
    gatt = gmid.astype(BF16)
    gvec_out[1:2, :] += row_sum(gatt.astype(F32))
    mixed = mixed_ref[...]
    gwo_out[...] += mm_tn(mixed, gatt)
    gmixed = mm_nt(gatt, wo[...]).astype(BF16)
    prod = gmixed.astype(F32) * mixed.astype(F32)
    q = q_ref[...]
    q_t = q.T
    g_t = gmixed.T
    dqs = []
    for h in range(HEADS):
        cols = slice(h * HD, (h + 1) * HD)
        inner = jnp.sum(prod[:, cols], axis=-1, keepdims=True)
        probs = jnp.exp(mm(q[:, cols], kt[cols, :]) - lse_ref[:, h : h + 1])
        gprobs = mm(gmixed[:, cols], vt[cols, :])
        gscores = (probs * (gprobs - inner)).astype(BF16)
        dqs.append(mm(gscores, kh[h]))
        dkt[cols, :] += mm(q_t[cols, :], gscores)
        dvt[cols, :] += mm(g_t[cols, :], probs.astype(BF16))
    dq_out[...] = (jnp.concatenate(dqs, axis=1) * (1.0 / math.sqrt(HD))).astype(BF16)

    @pl.when(step == pl.num_programs(1) - 1)
    def _():
        rn = rn_ref[:, 0].reshape(keys, C)
        dk = dkt[...].T.astype(BF16)
        dv = dvt[...].T
        gvec_out[0:1, :] += row_sum(dv)
        dv = dv.astype(BF16)
        gwk_out[...] += mm_tn(rn, dk)
        gwv_out[...] += mm_tn(rn, dv)
        grn = mm_nt(dk, wk[...]) + mm_nt(dv, wv[...])
        grn_out[...] = grn.astype(BF16).reshape(grn_out.shape)


def attend_back(q, lse, mixed, gmid, rn_all, vec, wk, wv, wo):
    tokens = q.shape[0]
    bands, scenes, per_band, _ = rn_all.shape
    keys = bands * per_band
    steps = tokens // scenes // QT
    tile = lambda s, i: (s * steps + i, 0)
    return pl.pallas_call(
        attend_back_kernel,
        name="attend_back",
        grid=(scenes, steps),
        in_specs=[
            pl.BlockSpec((QT, C), tile),
            pl.BlockSpec((QT, 128), tile),
            pl.BlockSpec((QT, C), tile),
            pl.BlockSpec((QT, C), tile),
            pl.BlockSpec((bands, 1, per_band, C), lambda s, i: (0, s, 0, 0)),
            full((16, C)),
            full((C, C)),
            full((C, C)),
            full((C, C)),
        ],
        out_specs=[
            pl.BlockSpec((QT, C), tile),
            pl.BlockSpec((bands, 1, per_band, C), lambda s, i: (0, s, 0, 0)),
            full((C, C)),
            full((C, C)),
            full((C, C)),
            full((8, C)),
        ],
        out_shape=(
            shape_of((tokens, C), BF16),
            shape_of(rn_all.shape, BF16),
            shape_of((C, C), F32),
            shape_of((C, C), F32),
            shape_of((C, C), F32),
            shape_of((8, C), F32),
        ),
        scratch_shapes=[
            pltpu.VMEM((C, keys), BF16),
            pltpu.VMEM((C, keys), BF16),
            pltpu.VMEM((HEADS, keys, HD), BF16),
            pltpu.VMEM((C, keys), F32),
            pltpu.VMEM((C, keys), F32),
        ],
        compiler_params=PARAMS,
    )(q, lse, mixed, gmid, rn_all, vec, wk, wv, wo)


def tail_kernel(
    x_ref, gmid_ref, dq_ref, grn_ref, red_ref, vec, wq, wr,
    gx_out, gwq_out, gwr_out, gvec_out, scr, gscr,
):
    @pl.when(pl.program_id(0) == 0)
    def _():
        for ref in (gwq_out, gwr_out, gvec_out):
            ref[...] = jnp.zeros_like(ref)

    runit, rrstd = norm_parts(red_ref[...])
    grn = grn_ref[...].astype(F32)
    gred = norm_back(grn, runit, rrstd, vec[V_RGAIN : V_RGAIN + 1, :]).astype(BF16)
    unit, rstd = norm_parts(x_ref[...].astype(F32))
    gain = vec[V_GAIN1 : V_GAIN1 + 1, :]
    normed = (unit * gain + vec[V_SHIFT1 : V_SHIFT1 + 1, :]).astype(BF16)
    split_tiles(scr, normed.astype(F32))
    pieces = patch_pieces(scr)
    back = {}
    for k in range(4):
        at = slice(k * C, (k + 1) * C)
        gwr_out[at, :] += mm_tn(pieces[k].astype(BF16), gred)
        back[k] = mm_nt(gred, wr[at, :]).reshape(TILE // (2 * W), 1, W // 2, C)
    for b in range(2):
        cols = jnp.concatenate([back[b], back[2 + b]], axis=1).reshape(TILE // 2, C)
        spot = pl.ds(b, TILE // 2, stride=2)
        gscr[0, spot, :] = cols[:, 0:128]
        gscr[1, spot, :] = cols[:, 128:256]
        gscr[2, spot, :] = jnp.concatenate(
            [cols[:, 256:320], jnp.zeros((TILE // 2, 64), F32)], axis=1
        )
    dq = dq_ref[...]
    gwq_out[...] += mm_tn(normed, dq)
    placed = jnp.concatenate([gscr[0], gscr[1], gscr[2][:, 0:64]], axis=1)
    gnormed = mm_nt(dq, wq[...]) + placed
    gx_out[...] = gmid_ref[...] + norm_back(gnormed, unit, rstd, gain)
    gvec_out[0:1, :] += row_sum(dq.astype(F32))
    gvec_out[1:2, :] += row_sum(gred.astype(F32))
    gvec_out[2:3, :] += row_sum(grn * runit)
    gvec_out[3:4, :] += row_sum(grn)
    gvec_out[4:5, :] += row_sum(gnormed * unit)
    gvec_out[5:6, :] += row_sum(gnormed)


def tail(x, gmid, dq, grn, red, vec, wq, wr):
    tokens = x.shape[0]
    tile = pl.BlockSpec((TILE, C), lambda i: (i, 0))
    rtile = pl.BlockSpec((RTILE, C), lambda i: (i, 0))
    return pl.pallas_call(
        tail_kernel,
        name="tail",
        grid=(tokens // TILE,),
        in_specs=[
            tile, tile, tile, rtile, rtile, full((16, C)), full((C, C)), full((4 * C, C))
        ],
        out_specs=[tile, full((C, C)), full((4 * C, C)), full((8, C))],
        out_shape=(
            shape_of((tokens, C), F32),
            shape_of((C, C), F32),
            shape_of((4 * C, C), F32),
            shape_of((8, C), F32),
        ),
        scratch_shapes=[pltpu.VMEM((3, TILE, 128), F32), pltpu.VMEM((3, TILE, 128), F32)],
        compiler_params=PARAMS,
    )(x, gmid, dq, grn, red, vec, wq, wr)


ANY = pl.BlockSpec(memory_space=pl.ANY)
VM = pl.BlockSpec(memory_space=pltpu.VMEM)


def flip(value, by):
    return value + by * (1 - 2 * value)


def remote(src, dst, send, recv, where):
    return pltpu.make_async_remote_copy(
        src_ref=src,
        dst_ref=dst,
        send_sem=send,
        recv_sem=recv,
        device_id=where,
        device_id_type=pl.DeviceIdType.MESH,
    )


def greet(places):
    barrier = pltpu.get_barrier_semaphore()
    count = 0
    for place, there in places:
        if there is None:
            pl.semaphore_signal(
                barrier, inc=1, device_id=place, device_id_type=pl.DeviceIdType.MESH
            )
            count = count + 1
        else:

            @pl.when(there)
            def _():
                pl.semaphore_signal(
                    barrier, inc=1, device_id=place, device_id_type=pl.DeviceIdType.MESH
                )

            count = count + there.astype(jnp.int32)
    pl.semaphore_wait(barrier, count)


def comm_params(number):
    return pltpu.CompilerParams(
        collective_id=number, has_side_effects=True, vmem_limit_bytes=60 * 1024 * 1024
    )


class Place:
    def __init__(self):
        dp, space = lax.axis_index("dp"), lax.axis_index("space")
        self.z, self.x = dp // 2, dp % 2
        self.y, self.c = space // 2, space % 2
        self.line = lax.axis_size("dp") // 2

    def block(self, z, x, y, c):
        return ((z * 2 + x) * 2 + y) * 2 + c

    def device(self, z, x, y, c):
        return {"dp": z * 2 + x, "space": y * 2 + c}

    def spot(self, da, db, c):
        return (
            flip(self.x, da * (1 - c) + db * c),
            flip(self.y, db * (1 - c) + da * c),
        )

    def partners(self):
        ax, ay = self.spot(1, 0, self.c)
        bx, by = self.spot(0, 1, self.c)
        return (
            self.device(self.z, ax, ay, self.c),
            self.device(self.z, bx, by, self.c),
            self.device(self.z, self.x, self.y, 1 - self.c),
            self.device(self.z + 1, self.x, self.y, self.c),
            self.device(self.z - 1, self.x, self.y, self.c),
        )

    def meet(self):
        first, second, sibling, up, down = self.partners()
        greet(
            [
                (first, None),
                (second, None),
                (sibling, None),
                (up, self.z < self.line - 1),
                (down, self.z > 0),
            ]
        )


def gather_kernel(own, out, up_sem, down_sem, a_sem, b_sem, c_sem, recv):
    at = Place()
    line = at.line
    first, second, sibling, up, down = at.partners()
    at.meet()
    can_up, can_down = at.z < line - 1, at.z > 0

    def block_of(z, da, db):
        x, y = at.spot(da, db, at.c)
        return at.block(z, x, y, at.c)

    def push(index, src, sem, where):
        remote(src, out.at[index], sem, recv.at[index], where).start()

    def landed(index):
        remote(out.at[index], out.at[index], c_sem.at[0], recv.at[index], sibling).wait_recv()

    def slot_sends(z, da, db, src):
        index = block_of(z, da, db)
        if da == 0 and db == 0:
            push(index, src, a_sem.at[z], first)
        if db == 0:
            push(index, src, b_sem.at[da * line + z], second)
        push(index, src, c_sem.at[(da * 2 + db) * line + z], sibling)

    mine = block_of(at.z, 0, 0)

    @pl.when(can_up)
    def _():
        push(mine, own, up_sem.at[at.z], up)

    @pl.when(can_down)
    def _():
        push(mine, own, down_sem.at[at.z], down)

    slot_sends(at.z, 0, 0, own)
    out[mine] = own[...]

    def along(da, db, act):
        for d in range(1, line):

            @pl.when(at.z - d >= 0)
            def _():
                act(at.z - d, da, db, 1)

            @pl.when(at.z + d < line)
            def _():
                act(at.z + d, da, db, -1)

    def relay(z, da, db, way):
        index = block_of(z, da, db)
        landed(index)
        if da == 0 and db == 0:
            if way > 0:

                @pl.when(can_up)
                def _():
                    push(index, out.at[index], up_sem.at[z], up)

            else:

                @pl.when(can_down)
                def _():
                    push(index, out.at[index], down_sem.at[z], down)

        slot_sends(z, da, db, out.at[index])

    along(0, 0, relay)
    for da, db in ((1, 0), (0, 1), (1, 1)):
        relay(at.z, da, db, 0)
        along(da, db, relay)
    for da in range(2):
        for db in range(2):
            for z in range(line):
                x, y = at.spot(da, db, at.c)
                landed(at.block(z, x, y, 1 - at.c))
    def sent(sem, where):
        remote(own, out.at[mine], sem, recv.at[mine], where).wait_send()

    for z in range(line):

        @pl.when(jnp.logical_and(can_up, z <= at.z))
        def _():
            sent(up_sem.at[z], up)

        @pl.when(jnp.logical_and(can_down, z >= at.z))
        def _():
            sent(down_sem.at[z], down)

        sent(a_sem.at[z], first)
        for da in range(2):
            sent(b_sem.at[da * line + z], second)
            for db in range(2):
                sent(c_sem.at[(da * 2 + db) * line + z], sibling)


def gather_blocks(own):
    dma = pltpu.SemaphoreType.DMA
    return pl.pallas_call(
        gather_kernel,
        name="gather",
        out_shape=shape_of((BLOCKS,) + own.shape, own.dtype),
        in_specs=[VM],
        out_specs=VM,
        scratch_shapes=[dma((4,)), dma((4,)), dma((4,)), dma((8,)), dma((16,)), dma((BLOCKS,))],
        compiler_params=comm_params(1),
    )(own)


def scatter_kernel(
    parts, out, rc, acc, ra, acc2, rb, acc3, rup, rdown, sup, sdown,
    c_sem, a_sem, b_sem, up_sem, down_sem, c_in, a_in, b_in, up_in, down_in,
):
    at = Place()
    line = at.line
    first, second, sibling, up, down = at.partners()
    at.meet()
    can_up, can_down = at.z < line - 1, at.z > 0
    slots = [(da, db, z) for da in (1, 0) for db in (1, 0) for z in range(line)]

    def add(left, right):
        return (left.astype(F32) + right.astype(F32)).astype(BF16)

    def c_copy(k):
        da, db, z = slots[k]
        x, y = at.spot(da, db, 1 - at.c)
        return remote(
            parts.at[at.block(z, x, y, 1 - at.c)], rc.at[k], c_sem.at[k], c_in.at[k], sibling
        )

    def a_copy(j):
        return remote(acc.at[j], ra.at[j], a_sem.at[j], a_in.at[j], first)

    def b_copy(j):
        return remote(acc2.at[j], rb.at[j], b_sem.at[j], b_in.at[j], second)

    def up_copy(z):
        return remote(sup.at[z], rup.at[z], up_sem.at[z], up_in.at[z], up)

    def down_copy(z):
        return remote(sdown.at[z], rdown.at[z], down_sem.at[z], down_in.at[z], down)

    for k in range(4 * line):
        c_copy(k).start()
    for k in range(4 * line):
        c_copy(k).wait_recv()
        da, db, z = slots[k]
        x, y = at.spot(da, db, at.c)
        acc[k] = add(parts[at.block(z, x, y, at.c)], rc[k])
        if da:
            a_copy(k).start()
    for j in range(2 * line):
        a_copy(j).wait_recv()
        acc2[j] = add(acc[2 * line + j], ra[j])
        if j < line:
            b_copy(j).start()
    for z in range(line):
        b_copy(z).wait_recv()
        acc3[z] = add(acc2[line + z], rb[z])
    for z in reversed(range(line)):

        @pl.when(z > at.z)
        def _():
            sup[z] = acc3[z]

            @pl.when(can_down)
            def _():
                up_copy(z).wait_recv()
                sup[z] = add(acc3[z], rup[z])

            up_copy(z).start()

        mirror = line - 1 - z

        @pl.when(mirror < at.z)
        def _():
            sdown[mirror] = acc3[mirror]

            @pl.when(can_up)
            def _():
                down_copy(mirror).wait_recv()
                sdown[mirror] = add(acc3[mirror], rdown[mirror])

            down_copy(mirror).start()

    for z in range(line):

        @pl.when(z == at.z)
        def _():
            out[...] = acc3[z].astype(F32)

            @pl.when(can_down)
            def _():
                up_copy(z).wait_recv()
                out[...] += rup[z].astype(F32)

            @pl.when(can_up)
            def _():
                down_copy(z).wait_recv()
                out[...] += rdown[z].astype(F32)

    for k in range(4 * line):
        c_copy(k).wait_send()
    for j in range(2 * line):
        a_copy(j).wait_send()
    for z in range(line):
        b_copy(z).wait_send()

        @pl.when(z > at.z)
        def _():
            up_copy(z).wait_send()

        @pl.when(z < at.z)
        def _():
            down_copy(z).wait_send()


def scatter_blocks(parts):
    one = parts.shape[1:]
    dma = pltpu.SemaphoreType.DMA
    room = lambda n: pltpu.VMEM((n,) + one, BF16)
    return pl.pallas_call(
        scatter_kernel,
        name="scatter",
        out_shape=shape_of(one, F32),
        in_specs=[VM],
        out_specs=VM,
        scratch_shapes=[
            room(16), room(16), room(8), room(8), room(4), room(4),
            room(4), room(4), room(4), room(4),
        ]
        + [dma((n,)) for n in (16, 8, 4, 4, 4, 16, 8, 4, 4, 4)],
        compiler_params=comm_params(2),
    )(parts)


def bands_of():
    band = lax.axis_index("space")
    pair, core = band // 2, band % 2
    return band, pair * 2 + 1 - core, (1 - pair) * 2 + core


def swap_kernel(width, value, above, below, up_sem, down_sem, up_in, down_in, ready):
    band = lax.axis_index("space")
    rows = value.shape[1]
    ends = lax.axis_size("space") - 1
    down = remote(
        value.at[:, pl.ds(rows - width, width)], above, down_sem, down_in, {"space": band + 1}
    )
    up = remote(value.at[:, pl.ds(0, width)], below, up_sem, up_in, {"space": band - 1})

    @pl.when(band < ends)
    def _():
        down.start()

    @pl.when(band > 0)
    def _():
        up.start()

    def finish():
        @pl.when(band < ends)
        def _():
            down.wait_send()
            up.wait_recv()

        @pl.when(band > 0)
        def _():
            up.wait_send()
            down.wait_recv()

    return finish


def bands_meet(others):
    band = lax.axis_index("space")
    ends = lax.axis_size("space") - 1
    greet(
        [({"space": o}, None) for o in others]
        + [({"space": band + 1}, band < ends), ({"space": band - 1}, band > 0)]
    )


def share_kernel(
    rn, cot, rn_all, above, below, send, recv, own_sem, up_sem, down_sem, up_in, down_in
):
    band, sibling, across = bands_of()
    bands_meet((sibling, across))
    to_sibling = remote(rn, rn_all.at[band], send.at[0], recv.at[band], {"space": sibling})
    to_across = remote(rn, rn_all.at[band], send.at[1], recv.at[band], {"space": across})
    to_across.start()
    to_sibling.start()
    own = pltpu.make_async_copy(rn, rn_all.at[band], own_sem)
    own.start()
    finish = swap_kernel(1, cot, above, below, up_sem, down_sem, up_in, down_in, None)

    def landed(index):
        remote(rn, rn_all.at[index], send.at[0], recv.at[index], {"space": sibling}).wait_recv()

    landed(across)
    onward = remote(
        rn_all.at[across], rn_all.at[across], send.at[2], recv.at[across], {"space": sibling}
    )
    onward.start()
    landed(sibling)
    landed(across + sibling - band)
    own.wait()
    to_across.wait_send()
    to_sibling.wait_send()
    onward.wait_send()
    finish()


def share(rn, cot):
    bands = lax.axis_size("space")
    dma = pltpu.SemaphoreType.DMA
    edge = (cot.shape[0], 1) + cot.shape[2:]
    return pl.pallas_call(
        share_kernel,
        name="share",
        out_shape=(
            shape_of((bands,) + rn.shape, rn.dtype),
            shape_of(edge, cot.dtype),
            shape_of(edge, cot.dtype),
        ),
        in_specs=[VM, ANY],
        out_specs=(ANY, ANY, ANY),
        scratch_shapes=[dma((3,)), dma((bands,)), dma, dma, dma, dma, dma],
        compiler_params=comm_params(3),
    )(rn, cot)


def halo_kernel(value, above, below, up_sem, down_sem, up_in, down_in):
    bands_meet(())
    swap_kernel(2, value, above, below, up_sem, down_sem, up_in, down_in, None)()


def halo(value):
    dma = pltpu.SemaphoreType.DMA
    edge = (value.shape[0], 2) + value.shape[2:]
    return pl.pallas_call(
        halo_kernel,
        name="halo",
        out_shape=(shape_of(edge, value.dtype), shape_of(edge, value.dtype)),
        in_specs=[ANY],
        out_specs=(ANY, ANY),
        scratch_shapes=[dma, dma, dma, dma],
        compiler_params=comm_params(4),
    )(value)


def merge_kernel(parts, out, rc, acc, rb, c_sem, c_in, b_sem, b_in):
    band, sibling, across = bands_of()
    greet([({"space": sibling}, None), ({"space": across}, None)])
    far = across + sibling - band
    first = remote(parts.at[far], rc.at[0], c_sem.at[0], c_in.at[0], {"space": sibling})
    second = remote(parts.at[sibling], rc.at[1], c_sem.at[1], c_in.at[1], {"space": sibling})
    onward = remote(acc, rb, b_sem, b_in, {"space": across})
    first.start()
    second.start()
    first.wait_recv()
    acc[...] = (parts[across].astype(F32) + rc[0].astype(F32)).astype(BF16)
    onward.start()
    second.wait_recv()
    out[...] = parts[band].astype(F32) + rc[1].astype(F32)
    onward.wait_recv()
    out[...] += rb[...].astype(F32)
    first.wait_send()
    second.wait_send()
    onward.wait_send()


def merge(parts):
    one = parts.shape[1:]
    dma = pltpu.SemaphoreType.DMA
    return pl.pallas_call(
        merge_kernel,
        name="merge",
        out_shape=shape_of(one, F32),
        in_specs=[VM],
        out_specs=VM,
        scratch_shapes=[
            pltpu.VMEM((2,) + one, BF16),
            pltpu.VMEM(one, BF16),
            pltpu.VMEM(one, BF16),
            dma((2,)),
            dma((2,)),
            dma,
            dma,
        ],
        compiler_params=comm_params(5),
    )(parts)


def blocks_fit(size):
    return (
        lax.axis_size("dp") == 8 and lax.axis_size("space") == 4 and size == BLOCK_ROWS * C
    )


def gather_params(params):
    if blocks_fit(params.shape[0]):
        return gather_blocks(params.reshape(BLOCK_ROWS, C))
    flat = lax.all_gather(params, ("dp", "space"), axis=0, tiled=True)
    want = ROWS * C
    flat = flat[:want] if flat.shape[0] >= want else jnp.pad(flat, (0, want - flat.shape[0]))
    return flat.reshape(BLOCKS, BLOCK_ROWS, C)


def scatter_grads(blocks, size):
    if blocks_fit(size):
        return scatter_blocks(blocks).reshape(size)
    flat = blocks.reshape(-1)
    want = size * lax.axis_size("dp") * lax.axis_size("space")
    flat = flat[:want] if flat.shape[0] >= want else jnp.pad(flat, (0, want - flat.shape[0]))
    own = lax.psum_scatter(flat, ("dp", "space"), scatter_dimension=0, tiled=True)
    return own.astype(F32)


def on_device(scenes, params, cotangent):
    count, rows, breadth = scenes.shape[0], scenes.shape[1], scenes.shape[2]
    tokens = count * rows * breadth
    bands = lax.axis_size("space")
    per_band = rows * breadth // 4
    band = lax.axis_index("space")
    edge = jnp.stack([band > 0, band < bands - 1]).astype(F32)
    wq, wr, wk, wv, wo, we, ws, vec, hid = unpack(gather_params(params))
    x = scenes.reshape(tokens, C)
    q, red, rn = front(x, vec, wq, wr)
    rn_all, cot_top, cot_low = share(rn, cotangent)
    rn_all = rn_all.reshape(bands, count, per_band, C)
    mixed, lse, mid, n2 = attend(x, q, rn_all, vec, wk, wv, wo)
    n2 = n2.reshape(scenes.shape)
    n2_top, n2_low = halo(n2)
    y, gmid, gwe, gws, ghid, gvec2 = mix(
        n2, n2_top, n2_low, cotangent, cot_top, cot_low, mid, edge, vec, hid, we, ws
    )
    dq, grn_all, gwk, gwv, gwo, gvec1 = attend_back(
        q, lse, mixed, gmid, rn_all, vec, wk, wv, wo
    )
    grn = merge(grn_all.reshape(bands, count * per_band, C))
    gx, gwq, gwr, gvec0 = tail(x, gmid, dq, grn, red, vec, wq, wr)
    blocks = pack(gwq, gwr, gwk, gwv, gwo, gwe, gws, gvec0, gvec1, gvec2, ghid)
    shard = scatter_grads(blocks, params.shape[0])
    return y.reshape(scenes.shape), gx.reshape(scenes.shape), shard


def solution(mesh):
    band = P("dp", "space", None, None)
    flat = P(("dp", "space"))
    return jax.shard_map(
        on_device,
        mesh=mesh,
        in_specs=(band, flat, band),
        out_specs=(band, band, flat),
        check_vma=False,
    )
```

```python
import functools
import math

import jax
import jax.numpy as jnp
from jax import lax
from jax.experimental import pallas as pl
from jax.experimental.pallas import tpu as pltpu
from jax.sharding import PartitionSpec as P

C = 320
HEADS = 5
HD = 64
FF = 1280
W = 64
EPSILON = 1e-06
F32 = jnp.float32
BF16 = jnp.bfloat16

ROWS = 5184
USED_ROWS = 5175
BLOCKS = 32
BLOCK_ROWS = ROWS // BLOCKS
R_QUERY = 0
R_REDUCE = 321
R_KEYVAL = 1604
R_OUTPUT = 2245
R_EXPAND = 2570
R_HIDDEN = 3850
R_SHRINK = 3894
VECTOR_ROWS = (320, 1601, 1602, 1603, 2244, 2565, 2566, 2567, 2568, 2569, 5174)
(
    V_QUERY,
    V_REDUCE,
    V_RGAIN,
    V_RSHIFT,
    V_VALUE,
    V_OUTPUT,
    V_GAIN1,
    V_SHIFT1,
    V_GAIN2,
    V_SHIFT2,
    V_SHRINK,
) = range(11)
HIDDEN_ROWS = 11

PARAMS = pltpu.CompilerParams(vmem_limit_bytes=60 * 1024 * 1024)


def shape_of(dims, kind):
    return jax.ShapeDtypeStruct(dims, kind)


def mm(left, right):
    return jnp.dot(left, right, preferred_element_type=F32)


def mm_tn(left, right):
    return lax.dot_general(left, right, (((0,), (0,)), ((), ())), preferred_element_type=F32)


def mm_nt(left, right):
    return lax.dot_general(left, right, (((1,), (1,)), ((), ())), preferred_element_type=F32)


def mm_tt(left, right):
    return lax.dot_general(left, right, (((0,), (1,)), ((), ())), preferred_element_type=F32)


def norm_parts(values):
    center = values - jnp.mean(values, axis=-1, keepdims=True)
    rstd = lax.rsqrt(jnp.mean(center * center, axis=-1, keepdims=True) + EPSILON)
    return center * rstd, rstd


def norm_back(grad, unit, rstd, gain):
    scaled = grad * gain
    first = jnp.mean(scaled, axis=-1, keepdims=True)
    second = jnp.mean(scaled * unit, axis=-1, keepdims=True)
    return rstd * (scaled - first - unit * second)


def row_sum(values):
    return jnp.sum(values, axis=0, keepdims=True)


def full(dims):
    return pl.BlockSpec(dims, lambda *_: (0,) * len(dims))


def unpack_kernel(g_ref, wq, wr, wk, wv, wo, we, ws, vec, hid, rows, tiles):
    for i in range(BLOCKS):
        at = i * BLOCK_ROWS
        block = g_ref[i].astype(F32)
        rows[at : at + BLOCK_ROWS, :] = block
        tiles[0, at : at + BLOCK_ROWS, :] = block[:, 0:128]
        tiles[1, at : at + BLOCK_ROWS, :] = block[:, 128:256]
        tiles[2, at : at + BLOCK_ROWS, 0:64] = block[:, 256:320]

    def strided(start, count, step):
        parts = [tiles[t, pl.ds(start, count, stride=step), :] for t in range(3)]
        return jnp.concatenate([parts[0], parts[1], parts[2][:, 0:64]], axis=1)

    wq[...] = rows[R_QUERY : R_QUERY + C, :].astype(BF16)
    wr[...] = rows[R_REDUCE : R_REDUCE + 4 * C, :].astype(BF16)
    wk[...] = strided(R_KEYVAL, C, 2).astype(BF16)
    wv[...] = strided(R_KEYVAL + 1, C, 2).astype(BF16)
    wo[...] = rows[R_OUTPUT : R_OUTPUT + C, :].astype(BF16)
    ws[...] = rows[R_SHRINK : R_SHRINK + FF, :].astype(BF16)
    we[...] = jnp.concatenate([strided(R_EXPAND + j, C, 4) for j in range(4)], axis=1).astype(BF16)
    hid[0:HIDDEN_ROWS, :] = jnp.concatenate(
        [strided(R_HIDDEN + j, HIDDEN_ROWS, 4) for j in range(4)], axis=1
    )
    for i, row in enumerate(VECTOR_ROWS):
        vec[i : i + 1, :] = rows[row : row + 1, :]


def unpack(blocks):
    return pl.pallas_call(
        unpack_kernel,
        name="unpack",
        out_shape=(
            shape_of((C, C), BF16),
            shape_of((4 * C, C), BF16),
            shape_of((C, C), BF16),
            shape_of((C, C), BF16),
            shape_of((C, C), BF16),
            shape_of((C, FF), BF16),
            shape_of((FF, C), BF16),
            shape_of((16, C), F32),
            shape_of((16, FF), F32),
        ),
        scratch_shapes=[pltpu.VMEM((ROWS, C), F32), pltpu.VMEM((3, ROWS, 128), F32)],
        compiler_params=PARAMS,
    )(blocks)


def pack_kernel(gwq, gwr, gwk, gwv, gwo, gwe, gws, gvec0, gvec1, gvec2, ghid, out, tiles):
    def put(start, value):
        count = value.shape[0]
        tiles[0, start : start + count, :] = value[:, 0:128]
        tiles[1, start : start + count, :] = value[:, 128:256]
        tiles[2, start : start + count, 0:64] = value[:, 256:320]

    def put_strided(start, step, value):
        count = value.shape[0]
        tiles[0, pl.ds(start, count, stride=step), :] = value[:, 0:128]
        tiles[1, pl.ds(start, count, stride=step), :] = value[:, 128:256]
        tail = jnp.concatenate([value[:, 256:320], jnp.zeros((count, 64), F32)], axis=1)
        tiles[2, pl.ds(start, count, stride=step), :] = tail

    put(R_QUERY, gwq[...])
    put(R_REDUCE, gwr[...])
    put_strided(R_KEYVAL, 2, gwk[...])
    put_strided(R_KEYVAL + 1, 2, gwv[...])
    put(R_OUTPUT, gwo[...])
    put(R_SHRINK, gws[...].T)
    for j in range(4):
        put_strided(R_EXPAND + j, 4, gwe[:, C * j : C * j + C])
        put_strided(R_HIDDEN + j, 4, ghid[0:HIDDEN_ROWS, C * j : C * j + C])
    for source, names in (
        (gvec0, (V_QUERY, V_REDUCE, V_RGAIN, V_RSHIFT, V_GAIN1, V_SHIFT1)),
        (gvec1, (V_VALUE, V_OUTPUT)),
        (gvec2, (V_GAIN2, V_SHIFT2, V_SHRINK)),
    ):
        for i, name in enumerate(names):
            put(VECTOR_ROWS[name], source[i : i + 1, :])
    put(USED_ROWS, jnp.zeros((ROWS - USED_ROWS, C), F32))
    for i in range(BLOCKS):
        at = i * BLOCK_ROWS
        out[i, :, 0:128] = tiles[0, at : at + BLOCK_ROWS, :].astype(BF16)
        out[i, :, 128:256] = tiles[1, at : at + BLOCK_ROWS, :].astype(BF16)
        out[i, :, 256:320] = tiles[2, at : at + BLOCK_ROWS, 0:64].astype(BF16)


def pack(*pieces):
    return pl.pallas_call(
        pack_kernel,
        name="pack",
        out_shape=shape_of((BLOCKS, BLOCK_ROWS, C), BF16),
        scratch_shapes=[pltpu.VMEM((3, ROWS, 128), F32)],
        compiler_params=PARAMS,
    )(*pieces)


TILE = 8 * W
RTILE = TILE // 4


def split_tiles(scr, value):
    scr[0, :, :] = value[:, 0:128]
    scr[1, :, :] = value[:, 128:256]
    scr[2, :, 0:64] = value[:, 256:320]


def patch_pieces(scr):
    pieces = {}
    for b in range(2):
        parts = [scr[t, pl.ds(b, TILE // 2, stride=2), :] for t in range(3)]
        cols = jnp.concatenate([parts[0], parts[1], parts[2][:, 0:64]], axis=1)
        cols = cols.reshape(TILE // (2 * W), 2, W // 2, C)
        for a in range(2):
            pieces[2 * a + b] = cols[:, a].reshape(RTILE, C)
    return pieces


def front_kernel(x_ref, vec, wq, wr, q_out, red_out, rn_out, scr):
    unit, _ = norm_parts(x_ref[...].astype(F32))
    normed = (unit * vec[V_GAIN1 : V_GAIN1 + 1, :] + vec[V_SHIFT1 : V_SHIFT1 + 1, :]).astype(BF16)
    queries = (mm(normed, wq[...]) + vec[V_QUERY : V_QUERY + 1, :]).astype(BF16)
    q_out[...] = queries * jnp.asarray(1.0 / math.sqrt(HD), BF16)
    split_tiles(scr, normed.astype(F32))
    pieces = patch_pieces(scr)
    reduced = vec[V_REDUCE : V_REDUCE + 1, :]
    for k in range(4):
        reduced = reduced + mm(pieces[k].astype(BF16), wr[k * C : (k + 1) * C, :])
    red_out[...] = reduced
    unit, _ = norm_parts(reduced)
    rn_out[...] = (unit * vec[V_RGAIN : V_RGAIN + 1, :] + vec[V_RSHIFT : V_RSHIFT + 1, :]).astype(
        BF16
    )


def front(x, vec, wq, wr):
    tokens = x.shape[0]
    return pl.pallas_call(
        front_kernel,
        name="front",
        grid=(tokens // TILE,),
        in_specs=[
            pl.BlockSpec((TILE, C), lambda i: (i, 0)),
            full((16, C)),
            full((C, C)),
            full((4 * C, C)),
        ],
        out_specs=[
            pl.BlockSpec((TILE, C), lambda i: (i, 0)),
            pl.BlockSpec((RTILE, C), lambda i: (i, 0)),
            pl.BlockSpec((RTILE, C), lambda i: (i, 0)),
        ],
        out_shape=(
            shape_of((tokens, C), BF16),
            shape_of((tokens // 4, C), F32),
            shape_of((tokens // 4, C), BF16),
        ),
        scratch_shapes=[pltpu.VMEM((3, TILE, 128), F32)],
        compiler_params=PARAMS,
    )(x, vec, wq, wr)


QT = 256


def attend_kernel(
    x_ref, q_ref, rn_ref, vec, wk, wv, wo, mixed_out, lse_out, mid_out, n2_out, kt, vones
):
    keys = rn_ref.shape[0] * rn_ref.shape[2]

    @pl.when(pl.program_id(1) == 0)
    def _():
        rn = rn_ref[:, 0].reshape(keys, C)
        key = mm(rn, wk[...]).astype(BF16)
        value = (mm(rn, wv[...]) + vec[V_VALUE : V_VALUE + 1, :]).astype(BF16)
        kt[...] = key.T
        for h in range(HEADS):
            vones[h, :, 0:HD] = value[:, h * HD : (h + 1) * HD]
            vones[h, :, HD:] = jnp.ones((keys, HD), BF16)

    lane = lax.broadcasted_iota(jnp.int32, (QT, 128), 1)
    lses = jnp.zeros((QT, 128), F32)
    outs = []
    for h in range(HEADS):
        scores = mm(q_ref[:, h * HD : (h + 1) * HD], kt[h * HD : (h + 1) * HD, :])
        top = jnp.max(scores, axis=-1, keepdims=True)
        probs = jnp.exp(scores - top).astype(BF16)
        both = mm(probs, vones[h])
        outs.append(both[:, 0:HD] / both[:, HD:])
        lses = jnp.where(lane == h, top + jnp.log(both[:, HD : HD + 1]), lses)
    mixed = jnp.concatenate(outs, axis=1).astype(BF16)
    mixed_out[...] = mixed
    lse_out[...] = lses
    middle = x_ref[...].astype(F32) + mm(mixed, wo[...]) + vec[V_OUTPUT : V_OUTPUT + 1, :]
    mid_out[...] = middle
    unit, _ = norm_parts(middle)
    n2_out[...] = (unit * vec[V_GAIN2 : V_GAIN2 + 1, :] + vec[V_SHIFT2 : V_SHIFT2 + 1, :]).astype(
        BF16
    )


def attend(x, q, rn_all, vec, wk, wv, wo):
    tokens = x.shape[0]
    bands, scenes, per_band, _ = rn_all.shape
    keys = bands * per_band
    steps = tokens // scenes // QT
    tile = lambda s, i: (s * steps + i, 0)
    return pl.pallas_call(
        attend_kernel,
        name="attend",
        grid=(scenes, steps),
        in_specs=[
            pl.BlockSpec((QT, C), tile),
            pl.BlockSpec((QT, C), tile),
            pl.BlockSpec((bands, 1, per_band, C), lambda s, i: (0, s, 0, 0)),
            full((16, C)),
            full((C, C)),
            full((C, C)),
            full((C, C)),
        ],
        out_specs=[
            pl.BlockSpec((QT, C), tile),
            pl.BlockSpec((QT, 128), tile),
            pl.BlockSpec((QT, C), tile),
            pl.BlockSpec((QT, C), tile),
        ],
        out_shape=(
            shape_of((tokens, C), BF16),
            shape_of((tokens, 128), F32),
            shape_of((tokens, C), F32),
            shape_of((tokens, C), BF16),
        ),
        scratch_shapes=[pltpu.VMEM((C, keys), BF16), pltpu.VMEM((HEADS, keys, 2 * HD), BF16)],
        compiler_params=PARAMS,
    )(x, q, rn_all, vec, wk, wv, wo)


CH = 256


SHRINK_IN = math.sqrt(0.5 * math.log2(math.e))
SLOPE = 1.0 / (math.sqrt(2.0 * math.pi) * SHRINK_IN)
ACT_SCALE = SLOPE / SHRINK_IN
ERF_RATE = 0.3275911 * math.sqrt(0.5) / SHRINK_IN
ERF_TERMS = [
    0.5 * k / SLOPE
    for k in (0.254829592, -0.284496736, 1.421413741, -1.453152027, 1.061405429)
]


def gelu_parts(u):
    size = jnp.abs(u)
    t = 1.0 / (1.0 + ERF_RATE * size)
    poly = ERF_TERMS[4]
    for term in ERF_TERMS[3::-1]:
        poly = term + t * poly
    bell = jnp.exp2(-(u * u))
    tail = (t * poly) * bell
    return jnp.where(u >= 0, 1.0 / SLOPE - tail, tail), bell


def mix_kernel(
    n2, n2_top, n2_low, cot, cot_top, cot_low, mid, edge, vec, hid, we, ws,
    y_out, gmid_out, gwe_out, gws_out, ghid_out, gvec_out,
    nx, cx, nt, ct, e_scr, e_low, ga_scr, gc_scr, act_scr, ge_scr, branch, gn2,
):
    step = pl.program_id(0)
    scenes, rows = n2.shape[0], n2.shape[1]
    ext = (rows + 4) * W
    gext = (rows + 2) * W
    own = rows * W
    top, low = edge[0], edge[1]

    @pl.when(step == 0)
    def _():
        def inside(value, there):
            return jnp.where(there > 0, value.astype(F32), 0.0).astype(BF16)

        for s in range(scenes):
            mine = n2[s].reshape(own, C)
            nx[s * ext : s * ext + 2 * W, :] = n2_top[s].reshape(2 * W, C)
            nx[s * ext + 2 * W : s * ext + 2 * W + own, :] = mine
            nx[s * ext + 2 * W + own : (s + 1) * ext, :] = n2_low[s].reshape(2 * W, C)
            nt[0:C, s * own : (s + 1) * own] = mine.T
            mine = cot[s].reshape(own, C)
            cx[s * gext : s * gext + W, :] = inside(cot_top[s].reshape(W, C), top)
            cx[s * gext + W : s * gext + W + own, :] = mine
            cx[s * gext + W + own : (s + 1) * gext, :] = inside(cot_low[s].reshape(W, C), low)
            ct[:, s * own : (s + 1) * own] = mine.T
        nt[C:, :] = jnp.ones((16, scenes * own), BF16)
        branch[...] = jnp.zeros_like(branch)
        gn2[...] = jnp.zeros_like(gn2)

    wcol = we[...]
    wrow = ws[...]
    body = (mm(nx[...], wcol) + hid[0:1, :]).astype(BF16)
    e_low[...] = body
    e_scr[...] = body.astype(F32)
    ga_scr[...] = mm_nt(cx[...], wrow)
    for there, start in ((top, 0), (low, 2 * W + own)):

        @pl.when(there == 0)
        def _():
            for s in range(scenes):
                e_scr[s * ext + start : s * ext + start + 2 * W, :] = jnp.zeros((2 * W, CH), F32)

    col = lax.broadcasted_iota(jnp.int32, (8, CH), 0)
    first, last = col == 0, col == 7

    def right(value):
        moved = pltpu.roll(value, 1, axis=0)
        return jnp.concatenate([jnp.where(first, 0.0, moved[0:8]), moved[8:]], axis=0)

    def left(value):
        moved = pltpu.roll(value, W - 1, axis=0)
        return jnp.concatenate([moved[: W - 8], jnp.where(last, 0.0, moved[W - 8 :])], axis=0)

    def fold(value):
        value = value[0:32] + value[32:64]
        value = value[0:16] + value[16:32]
        return (value[0:8] + value[8:16]).astype(F32)

    taps = [hid[1 + k : 2 + k, :] * SHRINK_IN for k in range(9)]
    low_taps = [hid[1 + k : 2 + k, :].astype(BF16) for k in range(9)]
    conv_bias = hid[10:11, :] * SHRINK_IN

    for s in range(scenes):

        def forward(r, carry):
            at = pl.multiple_of(s * ext + r * W, W)
            lines = [e_scr[pl.ds(at + a * W, W), :] for a in range(3)]
            sums = [
                lines[0] * taps[b] + lines[1] * taps[3 + b] + lines[2] * taps[6 + b]
                for b in range(3)
            ]
            u = conv_bias + right(sums[0]) + sums[1] + left(sums[2])
            cdf, bell = gelu_parts(u)
            gat = pl.multiple_of(s * gext + r * W, W)
            gc = ga_scr[pl.ds(gat, W), :] * (cdf + u * bell)
            act_scr[pl.ds(gat, W), :] = (u * cdf).astype(BF16)
            gc_scr[0, pl.ds(gat, W), :] = left(gc).astype(BF16)
            gc_scr[1, pl.ds(gat, W), :] = gc.astype(BF16)
            gc_scr[2, pl.ds(gat, W), :] = right(gc).astype(BF16)
            return carry

        lax.fori_loop(0, rows + 2, forward, 0)

    def backward(s, r, carry):
        line = e_low[pl.ds(pl.multiple_of(s * ext + (r + 2) * W, W), W), :]
        grads = list(carry)
        total = None
        for a in range(3):
            gat = pl.multiple_of(s * gext + (r + 2 - a) * W, W)
            for b in range(3):
                g = gc_scr[b, pl.ds(gat, W), :]
                term = g * low_taps[3 * a + b]
                total = term if total is None else total + term
                grads[3 * a + b] = grads[3 * a + b] + fold(g * line)
                if a == 1 and b == 1:
                    grads[9] = grads[9] + fold(g)
        ge_scr[pl.ds(pl.multiple_of(s * own + r * W, W), W), :] = total
        return tuple(grads)

    sums = tuple(jnp.zeros((8, CH), F32) for _ in range(10))
    for s in range(scenes):
        sums = lax.fori_loop(0, rows, functools.partial(backward, s), sums)
    for k in range(10):
        ghid_out[1 + k : 2 + k, :] = row_sum(sums[k]) * SLOPE

    ge = ge_scr[...]
    grads = mm(nt[...], ge)
    gwe_out[...] = grads[0:C, :] * SLOPE
    ghid_out[0:1, :] = grads[C : C + 1, :] * SLOPE
    gn2[...] += mm_nt(ge, wcol)
    gws = None
    for s in range(scenes):
        at = slice(s * own, (s + 1) * own)
        act = act_scr[s * gext + W : s * gext + W + own, :]
        branch[at, :] += mm(act, wrow)
        term = mm(ct[:, at], act)
        gws = term if gws is None else gws + term
    gws_out[...] = gws * ACT_SCALE

    @pl.when(step == pl.num_programs(0) - 1)
    def _():
        size = 4 * W
        per = own // size
        gain = vec[V_GAIN2 : V_GAIN2 + 1, :]

        def finish(i, carry):
            at = pl.multiple_of(i * size, size)
            s = i // per
            line = (i % per) * 4
            middle = mid[pl.ds(at, size), :]
            y_out[pl.ds(at, size), :] = (
                middle + branch[pl.ds(at, size), :] * ACT_SCALE + vec[V_SHRINK : V_SHRINK + 1, :]
            ).astype(BF16)
            grad = gn2[pl.ds(at, size), :] * SLOPE
            unit, rstd = norm_parts(middle)
            direct = cot[s, pl.ds(line, 4)].reshape(size, C).astype(F32)
            gmid_out[pl.ds(at, size), :] = direct + norm_back(grad, unit, rstd, gain)
            return (
                carry[0] + row_sum(grad * unit),
                carry[1] + row_sum(grad),
                carry[2] + row_sum(direct),
            )

        zero = jnp.zeros((1, C), F32)
        sums = lax.fori_loop(0, scenes * per, finish, (zero, zero, zero))
        for i in range(3):
            gvec_out[i : i + 1, :] = sums[i]


def mix(n2, n2_top, n2_low, cot, cot_top, cot_low, mid, edge, vec, hid, we, ws):
    scenes, rows = n2.shape[0], n2.shape[1]
    tokens = scenes * rows * W
    ext = scenes * (rows + 4) * W
    gext = scenes * (rows + 2) * W
    once = dict(pipeline_mode=pl.Buffered(1))
    whole = lambda a: pl.BlockSpec(a.shape, lambda j: (0,) * a.ndim, **once)
    return pl.pallas_call(
        mix_kernel,
        name="mix",
        grid=(FF // CH,),
        in_specs=[
            whole(n2),
            whole(n2_top),
            whole(n2_low),
            whole(cot),
            whole(cot_top),
            whole(cot_low),
            whole(mid),
            pl.BlockSpec(memory_space=pltpu.SMEM),
            whole(vec),
            pl.BlockSpec((16, CH), lambda j: (0, j)),
            pl.BlockSpec((C, CH), lambda j: (0, j)),
            pl.BlockSpec((CH, C), lambda j: (j, 0)),
        ],
        out_specs=[
            full((tokens, C)),
            full((tokens, C)),
            pl.BlockSpec((C, CH), lambda j: (0, j)),
            pl.BlockSpec((C, CH), lambda j: (0, j)),
            pl.BlockSpec((16, CH), lambda j: (0, j)),
            full((8, C)),
        ],
        out_shape=(
            shape_of((tokens, C), BF16),
            shape_of((tokens, C), F32),
            shape_of((C, FF), F32),
            shape_of((C, FF), F32),
            shape_of((16, FF), F32),
            shape_of((8, C), F32),
        ),
        scratch_shapes=[
            pltpu.VMEM((ext, C), BF16),
            pltpu.VMEM((gext, C), BF16),
            pltpu.VMEM((C + 16, tokens), BF16),
            pltpu.VMEM((C, tokens), BF16),
            pltpu.VMEM((ext, CH), F32),
            pltpu.VMEM((ext, CH), BF16),
            pltpu.VMEM((gext, CH), F32),
            pltpu.VMEM((3, gext, CH), BF16),
            pltpu.VMEM((gext, CH), BF16),
            pltpu.VMEM((tokens, CH), BF16),
            pltpu.VMEM((tokens, C), F32),
            pltpu.VMEM((tokens, C), F32),
        ],
        compiler_params=PARAMS,
    )(n2, n2_top, n2_low, cot, cot_top, cot_low, mid, edge, vec, hid, we, ws)


def attend_back_kernel(
    q_ref, lse_ref, mixed_ref, gmid_ref, rn_ref, vec, wk, wv, wo,
    dq_out, grn_out, gwk_out, gwv_out, gwo_out, gvec_out,
    kt, vt, kh, dkt, dvt,
):
    scene, step = pl.program_id(0), pl.program_id(1)
    keys = rn_ref.shape[0] * rn_ref.shape[2]
    start = jnp.logical_and(scene == 0, step == 0)

    @pl.when(start)
    def _():
        for ref in (gwk_out, gwv_out, gwo_out, gvec_out):
            ref[...] = jnp.zeros_like(ref)

    @pl.when(step == 0)
    def _():
        rn = rn_ref[:, 0].reshape(keys, C)
        key = mm(rn, wk[...]).astype(BF16)
        value = (mm(rn, wv[...]) + vec[V_VALUE : V_VALUE + 1, :]).astype(BF16)
        kt[...] = key.T
        vt[...] = value.T
        for h in range(HEADS):
            kh[h] = key[:, h * HD : (h + 1) * HD]
        dkt[...] = jnp.zeros_like(dkt)
        dvt[...] = jnp.zeros_like(dvt)

    gmid = gmid_ref[...]
    gatt = gmid.astype(BF16)
    gvec_out[1:2, :] += row_sum(gatt.astype(F32))
    mixed = mixed_ref[...]
    gwo_out[...] += mm_tn(mixed, gatt)
    gmixed = mm_nt(gatt, wo[...]).astype(BF16)
    prod = gmixed.astype(F32) * mixed.astype(F32)
    q = q_ref[...]
    q_t = q.T
    g_t = gmixed.T
    dqs = []
    for h in range(HEADS):
        cols = slice(h * HD, (h + 1) * HD)
        inner = jnp.sum(prod[:, cols], axis=-1, keepdims=True)
        probs = jnp.exp(mm(q[:, cols], kt[cols, :]) - lse_ref[:, h : h + 1])
        gprobs = mm(gmixed[:, cols], vt[cols, :])
        gscores = (probs * (gprobs - inner)).astype(BF16)
        dqs.append(mm(gscores, kh[h]))
        dkt[cols, :] += mm(q_t[cols, :], gscores)
        dvt[cols, :] += mm(g_t[cols, :], probs.astype(BF16))
    dq_out[...] = (jnp.concatenate(dqs, axis=1) * (1.0 / math.sqrt(HD))).astype(BF16)

    @pl.when(step == pl.num_programs(1) - 1)
    def _():
        rn = rn_ref[:, 0].reshape(keys, C)
        dk = dkt[...].T.astype(BF16)
        dv = dvt[...].T
        gvec_out[0:1, :] += row_sum(dv)
        dv = dv.astype(BF16)
        gwk_out[...] += mm_tn(rn, dk)
        gwv_out[...] += mm_tn(rn, dv)
        grn = mm_nt(dk, wk[...]) + mm_nt(dv, wv[...])
        grn_out[...] = grn.astype(BF16).reshape(grn_out.shape)


def attend_back(q, lse, mixed, gmid, rn_all, vec, wk, wv, wo):
    tokens = q.shape[0]
    bands, scenes, per_band, _ = rn_all.shape
    keys = bands * per_band
    steps = tokens // scenes // QT
    tile = lambda s, i: (s * steps + i, 0)
    return pl.pallas_call(
        attend_back_kernel,
        name="attend_back",
        grid=(scenes, steps),
        in_specs=[
            pl.BlockSpec((QT, C), tile),
            pl.BlockSpec((QT, 128), tile),
            pl.BlockSpec((QT, C), tile),
            pl.BlockSpec((QT, C), tile),
            pl.BlockSpec((bands, 1, per_band, C), lambda s, i: (0, s, 0, 0)),
            full((16, C)),
            full((C, C)),
            full((C, C)),
            full((C, C)),
        ],
        out_specs=[
            pl.BlockSpec((QT, C), tile),
            pl.BlockSpec((bands, 1, per_band, C), lambda s, i: (0, s, 0, 0)),
            full((C, C)),
            full((C, C)),
            full((C, C)),
            full((8, C)),
        ],
        out_shape=(
            shape_of((tokens, C), BF16),
            shape_of(rn_all.shape, BF16),
            shape_of((C, C), F32),
            shape_of((C, C), F32),
            shape_of((C, C), F32),
            shape_of((8, C), F32),
        ),
        scratch_shapes=[
            pltpu.VMEM((C, keys), BF16),
            pltpu.VMEM((C, keys), BF16),
            pltpu.VMEM((HEADS, keys, HD), BF16),
            pltpu.VMEM((C, keys), F32),
            pltpu.VMEM((C, keys), F32),
        ],
        compiler_params=PARAMS,
    )(q, lse, mixed, gmid, rn_all, vec, wk, wv, wo)


def tail_kernel(
    x_ref, gmid_ref, dq_ref, grn_ref, red_ref, vec, wq, wr,
    gx_out, gwq_out, gwr_out, gvec_out, scr, gscr,
):
    @pl.when(pl.program_id(0) == 0)
    def _():
        for ref in (gwq_out, gwr_out, gvec_out):
            ref[...] = jnp.zeros_like(ref)

    runit, rrstd = norm_parts(red_ref[...])
    grn = grn_ref[...].astype(F32)
    gred = norm_back(grn, runit, rrstd, vec[V_RGAIN : V_RGAIN + 1, :]).astype(BF16)
    unit, rstd = norm_parts(x_ref[...].astype(F32))
    gain = vec[V_GAIN1 : V_GAIN1 + 1, :]
    normed = (unit * gain + vec[V_SHIFT1 : V_SHIFT1 + 1, :]).astype(BF16)
    split_tiles(scr, normed.astype(F32))
    pieces = patch_pieces(scr)
    back = {}
    for k in range(4):
        at = slice(k * C, (k + 1) * C)
        gwr_out[at, :] += mm_tn(pieces[k].astype(BF16), gred)
        back[k] = mm_nt(gred, wr[at, :]).reshape(TILE // (2 * W), 1, W // 2, C)
    for b in range(2):
        cols = jnp.concatenate([back[b], back[2 + b]], axis=1).reshape(TILE // 2, C)
        spot = pl.ds(b, TILE // 2, stride=2)
        gscr[0, spot, :] = cols[:, 0:128]
        gscr[1, spot, :] = cols[:, 128:256]
        gscr[2, spot, :] = jnp.concatenate(
            [cols[:, 256:320], jnp.zeros((TILE // 2, 64), F32)], axis=1
        )
    dq = dq_ref[...]
    gwq_out[...] += mm_tn(normed, dq)
    placed = jnp.concatenate([gscr[0], gscr[1], gscr[2][:, 0:64]], axis=1)
    gnormed = mm_nt(dq, wq[...]) + placed
    gx_out[...] = gmid_ref[...] + norm_back(gnormed, unit, rstd, gain)
    gvec_out[0:1, :] += row_sum(dq.astype(F32))
    gvec_out[1:2, :] += row_sum(gred.astype(F32))
    gvec_out[2:3, :] += row_sum(grn * runit)
    gvec_out[3:4, :] += row_sum(grn)
    gvec_out[4:5, :] += row_sum(gnormed * unit)
    gvec_out[5:6, :] += row_sum(gnormed)


def tail(x, gmid, dq, grn, red, vec, wq, wr):
    tokens = x.shape[0]
    tile = pl.BlockSpec((TILE, C), lambda i: (i, 0))
    rtile = pl.BlockSpec((RTILE, C), lambda i: (i, 0))
    return pl.pallas_call(
        tail_kernel,
        name="tail",
        grid=(tokens // TILE,),
        in_specs=[
            tile, tile, tile, rtile, rtile, full((16, C)), full((C, C)), full((4 * C, C))
        ],
        out_specs=[tile, full((C, C)), full((4 * C, C)), full((8, C))],
        out_shape=(
            shape_of((tokens, C), F32),
            shape_of((C, C), F32),
            shape_of((4 * C, C), F32),
            shape_of((8, C), F32),
        ),
        scratch_shapes=[pltpu.VMEM((3, TILE, 128), F32), pltpu.VMEM((3, TILE, 128), F32)],
        compiler_params=PARAMS,
    )(x, gmid, dq, grn, red, vec, wq, wr)


ANY = pl.BlockSpec(memory_space=pl.ANY)
VM = pl.BlockSpec(memory_space=pltpu.VMEM)


def flip(value, by):
    return value + by * (1 - 2 * value)


def remote(src, dst, send, recv, where):
    return pltpu.make_async_remote_copy(
        src_ref=src,
        dst_ref=dst,
        send_sem=send,
        recv_sem=recv,
        device_id=where,
        device_id_type=pl.DeviceIdType.MESH,
    )


def greet(places):
    barrier = pltpu.get_barrier_semaphore()
    count = 0
    for place, there in places:
        if there is None:
            pl.semaphore_signal(
                barrier, inc=1, device_id=place, device_id_type=pl.DeviceIdType.MESH
            )
            count = count + 1
        else:

            @pl.when(there)
            def _():
                pl.semaphore_signal(
                    barrier, inc=1, device_id=place, device_id_type=pl.DeviceIdType.MESH
                )

            count = count + there.astype(jnp.int32)
    pl.semaphore_wait(barrier, count)


def comm_params(number):
    return pltpu.CompilerParams(
        collective_id=number, has_side_effects=True, vmem_limit_bytes=60 * 1024 * 1024
    )


class Place:
    def __init__(self):
        dp, space = lax.axis_index("dp"), lax.axis_index("space")
        self.z, self.x = dp // 2, dp % 2
        self.y, self.c = space // 2, space % 2
        self.line = lax.axis_size("dp") // 2

    def block(self, z, x, y, c):
        return ((z * 2 + x) * 2 + y) * 2 + c

    def device(self, z, x, y, c):
        return {"dp": z * 2 + x, "space": y * 2 + c}

    def spot(self, da, db, c):
        return (
            flip(self.x, da * (1 - c) + db * c),
            flip(self.y, db * (1 - c) + da * c),
        )

    def partners(self):
        ax, ay = self.spot(1, 0, self.c)
        bx, by = self.spot(0, 1, self.c)
        return (
            self.device(self.z, ax, ay, self.c),
            self.device(self.z, bx, by, self.c),
            self.device(self.z, self.x, self.y, 1 - self.c),
            self.device(self.z + 1, self.x, self.y, self.c),
            self.device(self.z - 1, self.x, self.y, self.c),
        )

    def meet(self):
        first, second, sibling, up, down = self.partners()
        greet(
            [
                (first, None),
                (second, None),
                (sibling, None),
                (up, self.z < self.line - 1),
                (down, self.z > 0),
            ]
        )


def gather_kernel(own, out, up_sem, down_sem, a_sem, b_sem, c_sem, recv):
    at = Place()
    line = at.line
    first, second, sibling, up, down = at.partners()
    at.meet()
    can_up, can_down = at.z < line - 1, at.z > 0

    def block_of(z, da, db):
        x, y = at.spot(da, db, at.c)
        return at.block(z, x, y, at.c)

    def push(index, src, sem, where):
        remote(src, out.at[index], sem, recv.at[index], where).start()

    def landed(index):
        remote(out.at[index], out.at[index], c_sem.at[0], recv.at[index], sibling).wait_recv()

    def slot_sends(z, da, db, src):
        index = block_of(z, da, db)
        if da == 0 and db == 0:
            push(index, src, a_sem.at[z], first)
        if db == 0:
            push(index, src, b_sem.at[da * line + z], second)
        push(index, src, c_sem.at[(da * 2 + db) * line + z], sibling)

    mine = block_of(at.z, 0, 0)

    @pl.when(can_up)
    def _():
        push(mine, own, up_sem.at[at.z], up)

    @pl.when(can_down)
    def _():
        push(mine, own, down_sem.at[at.z], down)

    slot_sends(at.z, 0, 0, own)
    out[mine] = own[...]

    def along(da, db, act):
        for d in range(1, line):

            @pl.when(at.z - d >= 0)
            def _():
                act(at.z - d, da, db, 1)

            @pl.when(at.z + d < line)
            def _():
                act(at.z + d, da, db, -1)

    def relay(z, da, db, way):
        index = block_of(z, da, db)
        landed(index)
        if da == 0 and db == 0:
            if way > 0:

                @pl.when(can_up)
                def _():
                    push(index, out.at[index], up_sem.at[z], up)

            else:

                @pl.when(can_down)
                def _():
                    push(index, out.at[index], down_sem.at[z], down)

        slot_sends(z, da, db, out.at[index])

    along(0, 0, relay)
    for da, db in ((1, 0), (0, 1), (1, 1)):
        relay(at.z, da, db, 0)
        along(da, db, relay)
    for da in range(2):
        for db in range(2):
            for z in range(line):
                x, y = at.spot(da, db, at.c)
                landed(at.block(z, x, y, 1 - at.c))
    def sent(sem, where):
        remote(own, out.at[mine], sem, recv.at[mine], where).wait_send()

    for z in range(line):

        @pl.when(jnp.logical_and(can_up, z <= at.z))
        def _():
            sent(up_sem.at[z], up)

        @pl.when(jnp.logical_and(can_down, z >= at.z))
        def _():
            sent(down_sem.at[z], down)

        sent(a_sem.at[z], first)
        for da in range(2):
            sent(b_sem.at[da * line + z], second)
            for db in range(2):
                sent(c_sem.at[(da * 2 + db) * line + z], sibling)


def gather_blocks(own):
    dma = pltpu.SemaphoreType.DMA
    return pl.pallas_call(
        gather_kernel,
        name="gather",
        out_shape=shape_of((BLOCKS,) + own.shape, own.dtype),
        in_specs=[VM],
        out_specs=VM,
        scratch_shapes=[dma((4,)), dma((4,)), dma((4,)), dma((8,)), dma((16,)), dma((BLOCKS,))],
        compiler_params=comm_params(1),
    )(own)


def scatter_kernel(
    parts, out, rc, acc, ra, acc2, rb, acc3, rup, rdown, sup, sdown,
    c_sem, a_sem, b_sem, up_sem, down_sem, c_in, a_in, b_in, up_in, down_in,
):
    at = Place()
    line = at.line
    first, second, sibling, up, down = at.partners()
    at.meet()
    can_up, can_down = at.z < line - 1, at.z > 0
    slots = [(da, db, z) for da in (1, 0) for db in (1, 0) for z in range(line)]

    def add(left, right):
        return (left.astype(F32) + right.astype(F32)).astype(BF16)

    def c_copy(k):
        da, db, z = slots[k]
        x, y = at.spot(da, db, 1 - at.c)
        return remote(
            parts.at[at.block(z, x, y, 1 - at.c)], rc.at[k], c_sem.at[k], c_in.at[k], sibling
        )

    def a_copy(j):
        return remote(acc.at[j], ra.at[j], a_sem.at[j], a_in.at[j], first)

    def b_copy(j):
        return remote(acc2.at[j], rb.at[j], b_sem.at[j], b_in.at[j], second)

    def up_copy(z):
        return remote(sup.at[z], rup.at[z], up_sem.at[z], up_in.at[z], up)

    def down_copy(z):
        return remote(sdown.at[z], rdown.at[z], down_sem.at[z], down_in.at[z], down)

    for k in range(4 * line):
        c_copy(k).start()
    for k in range(4 * line):
        c_copy(k).wait_recv()
        da, db, z = slots[k]
        x, y = at.spot(da, db, at.c)
        acc[k] = add(parts[at.block(z, x, y, at.c)], rc[k])
        if da:
            a_copy(k).start()
    for j in range(2 * line):
        a_copy(j).wait_recv()
        acc2[j] = add(acc[2 * line + j], ra[j])
        if j < line:
            b_copy(j).start()
    for z in range(line):
        b_copy(z).wait_recv()
        acc3[z] = add(acc2[line + z], rb[z])
    for z in reversed(range(line)):

        @pl.when(z > at.z)
        def _():
            sup[z] = acc3[z]

            @pl.when(can_down)
            def _():
                up_copy(z).wait_recv()
                sup[z] = add(acc3[z], rup[z])

            up_copy(z).start()

        mirror = line - 1 - z

        @pl.when(mirror < at.z)
        def _():
            sdown[mirror] = acc3[mirror]

            @pl.when(can_up)
            def _():
                down_copy(mirror).wait_recv()
                sdown[mirror] = add(acc3[mirror], rdown[mirror])

            down_copy(mirror).start()

    for z in range(line):

        @pl.when(z == at.z)
        def _():
            out[...] = acc3[z].astype(F32)

            @pl.when(can_down)
            def _():
                up_copy(z).wait_recv()
                out[...] += rup[z].astype(F32)

            @pl.when(can_up)
            def _():
                down_copy(z).wait_recv()
                out[...] += rdown[z].astype(F32)

    for k in range(4 * line):
        c_copy(k).wait_send()
    for j in range(2 * line):
        a_copy(j).wait_send()
    for z in range(line):
        b_copy(z).wait_send()

        @pl.when(z > at.z)
        def _():
            up_copy(z).wait_send()

        @pl.when(z < at.z)
        def _():
            down_copy(z).wait_send()


def scatter_blocks(parts):
    one = parts.shape[1:]
    dma = pltpu.SemaphoreType.DMA
    room = lambda n: pltpu.VMEM((n,) + one, BF16)
    return pl.pallas_call(
        scatter_kernel,
        name="scatter",
        out_shape=shape_of(one, F32),
        in_specs=[VM],
        out_specs=VM,
        scratch_shapes=[
            room(16), room(16), room(8), room(8), room(4), room(4),
            room(4), room(4), room(4), room(4),
        ]
        + [dma((n,)) for n in (16, 8, 4, 4, 4, 16, 8, 4, 4, 4)],
        compiler_params=comm_params(2),
    )(parts)


def bands_of():
    band = lax.axis_index("space")
    pair, core = band // 2, band % 2
    return band, pair * 2 + 1 - core, (1 - pair) * 2 + core


def swap_kernel(width, value, above, below, up_sem, down_sem, up_in, down_in, ready):
    band = lax.axis_index("space")
    rows = value.shape[1]
    ends = lax.axis_size("space") - 1
    down = remote(
        value.at[:, pl.ds(rows - width, width)], above, down_sem, down_in, {"space": band + 1}
    )
    up = remote(value.at[:, pl.ds(0, width)], below, up_sem, up_in, {"space": band - 1})

    @pl.when(band < ends)
    def _():
        down.start()

    @pl.when(band > 0)
    def _():
        up.start()

    def finish():
        @pl.when(band < ends)
        def _():
            down.wait_send()
            up.wait_recv()

        @pl.when(band > 0)
        def _():
            up.wait_send()
            down.wait_recv()

    return finish


def bands_meet(others):
    band = lax.axis_index("space")
    ends = lax.axis_size("space") - 1
    greet(
        [({"space": o}, None) for o in others]
        + [({"space": band + 1}, band < ends), ({"space": band - 1}, band > 0)]
    )


def share_kernel(
    rn, cot, rn_all, above, below, send, recv, own_sem, up_sem, down_sem, up_in, down_in
):
    band, sibling, across = bands_of()
    bands_meet((sibling, across))
    to_sibling = remote(rn, rn_all.at[band], send.at[0], recv.at[band], {"space": sibling})
    to_across = remote(rn, rn_all.at[band], send.at[1], recv.at[band], {"space": across})
    to_across.start()
    to_sibling.start()
    own = pltpu.make_async_copy(rn, rn_all.at[band], own_sem)
    own.start()
    finish = swap_kernel(1, cot, above, below, up_sem, down_sem, up_in, down_in, None)

    def landed(index):
        remote(rn, rn_all.at[index], send.at[0], recv.at[index], {"space": sibling}).wait_recv()

    landed(across)
    onward = remote(
        rn_all.at[across], rn_all.at[across], send.at[2], recv.at[across], {"space": sibling}
    )
    onward.start()
    landed(sibling)
    landed(across + sibling - band)
    own.wait()
    to_across.wait_send()
    to_sibling.wait_send()
    onward.wait_send()
    finish()


def share(rn, cot):
    bands = lax.axis_size("space")
    dma = pltpu.SemaphoreType.DMA
    edge = (cot.shape[0], 1) + cot.shape[2:]
    return pl.pallas_call(
        share_kernel,
        name="share",
        out_shape=(
            shape_of((bands,) + rn.shape, rn.dtype),
            shape_of(edge, cot.dtype),
            shape_of(edge, cot.dtype),
        ),
        in_specs=[VM, ANY],
        out_specs=(ANY, ANY, ANY),
        scratch_shapes=[dma((3,)), dma((bands,)), dma, dma, dma, dma, dma],
        compiler_params=comm_params(3),
    )(rn, cot)


def halo_kernel(value, above, below, up_sem, down_sem, up_in, down_in):
    bands_meet(())
    swap_kernel(2, value, above, below, up_sem, down_sem, up_in, down_in, None)()


def halo(value):
    dma = pltpu.SemaphoreType.DMA
    edge = (value.shape[0], 2) + value.shape[2:]
    return pl.pallas_call(
        halo_kernel,
        name="halo",
        out_shape=(shape_of(edge, value.dtype), shape_of(edge, value.dtype)),
        in_specs=[ANY],
        out_specs=(ANY, ANY),
        scratch_shapes=[dma, dma, dma, dma],
        compiler_params=comm_params(4),
    )(value)


def merge_kernel(parts, out, rc, acc, rb, c_sem, c_in, b_sem, b_in):
    band, sibling, across = bands_of()
    greet([({"space": sibling}, None), ({"space": across}, None)])
    far = across + sibling - band
    first = remote(parts.at[far], rc.at[0], c_sem.at[0], c_in.at[0], {"space": sibling})
    second = remote(parts.at[sibling], rc.at[1], c_sem.at[1], c_in.at[1], {"space": sibling})
    onward = remote(acc, rb, b_sem, b_in, {"space": across})
    first.start()
    second.start()
    first.wait_recv()
    acc[...] = (parts[across].astype(F32) + rc[0].astype(F32)).astype(BF16)
    onward.start()
    second.wait_recv()
    out[...] = parts[band].astype(F32) + rc[1].astype(F32)
    onward.wait_recv()
    out[...] += rb[...].astype(F32)
    first.wait_send()
    second.wait_send()
    onward.wait_send()


def merge(parts):
    one = parts.shape[1:]
    dma = pltpu.SemaphoreType.DMA
    return pl.pallas_call(
        merge_kernel,
        name="merge",
        out_shape=shape_of(one, F32),
        in_specs=[VM],
        out_specs=VM,
        scratch_shapes=[
            pltpu.VMEM((2,) + one, BF16),
            pltpu.VMEM(one, BF16),
            pltpu.VMEM(one, BF16),
            dma((2,)),
            dma((2,)),
            dma,
            dma,
        ],
        compiler_params=comm_params(5),
    )(parts)


def blocks_fit(size):
    return (
        lax.axis_size("dp") == 8 and lax.axis_size("space") == 4 and size == BLOCK_ROWS * C
    )


def gather_params(params):
    if blocks_fit(params.shape[0]):
        return gather_blocks(params.reshape(BLOCK_ROWS, C))
    flat = lax.all_gather(params, ("dp", "space"), axis=0, tiled=True)
    want = ROWS * C
    flat = flat[:want] if flat.shape[0] >= want else jnp.pad(flat, (0, want - flat.shape[0]))
    return flat.reshape(BLOCKS, BLOCK_ROWS, C)


def scatter_grads(blocks, size):
    if blocks_fit(size):
        return scatter_blocks(blocks).reshape(size)
    flat = blocks.reshape(-1)
    want = size * lax.axis_size("dp") * lax.axis_size("space")
    flat = flat[:want] if flat.shape[0] >= want else jnp.pad(flat, (0, want - flat.shape[0]))
    own = lax.psum_scatter(flat, ("dp", "space"), scatter_dimension=0, tiled=True)
    return own.astype(F32)


def on_device(scenes, params, cotangent):
    count, rows, breadth = scenes.shape[0], scenes.shape[1], scenes.shape[2]
    tokens = count * rows * breadth
    bands = lax.axis_size("space")
    per_band = rows * breadth // 4
    band = lax.axis_index("space")
    edge = jnp.stack([band > 0, band < bands - 1]).astype(F32)
    wq, wr, wk, wv, wo, we, ws, vec, hid = unpack(gather_params(params))
    x = scenes.reshape(tokens, C)
    q, red, rn = front(x, vec, wq, wr)
    rn_all, cot_top, cot_low = share(rn, cotangent)
    rn_all = rn_all.reshape(bands, count, per_band, C)
    mixed, lse, mid, n2 = attend(x, q, rn_all, vec, wk, wv, wo)
    n2 = n2.reshape(scenes.shape)
    n2_top, n2_low = halo(n2)
    y, gmid, gwe, gws, ghid, gvec2 = mix(
        n2, n2_top, n2_low, cotangent, cot_top, cot_low, mid, edge, vec, hid, we, ws
    )
    dq, grn_all, gwk, gwv, gwo, gvec1 = attend_back(
        q, lse, mixed, gmid, rn_all, vec, wk, wv, wo
    )
    grn = merge(grn_all.reshape(bands, count * per_band, C))
    gx, gwq, gwr, gvec0 = tail(x, gmid, dq, grn, red, vec, wq, wr)
    blocks = pack(gwq, gwr, gwk, gwv, gwo, gwe, gws, gvec0, gvec1, gvec2, ghid)
    shard = scatter_grads(blocks, params.shape[0])
    return y.reshape(scenes.shape), gx.reshape(scenes.shape), shard


def solution(mesh):
    band = P("dp", "space", None, None)
    flat = P(("dp", "space"))
    return jax.shard_map(
        on_device,
        mesh=mesh,
        in_specs=(band, flat, band),
        out_specs=(band, band, flat),
        check_vma=False,
    )
```

```python
import functools
import math

import jax
import jax.numpy as jnp
from jax import lax
from jax.experimental import pallas as pl
from jax.experimental.pallas import tpu as pltpu
from jax.sharding import PartitionSpec as P

C = 320
HEADS = 5
HD = 64
FF = 1280
W = 64
EPSILON = 1e-06
F32 = jnp.float32
BF16 = jnp.bfloat16

ROWS = 5184
USED_ROWS = 5175
BLOCKS = 32
BLOCK_ROWS = ROWS // BLOCKS
R_QUERY = 0
R_REDUCE = 321
R_KEYVAL = 1604
R_OUTPUT = 2245
R_EXPAND = 2570
R_HIDDEN = 3850
R_SHRINK = 3894
VECTOR_ROWS = (320, 1601, 1602, 1603, 2244, 2565, 2566, 2567, 2568, 2569, 5174)
(
    V_QUERY,
    V_REDUCE,
    V_RGAIN,
    V_RSHIFT,
    V_VALUE,
    V_OUTPUT,
    V_GAIN1,
    V_SHIFT1,
    V_GAIN2,
    V_SHIFT2,
    V_SHRINK,
) = range(11)
HIDDEN_ROWS = 11

PARAMS = pltpu.CompilerParams(vmem_limit_bytes=60 * 1024 * 1024)


def shape_of(dims, kind):
    return jax.ShapeDtypeStruct(dims, kind)


def mm(left, right):
    return jnp.dot(left, right, preferred_element_type=F32)


def mm_tn(left, right):
    return lax.dot_general(left, right, (((0,), (0,)), ((), ())), preferred_element_type=F32)


def mm_nt(left, right):
    return lax.dot_general(left, right, (((1,), (1,)), ((), ())), preferred_element_type=F32)


def mm_tt(left, right):
    return lax.dot_general(left, right, (((0,), (1,)), ((), ())), preferred_element_type=F32)


def norm_parts(values):
    center = values - jnp.mean(values, axis=-1, keepdims=True)
    rstd = lax.rsqrt(jnp.mean(center * center, axis=-1, keepdims=True) + EPSILON)
    return center * rstd, rstd


def norm_back(grad, unit, rstd, gain):
    scaled = grad * gain
    first = jnp.mean(scaled, axis=-1, keepdims=True)
    second = jnp.mean(scaled * unit, axis=-1, keepdims=True)
    return rstd * (scaled - first - unit * second)


def row_sum(values):
    return jnp.sum(values, axis=0, keepdims=True)


def full(dims):
    return pl.BlockSpec(dims, lambda *_: (0,) * len(dims))


def unpack_kernel(g_ref, wq, wr, wk, wv, wo, we, ws, vec, hid, rows, tiles):
    for i in range(BLOCKS):
        at = i * BLOCK_ROWS
        block = restore(g_ref[i].astype(F32).reshape(2 * PART, 128))
        rows[at : at + BLOCK_ROWS, :] = block
        tiles[0, at : at + BLOCK_ROWS, :] = block[:, 0:128]
        tiles[1, at : at + BLOCK_ROWS, :] = block[:, 128:256]
        tiles[2, at : at + BLOCK_ROWS, 0:64] = block[:, 256:320]

    def strided(start, count, step):
        parts = [tiles[t, pl.ds(start, count, stride=step), :] for t in range(3)]
        return jnp.concatenate([parts[0], parts[1], parts[2][:, 0:64]], axis=1)

    wq[...] = rows[R_QUERY : R_QUERY + C, :].astype(BF16)
    wr[...] = rows[R_REDUCE : R_REDUCE + 4 * C, :].astype(BF16)
    wk[...] = strided(R_KEYVAL, C, 2).astype(BF16)
    wv[...] = strided(R_KEYVAL + 1, C, 2).astype(BF16)
    wo[...] = rows[R_OUTPUT : R_OUTPUT + C, :].astype(BF16)
    ws[...] = rows[R_SHRINK : R_SHRINK + FF, :].astype(BF16)
    we[...] = jnp.concatenate([strided(R_EXPAND + j, C, 4) for j in range(4)], axis=1).astype(BF16)
    hid[0:HIDDEN_ROWS, :] = jnp.concatenate(
        [strided(R_HIDDEN + j, HIDDEN_ROWS, 4) for j in range(4)], axis=1
    )
    for i, row in enumerate(VECTOR_ROWS):
        vec[i : i + 1, :] = rows[row : row + 1, :]


def unpack(blocks):
    return pl.pallas_call(
        unpack_kernel,
        name="unpack",
        out_shape=(
            shape_of((C, C), BF16),
            shape_of((4 * C, C), BF16),
            shape_of((C, C), BF16),
            shape_of((C, C), BF16),
            shape_of((C, C), BF16),
            shape_of((C, FF), BF16),
            shape_of((FF, C), BF16),
            shape_of((16, C), F32),
            shape_of((16, FF), F32),
        ),
        scratch_shapes=[pltpu.VMEM((ROWS, C), F32), pltpu.VMEM((3, ROWS, 128), F32)],
        compiler_params=PARAMS,
    )(blocks)


def pack_kernel(gwq, gwr, gwk, gwv, gwo, gwe, gws, gvec0, gvec1, gvec2, ghid, out, tiles):
    def put(start, value):
        count = value.shape[0]
        tiles[0, start : start + count, :] = value[:, 0:128]
        tiles[1, start : start + count, :] = value[:, 128:256]
        tiles[2, start : start + count, 0:64] = value[:, 256:320]

    def put_strided(start, step, value):
        count = value.shape[0]
        tiles[0, pl.ds(start, count, stride=step), :] = value[:, 0:128]
        tiles[1, pl.ds(start, count, stride=step), :] = value[:, 128:256]
        tail = jnp.concatenate([value[:, 256:320], jnp.zeros((count, 64), F32)], axis=1)
        tiles[2, pl.ds(start, count, stride=step), :] = tail

    put(R_QUERY, gwq[...])
    put(R_REDUCE, gwr[...])
    put_strided(R_KEYVAL, 2, gwk[...].T)
    put_strided(R_KEYVAL + 1, 2, gwv[...].T)
    put(R_OUTPUT, gwo[...])
    put(R_SHRINK, gws[...].T)
    for j in range(4):
        put_strided(R_EXPAND + j, 4, gwe[:, C * j : C * j + C])
        put_strided(R_HIDDEN + j, 4, ghid[0:HIDDEN_ROWS, C * j : C * j + C])
    for source, names in (
        (gvec0, (V_QUERY, V_REDUCE, V_RGAIN, V_RSHIFT, V_GAIN1, V_SHIFT1)),
        (gvec2, (V_GAIN2, V_SHIFT2, V_SHRINK)),
    ):
        for i, name in enumerate(names):
            put(VECTOR_ROWS[name], source[i : i + 1, :])
    put(VECTOR_ROWS[V_VALUE], gvec1[0:1, :])
    put(VECTOR_ROWS[V_OUTPUT], gvec1[8:9, :])
    put(USED_ROWS, jnp.zeros((ROWS - USED_ROWS, C), F32))
    half = BLOCK_ROWS // 2
    spare = jnp.zeros((2 * PART - 2 * BLOCK_ROWS - half, 128), F32)
    for i in range(BLOCKS):
        at = i * BLOCK_ROWS
        tail = jnp.concatenate(
            [
                tiles[2, at : at + half, 0:64],
                tiles[2, at + half : at + BLOCK_ROWS, 0:64],
            ],
            axis=1,
        )
        rows = [tiles[0, at : at + BLOCK_ROWS, :], tiles[1, at : at + BLOCK_ROWS, :], tail, spare]
        out[i] = jnp.concatenate(rows, axis=0).reshape(2, PART, 128).astype(BF16)


def pack(*pieces):
    return pl.pallas_call(
        pack_kernel,
        name="pack",
        out_shape=shape_of((BLOCKS, 2, PART, 128), BF16),
        scratch_shapes=[pltpu.VMEM((3, ROWS, 128), F32)],
        compiler_params=PARAMS,
    )(*pieces)


TILE = 8 * W
RTILE = TILE // 4


def split_tiles(scr, value):
    scr[0, :, :] = value[:, 0:128]
    scr[1, :, :] = value[:, 128:256]
    scr[2, :, 0:64] = value[:, 256:320]


def patch_pieces(scr):
    pieces = {}
    for b in range(2):
        parts = [scr[t, pl.ds(b, TILE // 2, stride=2), :] for t in range(3)]
        cols = jnp.concatenate([parts[0], parts[1], parts[2][:, 0:64]], axis=1)
        cols = cols.reshape(TILE // (2 * W), 2, W // 2, C)
        for a in range(2):
            pieces[2 * a + b] = cols[:, a].reshape(RTILE, C)
    return pieces


def front_kernel(x_ref, vec, wq, wr, q_out, red_out, rn_out, scr):
    unit, _ = norm_parts(x_ref[...].astype(F32))
    normed = (unit * vec[V_GAIN1 : V_GAIN1 + 1, :] + vec[V_SHIFT1 : V_SHIFT1 + 1, :]).astype(BF16)
    queries = (mm(normed, wq[...]) + vec[V_QUERY : V_QUERY + 1, :]).astype(BF16)
    q_out[...] = queries * jnp.asarray(1.0 / math.sqrt(HD), BF16)
    split_tiles(scr, normed.astype(F32))
    pieces = patch_pieces(scr)
    reduced = vec[V_REDUCE : V_REDUCE + 1, :]
    for k in range(4):
        reduced = reduced + mm(pieces[k].astype(BF16), wr[k * C : (k + 1) * C, :])
    red_out[...] = reduced
    unit, _ = norm_parts(reduced)
    rn_out[...] = (unit * vec[V_RGAIN : V_RGAIN + 1, :] + vec[V_RSHIFT : V_RSHIFT + 1, :]).astype(
        BF16
    )


def front(x, vec, wq, wr):
    tokens = x.shape[0]
    return pl.pallas_call(
        front_kernel,
        name="front",
        grid=(tokens // TILE,),
        in_specs=[
            pl.BlockSpec((TILE, C), lambda i: (i, 0)),
            full((16, C)),
            full((C, C)),
            full((4 * C, C)),
        ],
        out_specs=[
            pl.BlockSpec((TILE, C), lambda i: (i, 0)),
            pl.BlockSpec((RTILE, C), lambda i: (i, 0)),
            pl.BlockSpec((RTILE, C), lambda i: (i, 0)),
        ],
        out_shape=(
            shape_of((tokens, C), BF16),
            shape_of((tokens // 4, C), F32),
            shape_of((tokens // 4, C), BF16),
        ),
        scratch_shapes=[pltpu.VMEM((3, TILE, 128), F32)],
        compiler_params=PARAMS,
    )(x, vec, wq, wr)


QT = 512


def attend_kernel(
    x_ref, q_ref, rn_ref, vec, wk, wv, wo,
    mixed_out, inv_out, mid_out, n2_out, p_out, key_out, vt_out, kt, vones,
):
    keys = rn_ref.shape[0] * rn_ref.shape[2]

    @pl.when(pl.program_id(1) == 0)
    def _():
        rn = rn_ref[:, 0].reshape(keys, C)
        key = mm(rn, wk[...]).astype(BF16)
        value = (mm(rn, wv[...]) + vec[V_VALUE : V_VALUE + 1, :]).astype(BF16)
        key_out[0] = key
        vt_out[0] = value.T
        kt[...] = key.T
        for h in range(HEADS):
            vones[h, :, 0:HD] = value[:, h * HD : (h + 1) * HD]
            vones[h, :, HD:] = jnp.ones((keys, HD), BF16)

    outs, invs = [], []
    for h in range(HEADS):
        scores = mm(q_ref[:, h * HD : (h + 1) * HD], kt[h * HD : (h + 1) * HD, :])
        top = jnp.max(scores, axis=-1, keepdims=True)
        probs = jnp.exp(scores - top).astype(BF16)
        p_out[0, h] = probs
        both = mm(probs, vones[h])
        inv = 1.0 / both[:, HD:]
        outs.append(both[:, 0:HD] * inv)
        invs.append(inv)
    inv_out[...] = jnp.concatenate(invs, axis=1)
    mixed = jnp.concatenate(outs, axis=1).astype(BF16)
    mixed_out[...] = mixed
    middle = x_ref[...].astype(F32) + mm(mixed, wo[...]) + vec[V_OUTPUT : V_OUTPUT + 1, :]
    mid_out[...] = middle
    unit, _ = norm_parts(middle)
    n2_out[...] = (unit * vec[V_GAIN2 : V_GAIN2 + 1, :] + vec[V_SHIFT2 : V_SHIFT2 + 1, :]).astype(
        BF16
    )


def attend(x, q, rn_all, vec, wk, wv, wo):
    tokens = x.shape[0]
    bands, scenes, per_band, _ = rn_all.shape
    keys = bands * per_band
    per_scene = tokens // scenes
    steps = per_scene // QT
    tile = pl.BlockSpec((QT, C), lambda s, i: (s * steps + i, 0))
    return pl.pallas_call(
        attend_kernel,
        name="attend",
        grid=(scenes, steps),
        in_specs=[
            tile,
            tile,
            pl.BlockSpec((bands, 1, per_band, C), lambda s, i: (0, s, 0, 0)),
            full((16, C)),
            full((C, C)),
            full((C, C)),
            full((C, C)),
        ],
        out_specs=[
            tile,
            tile,
            tile,
            tile,
            pl.BlockSpec((1, HEADS, QT, keys), lambda s, i: (s, 0, i, 0)),
            pl.BlockSpec((1, keys, C), lambda s, i: (s, 0, 0)),
            pl.BlockSpec((1, C, keys), lambda s, i: (s, 0, 0)),
        ],
        out_shape=(
            shape_of((tokens, C), BF16),
            shape_of((tokens, C), F32),
            shape_of((tokens, C), F32),
            shape_of((tokens, C), BF16),
            shape_of((scenes, HEADS, per_scene, keys), BF16),
            shape_of((scenes, keys, C), BF16),
            shape_of((scenes, C, keys), BF16),
        ),
        scratch_shapes=[pltpu.VMEM((C, keys), BF16), pltpu.VMEM((HEADS, keys, 2 * HD), BF16)],
        compiler_params=PARAMS,
    )(x, q, rn_all, vec, wk, wv, wo)


CH = 256


SHRINK_IN = math.sqrt(0.5 * math.log2(math.e))
SLOPE = 1.0 / (math.sqrt(2.0 * math.pi) * SHRINK_IN)
ACT_SCALE = SLOPE / SHRINK_IN
ERF_RATE = 0.3275911 * math.sqrt(0.5) / SHRINK_IN
ERF_TERMS = [
    0.5 * k / SLOPE
    for k in (0.254829592, -0.284496736, 1.421413741, -1.453152027, 1.061405429)
]


def gelu_parts(u):
    size = jnp.abs(u)
    t = 1.0 / (1.0 + ERF_RATE * size)
    poly = ERF_TERMS[4]
    for term in ERF_TERMS[3::-1]:
        poly = term + t * poly
    bell = jnp.exp2(-(u * u))
    tail = (t * poly) * bell
    return jnp.where(u >= 0, 1.0 / SLOPE - tail, tail), bell


def mix_kernel(
    n2, n2_top, n2_low, cot, cot_top, cot_low, mid, edge, vec, hid, we, ws,
    y_out, gmid_out, gwe_out, gws_out, ghid_out, gvec_out,
    nx, cx, nt, ct, e_scr, e_low, ga_scr, gc_scr, act_scr, ge_scr, branch, gn2,
):
    step = pl.program_id(0)
    scenes, rows = n2.shape[0], n2.shape[1]
    ext = (rows + 4) * W
    gext = (rows + 2) * W
    own = rows * W
    top, low = edge[0], edge[1]

    @pl.when(step == 0)
    def _():
        def inside(value, there):
            return jnp.where(there > 0, value.astype(F32), 0.0).astype(BF16)

        for s in range(scenes):
            mine = n2[s].reshape(own, C)
            nx[s * ext : s * ext + 2 * W, :] = n2_top[s].reshape(2 * W, C)
            nx[s * ext + 2 * W : s * ext + 2 * W + own, :] = mine
            nx[s * ext + 2 * W + own : (s + 1) * ext, :] = n2_low[s].reshape(2 * W, C)
            nt[0:C, s * own : (s + 1) * own] = mine.T
            mine = cot[s].reshape(own, C)
            cx[s * gext : s * gext + W, :] = inside(cot_top[s].reshape(W, C), top)
            cx[s * gext + W : s * gext + W + own, :] = mine
            cx[s * gext + W + own : (s + 1) * gext, :] = inside(cot_low[s].reshape(W, C), low)
            ct[:, s * own : (s + 1) * own] = mine.T
        nt[C:, :] = jnp.ones((16, scenes * own), BF16)
        branch[...] = jnp.zeros_like(branch)
        gn2[...] = jnp.zeros_like(gn2)

    wcol = we[...]
    wrow = ws[...]
    body = (mm(nx[...], wcol) + hid[0:1, :]).astype(BF16)
    e_low[...] = body
    e_scr[...] = body.astype(F32)
    ga_scr[...] = mm_nt(cx[...], wrow)
    for there, start in ((top, 0), (low, 2 * W + own)):

        @pl.when(there == 0)
        def _():
            for s in range(scenes):
                e_scr[s * ext + start : s * ext + start + 2 * W, :] = jnp.zeros((2 * W, CH), F32)

    col = lax.broadcasted_iota(jnp.int32, (8, CH), 0)
    first, last = col == 0, col == 7

    def right(value):
        moved = pltpu.roll(value, 1, axis=0)
        return jnp.concatenate([jnp.where(first, 0.0, moved[0:8]), moved[8:]], axis=0)

    def left(value):
        moved = pltpu.roll(value, W - 1, axis=0)
        return jnp.concatenate([moved[: W - 8], jnp.where(last, 0.0, moved[W - 8 :])], axis=0)

    def fold(value):
        value = value[0:32] + value[32:64]
        value = value[0:16] + value[16:32]
        return (value[0:8] + value[8:16]).astype(F32)

    taps = [hid[1 + k : 2 + k, :] * SHRINK_IN for k in range(9)]
    low_taps = [hid[1 + k : 2 + k, :].astype(BF16) for k in range(9)]
    conv_bias = hid[10:11, :] * SHRINK_IN

    for s in range(scenes):

        def forward(r, carry):
            at = pl.multiple_of(s * ext + r * W, W)
            lines = [e_scr[pl.ds(at + a * W, W), :] for a in range(3)]
            sums = [
                lines[0] * taps[b] + lines[1] * taps[3 + b] + lines[2] * taps[6 + b]
                for b in range(3)
            ]
            u = conv_bias + right(sums[0]) + sums[1] + left(sums[2])
            cdf, bell = gelu_parts(u)
            gat = pl.multiple_of(s * gext + r * W, W)
            gc = ga_scr[pl.ds(gat, W), :] * (cdf + u * bell)
            act_scr[pl.ds(gat, W), :] = (u * cdf).astype(BF16)
            gc_scr[0, pl.ds(gat, W), :] = left(gc).astype(BF16)
            gc_scr[1, pl.ds(gat, W), :] = gc.astype(BF16)
            gc_scr[2, pl.ds(gat, W), :] = right(gc).astype(BF16)
            return carry

        lax.fori_loop(0, rows + 2, forward, 0)

    def backward(s, r, carry):
        line = e_low[pl.ds(pl.multiple_of(s * ext + (r + 2) * W, W), W), :]
        grads = list(carry)
        total = None
        for a in range(3):
            gat = pl.multiple_of(s * gext + (r + 2 - a) * W, W)
            for b in range(3):
                g = gc_scr[b, pl.ds(gat, W), :]
                term = g * low_taps[3 * a + b]
                total = term if total is None else total + term
                grads[3 * a + b] = grads[3 * a + b] + fold(g * line)
                if a == 1 and b == 1:
                    grads[9] = grads[9] + fold(g)
        ge_scr[pl.ds(pl.multiple_of(s * own + r * W, W), W), :] = total
        return tuple(grads)

    sums = tuple(jnp.zeros((8, CH), F32) for _ in range(10))
    for s in range(scenes):
        sums = lax.fori_loop(0, rows, functools.partial(backward, s), sums)
    for k in range(10):
        ghid_out[1 + k : 2 + k, :] = row_sum(sums[k]) * SLOPE

    ge = ge_scr[...]
    grads = mm(nt[...], ge)
    gwe_out[...] = grads[0:C, :] * SLOPE
    ghid_out[0:1, :] = grads[C : C + 1, :] * SLOPE
    gn2[...] += mm_nt(ge, wcol)
    gws = None
    for s in range(scenes):
        at = slice(s * own, (s + 1) * own)
        act = act_scr[s * gext + W : s * gext + W + own, :]
        branch[at, :] += mm(act, wrow)
        term = mm(ct[:, at], act)
        gws = term if gws is None else gws + term
    gws_out[...] = gws * ACT_SCALE

    @pl.when(step == pl.num_programs(0) - 1)
    def _():
        size = 4 * W
        per = own // size
        gain = vec[V_GAIN2 : V_GAIN2 + 1, :]

        def finish(i, carry):
            at = pl.multiple_of(i * size, size)
            s = i // per
            line = (i % per) * 4
            middle = mid[pl.ds(at, size), :]
            y_out[pl.ds(at, size), :] = (
                middle + branch[pl.ds(at, size), :] * ACT_SCALE + vec[V_SHRINK : V_SHRINK + 1, :]
            ).astype(BF16)
            grad = gn2[pl.ds(at, size), :] * SLOPE
            unit, rstd = norm_parts(middle)
            direct = cot[s, pl.ds(line, 4)].reshape(size, C).astype(F32)
            gmid_out[pl.ds(at, size), :] = direct + norm_back(grad, unit, rstd, gain)
            return (
                carry[0] + row_sum(grad * unit),
                carry[1] + row_sum(grad),
                carry[2] + row_sum(direct),
            )

        zero = jnp.zeros((1, C), F32)
        sums = lax.fori_loop(0, scenes * per, finish, (zero, zero, zero))
        for i in range(3):
            gvec_out[i : i + 1, :] = sums[i]


def mix(n2, n2_top, n2_low, cot, cot_top, cot_low, mid, edge, vec, hid, we, ws):
    scenes, rows = n2.shape[0], n2.shape[1]
    tokens = scenes * rows * W
    ext = scenes * (rows + 4) * W
    gext = scenes * (rows + 2) * W
    once = dict(pipeline_mode=pl.Buffered(1))
    whole = lambda a: pl.BlockSpec(a.shape, lambda j: (0,) * a.ndim, **once)
    return pl.pallas_call(
        mix_kernel,
        name="mix",
        grid=(FF // CH,),
        in_specs=[
            whole(n2),
            whole(n2_top),
            whole(n2_low),
            whole(cot),
            whole(cot_top),
            whole(cot_low),
            whole(mid),
            pl.BlockSpec(memory_space=pltpu.SMEM),
            whole(vec),
            pl.BlockSpec((16, CH), lambda j: (0, j)),
            pl.BlockSpec((C, CH), lambda j: (0, j)),
            pl.BlockSpec((CH, C), lambda j: (j, 0)),
        ],
        out_specs=[
            full((tokens, C)),
            full((tokens, C)),
            pl.BlockSpec((C, CH), lambda j: (0, j)),
            pl.BlockSpec((C, CH), lambda j: (0, j)),
            pl.BlockSpec((16, CH), lambda j: (0, j)),
            full((8, C)),
        ],
        out_shape=(
            shape_of((tokens, C), BF16),
            shape_of((tokens, C), F32),
            shape_of((C, FF), F32),
            shape_of((C, FF), F32),
            shape_of((16, FF), F32),
            shape_of((8, C), F32),
        ),
        scratch_shapes=[
            pltpu.VMEM((ext, C), BF16),
            pltpu.VMEM((gext, C), BF16),
            pltpu.VMEM((C + 16, tokens), BF16),
            pltpu.VMEM((C, tokens), BF16),
            pltpu.VMEM((ext, CH), F32),
            pltpu.VMEM((ext, CH), BF16),
            pltpu.VMEM((gext, CH), F32),
            pltpu.VMEM((3, gext, CH), BF16),
            pltpu.VMEM((gext, CH), BF16),
            pltpu.VMEM((tokens, CH), BF16),
            pltpu.VMEM((tokens, C), F32),
            pltpu.VMEM((tokens, C), F32),
        ],
        compiler_params=PARAMS,
    )(n2, n2_top, n2_low, cot, cot_top, cot_low, mid, edge, vec, hid, we, ws)


QTB = 256


def attend_back_kernel(
    q_ref, inv_ref, mixed_ref, gmid_ref, p_ref, key_ref, vt_ref, rn_ref, wk, wv, wo,
    dq_out, grn_out, gwk_out, gwv_out, gwo_out, gvec_out, kh, dkt, dvt,
):
    scene, step = pl.program_id(0), pl.program_id(1)
    keys = rn_ref.shape[0] * rn_ref.shape[2]

    @pl.when(jnp.logical_and(scene == 0, step == 0))
    def _():
        for ref in (gwk_out, gwv_out, gwo_out, gvec_out):
            ref[...] = jnp.zeros_like(ref)

    @pl.when(step == 0)
    def _():
        for h in range(HEADS):
            kh[h] = key_ref[0, :, h * HD : (h + 1) * HD]
        dkt[...] = jnp.zeros_like(dkt)
        dvt[...] = jnp.zeros_like(dvt)

    gatt = gmid_ref[...].astype(BF16)
    gvec_out[8:9, :] += row_sum(gatt.astype(F32))
    mixed = mixed_ref[...]
    gwo_out[...] += mm_tn(mixed, gatt)
    scaled = (mm_nt(gatt, wo[...]) * inv_ref[...]).astype(BF16)
    prod = scaled.astype(F32) * mixed.astype(F32)
    q_t = q_ref[...].T
    g_t = scaled.T
    dqs = []
    for h in range(HEADS):
        cols = slice(h * HD, (h + 1) * HD)
        inner = jnp.sum(prod[:, cols], axis=-1, keepdims=True)
        probs = p_ref[0, h]
        gprobs = mm(scaled[:, cols], vt_ref[0, cols, :])
        gscores = (probs.astype(F32) * (gprobs - inner)).astype(BF16)
        dqs.append(mm(gscores, kh[h]))
        dkt[cols, :] += mm(q_t[cols, :], gscores)
        dvt[cols, :] += mm(g_t[cols, :], probs)
    dq_out[...] = (jnp.concatenate(dqs, axis=1) * (1.0 / math.sqrt(HD))).astype(BF16)

    @pl.when(step == pl.num_programs(1) - 1)
    def _():
        rn = rn_ref[:, 0].reshape(keys, C)
        dk = dkt[...].astype(BF16)
        dv = dvt[...].astype(BF16)
        gvec_out[0:8, :] += mm_nt(jnp.ones((8, keys), BF16), dv)
        gwk_out[...] += mm(dk, rn)
        gwv_out[...] += mm(dv, rn)
        grn = (mm(wk[...], dk) + mm(wv[...], dv)).astype(BF16)
        grn_out[...] = grn.T.reshape(grn_out.shape)


def attend_back(q, inv, mixed, gmid, p, key, vt, rn_all, wk, wv, wo):
    tokens = q.shape[0]
    bands, scenes, per_band, _ = rn_all.shape
    keys = bands * per_band
    steps = tokens // scenes // QTB
    tile = pl.BlockSpec((QTB, C), lambda s, i: (s * steps + i, 0))
    return pl.pallas_call(
        attend_back_kernel,
        name="attend_back",
        grid=(scenes, steps),
        in_specs=[
            tile,
            tile,
            tile,
            tile,
            pl.BlockSpec((1, HEADS, QTB, keys), lambda s, i: (s, 0, i, 0)),
            pl.BlockSpec((1, keys, C), lambda s, i: (s, 0, 0)),
            pl.BlockSpec((1, C, keys), lambda s, i: (s, 0, 0)),
            pl.BlockSpec((bands, 1, per_band, C), lambda s, i: (0, s, 0, 0)),
            full((C, C)),
            full((C, C)),
            full((C, C)),
        ],
        out_specs=[
            tile,
            pl.BlockSpec((bands, 1, per_band, C), lambda s, i: (0, s, 0, 0)),
            full((C, C)),
            full((C, C)),
            full((C, C)),
            full((16, C)),
        ],
        out_shape=(
            shape_of((tokens, C), BF16),
            shape_of(rn_all.shape, BF16),
            shape_of((C, C), F32),
            shape_of((C, C), F32),
            shape_of((C, C), F32),
            shape_of((16, C), F32),
        ),
        scratch_shapes=[
            pltpu.VMEM((HEADS, keys, HD), BF16),
            pltpu.VMEM((C, keys), F32),
            pltpu.VMEM((C, keys), F32),
        ],
        compiler_params=PARAMS,
    )(q, inv, mixed, gmid, p, key, vt, rn_all, wk, wv, wo)


def tail_kernel(
    x_ref, gmid_ref, dq_ref, grn_ref, red_ref, vec, wq, wr,
    gx_out, gwq_out, gwr_out, gvec_out, scr, gscr,
):
    @pl.when(pl.program_id(0) == 0)
    def _():
        for ref in (gwq_out, gwr_out, gvec_out):
            ref[...] = jnp.zeros_like(ref)

    runit, rrstd = norm_parts(red_ref[...])
    grn = grn_ref[...].astype(F32)
    gred = norm_back(grn, runit, rrstd, vec[V_RGAIN : V_RGAIN + 1, :]).astype(BF16)
    unit, rstd = norm_parts(x_ref[...].astype(F32))
    gain = vec[V_GAIN1 : V_GAIN1 + 1, :]
    normed = (unit * gain + vec[V_SHIFT1 : V_SHIFT1 + 1, :]).astype(BF16)
    split_tiles(scr, normed.astype(F32))
    pieces = patch_pieces(scr)
    back = {}
    for k in range(4):
        at = slice(k * C, (k + 1) * C)
        gwr_out[at, :] += mm_tn(pieces[k].astype(BF16), gred)
        back[k] = mm_nt(gred, wr[at, :]).reshape(TILE // (2 * W), 1, W // 2, C)
    for b in range(2):
        cols = jnp.concatenate([back[b], back[2 + b]], axis=1).reshape(TILE // 2, C)
        spot = pl.ds(b, TILE // 2, stride=2)
        gscr[0, spot, :] = cols[:, 0:128]
        gscr[1, spot, :] = cols[:, 128:256]
        gscr[2, spot, :] = jnp.concatenate(
            [cols[:, 256:320], jnp.zeros((TILE // 2, 64), F32)], axis=1
        )
    dq = dq_ref[...]
    gwq_out[...] += mm_tn(normed, dq)
    placed = jnp.concatenate([gscr[0], gscr[1], gscr[2][:, 0:64]], axis=1)
    gnormed = mm_nt(dq, wq[...]) + placed
    gx_out[...] = gmid_ref[...] + norm_back(gnormed, unit, rstd, gain)
    gvec_out[0:1, :] += row_sum(dq.astype(F32))
    gvec_out[1:2, :] += row_sum(gred.astype(F32))
    gvec_out[2:3, :] += row_sum(grn * runit)
    gvec_out[3:4, :] += row_sum(grn)
    gvec_out[4:5, :] += row_sum(gnormed * unit)
    gvec_out[5:6, :] += row_sum(gnormed)


def tail(x, gmid, dq, grn, red, vec, wq, wr):
    tokens = x.shape[0]
    tile = pl.BlockSpec((TILE, C), lambda i: (i, 0))
    rtile = pl.BlockSpec((RTILE, C), lambda i: (i, 0))
    return pl.pallas_call(
        tail_kernel,
        name="tail",
        grid=(tokens // TILE,),
        in_specs=[
            tile, tile, tile, rtile, rtile, full((16, C)), full((C, C)), full((4 * C, C))
        ],
        out_specs=[tile, full((C, C)), full((4 * C, C)), full((8, C))],
        out_shape=(
            shape_of((tokens, C), F32),
            shape_of((C, C), F32),
            shape_of((4 * C, C), F32),
            shape_of((8, C), F32),
        ),
        scratch_shapes=[pltpu.VMEM((3, TILE, 128), F32), pltpu.VMEM((3, TILE, 128), F32)],
        compiler_params=PARAMS,
    )(x, gmid, dq, grn, red, vec, wq, wr)


ANY = pl.BlockSpec(memory_space=pl.ANY)
VM = pl.BlockSpec(memory_space=pltpu.VMEM)


def flip(value, by):
    return value + by * (1 - 2 * value)


def remote(src, dst, send, recv, where):
    return pltpu.make_async_remote_copy(
        src_ref=src,
        dst_ref=dst,
        send_sem=send,
        recv_sem=recv,
        device_id=where,
        device_id_type=pl.DeviceIdType.MESH,
    )


def greet(places):
    barrier = pltpu.get_barrier_semaphore()
    count = 0
    for place, there in places:
        if there is None:
            pl.semaphore_signal(
                barrier, inc=1, device_id=place, device_id_type=pl.DeviceIdType.MESH
            )
            count = count + 1
        else:

            @pl.when(there)
            def _():
                pl.semaphore_signal(
                    barrier, inc=1, device_id=place, device_id_type=pl.DeviceIdType.MESH
                )

            count = count + there.astype(jnp.int32)
    pl.semaphore_wait(barrier, count)


def comm_params(number):
    return pltpu.CompilerParams(
        collective_id=number, has_side_effects=True, vmem_limit_bytes=60 * 1024 * 1024
    )


class Place:
    def __init__(self):
        dp, space = lax.axis_index("dp"), lax.axis_index("space")
        self.z, self.x = dp // 2, dp % 2
        self.y, self.c = space // 2, space % 2
        self.line = lax.axis_size("dp") // 2

    def block(self, z, x, y, c):
        return ((z * 2 + x) * 2 + y) * 2 + c

    def device(self, z, x, y, c):
        return {"dp": z * 2 + x, "space": y * 2 + c}

    def spot(self, da, db, c):
        return (
            flip(self.x, da * (1 - c) + db * c),
            flip(self.y, db * (1 - c) + da * c),
        )

    def partners(self):
        ax, ay = self.spot(1, 0, self.c)
        bx, by = self.spot(0, 1, self.c)
        return (
            self.device(self.z, ax, ay, self.c),
            self.device(self.z, bx, by, self.c),
            self.device(self.z, self.x, self.y, 1 - self.c),
            self.device(self.z + 1, self.x, self.y, self.c),
            self.device(self.z - 1, self.x, self.y, self.c),
        )

    def meet(self):
        first, second, sibling, up, down = self.partners()
        greet(
            [
                (first, None),
                (second, None),
                (sibling, None),
                (up, self.z < self.line - 1),
                (down, self.z > 0),
            ]
        )


DMA = pltpu.SemaphoreType.DMA
PART = 208


def compact(block):
    half = BLOCK_ROWS // 2
    tail = jnp.concatenate([block[:half, 256:], block[half:, 256:]], axis=1)
    spare = jnp.zeros((2 * PART - 2 * BLOCK_ROWS - half, 128), block.dtype)
    return jnp.concatenate([block[:, 0:128], block[:, 128:256], tail, spare], axis=0)


def restore(rows):
    half = BLOCK_ROWS // 2
    tail = rows[2 * BLOCK_ROWS : 2 * BLOCK_ROWS + half]
    return jnp.concatenate(
        [
            rows[:BLOCK_ROWS],
            rows[BLOCK_ROWS : 2 * BLOCK_ROWS],
            jnp.concatenate([tail[:, 0:64], tail[:, 64:128]], axis=0),
        ],
        axis=1,
    )


PLANE = [(da, db) for da in range(2) for db in range(2)]


def gather_kernel(own_ref, out, own, p_z, p_a, p_b, p_c, q_z, q_a, q_b, q_c, recv):
    at = Place()
    line = at.line
    first, second, sibling, up, down = at.partners()
    own[...] = compact(own_ref[...].astype(F32)).reshape(2, PART, 128).astype(BF16)
    at.meet()
    can_up, can_down = at.z < line - 1, at.z > 0

    def index_of(z, da, db, c):
        x, y = at.spot(da, db, at.c)
        return at.block(z, x, y, c)

    def push(part, index, src, sem, where):
        remote(src, out.at[index, part], sem, recv.at[index, part], where).start()

    def landed(part, index):
        remote(
            out.at[index, part], out.at[index, part], p_a.at[0], recv.at[index, part], sibling
        ).wait_recv()

    def here(part, index, is_own):
        return own.at[part] if is_own else out.at[index, part]

    def along_z(part, z, k, index, src, way, sems):
        if way >= 0:

            @pl.when(can_up)
            def _():
                push(part, index, src, sems.at[0, k, z], up)

        if way <= 0:

            @pl.when(can_down)
            def _():
                push(part, index, src, sems.at[1, k, z], down)

    def first_order(z, da, db, way, is_own=False):
        index = index_of(z, da, db, at.c)
        if not is_own:
            landed(0, index)
        src = here(0, index, is_own)
        if da == 0 and db == 0:
            along_z(0, z, 0, index, src, way, p_z)
            push(0, index, src, p_a.at[z], first)
        if db == 0:
            push(0, index, src, p_b.at[da, z], second)
        push(0, index, src, p_c.at[2 * da + db, z], sibling)

    def second_order(z, da, db, way, is_own=False):
        index = index_of(z, da, db, at.c)
        if not is_own:
            landed(1, index)
        src = here(1, index, is_own)
        if way == 0:
            if da == 0 and db == 0:
                push(1, index, src, q_a, first)
            if db == 0:
                push(1, index, src, q_b.at[da], second)
        along_z(1, z, 2 * da + db, index, src, way, q_z)
        push(1, index, src, q_c.at[2 * da + db, z], sibling)

    def hop(d, order, places):
        for z in range(line):
            if z >= d:

                @pl.when(at.z == z)
                def _():
                    for da, db in places:
                        order(z - d, da, db, 1)

            if z + d < line:

                @pl.when(at.z == z)
                def _():
                    for da, db in places:
                        order(z + d, da, db, -1)

    def flat_hops(da, db):
        first_order(at.z, da, db, 0)
        for d in range(1, line):
            hop(d, lambda z, da, db, way: first_order(z, da, db, way), [(da, db)])

    second_order(at.z, 0, 0, 0, True)
    first_order(at.z, 0, 0, 0, True)
    mine = index_of(at.z, 0, 0, at.c)
    out[mine] = own[...]
    second_order(at.z, 1, 0, 0)
    hop(1, first_order, [(0, 0)])
    second_order(at.z, 0, 1, 0)
    second_order(at.z, 1, 1, 0)
    hop(2, first_order, [(0, 0)])
    hop(1, second_order, PLANE)
    hop(3, first_order, [(0, 0)])
    flat_hops(1, 0)
    hop(2, second_order, PLANE)
    flat_hops(0, 1)
    flat_hops(1, 1)
    hop(3, second_order, PLANE)
    for z in range(line):
        for da, db in PLANE:
            for part in range(2):
                landed(part, index_of(z, da, db, 1 - at.c))

    def sent(part, sem, where):
        remote(own.at[part], out.at[mine, part], sem, recv.at[mine, part], where).wait_send()

    sent(1, q_a, first)
    for z in range(line):
        for k in range(4):
            sent(0, p_c.at[k, z], sibling)
            sent(1, q_c.at[k, z], sibling)
        sent(0, p_a.at[z], first)
        for da in range(2):
            sent(0, p_b.at[da, z], second)

        @pl.when(jnp.logical_and(can_up, z <= at.z))
        def _():
            sent(0, p_z.at[0, 0, z], up)
            for k in range(4):
                sent(1, q_z.at[0, k, z], up)

        @pl.when(jnp.logical_and(can_down, z >= at.z))
        def _():
            sent(0, p_z.at[1, 0, z], down)
            for k in range(4):
                sent(1, q_z.at[1, k, z], down)

    for da in range(2):
        sent(1, q_b.at[da], second)


def gather_blocks(own):
    return pl.pallas_call(
        gather_kernel,
        name="gather",
        out_shape=shape_of((BLOCKS, 2, PART, 128), BF16),
        in_specs=[VM],
        out_specs=VM,
        scratch_shapes=[
            pltpu.VMEM((2, PART, 128), BF16),
            DMA((2, 1, 4)), DMA((4,)), DMA((2, 4)), DMA((4, 4)),
            DMA((2, 4, 4)), DMA, DMA((2,)), DMA((4, 4)),
            DMA((BLOCKS, 2)),
        ],
        compiler_params=comm_params(1),
    )(own)


def scatter_kernel(
    parts, out,
    rc, acc, ra, acc2, rb, acc3, rz, sz,
    qc, qacc, qrz, qsz, qplane, qra, qacc2, qrb,
    c_out, a_out, b_out, z_out, qc_out, qz_out, qa_out, qb_out,
    c_in, a_in, b_in, z_in, qc_in, qz_in, qa_in, qb_in,
):
    at = Place()
    line = at.line
    first, second, sibling, up, down = at.partners()
    at.meet()
    slots = [(da, db, z) for da in (1, 0) for db in (1, 0) for z in range(line)]

    def add(*terms):
        total = terms[0].astype(F32)
        for term in terms[1:]:
            total = total + term.astype(F32)
        return total.astype(BF16)

    def source(k, c):
        da, db, z = slots[k]
        x, y = at.spot(da, db, c)
        return at.block(z, x, y, c)

    def c_copy(k):
        src = parts.at[source(k, 1 - at.c), 0]
        return remote(src, rc.at[k], c_out.at[k], c_in.at[k], sibling)

    def qc_copy(k):
        src = parts.at[source(k, 1 - at.c), 1]
        return remote(src, qc.at[k], qc_out.at[k], qc_in.at[k], sibling)

    def a_copy(j):
        return remote(acc.at[j], ra.at[j], a_out.at[j], a_in.at[j], first)

    def b_copy(j):
        return remote(acc2.at[j], rb.at[j], b_out.at[j], b_in.at[j], second)

    def z_copy(way, z):
        return remote(
            sz.at[way, z], rz.at[way, z], z_out.at[way, z], z_in.at[way, z], (up, down)[way]
        )

    def qz_copy(way, k, src=None):
        src = qsz.at[way, k] if src is None else src
        return remote(src, qrz.at[way, k], qz_out.at[way, k], qz_in.at[way, k], (up, down)[way])

    def qa_copy(j):
        return remote(qplane.at[j], qra.at[j], qa_out.at[j], qa_in.at[j], first)

    def qb_copy():
        return remote(qacc2.at[0], qrb, qb_out, qb_in, second)

    count = 4 * line
    for k in range(count):
        qc_copy(k).start()
        c_copy(k).start()
    for k in range(count):
        da, db, z = slots[k]
        qc_copy(k).wait_recv()
        mine = source(k, at.c)
        qacc[k] = add(parts[mine, 1], qc[k])
        if z > 0:

            @pl.when(at.z == 0)
            def _():
                qz_copy(0, k, qacc.at[k]).start()

        if z < line - 1:

            @pl.when(at.z == line - 1)
            def _():
                qz_copy(1, k, qacc.at[k]).start()

        c_copy(k).wait_recv()
        acc[k] = add(parts[mine, 0], rc[k])
        if da:
            a_copy(k).start()

    def q_hop(d):
        for k in range(count):
            z = slots[k][2]
            if z >= d:

                @pl.when(at.z == d)
                def _():
                    qz_copy(0, k).wait_recv()
                    if z > d:
                        qsz[0, k] = add(qacc[k], qrz[0, k])
                        qz_copy(0, k).start()

            if z <= line - 1 - d:

                @pl.when(at.z == line - 1 - d)
                def _():
                    qz_copy(1, k).wait_recv()
                    if z < line - 1 - d:
                        qsz[1, k] = add(qacc[k], qrz[1, k])
                        qz_copy(1, k).start()

    def p_hop(d):
        for z in reversed(range(d, line)):

            @pl.when(at.z == d)
            def _():
                if d > 0:
                    z_copy(0, z).wait_recv()
                if z > d:
                    sz[0, z] = add(acc3[z], rz[0, z]) if d > 0 else acc3[z]
                    z_copy(0, z).start()

        for z in range(line - d):

            @pl.when(at.z == line - 1 - d)
            def _():
                if d > 0:
                    z_copy(1, z).wait_recv()
                if z < line - 1 - d:
                    sz[1, z] = add(acc3[z], rz[1, z]) if d > 0 else acc3[z]
                    z_copy(1, z).start()

    def inflows(z):
        return [way for way, there in ((0, z > 0), (1, z < line - 1)) if there]

    for j in range(line):
        a_copy(j).wait_recv()
        acc2[j] = add(acc[2 * line + j], ra[j])
        b_copy(j).start()
    q_hop(1)
    for j in range(line, 2 * line):
        a_copy(j).wait_recv()
        acc2[j] = add(acc[2 * line + j], ra[j])
    q_hop(2)
    for z in range(line):
        b_copy(z).wait_recv()
        acc3[z] = add(acc2[line + z], rb[z])
    p_hop(0)
    q_hop(3)
    for z in range(line):

        @pl.when(at.z == z)
        def _():
            for j in range(4):
                k = j * line + z
                qplane[j] = add(qacc[k], *[qrz[way, k] for way in inflows(z)])

    qa_copy(0).start()
    qa_copy(1).start()
    p_hop(1)
    for j in range(2):
        qa_copy(j).wait_recv()
        qacc2[j] = add(qplane[2 + j], qra[j])
        if j == 0:
            qb_copy().start()
    p_hop(2)
    qb_copy().wait_recv()
    q_total = qacc2[1].astype(F32) + qrb[...].astype(F32)
    p_hop(3)
    for z in range(line):

        @pl.when(at.z == z)
        def _():
            total = acc3[z].astype(F32)
            for way in inflows(z):
                total = total + rz[way, z].astype(F32)
            out[...] = restore(jnp.concatenate([total, q_total], axis=0))

    for k in range(count):
        c_copy(k).wait_send()
        qc_copy(k).wait_send()
        z = slots[k][2]

        @pl.when(at.z < z)
        def _():
            qz_copy(0, k).wait_send()

        @pl.when(at.z > z)
        def _():
            qz_copy(1, k).wait_send()

    for j in range(2 * line):
        a_copy(j).wait_send()
    for z in range(line):
        b_copy(z).wait_send()

        @pl.when(at.z < z)
        def _():
            z_copy(0, z).wait_send()

        @pl.when(at.z > z)
        def _():
            z_copy(1, z).wait_send()

    qa_copy(0).wait_send()
    qa_copy(1).wait_send()
    qb_copy().wait_send()


def scatter_blocks(parts):
    room = lambda *n: pltpu.VMEM(n + (PART, 128), BF16)
    sems = lambda: [
        DMA((16,)), DMA((8,)), DMA((4,)), DMA((2, 4)), DMA((16,)), DMA((2, 16)), DMA((2,)), DMA,
    ]
    return pl.pallas_call(
        scatter_kernel,
        name="scatter",
        out_shape=shape_of((BLOCK_ROWS, C), F32),
        in_specs=[VM],
        out_specs=VM,
        scratch_shapes=[
            room(16), room(16), room(8), room(8), room(4), room(4), room(2, 4), room(2, 4),
            room(16), room(16), room(2, 16), room(2, 16), room(4), room(2), room(2), room(),
        ]
        + sems()
        + sems(),
        compiler_params=comm_params(2),
    )(parts)


def bands_of():
    band = lax.axis_index("space")
    pair, core = band // 2, band % 2
    return band, pair * 2 + 1 - core, (1 - pair) * 2 + core


def swap_kernel(width, value, above, below, up_sem, down_sem, up_in, down_in, ready):
    band = lax.axis_index("space")
    rows = value.shape[1]
    ends = lax.axis_size("space") - 1
    down = remote(
        value.at[:, pl.ds(rows - width, width)], above, down_sem, down_in, {"space": band + 1}
    )
    up = remote(value.at[:, pl.ds(0, width)], below, up_sem, up_in, {"space": band - 1})

    @pl.when(band < ends)
    def _():
        down.start()

    @pl.when(band > 0)
    def _():
        up.start()

    def finish():
        @pl.when(band < ends)
        def _():
            down.wait_send()
            up.wait_recv()

        @pl.when(band > 0)
        def _():
            up.wait_send()
            down.wait_recv()

    return finish


def bands_meet(others):
    band = lax.axis_index("space")
    ends = lax.axis_size("space") - 1
    greet(
        [({"space": o}, None) for o in others]
        + [({"space": band + 1}, band < ends), ({"space": band - 1}, band > 0)]
    )


def share_kernel(
    rn, cot, rn_all, above, below, send, recv, own_sem, up_sem, down_sem, up_in, down_in
):
    band, sibling, across = bands_of()
    bands_meet((sibling, across))
    to_sibling = remote(rn, rn_all.at[band], send.at[0], recv.at[band], {"space": sibling})
    to_across = remote(rn, rn_all.at[band], send.at[1], recv.at[band], {"space": across})
    to_across.start()
    to_sibling.start()
    own = pltpu.make_async_copy(rn, rn_all.at[band], own_sem)
    own.start()
    finish = swap_kernel(1, cot, above, below, up_sem, down_sem, up_in, down_in, None)

    def landed(index):
        remote(rn, rn_all.at[index], send.at[0], recv.at[index], {"space": sibling}).wait_recv()

    landed(across)
    onward = remote(
        rn_all.at[across], rn_all.at[across], send.at[2], recv.at[across], {"space": sibling}
    )
    onward.start()
    landed(sibling)
    landed(across + sibling - band)
    own.wait()
    to_across.wait_send()
    to_sibling.wait_send()
    onward.wait_send()
    finish()


def share(rn, cot):
    bands = lax.axis_size("space")
    dma = pltpu.SemaphoreType.DMA
    edge = (cot.shape[0], 1) + cot.shape[2:]
    return pl.pallas_call(
        share_kernel,
        name="share",
        out_shape=(
            shape_of((bands,) + rn.shape, rn.dtype),
            shape_of(edge, cot.dtype),
            shape_of(edge, cot.dtype),
        ),
        in_specs=[VM, ANY],
        out_specs=(ANY, ANY, ANY),
        scratch_shapes=[dma((3,)), dma((bands,)), dma, dma, dma, dma, dma],
        compiler_params=comm_params(3),
    )(rn, cot)


def halo_kernel(value, above, below, up_sem, down_sem, up_in, down_in):
    bands_meet(())
    swap_kernel(2, value, above, below, up_sem, down_sem, up_in, down_in, None)()


def halo(value):
    dma = pltpu.SemaphoreType.DMA
    edge = (value.shape[0], 2) + value.shape[2:]
    return pl.pallas_call(
        halo_kernel,
        name="halo",
        out_shape=(shape_of(edge, value.dtype), shape_of(edge, value.dtype)),
        in_specs=[ANY],
        out_specs=(ANY, ANY),
        scratch_shapes=[dma, dma, dma, dma],
        compiler_params=comm_params(4),
    )(value)


def merge_kernel(parts, out, rc, acc, rb, c_sem, c_in, b_sem, b_in):
    band, sibling, across = bands_of()
    greet([({"space": sibling}, None), ({"space": across}, None)])
    far = across + sibling - band
    first = remote(parts.at[far], rc.at[0], c_sem.at[0], c_in.at[0], {"space": sibling})
    second = remote(parts.at[sibling], rc.at[1], c_sem.at[1], c_in.at[1], {"space": sibling})
    onward = remote(acc, rb, b_sem, b_in, {"space": across})
    first.start()
    second.start()
    first.wait_recv()
    acc[...] = (parts[across].astype(F32) + rc[0].astype(F32)).astype(BF16)
    onward.start()
    second.wait_recv()
    out[...] = parts[band].astype(F32) + rc[1].astype(F32)
    onward.wait_recv()
    out[...] += rb[...].astype(F32)
    first.wait_send()
    second.wait_send()
    onward.wait_send()


def merge(parts):
    one = parts.shape[1:]
    dma = pltpu.SemaphoreType.DMA
    return pl.pallas_call(
        merge_kernel,
        name="merge",
        out_shape=shape_of(one, F32),
        in_specs=[VM],
        out_specs=VM,
        scratch_shapes=[
            pltpu.VMEM((2,) + one, BF16),
            pltpu.VMEM(one, BF16),
            pltpu.VMEM(one, BF16),
            dma((2,)),
            dma((2,)),
            dma,
            dma,
        ],
        compiler_params=comm_params(5),
    )(parts)


def blocks_fit(size):
    return (
        lax.axis_size("dp") == 8 and lax.axis_size("space") == 4 and size == BLOCK_ROWS * C
    )


def gather_params(params):
    if blocks_fit(params.shape[0]):
        return gather_blocks(params.reshape(BLOCK_ROWS, C))
    flat = lax.all_gather(params, ("dp", "space"), axis=0, tiled=True)
    want = ROWS * C
    flat = flat[:want] if flat.shape[0] >= want else jnp.pad(flat, (0, want - flat.shape[0]))
    blocks = jax.vmap(compact)(flat.reshape(BLOCKS, BLOCK_ROWS, C))
    return blocks.reshape(BLOCKS, 2, PART, 128)


def scatter_grads(blocks, size):
    if blocks_fit(size):
        return scatter_blocks(blocks).reshape(size)
    flat = jax.vmap(restore)(blocks.reshape(BLOCKS, 2 * PART, 128)).reshape(-1)
    want = size * lax.axis_size("dp") * lax.axis_size("space")
    flat = flat[:want] if flat.shape[0] >= want else jnp.pad(flat, (0, want - flat.shape[0]))
    own = lax.psum_scatter(flat, ("dp", "space"), scatter_dimension=0, tiled=True)
    return own.astype(F32)


def on_device(scenes, params, cotangent):
    count, rows, breadth = scenes.shape[0], scenes.shape[1], scenes.shape[2]
    tokens = count * rows * breadth
    bands = lax.axis_size("space")
    per_band = rows * breadth // 4
    band = lax.axis_index("space")
    edge = jnp.stack([band > 0, band < bands - 1]).astype(F32)
    wq, wr, wk, wv, wo, we, ws, vec, hid = unpack(gather_params(params))
    x = scenes.reshape(tokens, C)
    q, red, rn = front(x, vec, wq, wr)
    rn_all, cot_top, cot_low = share(rn, cotangent)
    rn_all = rn_all.reshape(bands, count, per_band, C)
    mixed, inv, mid, n2, p, key, vt = attend(x, q, rn_all, vec, wk, wv, wo)
    n2 = n2.reshape(scenes.shape)
    n2_top, n2_low = halo(n2)
    y, gmid, gwe, gws, ghid, gvec2 = mix(
        n2, n2_top, n2_low, cotangent, cot_top, cot_low, mid, edge, vec, hid, we, ws
    )
    dq, grn_all, gwk, gwv, gwo, gvec1 = attend_back(
        q, inv, mixed, gmid, p, key, vt, rn_all, wk, wv, wo
    )
    grn = merge(grn_all.reshape(bands, count * per_band, C))
    gx, gwq, gwr, gvec0 = tail(x, gmid, dq, grn, red, vec, wq, wr)
    blocks = pack(gwq, gwr, gwk, gwv, gwo, gwe, gws, gvec0, gvec1, gvec2, ghid)
    shard = scatter_grads(blocks, params.shape[0])
    return y.reshape(scenes.shape), gx.reshape(scenes.shape), shard


def solution(mesh):
    band = P("dp", "space", None, None)
    flat = P(("dp", "space"))
    return jax.shard_map(
        on_device,
        mesh=mesh,
        in_specs=(band, flat, band),
        out_specs=(band, band, flat),
        check_vma=False,
    )
```

```python
import functools
import math

import jax
import jax.numpy as jnp
from jax import lax
from jax.experimental import pallas as pl
from jax.experimental.pallas import tpu as pltpu
from jax.sharding import PartitionSpec as P

C = 320
HEADS = 5
HD = 64
FF = 1280
W = 64
EPSILON = 1e-06
F32 = jnp.float32
BF16 = jnp.bfloat16

ROWS = 5184
USED_ROWS = 5175
BLOCKS = 32
BLOCK_ROWS = ROWS // BLOCKS
R_QUERY = 0
R_REDUCE = 321
R_KEYVAL = 1604
R_OUTPUT = 2245
R_EXPAND = 2570
R_HIDDEN = 3850
R_SHRINK = 3894
VECTOR_ROWS = (320, 1601, 1602, 1603, 2244, 2565, 2566, 2567, 2568, 2569, 5174)
(
    V_QUERY,
    V_REDUCE,
    V_RGAIN,
    V_RSHIFT,
    V_VALUE,
    V_OUTPUT,
    V_GAIN1,
    V_SHIFT1,
    V_GAIN2,
    V_SHIFT2,
    V_SHRINK,
) = range(11)
HIDDEN_ROWS = 11

ROOM = dict(
    unpack=30, front=14, attend=34, mix=30, attend_back=26, tail=16, pack=32,
    gather=8, scatter=18, share=3, halo=2, merge=8,
)


def params(name):
    return pltpu.CompilerParams(vmem_limit_bytes=ROOM[name] * 1024 * 1024)


ANY = pl.BlockSpec(memory_space=pl.ANY)
VM = pl.BlockSpec(memory_space=pltpu.VMEM)


def shape_of(dims, kind):
    return jax.ShapeDtypeStruct(dims, kind)


def mm(left, right):
    return jnp.dot(left, right, preferred_element_type=F32)


def mm_tn(left, right):
    return lax.dot_general(left, right, (((0,), (0,)), ((), ())), preferred_element_type=F32)


def mm_nt(left, right):
    return lax.dot_general(left, right, (((1,), (1,)), ((), ())), preferred_element_type=F32)


def mm_tt(left, right):
    return lax.dot_general(left, right, (((0,), (1,)), ((), ())), preferred_element_type=F32)


def norm_parts(values):
    center = values - jnp.mean(values, axis=-1, keepdims=True)
    rstd = lax.rsqrt(jnp.mean(center * center, axis=-1, keepdims=True) + EPSILON)
    return center * rstd, rstd


def norm_back(grad, unit, rstd, gain):
    scaled = grad * gain
    first = jnp.mean(scaled, axis=-1, keepdims=True)
    second = jnp.mean(scaled * unit, axis=-1, keepdims=True)
    return rstd * (scaled - first - unit * second)


def row_sum(values):
    return jnp.sum(values, axis=0, keepdims=True)


def full(dims):
    return pl.BlockSpec(dims, lambda *_: (0,) * len(dims))


def unpack_kernel(g_ref, wq, wr, wk, wv, wo, we, ws, vec, hid, rows, tiles):
    for i in range(BLOCKS):
        at = i * BLOCK_ROWS
        block = restore(g_ref[i].astype(F32).reshape(2 * PART, 128))
        rows[at : at + BLOCK_ROWS, :] = block
        tiles[0, at : at + BLOCK_ROWS, :] = block[:, 0:128]
        tiles[1, at : at + BLOCK_ROWS, :] = block[:, 128:256]
        tiles[2, at : at + BLOCK_ROWS, 0:64] = block[:, 256:320]

    def strided(start, count, step):
        parts = [tiles[t, pl.ds(start, count, stride=step), :] for t in range(3)]
        return jnp.concatenate([parts[0], parts[1], parts[2][:, 0:64]], axis=1)

    wq[...] = rows[R_QUERY : R_QUERY + C, :].astype(BF16)
    wr[...] = rows[R_REDUCE : R_REDUCE + 4 * C, :].astype(BF16)
    wk[...] = strided(R_KEYVAL, C, 2).astype(BF16)
    wv[...] = strided(R_KEYVAL + 1, C, 2).astype(BF16)
    wo[...] = rows[R_OUTPUT : R_OUTPUT + C, :].astype(BF16)
    ws[...] = rows[R_SHRINK : R_SHRINK + FF, :].astype(BF16)
    we[...] = jnp.concatenate([strided(R_EXPAND + j, C, 4) for j in range(4)], axis=1).astype(BF16)
    hid[0:HIDDEN_ROWS, :] = jnp.concatenate(
        [strided(R_HIDDEN + j, HIDDEN_ROWS, 4) for j in range(4)], axis=1
    )
    for i, row in enumerate(VECTOR_ROWS):
        vec[i : i + 1, :] = rows[row : row + 1, :]


def unpack(blocks):
    return pl.pallas_call(
        unpack_kernel,
        name="unpack",
        out_shape=(
            shape_of((C, C), BF16),
            shape_of((4 * C, C), BF16),
            shape_of((C, C), BF16),
            shape_of((C, C), BF16),
            shape_of((C, C), BF16),
            shape_of((C, FF), BF16),
            shape_of((FF, C), BF16),
            shape_of((16, C), F32),
            shape_of((16, FF), F32),
        ),
        scratch_shapes=[pltpu.VMEM((ROWS, C), F32), pltpu.VMEM((3, ROWS, 128), F32)],
        compiler_params=params("unpack"),
    )(blocks)


def pack_kernel(gwq, gwr, gwk, gwv, gwo, gwe, gws, gvec0, gvec1, gvec2, ghid, out, tiles):
    def put(start, value):
        count = value.shape[0]
        tiles[0, start : start + count, :] = value[:, 0:128]
        tiles[1, start : start + count, :] = value[:, 128:256]
        tiles[2, start : start + count, 0:64] = value[:, 256:320]

    def put_strided(start, step, value):
        count = value.shape[0]
        tiles[0, pl.ds(start, count, stride=step), :] = value[:, 0:128]
        tiles[1, pl.ds(start, count, stride=step), :] = value[:, 128:256]
        tail = jnp.concatenate([value[:, 256:320], jnp.zeros((count, 64), F32)], axis=1)
        tiles[2, pl.ds(start, count, stride=step), :] = tail

    put(R_QUERY, gwq[...])
    put(R_REDUCE, gwr[...])
    put_strided(R_KEYVAL, 2, gwk[...].T)
    put_strided(R_KEYVAL + 1, 2, gwv[...].T)
    put(R_OUTPUT, gwo[...])
    put(R_SHRINK, gws[...].T)
    for j in range(4):
        put_strided(R_EXPAND + j, 4, gwe[:, C * j : C * j + C])
        put_strided(R_HIDDEN + j, 4, ghid[0:HIDDEN_ROWS, C * j : C * j + C])
    for source, names in (
        (gvec0, (V_QUERY, V_REDUCE, V_RGAIN, V_RSHIFT, V_GAIN1, V_SHIFT1)),
        (gvec2, (V_GAIN2, V_SHIFT2, V_SHRINK)),
    ):
        for i, name in enumerate(names):
            put(VECTOR_ROWS[name], source[i : i + 1, :])
    put(VECTOR_ROWS[V_VALUE], gvec1[0:1, :])
    put(VECTOR_ROWS[V_OUTPUT], gvec1[8:9, :])
    put(USED_ROWS, jnp.zeros((ROWS - USED_ROWS, C), F32))
    half = BLOCK_ROWS // 2
    spare = jnp.zeros((2 * PART - 2 * BLOCK_ROWS - half, 128), F32)
    for i in range(BLOCKS):
        at = i * BLOCK_ROWS
        tail = jnp.concatenate(
            [
                tiles[2, at : at + half, 0:64],
                tiles[2, at + half : at + BLOCK_ROWS, 0:64],
            ],
            axis=1,
        )
        rows = [tiles[0, at : at + BLOCK_ROWS, :], tiles[1, at : at + BLOCK_ROWS, :], tail, spare]
        out[i] = jnp.concatenate(rows, axis=0).reshape(2, PART, 128).astype(BF16)


def pack(*pieces):
    return pl.pallas_call(
        pack_kernel,
        name="pack",
        out_shape=shape_of((BLOCKS, 2, PART, 128), BF16),
        scratch_shapes=[pltpu.VMEM((3, ROWS, 128), F32)],
        compiler_params=params("pack"),
    )(*pieces)


TILE = 8 * W
RTILE = TILE // 4


def split_tiles(scr, value):
    scr[0, :, :] = value[:, 0:128]
    scr[1, :, :] = value[:, 128:256]
    scr[2, :, 0:64] = value[:, 256:320]


def patch_pieces(scr):
    pieces = {}
    for b in range(2):
        parts = [scr[t, pl.ds(b, TILE // 2, stride=2), :] for t in range(3)]
        cols = jnp.concatenate([parts[0], parts[1], parts[2][:, 0:64]], axis=1)
        cols = cols.reshape(TILE // (2 * W), 2, W // 2, C)
        for a in range(2):
            pieces[2 * a + b] = cols[:, a].reshape(RTILE, C)
    return pieces


def front_kernel(x_ref, vec, wq, wr, q_out, red_out, rn_out, scr):
    unit, _ = norm_parts(x_ref[...].astype(F32))
    normed = (unit * vec[V_GAIN1 : V_GAIN1 + 1, :] + vec[V_SHIFT1 : V_SHIFT1 + 1, :]).astype(BF16)
    queries = (mm(normed, wq[...]) + vec[V_QUERY : V_QUERY + 1, :]).astype(BF16)
    q_out[...] = queries * jnp.asarray(1.0 / math.sqrt(HD), BF16)
    split_tiles(scr, normed.astype(F32))
    pieces = patch_pieces(scr)
    reduced = vec[V_REDUCE : V_REDUCE + 1, :]
    for k in range(4):
        reduced = reduced + mm(pieces[k].astype(BF16), wr[k * C : (k + 1) * C, :])
    red_out[...] = reduced
    unit, _ = norm_parts(reduced)
    rn_out[...] = (unit * vec[V_RGAIN : V_RGAIN + 1, :] + vec[V_RSHIFT : V_RSHIFT + 1, :]).astype(
        BF16
    )


def front(x, vec, wq, wr):
    tokens = x.shape[0]
    return pl.pallas_call(
        front_kernel,
        name="front",
        grid=(tokens // TILE,),
        in_specs=[
            pl.BlockSpec((TILE, C), lambda i: (i, 0)),
            full((16, C)),
            full((C, C)),
            full((4 * C, C)),
        ],
        out_specs=[
            pl.BlockSpec((TILE, C), lambda i: (i, 0)),
            pl.BlockSpec((RTILE, C), lambda i: (i, 0)),
            pl.BlockSpec((RTILE, C), lambda i: (i, 0)),
        ],
        out_shape=(
            shape_of((tokens, C), BF16),
            shape_of((tokens // 4, C), F32),
            shape_of((tokens // 4, C), BF16),
        ),
        scratch_shapes=[pltpu.VMEM((3, TILE, 128), F32)],
        compiler_params=params("front"),
    )(x, vec, wq, wr)


QT = 512


def attend_kernel(
    x_ref, q_ref, rn_ref, vec, wk, wv, wo,
    mixed_out, inv_out, mid_out, n2_out, p_out, key_out, vt_out, kt, vones,
):
    keys = rn_ref.shape[0] * rn_ref.shape[2]

    @pl.when(pl.program_id(1) == 0)
    def _():
        rn = rn_ref[:, 0].reshape(keys, C)
        key = mm(rn, wk[...]).astype(BF16)
        value = (mm(rn, wv[...]) + vec[V_VALUE : V_VALUE + 1, :]).astype(BF16)
        key_out[0] = key
        vt_out[0] = value.T
        kt[...] = key.T
        for h in range(HEADS):
            vones[h, :, 0:HD] = value[:, h * HD : (h + 1) * HD]
            vones[h, :, HD:] = jnp.ones((keys, HD), BF16)

    lane = lax.broadcasted_iota(jnp.int32, (QT, 128), 1)
    invs = jnp.zeros((QT, 128), F32)
    outs = []
    for h in range(HEADS):
        scores = mm(q_ref[:, h * HD : (h + 1) * HD], kt[h * HD : (h + 1) * HD, :])
        top = jnp.max(scores, axis=-1, keepdims=True)
        probs = jnp.exp(scores - top).astype(BF16)
        p_out[0, h] = probs
        both = mm(probs, vones[h])
        inv = 1.0 / both[:, HD:]
        outs.append(both[:, 0:HD] * inv)
        invs = jnp.where(lane == h, inv[:, 0:1], invs)
    inv_out[...] = invs
    mixed = jnp.concatenate(outs, axis=1).astype(BF16)
    mixed_out[...] = mixed
    middle = x_ref[...].astype(F32) + mm(mixed, wo[...]) + vec[V_OUTPUT : V_OUTPUT + 1, :]
    mid_out[...] = middle
    unit, _ = norm_parts(middle)
    n2_out[...] = (unit * vec[V_GAIN2 : V_GAIN2 + 1, :] + vec[V_SHIFT2 : V_SHIFT2 + 1, :]).astype(
        BF16
    )


def attend(x, q, rn_all, vec, wk, wv, wo):
    tokens = x.shape[0]
    bands, scenes, per_band, _ = rn_all.shape
    keys = bands * per_band
    per_scene = tokens // scenes
    steps = per_scene // QT
    tile = pl.BlockSpec((QT, C), lambda s, i: (s * steps + i, 0))
    return pl.pallas_call(
        attend_kernel,
        name="attend",
        grid=(scenes, steps),
        in_specs=[
            tile,
            tile,
            pl.BlockSpec((bands, 1, per_band, C), lambda s, i: (0, s, 0, 0)),
            full((16, C)),
            full((C, C)),
            full((C, C)),
            full((C, C)),
        ],
        out_specs=[
            tile,
            pl.BlockSpec((QT, 128), lambda s, i: (s * steps + i, 0)),
            tile,
            tile,
            pl.BlockSpec((1, HEADS, QT, keys), lambda s, i: (s, 0, i, 0)),
            pl.BlockSpec((1, keys, C), lambda s, i: (s, 0, 0)),
            pl.BlockSpec((1, C, keys), lambda s, i: (s, 0, 0)),
        ],
        out_shape=(
            shape_of((tokens, C), BF16),
            shape_of((tokens, 128), F32),
            shape_of((tokens, C), F32),
            shape_of((tokens, C), BF16),
            shape_of((scenes, HEADS, per_scene, keys), BF16),
            shape_of((scenes, keys, C), BF16),
            shape_of((scenes, C, keys), BF16),
        ),
        scratch_shapes=[pltpu.VMEM((C, keys), BF16), pltpu.VMEM((HEADS, keys, 2 * HD), BF16)],
        compiler_params=params("attend"),
    )(x, q, rn_all, vec, wk, wv, wo)


CH = 256


SHRINK_IN = math.sqrt(0.5 * math.log2(math.e))
SLOPE = 1.0 / (math.sqrt(2.0 * math.pi) * SHRINK_IN)
ACT_SCALE = SLOPE / SHRINK_IN
ERF_RATE = 0.3275911 * math.sqrt(0.5) / SHRINK_IN
ERF_TERMS = [
    0.5 * k / SLOPE
    for k in (0.254829592, -0.284496736, 1.421413741, -1.453152027, 1.061405429)
]


def gelu_parts(u):
    size = jnp.abs(u)
    t = 1.0 / (1.0 + ERF_RATE * size)
    poly = ERF_TERMS[4]
    for term in ERF_TERMS[3::-1]:
        poly = term + t * poly
    bell = jnp.exp2(-(u * u))
    tail = (t * poly) * bell
    return jnp.where(u >= 0, 1.0 / SLOPE - tail, tail), bell


def mix_kernel(
    n2, n2_top, n2_low, cot, cot_top, cot_low, mid, edge, vec, hid, we, ws,
    y_out, gmid_out, gwe_out, gws_out, ghid_out, gvec_out,
    nx, cx, nt, ct, e_scr, e_low, ga_scr, gc_scr, act_scr, ge_scr, branch, gn2,
):
    scenes, rows = n2.shape[0], n2.shape[1]
    ext = (rows + 4) * W
    gext = (rows + 2) * W
    own = rows * W
    top, low = edge[0], edge[1]

    def inside(value, there):
        return jnp.where(there > 0, value.astype(F32), 0.0).astype(BF16)

    for s in range(scenes):
        mine = n2[s].reshape(own, C)
        nx[s * ext : s * ext + 2 * W, :] = n2_top[s].reshape(2 * W, C)
        nx[s * ext + 2 * W : s * ext + 2 * W + own, :] = mine
        nx[s * ext + 2 * W + own : (s + 1) * ext, :] = n2_low[s].reshape(2 * W, C)
        nt[0:C, s * own : (s + 1) * own] = mine.T
        mine = cot[s].reshape(own, C)
        cx[s * gext : s * gext + W, :] = inside(cot_top[s].reshape(W, C), top)
        cx[s * gext + W : s * gext + W + own, :] = mine
        cx[s * gext + W + own : (s + 1) * gext, :] = inside(cot_low[s].reshape(W, C), low)
        ct[:, s * own : (s + 1) * own] = mine.T
    nt[C:, :] = jnp.ones((16, scenes * own), BF16)
    branch[...] = jnp.zeros_like(branch)
    gn2[...] = jnp.zeros_like(gn2)

    def chunk(step, carry):
        cols = pl.ds(pl.multiple_of(step * CH, CH), CH)
        wcol = we[:, cols]
        wrow = ws[cols, :]
        body = (mm(nx[...], wcol) + hid[0:1, cols]).astype(BF16)
        e_low[...] = body
        e_scr[...] = body.astype(F32)
        ga_scr[...] = mm_nt(cx[...], wrow)
        for there, start in ((top, 0), (low, 2 * W + own)):

            @pl.when(there == 0)
            def _():
                for s in range(scenes):
                    e_scr[s * ext + start : s * ext + start + 2 * W, :] = jnp.zeros((2 * W, CH), F32)

        col = lax.broadcasted_iota(jnp.int32, (8, CH), 0)
        first, last = col == 0, col == 7

        def right(value):
            moved = pltpu.roll(value, 1, axis=0)
            return jnp.concatenate([jnp.where(first, 0.0, moved[0:8]), moved[8:]], axis=0)

        def left(value):
            moved = pltpu.roll(value, W - 1, axis=0)
            return jnp.concatenate([moved[: W - 8], jnp.where(last, 0.0, moved[W - 8 :])], axis=0)

        def fold(value):
            value = value[0:32] + value[32:64]
            value = value[0:16] + value[16:32]
            return (value[0:8] + value[8:16]).astype(F32)

        taps = [hid[1 + k : 2 + k, cols] * SHRINK_IN for k in range(9)]
        low_taps = [hid[1 + k : 2 + k, cols].astype(BF16) for k in range(9)]
        conv_bias = hid[10:11, cols] * SHRINK_IN

        for s in range(scenes):

            def forward(r, carry):
                at = pl.multiple_of(s * ext + r * W, W)
                lines = [e_scr[pl.ds(at + a * W, W), :] for a in range(3)]
                sums = [
                    lines[0] * taps[b] + lines[1] * taps[3 + b] + lines[2] * taps[6 + b]
                    for b in range(3)
                ]
                u = conv_bias + right(sums[0]) + sums[1] + left(sums[2])
                cdf, bell = gelu_parts(u)
                gat = pl.multiple_of(s * gext + r * W, W)
                gc = ga_scr[pl.ds(gat, W), :] * (cdf + u * bell)
                act_scr[pl.ds(gat, W), :] = (u * cdf).astype(BF16)
                gc_scr[0, pl.ds(gat, W), :] = left(gc).astype(BF16)
                gc_scr[1, pl.ds(gat, W), :] = gc.astype(BF16)
                gc_scr[2, pl.ds(gat, W), :] = right(gc).astype(BF16)
                return carry

            lax.fori_loop(0, rows + 2, forward, 0)

        def backward(s, r, carry):
            line = e_low[pl.ds(pl.multiple_of(s * ext + (r + 2) * W, W), W), :]
            grads = list(carry)
            total = None
            for a in range(3):
                gat = pl.multiple_of(s * gext + (r + 2 - a) * W, W)
                for b in range(3):
                    g = gc_scr[b, pl.ds(gat, W), :]
                    term = g * low_taps[3 * a + b]
                    total = term if total is None else total + term
                    grads[3 * a + b] = grads[3 * a + b] + fold(g * line)
                    if a == 1 and b == 1:
                        grads[9] = grads[9] + fold(g)
            ge_scr[pl.ds(pl.multiple_of(s * own + r * W, W), W), :] = total
            return tuple(grads)

        sums = tuple(jnp.zeros((8, CH), F32) for _ in range(10))
        for s in range(scenes):
            sums = lax.fori_loop(0, rows, functools.partial(backward, s), sums)
        for k in range(10):
            ghid_out[1 + k : 2 + k, cols] = row_sum(sums[k]) * SLOPE

        ge = ge_scr[...]
        grads = mm(nt[...], ge)
        gwe_out[:, cols] = grads[0:C, :] * SLOPE
        ghid_out[0:1, cols] = grads[C : C + 1, :] * SLOPE
        gn2[...] += mm_nt(ge, wcol)
        gws = None
        for s in range(scenes):
            at = slice(s * own, (s + 1) * own)
            act = act_scr[s * gext + W : s * gext + W + own, :]
            branch[at, :] += mm(act, wrow)
            term = mm(ct[:, at], act)
            gws = term if gws is None else gws + term
        gws_out[:, cols] = gws * ACT_SCALE
        return carry

    lax.fori_loop(0, FF // CH, chunk, 0)

    size = 4 * W
    per = own // size
    gain = vec[V_GAIN2 : V_GAIN2 + 1, :]

    def finish(i, carry):
        at = pl.multiple_of(i * size, size)
        s = i // per
        line = (i % per) * 4
        middle = mid[pl.ds(at, size), :]
        y_out[pl.ds(at, size), :] = (
            middle + branch[pl.ds(at, size), :] * ACT_SCALE + vec[V_SHRINK : V_SHRINK + 1, :]
        ).astype(BF16)
        grad = gn2[pl.ds(at, size), :] * SLOPE
        unit, rstd = norm_parts(middle)
        direct = cot[s, pl.ds(line, 4)].reshape(size, C).astype(F32)
        gmid_out[pl.ds(at, size), :] = direct + norm_back(grad, unit, rstd, gain)
        return (
            carry[0] + row_sum(grad * unit),
            carry[1] + row_sum(grad),
            carry[2] + row_sum(direct),
        )

    zero = jnp.zeros((1, C), F32)
    sums = lax.fori_loop(0, scenes * per, finish, (zero, zero, zero))
    for i in range(3):
        gvec_out[i : i + 1, :] = sums[i]


def mix(n2, n2_top, n2_low, cot, cot_top, cot_low, mid, edge, vec, hid, we, ws):
    scenes, rows = n2.shape[0], n2.shape[1]
    tokens = scenes * rows * W
    ext = scenes * (rows + 4) * W
    gext = scenes * (rows + 2) * W
    return pl.pallas_call(
        mix_kernel,
        name="mix",
        in_specs=[VM] * 7 + [pl.BlockSpec(memory_space=pltpu.SMEM)] + [VM] * 4,
        out_specs=[VM] * 6,
        out_shape=(
            shape_of((tokens, C), BF16),
            shape_of((tokens, C), F32),
            shape_of((C, FF), F32),
            shape_of((C, FF), F32),
            shape_of((16, FF), F32),
            shape_of((8, C), F32),
        ),
        scratch_shapes=[
            pltpu.VMEM((ext, C), BF16),
            pltpu.VMEM((gext, C), BF16),
            pltpu.VMEM((C + 16, tokens), BF16),
            pltpu.VMEM((C, tokens), BF16),
            pltpu.VMEM((ext, CH), F32),
            pltpu.VMEM((ext, CH), BF16),
            pltpu.VMEM((gext, CH), F32),
            pltpu.VMEM((3, gext, CH), BF16),
            pltpu.VMEM((gext, CH), BF16),
            pltpu.VMEM((tokens, CH), BF16),
            pltpu.VMEM((tokens, C), F32),
            pltpu.VMEM((tokens, C), F32),
        ],
        compiler_params=params("mix"),
    )(n2, n2_top, n2_low, cot, cot_top, cot_low, mid, edge, vec, hid, we, ws)


QTB = 256


def attend_back_kernel(
    q_ref, inv_ref, mixed_ref, gmid_ref, p_ref, key_ref, vt_ref, rn_ref, wk, wv, wo,
    dq_out, grn_out, gwk_out, gwv_out, gwo_out, gvec_out, kh, dkt, dvt,
):
    scene, step = pl.program_id(0), pl.program_id(1)
    keys = rn_ref.shape[0] * rn_ref.shape[2]

    @pl.when(jnp.logical_and(scene == 0, step == 0))
    def _():
        for ref in (gwk_out, gwv_out, gwo_out, gvec_out):
            ref[...] = jnp.zeros_like(ref)

    @pl.when(step == 0)
    def _():
        for h in range(HEADS):
            kh[h] = key_ref[0, :, h * HD : (h + 1) * HD]
        dkt[...] = jnp.zeros_like(dkt)
        dvt[...] = jnp.zeros_like(dvt)

    gatt = gmid_ref[...].astype(BF16)
    gvec_out[8:9, :] += row_sum(gatt.astype(F32))
    mixed = mixed_ref[...]
    gwo_out[...] += mm_tn(mixed, gatt)
    inv = jnp.concatenate(
        [jnp.broadcast_to(inv_ref[:, h : h + 1], (QTB, HD)) for h in range(HEADS)], axis=1
    )
    scaled = (mm_nt(gatt, wo[...]) * inv).astype(BF16)
    prod = scaled.astype(F32) * mixed.astype(F32)
    q_t = q_ref[...].T
    g_t = scaled.T
    dqs = []
    for h in range(HEADS):
        cols = slice(h * HD, (h + 1) * HD)
        inner = jnp.sum(prod[:, cols], axis=-1, keepdims=True)
        probs = p_ref[0, h]
        gprobs = mm(scaled[:, cols], vt_ref[0, cols, :])
        gscores = (probs.astype(F32) * (gprobs - inner)).astype(BF16)
        dqs.append(mm(gscores, kh[h]))
        dkt[cols, :] += mm(q_t[cols, :], gscores)
        dvt[cols, :] += mm(g_t[cols, :], probs)
    dq_out[...] = (jnp.concatenate(dqs, axis=1) * (1.0 / math.sqrt(HD))).astype(BF16)

    @pl.when(step == pl.num_programs(1) - 1)
    def _():
        rn = rn_ref[:, 0].reshape(keys, C)
        dk = dkt[...].astype(BF16)
        dv = dvt[...].astype(BF16)
        gvec_out[0:8, :] += mm_nt(jnp.ones((8, keys), BF16), dv)
        gwk_out[...] += mm(dk, rn)
        gwv_out[...] += mm(dv, rn)
        grn = (mm(wk[...], dk) + mm(wv[...], dv)).astype(BF16)
        grn_out[...] = grn.T.reshape(grn_out.shape)


def attend_back(q, inv, mixed, gmid, p, key, vt, rn_all, wk, wv, wo):
    tokens = q.shape[0]
    bands, scenes, per_band, _ = rn_all.shape
    keys = bands * per_band
    steps = tokens // scenes // QTB
    tile = pl.BlockSpec((QTB, C), lambda s, i: (s * steps + i, 0))
    return pl.pallas_call(
        attend_back_kernel,
        name="attend_back",
        grid=(scenes, steps),
        in_specs=[
            tile,
            pl.BlockSpec((QTB, 128), lambda s, i: (s * steps + i, 0)),
            tile,
            tile,
            pl.BlockSpec((1, HEADS, QTB, keys), lambda s, i: (s, 0, i, 0)),
            pl.BlockSpec((1, keys, C), lambda s, i: (s, 0, 0)),
            pl.BlockSpec((1, C, keys), lambda s, i: (s, 0, 0)),
            pl.BlockSpec((bands, 1, per_band, C), lambda s, i: (0, s, 0, 0)),
            full((C, C)),
            full((C, C)),
            full((C, C)),
        ],
        out_specs=[
            tile,
            pl.BlockSpec((bands, 1, per_band, C), lambda s, i: (0, s, 0, 0)),
            full((C, C)),
            full((C, C)),
            full((C, C)),
            full((16, C)),
        ],
        out_shape=(
            shape_of((tokens, C), BF16),
            shape_of(rn_all.shape, BF16),
            shape_of((C, C), F32),
            shape_of((C, C), F32),
            shape_of((C, C), F32),
            shape_of((16, C), F32),
        ),
        scratch_shapes=[
            pltpu.VMEM((HEADS, keys, HD), BF16),
            pltpu.VMEM((C, keys), F32),
            pltpu.VMEM((C, keys), F32),
        ],
        compiler_params=params("attend_back"),
    )(q, inv, mixed, gmid, p, key, vt, rn_all, wk, wv, wo)


def tail_kernel(
    x_ref, gmid_ref, dq_ref, grn_ref, red_ref, vec, wq, wr,
    gx_out, gwq_out, gwr_out, gvec_out, scr, gscr,
):
    @pl.when(pl.program_id(0) == 0)
    def _():
        for ref in (gwq_out, gwr_out, gvec_out):
            ref[...] = jnp.zeros_like(ref)

    runit, rrstd = norm_parts(red_ref[...])
    grn = grn_ref[...].astype(F32)
    gred = norm_back(grn, runit, rrstd, vec[V_RGAIN : V_RGAIN + 1, :]).astype(BF16)
    unit, rstd = norm_parts(x_ref[...].astype(F32))
    gain = vec[V_GAIN1 : V_GAIN1 + 1, :]
    normed = (unit * gain + vec[V_SHIFT1 : V_SHIFT1 + 1, :]).astype(BF16)
    split_tiles(scr, normed.astype(F32))
    pieces = patch_pieces(scr)
    back = {}
    for k in range(4):
        at = slice(k * C, (k + 1) * C)
        gwr_out[at, :] += mm_tn(pieces[k].astype(BF16), gred)
        back[k] = mm_nt(gred, wr[at, :]).reshape(TILE // (2 * W), 1, W // 2, C)
    for b in range(2):
        cols = jnp.concatenate([back[b], back[2 + b]], axis=1).reshape(TILE // 2, C)
        spot = pl.ds(b, TILE // 2, stride=2)
        gscr[0, spot, :] = cols[:, 0:128]
        gscr[1, spot, :] = cols[:, 128:256]
        gscr[2, spot, :] = jnp.concatenate(
            [cols[:, 256:320], jnp.zeros((TILE // 2, 64), F32)], axis=1
        )
    dq = dq_ref[...]
    gwq_out[...] += mm_tn(normed, dq)
    placed = jnp.concatenate([gscr[0], gscr[1], gscr[2][:, 0:64]], axis=1)
    gnormed = mm_nt(dq, wq[...]) + placed
    gx_out[...] = gmid_ref[...] + norm_back(gnormed, unit, rstd, gain)
    gvec_out[0:1, :] += row_sum(dq.astype(F32))
    gvec_out[1:2, :] += row_sum(gred.astype(F32))
    gvec_out[2:3, :] += row_sum(grn * runit)
    gvec_out[3:4, :] += row_sum(grn)
    gvec_out[4:5, :] += row_sum(gnormed * unit)
    gvec_out[5:6, :] += row_sum(gnormed)


def tail(x, gmid, dq, grn, red, vec, wq, wr):
    tokens = x.shape[0]
    tile = pl.BlockSpec((TILE, C), lambda i: (i, 0))
    rtile = pl.BlockSpec((RTILE, C), lambda i: (i, 0))
    return pl.pallas_call(
        tail_kernel,
        name="tail",
        grid=(tokens // TILE,),
        in_specs=[
            tile, tile, tile, rtile, rtile, full((16, C)), full((C, C)), full((4 * C, C))
        ],
        out_specs=[tile, full((C, C)), full((4 * C, C)), full((8, C))],
        out_shape=(
            shape_of((tokens, C), F32),
            shape_of((C, C), F32),
            shape_of((4 * C, C), F32),
            shape_of((8, C), F32),
        ),
        scratch_shapes=[pltpu.VMEM((3, TILE, 128), F32), pltpu.VMEM((3, TILE, 128), F32)],
        compiler_params=params("tail"),
    )(x, gmid, dq, grn, red, vec, wq, wr)


def flip(value, by):
    return value + by * (1 - 2 * value)


def remote(src, dst, send, recv, where):
    return pltpu.make_async_remote_copy(
        src_ref=src,
        dst_ref=dst,
        send_sem=send,
        recv_sem=recv,
        device_id=where,
        device_id_type=pl.DeviceIdType.MESH,
    )


def greet(places):
    barrier = pltpu.get_barrier_semaphore()
    count = 0
    for place, there in places:
        if there is None:
            pl.semaphore_signal(
                barrier, inc=1, device_id=place, device_id_type=pl.DeviceIdType.MESH
            )
            count = count + 1
        else:

            @pl.when(there)
            def _():
                pl.semaphore_signal(
                    barrier, inc=1, device_id=place, device_id_type=pl.DeviceIdType.MESH
                )

            count = count + there.astype(jnp.int32)
    pl.semaphore_wait(barrier, count)


def comm_params(name, number):
    return pltpu.CompilerParams(
        collective_id=number, has_side_effects=True, vmem_limit_bytes=ROOM[name] * 1024 * 1024
    )


class Place:
    def __init__(self):
        dp, space = lax.axis_index("dp"), lax.axis_index("space")
        self.z, self.x = dp // 2, dp % 2
        self.y, self.c = space // 2, space % 2
        self.line = lax.axis_size("dp") // 2

    def block(self, z, x, y, c):
        return ((z * 2 + x) * 2 + y) * 2 + c

    def device(self, z, x, y, c):
        return {"dp": z * 2 + x, "space": y * 2 + c}

    def spot(self, da, db, c):
        return (
            flip(self.x, da * (1 - c) + db * c),
            flip(self.y, db * (1 - c) + da * c),
        )

    def partners(self):
        ax, ay = self.spot(1, 0, self.c)
        bx, by = self.spot(0, 1, self.c)
        return (
            self.device(self.z, ax, ay, self.c),
            self.device(self.z, bx, by, self.c),
            self.device(self.z, self.x, self.y, 1 - self.c),
            self.device(self.z + 1, self.x, self.y, self.c),
            self.device(self.z - 1, self.x, self.y, self.c),
        )

    def meet(self):
        first, second, sibling, up, down = self.partners()
        greet(
            [
                (first, None),
                (second, None),
                (sibling, None),
                (up, self.z < self.line - 1),
                (down, self.z > 0),
            ]
        )


DMA = pltpu.SemaphoreType.DMA
PART = 208


def compact(block):
    half = BLOCK_ROWS // 2
    tail = jnp.concatenate([block[:half, 256:], block[half:, 256:]], axis=1)
    spare = jnp.zeros((2 * PART - 2 * BLOCK_ROWS - half, 128), block.dtype)
    return jnp.concatenate([block[:, 0:128], block[:, 128:256], tail, spare], axis=0)


def restore(rows):
    half = BLOCK_ROWS // 2
    tail = rows[2 * BLOCK_ROWS : 2 * BLOCK_ROWS + half]
    return jnp.concatenate(
        [
            rows[:BLOCK_ROWS],
            rows[BLOCK_ROWS : 2 * BLOCK_ROWS],
            jnp.concatenate([tail[:, 0:64], tail[:, 64:128]], axis=0),
        ],
        axis=1,
    )


PLANE = [(da, db) for da in range(2) for db in range(2)]


def gather_kernel(own_ref, out, own, p_z, p_a, p_b, p_c, q_z, q_a, q_b, q_c, recv):
    at = Place()
    line = at.line
    first, second, sibling, up, down = at.partners()
    own[...] = compact(own_ref[...].astype(F32)).reshape(2, PART, 128).astype(BF16)
    at.meet()
    can_up, can_down = at.z < line - 1, at.z > 0

    def index_of(z, da, db, c):
        x, y = at.spot(da, db, at.c)
        return at.block(z, x, y, c)

    def push(part, index, src, sem, where):
        remote(src, out.at[index, part], sem, recv.at[index, part], where).start()

    def landed(part, index):
        remote(
            out.at[index, part], out.at[index, part], p_a.at[0], recv.at[index, part], sibling
        ).wait_recv()

    def here(part, index, is_own):
        return own.at[part] if is_own else out.at[index, part]

    def along_z(part, z, k, index, src, way, sems):
        if way >= 0:

            @pl.when(can_up)
            def _():
                push(part, index, src, sems.at[0, k, z], up)

        if way <= 0:

            @pl.when(can_down)
            def _():
                push(part, index, src, sems.at[1, k, z], down)

    def first_order(z, da, db, way, is_own=False):
        index = index_of(z, da, db, at.c)
        if not is_own:
            landed(0, index)
        src = here(0, index, is_own)
        if da == 0 and db == 0:
            along_z(0, z, 0, index, src, way, p_z)
            push(0, index, src, p_a.at[z], first)
        if db == 0:
            push(0, index, src, p_b.at[da, z], second)
        push(0, index, src, p_c.at[2 * da + db, z], sibling)

    def second_order(z, da, db, way, is_own=False):
        index = index_of(z, da, db, at.c)
        if not is_own:
            landed(1, index)
        src = here(1, index, is_own)
        if way == 0:
            if da == 0 and db == 0:
                push(1, index, src, q_a, first)
            if db == 0:
                push(1, index, src, q_b.at[da], second)
        along_z(1, z, 2 * da + db, index, src, way, q_z)
        push(1, index, src, q_c.at[2 * da + db, z], sibling)

    def hop(d, order, places):
        for z in range(line):
            if z >= d:

                @pl.when(at.z == z)
                def _():
                    for da, db in places:
                        order(z - d, da, db, 1)

            if z + d < line:

                @pl.when(at.z == z)
                def _():
                    for da, db in places:
                        order(z + d, da, db, -1)

    def flat_hops(da, db):
        first_order(at.z, da, db, 0)
        for d in range(1, line):
            hop(d, lambda z, da, db, way: first_order(z, da, db, way), [(da, db)])

    second_order(at.z, 0, 0, 0, True)
    first_order(at.z, 0, 0, 0, True)
    mine = index_of(at.z, 0, 0, at.c)
    out[mine] = own[...]
    second_order(at.z, 1, 0, 0)
    hop(1, first_order, [(0, 0)])
    second_order(at.z, 0, 1, 0)
    second_order(at.z, 1, 1, 0)
    hop(2, first_order, [(0, 0)])
    hop(1, second_order, PLANE)
    hop(3, first_order, [(0, 0)])
    flat_hops(1, 0)
    hop(2, second_order, PLANE)
    flat_hops(0, 1)
    flat_hops(1, 1)
    hop(3, second_order, PLANE)
    for z in range(line):
        for da, db in PLANE:
            for part in range(2):
                landed(part, index_of(z, da, db, 1 - at.c))

    def sent(part, sem, where):
        remote(own.at[part], out.at[mine, part], sem, recv.at[mine, part], where).wait_send()

    sent(1, q_a, first)
    for z in range(line):
        for k in range(4):
            sent(0, p_c.at[k, z], sibling)
            sent(1, q_c.at[k, z], sibling)
        sent(0, p_a.at[z], first)
        for da in range(2):
            sent(0, p_b.at[da, z], second)

        @pl.when(jnp.logical_and(can_up, z <= at.z))
        def _():
            sent(0, p_z.at[0, 0, z], up)
            for k in range(4):
                sent(1, q_z.at[0, k, z], up)

        @pl.when(jnp.logical_and(can_down, z >= at.z))
        def _():
            sent(0, p_z.at[1, 0, z], down)
            for k in range(4):
                sent(1, q_z.at[1, k, z], down)

    for da in range(2):
        sent(1, q_b.at[da], second)


def gather_blocks(own):
    return pl.pallas_call(
        gather_kernel,
        name="gather",
        out_shape=shape_of((BLOCKS, 2, PART, 128), BF16),
        in_specs=[VM],
        out_specs=VM,
        scratch_shapes=[
            pltpu.VMEM((2, PART, 128), BF16),
            DMA((2, 1, 4)), DMA((4,)), DMA((2, 4)), DMA((4, 4)),
            DMA((2, 4, 4)), DMA, DMA((2,)), DMA((4, 4)),
            DMA((BLOCKS, 2)),
        ],
        compiler_params=comm_params("gather", 1),
    )(own)


def scatter_kernel(
    parts, out,
    rc, acc, ra, acc2, rb, acc3, rz, sz,
    qc, qacc, qrz, qsz, qplane, qra, qacc2, qrb,
    c_out, a_out, b_out, z_out, qc_out, qz_out, qa_out, qb_out,
    c_in, a_in, b_in, z_in, qc_in, qz_in, qa_in, qb_in,
):
    at = Place()
    line = at.line
    first, second, sibling, up, down = at.partners()
    at.meet()
    slots = [(da, db, z) for da in (1, 0) for db in (1, 0) for z in range(line)]

    def add(*terms):
        total = terms[0].astype(F32)
        for term in terms[1:]:
            total = total + term.astype(F32)
        return total.astype(BF16)

    def source(k, c):
        da, db, z = slots[k]
        x, y = at.spot(da, db, c)
        return at.block(z, x, y, c)

    def c_copy(k):
        src = parts.at[source(k, 1 - at.c), 0]
        return remote(src, rc.at[k], c_out.at[k], c_in.at[k], sibling)

    def qc_copy(k):
        src = parts.at[source(k, 1 - at.c), 1]
        return remote(src, qc.at[k], qc_out.at[k], qc_in.at[k], sibling)

    def a_copy(j):
        return remote(acc.at[j], ra.at[j], a_out.at[j], a_in.at[j], first)

    def b_copy(j):
        return remote(acc2.at[j], rb.at[j], b_out.at[j], b_in.at[j], second)

    def z_copy(way, z):
        return remote(
            sz.at[way, z], rz.at[way, z], z_out.at[way, z], z_in.at[way, z], (up, down)[way]
        )

    def qz_copy(way, k, src=None):
        src = qsz.at[way, k] if src is None else src
        return remote(src, qrz.at[way, k], qz_out.at[way, k], qz_in.at[way, k], (up, down)[way])

    def qa_copy(j):
        return remote(qplane.at[j], qra.at[j], qa_out.at[j], qa_in.at[j], first)

    def qb_copy():
        return remote(qacc2.at[0], qrb, qb_out, qb_in, second)

    count = 4 * line
    for k in range(count):
        qc_copy(k).start()
        c_copy(k).start()
    for k in range(count):
        da, db, z = slots[k]
        qc_copy(k).wait_recv()
        mine = source(k, at.c)
        qacc[k] = add(parts[mine, 1], qc[k])
        if z > 0:

            @pl.when(at.z == 0)
            def _():
                qz_copy(0, k, qacc.at[k]).start()

        if z < line - 1:

            @pl.when(at.z == line - 1)
            def _():
                qz_copy(1, k, qacc.at[k]).start()

        c_copy(k).wait_recv()
        acc[k] = add(parts[mine, 0], rc[k])
        if da:
            a_copy(k).start()

    def q_hop(d):
        for k in range(count):
            z = slots[k][2]
            if z >= d:

                @pl.when(at.z == d)
                def _():
                    qz_copy(0, k).wait_recv()
                    if z > d:
                        qsz[0, k] = add(qacc[k], qrz[0, k])
                        qz_copy(0, k).start()

            if z <= line - 1 - d:

                @pl.when(at.z == line - 1 - d)
                def _():
                    qz_copy(1, k).wait_recv()
                    if z < line - 1 - d:
                        qsz[1, k] = add(qacc[k], qrz[1, k])
                        qz_copy(1, k).start()

    def p_hop(d):
        for z in reversed(range(d, line)):

            @pl.when(at.z == d)
            def _():
                if d > 0:
                    z_copy(0, z).wait_recv()
                if z > d:
                    sz[0, z] = add(acc3[z], rz[0, z]) if d > 0 else acc3[z]
                    z_copy(0, z).start()

        for z in range(line - d):

            @pl.when(at.z == line - 1 - d)
            def _():
                if d > 0:
                    z_copy(1, z).wait_recv()
                if z < line - 1 - d:
                    sz[1, z] = add(acc3[z], rz[1, z]) if d > 0 else acc3[z]
                    z_copy(1, z).start()

    def inflows(z):
        return [way for way, there in ((0, z > 0), (1, z < line - 1)) if there]

    for j in range(line):
        a_copy(j).wait_recv()
        acc2[j] = add(acc[2 * line + j], ra[j])
        b_copy(j).start()
    q_hop(1)
    for j in range(line, 2 * line):
        a_copy(j).wait_recv()
        acc2[j] = add(acc[2 * line + j], ra[j])
    q_hop(2)
    for z in range(line):
        b_copy(z).wait_recv()
        acc3[z] = add(acc2[line + z], rb[z])
    p_hop(0)
    q_hop(3)
    for z in range(line):

        @pl.when(at.z == z)
        def _():
            for j in range(4):
                k = j * line + z
                qplane[j] = add(qacc[k], *[qrz[way, k] for way in inflows(z)])

    qa_copy(0).start()
    qa_copy(1).start()
    p_hop(1)
    for j in range(2):
        qa_copy(j).wait_recv()
        qacc2[j] = add(qplane[2 + j], qra[j])
        if j == 0:
            qb_copy().start()
    p_hop(2)
    qb_copy().wait_recv()
    q_total = qacc2[1].astype(F32) + qrb[...].astype(F32)
    p_hop(3)
    for z in range(line):

        @pl.when(at.z == z)
        def _():
            total = acc3[z].astype(F32)
            for way in inflows(z):
                total = total + rz[way, z].astype(F32)
            out[...] = restore(jnp.concatenate([total, q_total], axis=0))

    for k in range(count):
        c_copy(k).wait_send()
        qc_copy(k).wait_send()
        z = slots[k][2]

        @pl.when(at.z < z)
        def _():
            qz_copy(0, k).wait_send()

        @pl.when(at.z > z)
        def _():
            qz_copy(1, k).wait_send()

    for j in range(2 * line):
        a_copy(j).wait_send()
    for z in range(line):
        b_copy(z).wait_send()

        @pl.when(at.z < z)
        def _():
            z_copy(0, z).wait_send()

        @pl.when(at.z > z)
        def _():
            z_copy(1, z).wait_send()

    qa_copy(0).wait_send()
    qa_copy(1).wait_send()
    qb_copy().wait_send()


def scatter_blocks(parts):
    room = lambda *n: pltpu.VMEM(n + (PART, 128), BF16)
    sems = lambda: [
        DMA((16,)), DMA((8,)), DMA((4,)), DMA((2, 4)), DMA((16,)), DMA((2, 16)), DMA((2,)), DMA,
    ]
    return pl.pallas_call(
        scatter_kernel,
        name="scatter",
        out_shape=shape_of((BLOCK_ROWS, C), F32),
        in_specs=[VM],
        out_specs=VM,
        scratch_shapes=[
            room(16), room(16), room(8), room(8), room(4), room(4), room(2, 4), room(2, 4),
            room(16), room(16), room(2, 16), room(2, 16), room(4), room(2), room(2), room(),
        ]
        + sems()
        + sems(),
        compiler_params=comm_params("scatter", 2),
    )(parts)


def bands_of():
    band = lax.axis_index("space")
    pair, core = band // 2, band % 2
    return band, pair * 2 + 1 - core, (1 - pair) * 2 + core


def swap_kernel(width, value, above, below, up_sem, down_sem, up_in, down_in, ready):
    band = lax.axis_index("space")
    rows = value.shape[1]
    ends = lax.axis_size("space") - 1
    down = remote(
        value.at[:, pl.ds(rows - width, width)], above, down_sem, down_in, {"space": band + 1}
    )
    up = remote(value.at[:, pl.ds(0, width)], below, up_sem, up_in, {"space": band - 1})

    @pl.when(band < ends)
    def _():
        down.start()

    @pl.when(band > 0)
    def _():
        up.start()

    def finish():
        @pl.when(band < ends)
        def _():
            down.wait_send()
            up.wait_recv()

        @pl.when(band > 0)
        def _():
            up.wait_send()
            down.wait_recv()

    return finish


def bands_meet(others):
    band = lax.axis_index("space")
    ends = lax.axis_size("space") - 1
    greet(
        [({"space": o}, None) for o in others]
        + [({"space": band + 1}, band < ends), ({"space": band - 1}, band > 0)]
    )


def share_kernel(
    rn, cot, rn_all, above, below, send, recv, own_sem, up_sem, down_sem, up_in, down_in
):
    band, sibling, across = bands_of()
    bands_meet((sibling, across))
    to_sibling = remote(rn, rn_all.at[band], send.at[0], recv.at[band], {"space": sibling})
    to_across = remote(rn, rn_all.at[band], send.at[1], recv.at[band], {"space": across})
    to_across.start()
    to_sibling.start()
    own = pltpu.make_async_copy(rn, rn_all.at[band], own_sem)
    own.start()
    finish = swap_kernel(1, cot, above, below, up_sem, down_sem, up_in, down_in, None)

    def landed(index):
        remote(rn, rn_all.at[index], send.at[0], recv.at[index], {"space": sibling}).wait_recv()

    landed(across)
    onward = remote(
        rn_all.at[across], rn_all.at[across], send.at[2], recv.at[across], {"space": sibling}
    )
    onward.start()
    landed(sibling)
    landed(across + sibling - band)
    own.wait()
    to_across.wait_send()
    to_sibling.wait_send()
    onward.wait_send()
    finish()


def share(rn, cot):
    bands = lax.axis_size("space")
    dma = pltpu.SemaphoreType.DMA
    edge = (cot.shape[0], 1) + cot.shape[2:]
    return pl.pallas_call(
        share_kernel,
        name="share",
        out_shape=(
            shape_of((bands,) + rn.shape, rn.dtype),
            shape_of(edge, cot.dtype),
            shape_of(edge, cot.dtype),
        ),
        in_specs=[VM, ANY],
        out_specs=(ANY, ANY, ANY),
        scratch_shapes=[dma((3,)), dma((bands,)), dma, dma, dma, dma, dma],
        compiler_params=comm_params("share", 3),
    )(rn, cot)


def halo_kernel(value, above, below, up_sem, down_sem, up_in, down_in):
    bands_meet(())
    swap_kernel(2, value, above, below, up_sem, down_sem, up_in, down_in, None)()


def halo(value):
    dma = pltpu.SemaphoreType.DMA
    edge = (value.shape[0], 2) + value.shape[2:]
    return pl.pallas_call(
        halo_kernel,
        name="halo",
        out_shape=(shape_of(edge, value.dtype), shape_of(edge, value.dtype)),
        in_specs=[ANY],
        out_specs=(ANY, ANY),
        scratch_shapes=[dma, dma, dma, dma],
        compiler_params=comm_params("halo", 4),
    )(value)


def merge_kernel(parts, out, rc, acc, rb, c_sem, c_in, b_sem, b_in):
    band, sibling, across = bands_of()
    greet([({"space": sibling}, None), ({"space": across}, None)])
    far = across + sibling - band
    first = remote(parts.at[far], rc.at[0], c_sem.at[0], c_in.at[0], {"space": sibling})
    second = remote(parts.at[sibling], rc.at[1], c_sem.at[1], c_in.at[1], {"space": sibling})
    onward = remote(acc, rb, b_sem, b_in, {"space": across})
    first.start()
    second.start()
    first.wait_recv()
    acc[...] = (parts[across].astype(F32) + rc[0].astype(F32)).astype(BF16)
    onward.start()
    second.wait_recv()
    out[...] = parts[band].astype(F32) + rc[1].astype(F32)
    onward.wait_recv()
    out[...] += rb[...].astype(F32)
    first.wait_send()
    second.wait_send()
    onward.wait_send()


def merge(parts):
    one = parts.shape[1:]
    dma = pltpu.SemaphoreType.DMA
    return pl.pallas_call(
        merge_kernel,
        name="merge",
        out_shape=shape_of(one, F32),
        in_specs=[VM],
        out_specs=VM,
        scratch_shapes=[
            pltpu.VMEM((2,) + one, BF16),
            pltpu.VMEM(one, BF16),
            pltpu.VMEM(one, BF16),
            dma((2,)),
            dma((2,)),
            dma,
            dma,
        ],
        compiler_params=comm_params("merge", 5),
    )(parts)


def blocks_fit(size):
    return (
        lax.axis_size("dp") == 8 and lax.axis_size("space") == 4 and size == BLOCK_ROWS * C
    )


def gather_flat(shard):
    if blocks_fit(shard.shape[0]):
        return gather_blocks(shard.reshape(BLOCK_ROWS, C))
    flat = lax.all_gather(shard, ("dp", "space"), axis=0, tiled=True)
    want = ROWS * C
    flat = flat[:want] if flat.shape[0] >= want else jnp.pad(flat, (0, want - flat.shape[0]))
    blocks = jax.vmap(compact)(flat.reshape(BLOCKS, BLOCK_ROWS, C))
    return blocks.reshape(BLOCKS, 2, PART, 128)


def scatter_grads(blocks, size):
    if blocks_fit(size):
        return scatter_blocks(blocks).reshape(size)
    flat = jax.vmap(restore)(blocks.reshape(BLOCKS, 2 * PART, 128)).reshape(-1)
    want = size * lax.axis_size("dp") * lax.axis_size("space")
    flat = flat[:want] if flat.shape[0] >= want else jnp.pad(flat, (0, want - flat.shape[0]))
    own = lax.psum_scatter(flat, ("dp", "space"), scatter_dimension=0, tiled=True)
    return own.astype(F32)


def on_device(scenes, shard, cotangent):
    count, rows, breadth = scenes.shape[0], scenes.shape[1], scenes.shape[2]
    tokens = count * rows * breadth
    bands = lax.axis_size("space")
    per_band = rows * breadth // 4
    band = lax.axis_index("space")
    edge = jnp.stack([band > 0, band < bands - 1]).astype(F32)
    wq, wr, wk, wv, wo, we, ws, vec, hid = unpack(gather_flat(shard))
    x = scenes.reshape(tokens, C)
    q, red, rn = front(x, vec, wq, wr)
    rn_all, cot_top, cot_low = share(rn, cotangent)
    rn_all = rn_all.reshape(bands, count, per_band, C)
    mixed, inv, mid, n2, p, key, vt = attend(x, q, rn_all, vec, wk, wv, wo)
    n2 = n2.reshape(scenes.shape)
    n2_top, n2_low = halo(n2)
    y, gmid, gwe, gws, ghid, gvec2 = mix(
        n2, n2_top, n2_low, cotangent, cot_top, cot_low, mid, edge, vec, hid, we, ws
    )
    dq, grn_all, gwk, gwv, gwo, gvec1 = attend_back(
        q, inv, mixed, gmid, p, key, vt, rn_all, wk, wv, wo
    )
    grn = merge(grn_all.reshape(bands, count * per_band, C))
    gx, gwq, gwr, gvec0 = tail(x, gmid, dq, grn, red, vec, wq, wr)
    blocks = pack(gwq, gwr, gwk, gwv, gwo, gwe, gws, gvec0, gvec1, gvec2, ghid)
    grads = scatter_grads(blocks, shard.shape[0])
    return y.reshape(scenes.shape), gx.reshape(scenes.shape), grads


def solution(mesh):
    band = P("dp", "space", None, None)
    flat = P(("dp", "space"))
    return jax.shard_map(
        on_device,
        mesh=mesh,
        in_specs=(band, flat, band),
        out_specs=(band, band, flat),
        check_vma=False,
    )
```

```python
import functools
import math

import jax
import jax.numpy as jnp
from jax import lax
from jax.experimental import pallas as pl
from jax.experimental.pallas import tpu as pltpu
from jax.sharding import PartitionSpec as P

C = 320
HEADS = 5
HD = 64
FF = 1280
W = 64
EPSILON = 1e-06
F32 = jnp.float32
BF16 = jnp.bfloat16

ROWS = 5184
USED_ROWS = 5175
BLOCKS = 32
BLOCK_ROWS = ROWS // BLOCKS
R_QUERY = 0
R_REDUCE = 321
R_KEYVAL = 1604
R_OUTPUT = 2245
R_EXPAND = 2570
R_HIDDEN = 3850
R_SHRINK = 3894
VECTOR_ROWS = (320, 1601, 1602, 1603, 2244, 2565, 2566, 2567, 2568, 2569, 5174)
(
    V_QUERY,
    V_REDUCE,
    V_RGAIN,
    V_RSHIFT,
    V_VALUE,
    V_OUTPUT,
    V_GAIN1,
    V_SHIFT1,
    V_GAIN2,
    V_SHIFT2,
    V_SHRINK,
) = range(11)
HIDDEN_ROWS = 11

ROOM = dict(
    unpack=30, front=14, attend=34, mix=33, attend_back=26, tail=16, pack=32,
    gather=8, scatter=18, share=3, halo=2, merge=8,
)


def params(name):
    return pltpu.CompilerParams(vmem_limit_bytes=ROOM[name] * 1024 * 1024)


ANY = pl.BlockSpec(memory_space=pl.ANY)
VM = pl.BlockSpec(memory_space=pltpu.VMEM)


def shape_of(dims, kind):
    return jax.ShapeDtypeStruct(dims, kind)


def mm(left, right):
    return jnp.dot(left, right, preferred_element_type=F32)


def mm_tn(left, right):
    return lax.dot_general(left, right, (((0,), (0,)), ((), ())), preferred_element_type=F32)


def mm_nt(left, right):
    return lax.dot_general(left, right, (((1,), (1,)), ((), ())), preferred_element_type=F32)


def mm_tt(left, right):
    return lax.dot_general(left, right, (((0,), (1,)), ((), ())), preferred_element_type=F32)


def norm_parts(values):
    center = values - jnp.mean(values, axis=-1, keepdims=True)
    rstd = lax.rsqrt(jnp.mean(center * center, axis=-1, keepdims=True) + EPSILON)
    return center * rstd, rstd


def norm_back(grad, unit, rstd, gain):
    scaled = grad * gain
    first = jnp.mean(scaled, axis=-1, keepdims=True)
    second = jnp.mean(scaled * unit, axis=-1, keepdims=True)
    return rstd * (scaled - first - unit * second)


def row_sum(values):
    return jnp.sum(values, axis=0, keepdims=True)


def full(dims):
    return pl.BlockSpec(dims, lambda *_: (0,) * len(dims))


def unpack_kernel(g_ref, wq, wr, wk, wv, wo, we, ws, vec, hid, rows, tiles):
    for i in range(BLOCKS):
        at = i * BLOCK_ROWS
        block = restore(g_ref[i].astype(F32))
        rows[at : at + BLOCK_ROWS, :] = block
        tiles[0, at : at + BLOCK_ROWS, :] = block[:, 0:128]
        tiles[1, at : at + BLOCK_ROWS, :] = block[:, 128:256]
        tiles[2, at : at + BLOCK_ROWS, 0:64] = block[:, 256:320]

    def strided(start, count, step):
        parts = [tiles[t, pl.ds(start, count, stride=step), :] for t in range(3)]
        return jnp.concatenate([parts[0], parts[1], parts[2][:, 0:64]], axis=1)

    wq[...] = rows[R_QUERY : R_QUERY + C, :].astype(BF16)
    wr[...] = rows[R_REDUCE : R_REDUCE + 4 * C, :].astype(BF16)
    wk[...] = strided(R_KEYVAL, C, 2).astype(BF16)
    wv[...] = strided(R_KEYVAL + 1, C, 2).astype(BF16)
    wo[...] = rows[R_OUTPUT : R_OUTPUT + C, :].astype(BF16)
    ws[...] = rows[R_SHRINK : R_SHRINK + FF, :].astype(BF16)
    we[...] = jnp.concatenate([strided(R_EXPAND + j, C, 4) for j in range(4)], axis=1).astype(BF16)
    hid[0:HIDDEN_ROWS, :] = jnp.concatenate(
        [strided(R_HIDDEN + j, HIDDEN_ROWS, 4) for j in range(4)], axis=1
    )
    for i, row in enumerate(VECTOR_ROWS):
        vec[i : i + 1, :] = rows[row : row + 1, :]


def unpack(blocks):
    return pl.pallas_call(
        unpack_kernel,
        name="unpack",
        out_shape=(
            shape_of((C, C), BF16),
            shape_of((4 * C, C), BF16),
            shape_of((C, C), BF16),
            shape_of((C, C), BF16),
            shape_of((C, C), BF16),
            shape_of((C, FF), BF16),
            shape_of((FF, C), BF16),
            shape_of((16, C), F32),
            shape_of((16, FF), F32),
        ),
        scratch_shapes=[pltpu.VMEM((ROWS, C), F32), pltpu.VMEM((3, ROWS, 128), F32)],
        compiler_params=params("unpack"),
    )(blocks)


def pack_kernel(gwq, gwr, gwk, gwv, gwo, gwe, gws, gvec0, gvec1, gvec2, ghid, out, tiles):
    def put(start, value):
        count = value.shape[0]
        tiles[0, start : start + count, :] = value[:, 0:128]
        tiles[1, start : start + count, :] = value[:, 128:256]
        tiles[2, start : start + count, 0:64] = value[:, 256:320]

    def put_strided(start, step, value):
        count = value.shape[0]
        tiles[0, pl.ds(start, count, stride=step), :] = value[:, 0:128]
        tiles[1, pl.ds(start, count, stride=step), :] = value[:, 128:256]
        tail = jnp.concatenate([value[:, 256:320], jnp.zeros((count, 64), F32)], axis=1)
        tiles[2, pl.ds(start, count, stride=step), :] = tail

    put(R_QUERY, gwq[...])
    put(R_REDUCE, gwr[...])
    put_strided(R_KEYVAL, 2, gwk[...].T)
    put_strided(R_KEYVAL + 1, 2, gwv[...].T)
    put(R_OUTPUT, gwo[...])
    put(R_SHRINK, gws[...].T)
    for j in range(4):
        put_strided(R_EXPAND + j, 4, gwe[:, C * j : C * j + C])
        put_strided(R_HIDDEN + j, 4, ghid[0:HIDDEN_ROWS, C * j : C * j + C])
    for source, names in (
        (gvec0, (V_QUERY, V_REDUCE, V_RGAIN, V_RSHIFT, V_GAIN1, V_SHIFT1)),
        (gvec2, (V_GAIN2, V_SHIFT2, V_SHRINK)),
    ):
        for i, name in enumerate(names):
            put(VECTOR_ROWS[name], source[i : i + 1, :])
    put(VECTOR_ROWS[V_VALUE], gvec1[0:1, :])
    put(VECTOR_ROWS[V_OUTPUT], gvec1[8:9, :])
    put(USED_ROWS, jnp.zeros((ROWS - USED_ROWS, C), F32))
    half = BLOCK_ROWS // 2
    spare = jnp.zeros((SPAN - 2 * BLOCK_ROWS - half, 128), F32)
    for i in range(BLOCKS):
        at = i * BLOCK_ROWS
        tail = jnp.concatenate(
            [
                tiles[2, at : at + half, 0:64],
                tiles[2, at + half : at + BLOCK_ROWS, 0:64],
            ],
            axis=1,
        )
        rows = [tiles[0, at : at + BLOCK_ROWS, :], tiles[1, at : at + BLOCK_ROWS, :], tail, spare]
        out[i] = jnp.concatenate(rows, axis=0).astype(BF16)


def pack(*pieces):
    return pl.pallas_call(
        pack_kernel,
        name="pack",
        out_shape=shape_of((BLOCKS, SPAN, 128), BF16),
        scratch_shapes=[pltpu.VMEM((3, ROWS, 128), F32)],
        compiler_params=params("pack"),
    )(*pieces)


TILE = 8 * W
RTILE = TILE // 4


def split_tiles(scr, value):
    scr[0, :, :] = value[:, 0:128]
    scr[1, :, :] = value[:, 128:256]
    scr[2, :, 0:64] = value[:, 256:320]


def patch_pieces(scr):
    pieces = {}
    for b in range(2):
        parts = [scr[t, pl.ds(b, TILE // 2, stride=2), :] for t in range(3)]
        cols = jnp.concatenate([parts[0], parts[1], parts[2][:, 0:64]], axis=1)
        cols = cols.reshape(TILE // (2 * W), 2, W // 2, C)
        for a in range(2):
            pieces[2 * a + b] = cols[:, a].reshape(RTILE, C)
    return pieces


def front_kernel(x_ref, vec, wq, wr, q_out, red_out, rn_out, scr):
    unit, _ = norm_parts(x_ref[...].astype(F32))
    normed = (unit * vec[V_GAIN1 : V_GAIN1 + 1, :] + vec[V_SHIFT1 : V_SHIFT1 + 1, :]).astype(BF16)
    queries = (mm(normed, wq[...]) + vec[V_QUERY : V_QUERY + 1, :]).astype(BF16)
    q_out[...] = queries * jnp.asarray(1.0 / math.sqrt(HD), BF16)
    split_tiles(scr, normed.astype(F32))
    pieces = patch_pieces(scr)
    reduced = vec[V_REDUCE : V_REDUCE + 1, :]
    for k in range(4):
        reduced = reduced + mm(pieces[k].astype(BF16), wr[k * C : (k + 1) * C, :])
    red_out[...] = reduced
    unit, _ = norm_parts(reduced)
    rn_out[...] = (unit * vec[V_RGAIN : V_RGAIN + 1, :] + vec[V_RSHIFT : V_RSHIFT + 1, :]).astype(
        BF16
    )


def front(x, vec, wq, wr):
    tokens = x.shape[0]
    return pl.pallas_call(
        front_kernel,
        name="front",
        grid=(tokens // TILE,),
        in_specs=[
            pl.BlockSpec((TILE, C), lambda i: (i, 0)),
            full((16, C)),
            full((C, C)),
            full((4 * C, C)),
        ],
        out_specs=[
            pl.BlockSpec((TILE, C), lambda i: (i, 0)),
            pl.BlockSpec((RTILE, C), lambda i: (i, 0)),
            pl.BlockSpec((RTILE, C), lambda i: (i, 0)),
        ],
        out_shape=(
            shape_of((tokens, C), BF16),
            shape_of((tokens // 4, C), F32),
            shape_of((tokens // 4, C), BF16),
        ),
        scratch_shapes=[pltpu.VMEM((3, TILE, 128), F32)],
        compiler_params=params("front"),
    )(x, vec, wq, wr)


QT = 512


def attend_kernel(
    x_ref, q_ref, rn_ref, vec, wk, wv, wo,
    mixed_out, inv_out, mid_out, n2_out, p_out, key_out, vt_out, kt, vones,
):
    keys = rn_ref.shape[0] * rn_ref.shape[2]

    @pl.when(pl.program_id(1) == 0)
    def _():
        rn = rn_ref[:, 0].reshape(keys, C)
        key = mm(rn, wk[...]).astype(BF16)
        value = (mm(rn, wv[...]) + vec[V_VALUE : V_VALUE + 1, :]).astype(BF16)
        key_out[0] = key
        vt_out[0] = value.T
        kt[...] = key.T
        for h in range(HEADS):
            vones[h, :, 0:HD] = value[:, h * HD : (h + 1) * HD]
            vones[h, :, HD:] = jnp.ones((keys, HD), BF16)

    lane = lax.broadcasted_iota(jnp.int32, (QT, 128), 1)
    invs = jnp.zeros((QT, 128), F32)
    outs = []
    for h in range(HEADS):
        scores = mm(q_ref[:, h * HD : (h + 1) * HD], kt[h * HD : (h + 1) * HD, :])
        top = jnp.max(scores, axis=-1, keepdims=True)
        probs = jnp.exp(scores - top).astype(BF16)
        p_out[0, h] = probs
        both = mm(probs, vones[h])
        inv = 1.0 / both[:, HD:]
        outs.append(both[:, 0:HD] * inv)
        invs = jnp.where(lane == h, inv[:, 0:1], invs)
    inv_out[...] = invs
    mixed = jnp.concatenate(outs, axis=1).astype(BF16)
    mixed_out[...] = mixed
    middle = x_ref[...].astype(F32) + mm(mixed, wo[...]) + vec[V_OUTPUT : V_OUTPUT + 1, :]
    mid_out[...] = middle
    unit, _ = norm_parts(middle)
    n2_out[...] = (unit * vec[V_GAIN2 : V_GAIN2 + 1, :] + vec[V_SHIFT2 : V_SHIFT2 + 1, :]).astype(
        BF16
    )


def attend(x, q, rn_all, vec, wk, wv, wo):
    tokens = x.shape[0]
    bands, scenes, per_band, _ = rn_all.shape
    keys = bands * per_band
    per_scene = tokens // scenes
    steps = per_scene // QT
    tile = pl.BlockSpec((QT, C), lambda s, i: (s * steps + i, 0))
    return pl.pallas_call(
        attend_kernel,
        name="attend",
        grid=(scenes, steps),
        in_specs=[
            tile,
            tile,
            pl.BlockSpec((bands, 1, per_band, C), lambda s, i: (0, s, 0, 0)),
            full((16, C)),
            full((C, C)),
            full((C, C)),
            full((C, C)),
        ],
        out_specs=[
            tile,
            pl.BlockSpec((QT, 128), lambda s, i: (s * steps + i, 0)),
            tile,
            tile,
            pl.BlockSpec((1, HEADS, QT, keys), lambda s, i: (s, 0, i, 0)),
            pl.BlockSpec((1, keys, C), lambda s, i: (s, 0, 0)),
            pl.BlockSpec((1, C, keys), lambda s, i: (s, 0, 0)),
        ],
        out_shape=(
            shape_of((tokens, C), BF16),
            shape_of((tokens, 128), F32),
            shape_of((tokens, C), F32),
            shape_of((tokens, C), BF16),
            shape_of((scenes, HEADS, per_scene, keys), BF16),
            shape_of((scenes, keys, C), BF16),
            shape_of((scenes, C, keys), BF16),
        ),
        scratch_shapes=[pltpu.VMEM((C, keys), BF16), pltpu.VMEM((HEADS, keys, 2 * HD), BF16)],
        compiler_params=params("attend"),
    )(x, q, rn_all, vec, wk, wv, wo)


CH = 256
AHEAD = 2


SHRINK_IN = math.sqrt(0.5 * math.log2(math.e))
SLOPE = 1.0 / (math.sqrt(2.0 * math.pi) * SHRINK_IN)
ACT_SCALE = SLOPE / SHRINK_IN
ERF_RATE = 0.3275911 * math.sqrt(0.5) / SHRINK_IN
ERF_TERMS = [
    0.5 * k / SLOPE
    for k in (0.254829592, -0.284496736, 1.421413741, -1.453152027, 1.061405429)
]


def gelu_parts(u):
    size = jnp.abs(u)
    t = 1.0 / (1.0 + ERF_RATE * size)
    poly = ERF_TERMS[4]
    for term in ERF_TERMS[3::-1]:
        poly = term + t * poly
    bell = jnp.exp2(-(u * u))
    tail = (t * poly) * bell
    return jnp.where(u >= 0, 1.0 / SLOPE - tail, tail), bell


def mix_kernel(
    n2, n2_top, n2_low, cot, cot_top, cot_low, mid, edge, vec, hid, we, ws,
    y_out, gmid_out, gwe_out, gws_out, ghid_out, gvec_out,
    nx, cx, nt, ct, wx, wt, e_scr, e_low, ga_scr, gc_scr, act_scr, ge_scr, branch, gn2,
):
    scenes, rows = n2.shape[0], n2.shape[1]
    ext = (rows + 4) * W
    gext = (rows + 2) * W
    own = rows * W
    top, low = edge[0], edge[1]

    def inside(value, there):
        return jnp.where(there > 0, value.astype(F32), 0.0).astype(BF16)

    for s in range(scenes):
        mine = n2[s].reshape(own, C)
        nx[s * ext : s * ext + 2 * W, 0:C] = inside(n2_top[s].reshape(2 * W, C), top)
        nx[s * ext + 2 * W : s * ext + 2 * W + own, 0:C] = mine
        nx[s * ext + 2 * W + own : (s + 1) * ext, 0:C] = inside(n2_low[s].reshape(2 * W, C), low)
        nx[s * ext : (s + 1) * ext, C:] = jnp.ones((ext, 64), BF16)
        for there, start in ((top, 0), (low, 2 * W + own)):

            @pl.when(there == 0)
            def _():
                spot = slice(s * ext + start, s * ext + start + 2 * W)
                nx[spot, C:] = jnp.zeros((2 * W, 64), BF16)

        nt[0:C, s * own : (s + 1) * own] = mine.T
        mine = cot[s].reshape(own, C)
        cx[s * gext : s * gext + W, :] = inside(cot_top[s].reshape(W, C), top)
        cx[s * gext + W : s * gext + W + own, :] = mine
        cx[s * gext + W + own : (s + 1) * gext, :] = inside(cot_low[s].reshape(W, C), low)
        ct[:, s * own : (s + 1) * own] = mine.T
    wx[0:C, :] = we[...]
    wx[C : C + 16, :] = jnp.concatenate(
        [hid[0:1, :], jnp.zeros((15, FF), F32)], axis=0
    ).astype(BF16)
    wx[C + 16 :, :] = jnp.zeros((48, FF), BF16)
    wt[...] = ws[...].T
    nt[C:, :] = jnp.ones((16, scenes * own), BF16)
    branch[...] = jnp.zeros_like(branch)
    gn2[...] = jnp.zeros_like(gn2)

    def chunk(step, carry):
        cols = pl.ds(pl.multiple_of(step * CH, CH), CH)
        wcol = we[:, cols]
        wrow = ws[cols, :]
        wx_col = wx[:, cols]
        wt_col = wt[:, cols]

        def expand(at, size):
            part = mm(nx[pl.ds(at, size), :], wx_col).astype(BF16)
            e_low[pl.ds(at, size), :] = part
            e_scr[pl.ds(at, size), :] = part.astype(F32)

        def activ_grad(at, size):
            ga_scr[pl.ds(at, size), :] = mm(cx[pl.ds(at, size), :], wt_col)

        col = lax.broadcasted_iota(jnp.int32, (8, CH), 0)
        first, last = col == 0, col == 7

        def right(value):
            moved = pltpu.roll(value, 1, axis=0)
            return jnp.concatenate([jnp.where(first, 0.0, moved[0:8]), moved[8:]], axis=0)

        def left(value):
            moved = pltpu.roll(value, W - 1, axis=0)
            return jnp.concatenate([moved[: W - 8], jnp.where(last, 0.0, moved[W - 8 :])], axis=0)

        def fold(value):
            value = value[0:32] + value[32:64]
            value = value[0:16] + value[16:32]
            return (value[0:8] + value[8:16]).astype(F32)

        taps = [hid[1 + k : 2 + k, cols] * SHRINK_IN for k in range(9)]
        low_taps = [hid[1 + k : 2 + k, cols].astype(BF16) for k in range(9)]
        conv_bias = hid[10:11, cols] * SHRINK_IN

        for s in range(scenes):

            def forward_row(r):
                at = pl.multiple_of(s * ext + r * W, W)
                lines = [e_scr[pl.ds(at + a * W, W), :] for a in range(3)]
                sums = [
                    lines[0] * taps[b] + lines[1] * taps[3 + b] + lines[2] * taps[6 + b]
                    for b in range(3)
                ]
                u = conv_bias + right(sums[0]) + sums[1] + left(sums[2])
                cdf, bell = gelu_parts(u)
                gat = pl.multiple_of(s * gext + r * W, W)
                gc = ga_scr[pl.ds(gat, W), :] * (cdf + u * bell)
                act_scr[pl.ds(gat, W), :] = (u * cdf).astype(BF16)
                gc_scr[0, pl.ds(gat, W), :] = left(gc).astype(BF16)
                gc_scr[1, pl.ds(gat, W), :] = gc.astype(BF16)
                gc_scr[2, pl.ds(gat, W), :] = right(gc).astype(BF16)

            def forward(i, carry):
                r = i * AHEAD
                for j in range(AHEAD):
                    forward_row(r + j)
                expand(pl.multiple_of(s * ext + (r + AHEAD + 2) * W, W), AHEAD * W)
                activ_grad(pl.multiple_of(s * gext + (r + AHEAD) * W, W), AHEAD * W)
                return carry

            expand(s * ext, (AHEAD + 2) * W)
            activ_grad(s * gext, AHEAD * W)
            lax.fori_loop(0, (rows + 2) // AHEAD, forward, 0)

        def backward(s, r, carry):
            line = e_low[pl.ds(pl.multiple_of(s * ext + (r + 2) * W, W), W), :]
            grads = list(carry)
            total = None
            for a in range(3):
                gat = pl.multiple_of(s * gext + (r + 2 - a) * W, W)
                for b in range(3):
                    g = gc_scr[b, pl.ds(gat, W), :]
                    term = g * low_taps[3 * a + b]
                    total = term if total is None else total + term
                    grads[3 * a + b] = grads[3 * a + b] + fold(g * line)
                    if a == 1 and b == 1:
                        grads[9] = grads[9] + fold(g)
            ge_scr[pl.ds(pl.multiple_of(s * own + r * W, W), W), :] = total
            return tuple(grads)

        sums = tuple(jnp.zeros((8, CH), F32) for _ in range(10))
        for s in range(scenes):
            sums = lax.fori_loop(0, rows, functools.partial(backward, s), sums)
        for k in range(10):
            ghid_out[1 + k : 2 + k, cols] = row_sum(sums[k]) * SLOPE

        ge = ge_scr[...]
        grads = mm(nt[...], ge)
        gwe_out[:, cols] = grads[0:C, :] * SLOPE
        ghid_out[0:1, cols] = grads[C : C + 1, :] * SLOPE
        gn2[...] += mm_nt(ge, wcol)
        gws = None
        for s in range(scenes):
            at = slice(s * own, (s + 1) * own)
            act = act_scr[s * gext + W : s * gext + W + own, :]
            branch[at, :] += mm(act, wrow)
            term = mm(ct[:, at], act)
            gws = term if gws is None else gws + term
        gws_out[:, cols] = gws * ACT_SCALE
        return carry

    lax.fori_loop(0, FF // CH, chunk, 0)

    size = 4 * W
    per = own // size
    gain = vec[V_GAIN2 : V_GAIN2 + 1, :]

    def finish(i, carry):
        at = pl.multiple_of(i * size, size)
        s = i // per
        line = (i % per) * 4
        middle = mid[pl.ds(at, size), :]
        y_out[pl.ds(at, size), :] = (
            middle + branch[pl.ds(at, size), :] * ACT_SCALE + vec[V_SHRINK : V_SHRINK + 1, :]
        ).astype(BF16)
        grad = gn2[pl.ds(at, size), :] * SLOPE
        unit, rstd = norm_parts(middle)
        direct = cot[s, pl.ds(line, 4)].reshape(size, C).astype(F32)
        gmid_out[pl.ds(at, size), :] = direct + norm_back(grad, unit, rstd, gain)
        return (
            carry[0] + row_sum(grad * unit),
            carry[1] + row_sum(grad),
            carry[2] + row_sum(direct),
        )

    zero = jnp.zeros((1, C), F32)
    sums = lax.fori_loop(0, scenes * per, finish, (zero, zero, zero))
    for i in range(3):
        gvec_out[i : i + 1, :] = sums[i]


def mix(n2, n2_top, n2_low, cot, cot_top, cot_low, mid, edge, vec, hid, we, ws):
    scenes, rows = n2.shape[0], n2.shape[1]
    tokens = scenes * rows * W
    ext = scenes * (rows + 4) * W
    gext = scenes * (rows + 2) * W
    return pl.pallas_call(
        mix_kernel,
        name="mix",
        in_specs=[VM] * 7 + [pl.BlockSpec(memory_space=pltpu.SMEM)] + [VM] * 4,
        out_specs=[VM] * 6,
        out_shape=(
            shape_of((tokens, C), BF16),
            shape_of((tokens, C), F32),
            shape_of((C, FF), F32),
            shape_of((C, FF), F32),
            shape_of((16, FF), F32),
            shape_of((8, C), F32),
        ),
        scratch_shapes=[
            pltpu.VMEM((ext + AHEAD * W, C + 64), BF16),
            pltpu.VMEM((gext + AHEAD * W, C), BF16),
            pltpu.VMEM((C + 16, tokens), BF16),
            pltpu.VMEM((C, tokens), BF16),
            pltpu.VMEM((C + 64, FF), BF16),
            pltpu.VMEM((C, FF), BF16),
            pltpu.VMEM((ext + AHEAD * W, CH), F32),
            pltpu.VMEM((ext + AHEAD * W, CH), BF16),
            pltpu.VMEM((gext + AHEAD * W, CH), F32),
            pltpu.VMEM((3, gext, CH), BF16),
            pltpu.VMEM((gext, CH), BF16),
            pltpu.VMEM((tokens, CH), BF16),
            pltpu.VMEM((tokens, C), F32),
            pltpu.VMEM((tokens, C), F32),
        ],
        compiler_params=params("mix"),
    )(n2, n2_top, n2_low, cot, cot_top, cot_low, mid, edge, vec, hid, we, ws)


QTB = 256


def attend_back_kernel(
    q_ref, inv_ref, mixed_ref, gmid_ref, p_ref, key_ref, vt_ref, rn_ref, wk, wv, wo,
    dq_out, grn_out, gwk_out, gwv_out, gwo_out, gvec_out, kh, dkt, dvt,
):
    scene, step = pl.program_id(0), pl.program_id(1)
    keys = rn_ref.shape[0] * rn_ref.shape[2]

    @pl.when(jnp.logical_and(scene == 0, step == 0))
    def _():
        for ref in (gwk_out, gwv_out, gwo_out, gvec_out):
            ref[...] = jnp.zeros_like(ref)

    @pl.when(step == 0)
    def _():
        for h in range(HEADS):
            kh[h] = key_ref[0, :, h * HD : (h + 1) * HD]
        dkt[...] = jnp.zeros_like(dkt)
        dvt[...] = jnp.zeros_like(dvt)

    gatt = gmid_ref[...].astype(BF16)
    gvec_out[8:9, :] += row_sum(gatt.astype(F32))
    mixed = mixed_ref[...]
    gwo_out[...] += mm_tn(mixed, gatt)
    inv = jnp.concatenate(
        [jnp.broadcast_to(inv_ref[:, h : h + 1], (QTB, HD)) for h in range(HEADS)], axis=1
    )
    scaled = (mm_nt(gatt, wo[...]) * inv).astype(BF16)
    prod = scaled.astype(F32) * mixed.astype(F32)
    q_t = q_ref[...].T
    g_t = scaled.T
    dqs = []
    for h in range(HEADS):
        cols = slice(h * HD, (h + 1) * HD)
        inner = jnp.sum(prod[:, cols], axis=-1, keepdims=True)
        probs = p_ref[0, h]
        gprobs = mm(scaled[:, cols], vt_ref[0, cols, :])
        gscores = (probs.astype(F32) * (gprobs - inner)).astype(BF16)
        dqs.append(mm(gscores, kh[h]))
        dkt[cols, :] += mm(q_t[cols, :], gscores)
        dvt[cols, :] += mm(g_t[cols, :], probs)
    dq_out[...] = (jnp.concatenate(dqs, axis=1) * (1.0 / math.sqrt(HD))).astype(BF16)

    @pl.when(step == pl.num_programs(1) - 1)
    def _():
        rn = rn_ref[:, 0].reshape(keys, C)
        dk = dkt[...].astype(BF16)
        dv = dvt[...].astype(BF16)
        gvec_out[0:8, :] += mm_nt(jnp.ones((8, keys), BF16), dv)
        gwk_out[...] += mm(dk, rn)
        gwv_out[...] += mm(dv, rn)
        grn = (mm(wk[...], dk) + mm(wv[...], dv)).astype(BF16)
        grn_out[...] = grn.T.reshape(grn_out.shape)


def attend_back(q, inv, mixed, gmid, p, key, vt, rn_all, wk, wv, wo):
    tokens = q.shape[0]
    bands, scenes, per_band, _ = rn_all.shape
    keys = bands * per_band
    steps = tokens // scenes // QTB
    tile = pl.BlockSpec((QTB, C), lambda s, i: (s * steps + i, 0))
    return pl.pallas_call(
        attend_back_kernel,
        name="attend_back",
        grid=(scenes, steps),
        in_specs=[
            tile,
            pl.BlockSpec((QTB, 128), lambda s, i: (s * steps + i, 0)),
            tile,
            tile,
            pl.BlockSpec((1, HEADS, QTB, keys), lambda s, i: (s, 0, i, 0)),
            pl.BlockSpec((1, keys, C), lambda s, i: (s, 0, 0)),
            pl.BlockSpec((1, C, keys), lambda s, i: (s, 0, 0)),
            pl.BlockSpec((bands, 1, per_band, C), lambda s, i: (0, s, 0, 0)),
            full((C, C)),
            full((C, C)),
            full((C, C)),
        ],
        out_specs=[
            tile,
            pl.BlockSpec((bands, 1, per_band, C), lambda s, i: (0, s, 0, 0)),
            full((C, C)),
            full((C, C)),
            full((C, C)),
            full((16, C)),
        ],
        out_shape=(
            shape_of((tokens, C), BF16),
            shape_of(rn_all.shape, BF16),
            shape_of((C, C), F32),
            shape_of((C, C), F32),
            shape_of((C, C), F32),
            shape_of((16, C), F32),
        ),
        scratch_shapes=[
            pltpu.VMEM((HEADS, keys, HD), BF16),
            pltpu.VMEM((C, keys), F32),
            pltpu.VMEM((C, keys), F32),
        ],
        compiler_params=params("attend_back"),
    )(q, inv, mixed, gmid, p, key, vt, rn_all, wk, wv, wo)


def tail_kernel(
    x_ref, gmid_ref, dq_ref, grn_ref, red_ref, vec, wq, wr,
    gx_out, gwq_out, gwr_out, gvec_out, scr, gscr,
):
    @pl.when(pl.program_id(0) == 0)
    def _():
        for ref in (gwq_out, gwr_out, gvec_out):
            ref[...] = jnp.zeros_like(ref)

    runit, rrstd = norm_parts(red_ref[...])
    grn = grn_ref[...].astype(F32)
    gred = norm_back(grn, runit, rrstd, vec[V_RGAIN : V_RGAIN + 1, :]).astype(BF16)
    unit, rstd = norm_parts(x_ref[...].astype(F32))
    gain = vec[V_GAIN1 : V_GAIN1 + 1, :]
    normed = (unit * gain + vec[V_SHIFT1 : V_SHIFT1 + 1, :]).astype(BF16)
    split_tiles(scr, normed.astype(F32))
    pieces = patch_pieces(scr)
    back = {}
    for k in range(4):
        at = slice(k * C, (k + 1) * C)
        gwr_out[at, :] += mm_tn(pieces[k].astype(BF16), gred)
        back[k] = mm_nt(gred, wr[at, :]).reshape(TILE // (2 * W), 1, W // 2, C)
    for b in range(2):
        cols = jnp.concatenate([back[b], back[2 + b]], axis=1).reshape(TILE // 2, C)
        spot = pl.ds(b, TILE // 2, stride=2)
        gscr[0, spot, :] = cols[:, 0:128]
        gscr[1, spot, :] = cols[:, 128:256]
        gscr[2, spot, :] = jnp.concatenate(
            [cols[:, 256:320], jnp.zeros((TILE // 2, 64), F32)], axis=1
        )
    dq = dq_ref[...]
    gwq_out[...] += mm_tn(normed, dq)
    placed = jnp.concatenate([gscr[0], gscr[1], gscr[2][:, 0:64]], axis=1)
    gnormed = mm_nt(dq, wq[...]) + placed
    gx_out[...] = gmid_ref[...] + norm_back(gnormed, unit, rstd, gain)
    gvec_out[0:1, :] += row_sum(dq.astype(F32))
    gvec_out[1:2, :] += row_sum(gred.astype(F32))
    gvec_out[2:3, :] += row_sum(grn * runit)
    gvec_out[3:4, :] += row_sum(grn)
    gvec_out[4:5, :] += row_sum(gnormed * unit)
    gvec_out[5:6, :] += row_sum(gnormed)


def tail(x, gmid, dq, grn, red, vec, wq, wr):
    tokens = x.shape[0]
    tile = pl.BlockSpec((TILE, C), lambda i: (i, 0))
    rtile = pl.BlockSpec((RTILE, C), lambda i: (i, 0))
    return pl.pallas_call(
        tail_kernel,
        name="tail",
        grid=(tokens // TILE,),
        in_specs=[
            tile, tile, tile, rtile, rtile, full((16, C)), full((C, C)), full((4 * C, C))
        ],
        out_specs=[tile, full((C, C)), full((4 * C, C)), full((8, C))],
        out_shape=(
            shape_of((tokens, C), F32),
            shape_of((C, C), F32),
            shape_of((4 * C, C), F32),
            shape_of((8, C), F32),
        ),
        scratch_shapes=[pltpu.VMEM((3, TILE, 128), F32), pltpu.VMEM((3, TILE, 128), F32)],
        compiler_params=params("tail"),
    )(x, gmid, dq, grn, red, vec, wq, wr)


def flip(value, by):
    return value + by * (1 - 2 * value)


def remote(src, dst, send, recv, where):
    return pltpu.make_async_remote_copy(
        src_ref=src,
        dst_ref=dst,
        send_sem=send,
        recv_sem=recv,
        device_id=where,
        device_id_type=pl.DeviceIdType.MESH,
    )


def greet(places):
    barrier = pltpu.get_barrier_semaphore()
    count = 0
    for place, there in places:
        if there is None:
            pl.semaphore_signal(
                barrier, inc=1, device_id=place, device_id_type=pl.DeviceIdType.MESH
            )
            count = count + 1
        else:

            @pl.when(there)
            def _():
                pl.semaphore_signal(
                    barrier, inc=1, device_id=place, device_id_type=pl.DeviceIdType.MESH
                )

            count = count + there.astype(jnp.int32)
    pl.semaphore_wait(barrier, count)


def comm_params(name, number):
    return pltpu.CompilerParams(
        collective_id=number, has_side_effects=True, vmem_limit_bytes=ROOM[name] * 1024 * 1024
    )


class Place:
    def __init__(self):
        dp, space = lax.axis_index("dp"), lax.axis_index("space")
        self.z, self.x = dp // 2, dp % 2
        self.y, self.c = space // 2, space % 2
        self.line = lax.axis_size("dp") // 2

    def block(self, z, x, y, c):
        return ((z * 2 + x) * 2 + y) * 2 + c

    def device(self, z, x, y, c):
        return {"dp": z * 2 + x, "space": y * 2 + c}

    def spot(self, da, db, c):
        return (
            flip(self.x, da * (1 - c) + db * c),
            flip(self.y, db * (1 - c) + da * c),
        )

    def partners(self):
        ax, ay = self.spot(1, 0, self.c)
        bx, by = self.spot(0, 1, self.c)
        return (
            self.device(self.z, ax, ay, self.c),
            self.device(self.z, bx, by, self.c),
            self.device(self.z, self.x, self.y, 1 - self.c),
            self.device(self.z + 1, self.x, self.y, self.c),
            self.device(self.z - 1, self.x, self.y, self.c),
        )

    def meet(self):
        first, second, sibling, up, down = self.partners()
        greet(
            [
                (first, None),
                (second, None),
                (sibling, None),
                (up, self.z < self.line - 1),
                (down, self.z > 0),
            ]
        )


DMA = pltpu.SemaphoreType.DMA
SPAN = 416
PART = 288
BOTH = (pl.ds(0, PART), pl.ds(PART, SPAN - PART))


def compact(block):
    half = BLOCK_ROWS // 2
    tail = jnp.concatenate([block[:half, 256:], block[half:, 256:]], axis=1)
    spare = jnp.zeros((SPAN - 2 * BLOCK_ROWS - half, 128), block.dtype)
    return jnp.concatenate([block[:, 0:128], block[:, 128:256], tail, spare], axis=0)


def restore(rows):
    half = BLOCK_ROWS // 2
    tail = rows[2 * BLOCK_ROWS : 2 * BLOCK_ROWS + half]
    return jnp.concatenate(
        [
            rows[:BLOCK_ROWS],
            rows[BLOCK_ROWS : 2 * BLOCK_ROWS],
            jnp.concatenate([tail[:, 0:64], tail[:, 64:128]], axis=0),
        ],
        axis=1,
    )


PLANE = [(da, db) for da in range(2) for db in range(2)]


def gather_kernel(own_ref, out, own, p_z, p_a, p_b, p_c, q_z, q_a, q_b, q_c, recv):
    at = Place()
    line = at.line
    first, second, sibling, up, down = at.partners()
    own[...] = compact(own_ref[...].astype(F32)).astype(BF16)
    at.meet()
    can_up, can_down = at.z < line - 1, at.z > 0

    def index_of(z, da, db, c):
        x, y = at.spot(da, db, at.c)
        return at.block(z, x, y, c)

    def push(part, index, src, sem, where):
        remote(src, out.at[index, BOTH[part]], sem, recv.at[index, part], where).start()

    def landed(part, index):
        remote(
            out.at[index, BOTH[part]], out.at[index, BOTH[part]], p_a.at[0], recv.at[index, part], sibling
        ).wait_recv()

    def here(part, index, is_own):
        return own.at[BOTH[part]] if is_own else out.at[index, BOTH[part]]

    def along_z(part, z, k, index, src, way, sems):
        if way >= 0:

            @pl.when(can_up)
            def _():
                push(part, index, src, sems.at[0, k, z], up)

        if way <= 0:

            @pl.when(can_down)
            def _():
                push(part, index, src, sems.at[1, k, z], down)

    def first_order(z, da, db, way, is_own=False):
        index = index_of(z, da, db, at.c)
        if not is_own:
            landed(0, index)
        src = here(0, index, is_own)
        if da == 0 and db == 0:
            along_z(0, z, 0, index, src, way, p_z)
            push(0, index, src, p_a.at[z], first)
        if db == 0:
            push(0, index, src, p_b.at[da, z], second)
        push(0, index, src, p_c.at[2 * da + db, z], sibling)

    def second_order(z, da, db, way, is_own=False):
        index = index_of(z, da, db, at.c)
        if not is_own:
            landed(1, index)
        src = here(1, index, is_own)
        if way == 0:
            if da == 0 and db == 0:
                push(1, index, src, q_a, first)
            if db == 0:
                push(1, index, src, q_b.at[da], second)
        along_z(1, z, 2 * da + db, index, src, way, q_z)
        push(1, index, src, q_c.at[2 * da + db, z], sibling)

    def hop(d, order, places):
        for z in range(line):
            if z >= d:

                @pl.when(at.z == z)
                def _():
                    for da, db in places:
                        order(z - d, da, db, 1)

            if z + d < line:

                @pl.when(at.z == z)
                def _():
                    for da, db in places:
                        order(z + d, da, db, -1)

    def flat_hops(da, db):
        first_order(at.z, da, db, 0)
        for d in range(1, line):
            hop(d, lambda z, da, db, way: first_order(z, da, db, way), [(da, db)])

    second_order(at.z, 0, 0, 0, True)
    first_order(at.z, 0, 0, 0, True)
    mine = index_of(at.z, 0, 0, at.c)
    out[mine] = own[...]
    second_order(at.z, 1, 0, 0)
    hop(1, first_order, [(0, 0)])
    second_order(at.z, 0, 1, 0)
    second_order(at.z, 1, 1, 0)
    hop(2, first_order, [(0, 0)])
    hop(1, second_order, PLANE)
    hop(3, first_order, [(0, 0)])
    flat_hops(1, 0)
    hop(2, second_order, PLANE)
    flat_hops(0, 1)
    flat_hops(1, 1)
    hop(3, second_order, PLANE)
    for z in range(line):
        for da, db in PLANE:
            for part in range(2):
                landed(part, index_of(z, da, db, 1 - at.c))

    def sent(part, sem, where):
        remote(own.at[BOTH[part]], out.at[mine, BOTH[part]], sem, recv.at[mine, part], where).wait_send()

    sent(1, q_a, first)
    for z in range(line):
        for k in range(4):
            sent(0, p_c.at[k, z], sibling)
            sent(1, q_c.at[k, z], sibling)
        sent(0, p_a.at[z], first)
        for da in range(2):
            sent(0, p_b.at[da, z], second)

        @pl.when(jnp.logical_and(can_up, z <= at.z))
        def _():
            sent(0, p_z.at[0, 0, z], up)
            for k in range(4):
                sent(1, q_z.at[0, k, z], up)

        @pl.when(jnp.logical_and(can_down, z >= at.z))
        def _():
            sent(0, p_z.at[1, 0, z], down)
            for k in range(4):
                sent(1, q_z.at[1, k, z], down)

    for da in range(2):
        sent(1, q_b.at[da], second)


def gather_blocks(own):
    return pl.pallas_call(
        gather_kernel,
        name="gather",
        out_shape=shape_of((BLOCKS, SPAN, 128), BF16),
        in_specs=[VM],
        out_specs=VM,
        scratch_shapes=[
            pltpu.VMEM((SPAN, 128), BF16),
            DMA((2, 1, 4)), DMA((4,)), DMA((2, 4)), DMA((4, 4)),
            DMA((2, 4, 4)), DMA, DMA((2,)), DMA((4, 4)),
            DMA((BLOCKS, 2)),
        ],
        compiler_params=comm_params("gather", 1),
    )(own)


def scatter_kernel(
    parts, out,
    rc, acc, ra, acc2, rb, acc3, rz, sz,
    qc, qacc, qrz, qsz, qplane, qra, qacc2, qrb,
    c_out, a_out, b_out, z_out, qc_out, qz_out, qa_out, qb_out,
    c_in, a_in, b_in, z_in, qc_in, qz_in, qa_in, qb_in,
):
    at = Place()
    line = at.line
    first, second, sibling, up, down = at.partners()
    at.meet()
    slots = [(da, db, z) for da in (1, 0) for db in (1, 0) for z in range(line)]

    def add(*terms):
        total = terms[0].astype(F32)
        for term in terms[1:]:
            total = total + term.astype(F32)
        return total.astype(BF16)

    def source(k, c):
        da, db, z = slots[k]
        x, y = at.spot(da, db, c)
        return at.block(z, x, y, c)

    def c_copy(k):
        src = parts.at[source(k, 1 - at.c), BOTH[0]]
        return remote(src, rc.at[k], c_out.at[k], c_in.at[k], sibling)

    def qc_copy(k):
        src = parts.at[source(k, 1 - at.c), BOTH[1]]
        return remote(src, qc.at[k], qc_out.at[k], qc_in.at[k], sibling)

    def a_copy(j):
        return remote(acc.at[j], ra.at[j], a_out.at[j], a_in.at[j], first)

    def b_copy(j):
        return remote(acc2.at[j], rb.at[j], b_out.at[j], b_in.at[j], second)

    def z_copy(way, z):
        return remote(
            sz.at[way, z], rz.at[way, z], z_out.at[way, z], z_in.at[way, z], (up, down)[way]
        )

    def qz_copy(way, k, src=None):
        src = qsz.at[way, k] if src is None else src
        return remote(src, qrz.at[way, k], qz_out.at[way, k], qz_in.at[way, k], (up, down)[way])

    def qa_copy(j):
        return remote(qplane.at[j], qra.at[j], qa_out.at[j], qa_in.at[j], first)

    def qb_copy():
        return remote(qacc2.at[0], qrb, qb_out, qb_in, second)

    count = 4 * line
    for k in range(count):
        qc_copy(k).start()
        c_copy(k).start()
    for k in range(count):
        da, db, z = slots[k]
        qc_copy(k).wait_recv()
        mine = source(k, at.c)
        qacc[k] = add(parts[mine, BOTH[1]], qc[k])
        if z > 0:

            @pl.when(at.z == 0)
            def _():
                qz_copy(0, k, qacc.at[k]).start()

        if z < line - 1:

            @pl.when(at.z == line - 1)
            def _():
                qz_copy(1, k, qacc.at[k]).start()

        c_copy(k).wait_recv()
        acc[k] = add(parts[mine, BOTH[0]], rc[k])
        if da:
            a_copy(k).start()

    def q_hop(d):
        for k in range(count):
            z = slots[k][2]
            if z >= d:

                @pl.when(at.z == d)
                def _():
                    qz_copy(0, k).wait_recv()
                    if z > d:
                        qsz[0, k] = add(qacc[k], qrz[0, k])
                        qz_copy(0, k).start()

            if z <= line - 1 - d:

                @pl.when(at.z == line - 1 - d)
                def _():
                    qz_copy(1, k).wait_recv()
                    if z < line - 1 - d:
                        qsz[1, k] = add(qacc[k], qrz[1, k])
                        qz_copy(1, k).start()

    def p_hop(d):
        for z in reversed(range(d, line)):

            @pl.when(at.z == d)
            def _():
                if d > 0:
                    z_copy(0, z).wait_recv()
                if z > d:
                    sz[0, z] = add(acc3[z], rz[0, z]) if d > 0 else acc3[z]
                    z_copy(0, z).start()

        for z in range(line - d):

            @pl.when(at.z == line - 1 - d)
            def _():
                if d > 0:
                    z_copy(1, z).wait_recv()
                if z < line - 1 - d:
                    sz[1, z] = add(acc3[z], rz[1, z]) if d > 0 else acc3[z]
                    z_copy(1, z).start()

    def inflows(z):
        return [way for way, there in ((0, z > 0), (1, z < line - 1)) if there]

    for j in range(line):
        a_copy(j).wait_recv()
        acc2[j] = add(acc[2 * line + j], ra[j])
        b_copy(j).start()
    q_hop(1)
    for j in range(line, 2 * line):
        a_copy(j).wait_recv()
        acc2[j] = add(acc[2 * line + j], ra[j])
    q_hop(2)
    for z in range(line):
        b_copy(z).wait_recv()
        acc3[z] = add(acc2[line + z], rb[z])
    p_hop(0)
    q_hop(3)
    for z in range(line):

        @pl.when(at.z == z)
        def _():
            for j in range(4):
                k = j * line + z
                qplane[j] = add(qacc[k], *[qrz[way, k] for way in inflows(z)])

    qa_copy(0).start()
    qa_copy(1).start()
    p_hop(1)
    for j in range(2):
        qa_copy(j).wait_recv()
        qacc2[j] = add(qplane[2 + j], qra[j])
        if j == 0:
            qb_copy().start()
    p_hop(2)
    qb_copy().wait_recv()
    q_total = qacc2[1].astype(F32) + qrb[...].astype(F32)
    p_hop(3)
    for z in range(line):

        @pl.when(at.z == z)
        def _():
            total = acc3[z].astype(F32)
            for way in inflows(z):
                total = total + rz[way, z].astype(F32)
            out[...] = restore(jnp.concatenate([total, q_total], axis=0))

    for k in range(count):
        c_copy(k).wait_send()
        qc_copy(k).wait_send()
        z = slots[k][2]

        @pl.when(at.z < z)
        def _():
            qz_copy(0, k).wait_send()

        @pl.when(at.z > z)
        def _():
            qz_copy(1, k).wait_send()

    for j in range(2 * line):
        a_copy(j).wait_send()
    for z in range(line):
        b_copy(z).wait_send()

        @pl.when(at.z < z)
        def _():
            z_copy(0, z).wait_send()

        @pl.when(at.z > z)
        def _():
            z_copy(1, z).wait_send()

    qa_copy(0).wait_send()
    qa_copy(1).wait_send()
    qb_copy().wait_send()


def scatter_blocks(parts):
    room = lambda *n: pltpu.VMEM(n + (PART, 128), BF16)
    less = lambda *n: pltpu.VMEM(n + (SPAN - PART, 128), BF16)
    sems = lambda: [
        DMA((16,)), DMA((8,)), DMA((4,)), DMA((2, 4)), DMA((16,)), DMA((2, 16)), DMA((2,)), DMA,
    ]
    return pl.pallas_call(
        scatter_kernel,
        name="scatter",
        out_shape=shape_of((BLOCK_ROWS, C), F32),
        in_specs=[VM],
        out_specs=VM,
        scratch_shapes=[
            room(16), room(16), room(8), room(8), room(4), room(4), room(2, 4), room(2, 4),
            less(16), less(16), less(2, 16), less(2, 16), less(4), less(2), less(2), less(),
        ]
        + sems()
        + sems(),
        compiler_params=comm_params("scatter", 2),
    )(parts)


def bands_of():
    band = lax.axis_index("space")
    pair, core = band // 2, band % 2
    return band, pair * 2 + 1 - core, (1 - pair) * 2 + core


def swap_kernel(width, value, above, below, up_sem, down_sem, up_in, down_in, ready):
    band = lax.axis_index("space")
    rows = value.shape[1]
    ends = lax.axis_size("space") - 1
    down = remote(
        value.at[:, pl.ds(rows - width, width)], above, down_sem, down_in, {"space": band + 1}
    )
    up = remote(value.at[:, pl.ds(0, width)], below, up_sem, up_in, {"space": band - 1})

    @pl.when(band < ends)
    def _():
        down.start()

    @pl.when(band > 0)
    def _():
        up.start()

    def finish():
        @pl.when(band < ends)
        def _():
            down.wait_send()
            up.wait_recv()

        @pl.when(band > 0)
        def _():
            up.wait_send()
            down.wait_recv()

    return finish


def bands_meet(others):
    band = lax.axis_index("space")
    ends = lax.axis_size("space") - 1
    greet(
        [({"space": o}, None) for o in others]
        + [({"space": band + 1}, band < ends), ({"space": band - 1}, band > 0)]
    )


def share_kernel(
    rn, cot, rn_all, above, below, send, recv, own_sem, up_sem, down_sem, up_in, down_in
):
    band, sibling, across = bands_of()
    bands_meet((sibling, across))
    to_sibling = remote(rn, rn_all.at[band], send.at[0], recv.at[band], {"space": sibling})
    to_across = remote(rn, rn_all.at[band], send.at[1], recv.at[band], {"space": across})
    to_across.start()
    to_sibling.start()
    own = pltpu.make_async_copy(rn, rn_all.at[band], own_sem)
    own.start()
    finish = swap_kernel(1, cot, above, below, up_sem, down_sem, up_in, down_in, None)

    def landed(index):
        remote(rn, rn_all.at[index], send.at[0], recv.at[index], {"space": sibling}).wait_recv()

    landed(across)
    onward = remote(
        rn_all.at[across], rn_all.at[across], send.at[2], recv.at[across], {"space": sibling}
    )
    onward.start()
    landed(sibling)
    landed(across + sibling - band)
    own.wait()
    to_across.wait_send()
    to_sibling.wait_send()
    onward.wait_send()
    finish()


def share(rn, cot):
    bands = lax.axis_size("space")
    dma = pltpu.SemaphoreType.DMA
    edge = (cot.shape[0], 1) + cot.shape[2:]
    return pl.pallas_call(
        share_kernel,
        name="share",
        out_shape=(
            shape_of((bands,) + rn.shape, rn.dtype),
            shape_of(edge, cot.dtype),
            shape_of(edge, cot.dtype),
        ),
        in_specs=[VM, ANY],
        out_specs=(ANY, ANY, ANY),
        scratch_shapes=[dma((3,)), dma((bands,)), dma, dma, dma, dma, dma],
        compiler_params=comm_params("share", 3),
    )(rn, cot)


def halo_kernel(value, above, below, up_sem, down_sem, up_in, down_in):
    bands_meet(())
    swap_kernel(2, value, above, below, up_sem, down_sem, up_in, down_in, None)()


def halo(value):
    dma = pltpu.SemaphoreType.DMA
    edge = (value.shape[0], 2) + value.shape[2:]
    return pl.pallas_call(
        halo_kernel,
        name="halo",
        out_shape=(shape_of(edge, value.dtype), shape_of(edge, value.dtype)),
        in_specs=[ANY],
        out_specs=(ANY, ANY),
        scratch_shapes=[dma, dma, dma, dma],
        compiler_params=comm_params("halo", 4),
    )(value)


def merge_kernel(parts, out, rc, acc, rb, c_sem, c_in, b_sem, b_in):
    band, sibling, across = bands_of()
    greet([({"space": sibling}, None), ({"space": across}, None)])
    far = across + sibling - band
    first = remote(parts.at[far], rc.at[0], c_sem.at[0], c_in.at[0], {"space": sibling})
    second = remote(parts.at[sibling], rc.at[1], c_sem.at[1], c_in.at[1], {"space": sibling})
    onward = remote(acc, rb, b_sem, b_in, {"space": across})
    first.start()
    second.start()
    first.wait_recv()
    acc[...] = (parts[across].astype(F32) + rc[0].astype(F32)).astype(BF16)
    onward.start()
    second.wait_recv()
    out[...] = parts[band].astype(F32) + rc[1].astype(F32)
    onward.wait_recv()
    out[...] += rb[...].astype(F32)
    first.wait_send()
    second.wait_send()
    onward.wait_send()


def merge(parts):
    one = parts.shape[1:]
    dma = pltpu.SemaphoreType.DMA
    return pl.pallas_call(
        merge_kernel,
        name="merge",
        out_shape=shape_of(one, F32),
        in_specs=[VM],
        out_specs=VM,
        scratch_shapes=[
            pltpu.VMEM((2,) + one, BF16),
            pltpu.VMEM(one, BF16),
            pltpu.VMEM(one, BF16),
            dma((2,)),
            dma((2,)),
            dma,
            dma,
        ],
        compiler_params=comm_params("merge", 5),
    )(parts)


def blocks_fit(size):
    return (
        lax.axis_size("dp") == 8 and lax.axis_size("space") == 4 and size == BLOCK_ROWS * C
    )


def gather_flat(shard):
    if blocks_fit(shard.shape[0]):
        return gather_blocks(shard.reshape(BLOCK_ROWS, C))
    flat = lax.all_gather(shard, ("dp", "space"), axis=0, tiled=True)
    want = ROWS * C
    flat = flat[:want] if flat.shape[0] >= want else jnp.pad(flat, (0, want - flat.shape[0]))
    blocks = jax.vmap(compact)(flat.reshape(BLOCKS, BLOCK_ROWS, C))
    return blocks


def scatter_grads(blocks, size):
    if blocks_fit(size):
        return scatter_blocks(blocks).reshape(size)
    flat = jax.vmap(restore)(blocks).reshape(-1)
    want = size * lax.axis_size("dp") * lax.axis_size("space")
    flat = flat[:want] if flat.shape[0] >= want else jnp.pad(flat, (0, want - flat.shape[0]))
    own = lax.psum_scatter(flat, ("dp", "space"), scatter_dimension=0, tiled=True)
    return own.astype(F32)


def on_device(scenes, shard, cotangent):
    count, rows, breadth = scenes.shape[0], scenes.shape[1], scenes.shape[2]
    tokens = count * rows * breadth
    bands = lax.axis_size("space")
    per_band = rows * breadth // 4
    band = lax.axis_index("space")
    edge = jnp.stack([band > 0, band < bands - 1]).astype(F32)
    wq, wr, wk, wv, wo, we, ws, vec, hid = unpack(gather_flat(shard))
    x = scenes.reshape(tokens, C)
    q, red, rn = front(x, vec, wq, wr)
    rn_all, cot_top, cot_low = share(rn, cotangent)
    rn_all = rn_all.reshape(bands, count, per_band, C)
    mixed, inv, mid, n2, p, key, vt = attend(x, q, rn_all, vec, wk, wv, wo)
    n2 = n2.reshape(scenes.shape)
    n2_top, n2_low = halo(n2)
    y, gmid, gwe, gws, ghid, gvec2 = mix(
        n2, n2_top, n2_low, cotangent, cot_top, cot_low, mid, edge, vec, hid, we, ws
    )
    dq, grn_all, gwk, gwv, gwo, gvec1 = attend_back(
        q, inv, mixed, gmid, p, key, vt, rn_all, wk, wv, wo
    )
    grn = merge(grn_all.reshape(bands, count * per_band, C))
    gx, gwq, gwr, gvec0 = tail(x, gmid, dq, grn, red, vec, wq, wr)
    blocks = pack(gwq, gwr, gwk, gwv, gwo, gwe, gws, gvec0, gvec1, gvec2, ghid)
    grads = scatter_grads(blocks, shard.shape[0])
    return y.reshape(scenes.shape), gx.reshape(scenes.shape), grads


def solution(mesh):
    band = P("dp", "space", None, None)
    flat = P(("dp", "space"))
    return jax.shard_map(
        on_device,
        mesh=mesh,
        in_specs=(band, flat, band),
        out_specs=(band, band, flat),
        check_vma=False,
    )
```

```python
import functools
import math

import jax
import jax.numpy as jnp
from jax import lax
from jax.experimental import pallas as pl
from jax.experimental.pallas import tpu as pltpu
from jax.sharding import PartitionSpec as P

C = 320
HEADS = 5
HD = 64
FF = 1280
W = 64
EPSILON = 1e-06
F32 = jnp.float32
BF16 = jnp.bfloat16

ROWS = 5184
USED_ROWS = 5175
BLOCKS = 32
BLOCK_ROWS = ROWS // BLOCKS
R_QUERY = 0
R_REDUCE = 321
R_KEYVAL = 1604
R_OUTPUT = 2245
R_EXPAND = 2570
R_HIDDEN = 3850
R_SHRINK = 3894
VECTOR_ROWS = (320, 1601, 1602, 1603, 2244, 2565, 2566, 2567, 2568, 2569, 5174)
(
    V_QUERY,
    V_REDUCE,
    V_RGAIN,
    V_RSHIFT,
    V_VALUE,
    V_OUTPUT,
    V_GAIN1,
    V_SHIFT1,
    V_GAIN2,
    V_SHIFT2,
    V_SHRINK,
) = range(11)
HIDDEN_ROWS = 11

ROOM = dict(
    unpack=30, front=14, attend=34, mix=32, attend_back=26, tail=15, pack=32,
    gather=8, scatter=18, share=3, halo=2,
)


def params(name):
    return pltpu.CompilerParams(vmem_limit_bytes=ROOM[name] * 1024 * 1024)


ANY = pl.BlockSpec(memory_space=pl.ANY)
VM = pl.BlockSpec(memory_space=pltpu.VMEM)


def shape_of(dims, kind):
    return jax.ShapeDtypeStruct(dims, kind)


def mm(left, right):
    return jnp.dot(left, right, preferred_element_type=F32)


def mm_tn(left, right):
    return lax.dot_general(left, right, (((0,), (0,)), ((), ())), preferred_element_type=F32)


def mm_nt(left, right):
    return lax.dot_general(left, right, (((1,), (1,)), ((), ())), preferred_element_type=F32)


def mm_tt(left, right):
    return lax.dot_general(left, right, (((0,), (1,)), ((), ())), preferred_element_type=F32)


def norm_parts(values):
    center = values - jnp.mean(values, axis=-1, keepdims=True)
    rstd = lax.rsqrt(jnp.mean(center * center, axis=-1, keepdims=True) + EPSILON)
    return center * rstd, rstd


def norm_back(grad, unit, rstd, gain):
    scaled = grad * gain
    first = jnp.mean(scaled, axis=-1, keepdims=True)
    second = jnp.mean(scaled * unit, axis=-1, keepdims=True)
    return rstd * (scaled - first - unit * second)


def row_sum(values):
    return jnp.sum(values, axis=0, keepdims=True)


def full(dims):
    return pl.BlockSpec(dims, lambda *_: (0,) * len(dims))


def unpack_kernel(g_ref, wq, wr, wk, wv, wo, we, ws, vec, hid, rows, tiles):
    for i in range(BLOCKS):
        at = i * BLOCK_ROWS
        block = restore(g_ref[i].astype(F32))
        rows[at : at + BLOCK_ROWS, :] = block
        tiles[0, at : at + BLOCK_ROWS, :] = block[:, 0:128]
        tiles[1, at : at + BLOCK_ROWS, :] = block[:, 128:256]
        tiles[2, at : at + BLOCK_ROWS, 0:64] = block[:, 256:320]

    def strided(start, count, step):
        parts = [tiles[t, pl.ds(start, count, stride=step), :] for t in range(3)]
        return jnp.concatenate([parts[0], parts[1], parts[2][:, 0:64]], axis=1)

    wq[...] = rows[R_QUERY : R_QUERY + C, :].astype(BF16)
    wr[...] = rows[R_REDUCE : R_REDUCE + 4 * C, :].astype(BF16)
    wk[...] = strided(R_KEYVAL, C, 2).astype(BF16)
    wv[...] = strided(R_KEYVAL + 1, C, 2).astype(BF16)
    wo[...] = rows[R_OUTPUT : R_OUTPUT + C, :].astype(BF16)
    ws[...] = rows[R_SHRINK : R_SHRINK + FF, :].astype(BF16)
    we[...] = jnp.concatenate([strided(R_EXPAND + j, C, 4) for j in range(4)], axis=1).astype(BF16)
    hid[0:HIDDEN_ROWS, :] = jnp.concatenate(
        [strided(R_HIDDEN + j, HIDDEN_ROWS, 4) for j in range(4)], axis=1
    )
    for i, row in enumerate(VECTOR_ROWS):
        vec[i : i + 1, :] = rows[row : row + 1, :]


def unpack(blocks):
    return pl.pallas_call(
        unpack_kernel,
        name="unpack",
        out_shape=(
            shape_of((C, C), BF16),
            shape_of((4 * C, C), BF16),
            shape_of((C, C), BF16),
            shape_of((C, C), BF16),
            shape_of((C, C), BF16),
            shape_of((C, FF), BF16),
            shape_of((FF, C), BF16),
            shape_of((16, C), F32),
            shape_of((16, FF), F32),
        ),
        scratch_shapes=[pltpu.VMEM((ROWS, C), F32), pltpu.VMEM((3, ROWS, 128), F32)],
        compiler_params=params("unpack"),
    )(blocks)


def pack_kernel(
    gwq, gwr, gwk, gwv, gwo, gwe, gws, gvec0, gvec1, gvec2, ghid, gmid, gnorm, out, gx, tiles
):
    gx[...] = gmid[...] + gnorm[...]

    def put(start, value):
        count = value.shape[0]
        tiles[0, start : start + count, :] = value[:, 0:128]
        tiles[1, start : start + count, :] = value[:, 128:256]
        tiles[2, start : start + count, 0:64] = value[:, 256:320]

    def put_strided(start, step, value):
        count = value.shape[0]
        tiles[0, pl.ds(start, count, stride=step), :] = value[:, 0:128]
        tiles[1, pl.ds(start, count, stride=step), :] = value[:, 128:256]
        tail = jnp.concatenate([value[:, 256:320], jnp.zeros((count, 64), F32)], axis=1)
        tiles[2, pl.ds(start, count, stride=step), :] = tail

    put(R_QUERY, gwq[...])
    put(R_REDUCE, gwr[...])
    put_strided(R_KEYVAL, 2, gwk[...].T)
    put_strided(R_KEYVAL + 1, 2, gwv[...].T)
    put(R_OUTPUT, gwo[...])
    put(R_SHRINK, gws[...].T)
    for j in range(4):
        put_strided(R_EXPAND + j, 4, gwe[:, C * j : C * j + C])
        put_strided(R_HIDDEN + j, 4, ghid[0:HIDDEN_ROWS, C * j : C * j + C])
    for source, names in (
        (gvec0, (V_QUERY, V_REDUCE, V_RGAIN, V_RSHIFT, V_GAIN1, V_SHIFT1)),
        (gvec2, (V_GAIN2, V_SHIFT2, V_SHRINK)),
    ):
        for i, name in enumerate(names):
            put(VECTOR_ROWS[name], source[i : i + 1, :])
    put(VECTOR_ROWS[V_VALUE], gvec1[0:1, :])
    put(VECTOR_ROWS[V_OUTPUT], gvec1[8:9, :])
    put(USED_ROWS, jnp.zeros((ROWS - USED_ROWS, C), F32))
    half = BLOCK_ROWS // 2
    spare = jnp.zeros((2 * SPAN - 2 * BLOCK_ROWS - half, 128), F32)
    for i in range(BLOCKS):
        at = i * BLOCK_ROWS
        tail = jnp.concatenate(
            [
                tiles[2, at : at + half, 0:64],
                tiles[2, at + half : at + BLOCK_ROWS, 0:64],
            ],
            axis=1,
        )
        rows = [tiles[0, at : at + BLOCK_ROWS, :], tiles[1, at : at + BLOCK_ROWS, :], tail, spare]
        rows = jnp.concatenate(rows, axis=0)
        out[i] = jnp.concatenate([rows[:SPAN], rows[SPAN:]], axis=1).astype(BF16)


def pack(*pieces):
    return pl.pallas_call(
        pack_kernel,
        name="pack",
        out_shape=(shape_of((BLOCKS, SPAN, 256), BF16), shape_of(pieces[-1].shape, F32)),
        scratch_shapes=[pltpu.VMEM((3, ROWS, 128), F32)],
        compiler_params=params("pack"),
    )(*pieces)


TILE = 8 * W
RTILE = TILE // 4


def split_tiles(scr, value):
    scr[0, :, :] = value[:, 0:128]
    scr[1, :, :] = value[:, 128:256]
    scr[2, :, 0:64] = value[:, 256:320]


def patch_pieces(scr):
    pieces = {}
    for b in range(2):
        parts = [scr[t, pl.ds(b, TILE // 2, stride=2), :] for t in range(3)]
        cols = jnp.concatenate([parts[0], parts[1], parts[2][:, 0:64]], axis=1)
        cols = cols.reshape(TILE // (2 * W), 2, W // 2, C)
        for a in range(2):
            pieces[2 * a + b] = cols[:, a].reshape(RTILE, C)
    return pieces


def front_kernel(x_ref, vec, wq, wr, q_out, red_out, rn_out, scr):
    unit, _ = norm_parts(x_ref[...].astype(F32))
    normed = (unit * vec[V_GAIN1 : V_GAIN1 + 1, :] + vec[V_SHIFT1 : V_SHIFT1 + 1, :]).astype(BF16)
    queries = (mm(normed, wq[...]) + vec[V_QUERY : V_QUERY + 1, :]).astype(BF16)
    q_out[...] = queries * jnp.asarray(1.0 / math.sqrt(HD), BF16)
    split_tiles(scr, normed.astype(F32))
    pieces = patch_pieces(scr)
    reduced = vec[V_REDUCE : V_REDUCE + 1, :]
    for k in range(4):
        reduced = reduced + mm(pieces[k].astype(BF16), wr[k * C : (k + 1) * C, :])
    red_out[...] = reduced
    unit, _ = norm_parts(reduced)
    rn_out[...] = (unit * vec[V_RGAIN : V_RGAIN + 1, :] + vec[V_RSHIFT : V_RSHIFT + 1, :]).astype(
        BF16
    )


def front(x, vec, wq, wr):
    tokens = x.shape[0]
    return pl.pallas_call(
        front_kernel,
        name="front",
        grid=(tokens // TILE,),
        in_specs=[
            pl.BlockSpec((TILE, C), lambda i: (i, 0)),
            full((16, C)),
            full((C, C)),
            full((4 * C, C)),
        ],
        out_specs=[
            pl.BlockSpec((TILE, C), lambda i: (i, 0)),
            pl.BlockSpec((RTILE, C), lambda i: (i, 0)),
            pl.BlockSpec((RTILE, C), lambda i: (i, 0)),
        ],
        out_shape=(
            shape_of((tokens, C), BF16),
            shape_of((tokens // 4, C), F32),
            shape_of((tokens // 4, C), BF16),
        ),
        scratch_shapes=[pltpu.VMEM((3, TILE, 128), F32)],
        compiler_params=params("front"),
    )(x, vec, wq, wr)


QT = 512


def attend_kernel(
    x_ref, q_ref, rn_ref, vec, wk, wv, wo,
    mixed_out, inv_out, mid_out, n2_out, p_out, key_out, vt_out, kt, vones,
):
    keys = rn_ref.shape[0] * rn_ref.shape[2]

    @pl.when(pl.program_id(1) == 0)
    def _():
        rn = rn_ref[:, 0].reshape(keys, C)
        key = mm(rn, wk[...]).astype(BF16)
        value = (mm(rn, wv[...]) + vec[V_VALUE : V_VALUE + 1, :]).astype(BF16)
        key_out[0] = key
        vt_out[0] = value.T
        kt[...] = key.T
        for h in range(HEADS):
            vones[h, :, 0:HD] = value[:, h * HD : (h + 1) * HD]
            vones[h, :, HD:] = jnp.ones((keys, HD), BF16)

    lane = lax.broadcasted_iota(jnp.int32, (QT, 128), 1)
    invs = jnp.zeros((QT, 128), F32)
    outs = []
    for h in range(HEADS):
        scores = mm(q_ref[:, h * HD : (h + 1) * HD], kt[h * HD : (h + 1) * HD, :])
        top = jnp.max(scores, axis=-1, keepdims=True)
        probs = jnp.exp(scores - top).astype(BF16)
        p_out[0, h] = probs
        both = mm(probs, vones[h])
        inv = 1.0 / both[:, HD:]
        outs.append(both[:, 0:HD] * inv)
        invs = jnp.where(lane == h, inv[:, 0:1], invs)
    inv_out[...] = invs
    mixed = jnp.concatenate(outs, axis=1).astype(BF16)
    mixed_out[...] = mixed
    middle = x_ref[...].astype(F32) + mm(mixed, wo[...]) + vec[V_OUTPUT : V_OUTPUT + 1, :]
    mid_out[...] = middle
    unit, _ = norm_parts(middle)
    n2_out[...] = (unit * vec[V_GAIN2 : V_GAIN2 + 1, :] + vec[V_SHIFT2 : V_SHIFT2 + 1, :]).astype(
        BF16
    )


def attend(x, q, rn_all, vec, wk, wv, wo):
    tokens = x.shape[0]
    bands, scenes, per_band, _ = rn_all.shape
    keys = bands * per_band
    per_scene = tokens // scenes
    steps = per_scene // QT
    tile = pl.BlockSpec((QT, C), lambda s, i: (s * steps + i, 0))
    return pl.pallas_call(
        attend_kernel,
        name="attend",
        grid=(scenes, steps),
        in_specs=[
            tile,
            tile,
            pl.BlockSpec((bands, 1, per_band, C), lambda s, i: (0, s, 0, 0)),
            full((16, C)),
            full((C, C)),
            full((C, C)),
            full((C, C)),
        ],
        out_specs=[
            tile,
            pl.BlockSpec((QT, 128), lambda s, i: (s * steps + i, 0)),
            tile,
            tile,
            pl.BlockSpec((1, HEADS, QT, keys), lambda s, i: (s, 0, i, 0)),
            pl.BlockSpec((1, keys, C), lambda s, i: (s, 0, 0)),
            pl.BlockSpec((1, C, keys), lambda s, i: (s, 0, 0)),
        ],
        out_shape=(
            shape_of((tokens, C), BF16),
            shape_of((tokens, 128), F32),
            shape_of((tokens, C), F32),
            shape_of((tokens, C), BF16),
            shape_of((scenes, HEADS, per_scene, keys), BF16),
            shape_of((scenes, keys, C), BF16),
            shape_of((scenes, C, keys), BF16),
        ),
        scratch_shapes=[pltpu.VMEM((C, keys), BF16), pltpu.VMEM((HEADS, keys, 2 * HD), BF16)],
        compiler_params=params("attend"),
    )(x, q, rn_all, vec, wk, wv, wo)


CH = 256
AHEAD = 2


SHRINK_IN = math.sqrt(0.5 * math.log2(math.e))
SLOPE = 1.0 / (math.sqrt(2.0 * math.pi) * SHRINK_IN)
ACT_SCALE = SLOPE / SHRINK_IN
ERF_RATE = 0.3275911 * math.sqrt(0.5) / SHRINK_IN
ERF_TERMS = [
    0.5 * k / SLOPE
    for k in (0.254829592, -0.284496736, 1.421413741, -1.453152027, 1.061405429)
]


def gelu_parts(u):
    size = jnp.abs(u)
    t = 1.0 / (1.0 + ERF_RATE * size)
    poly = ERF_TERMS[4]
    for term in ERF_TERMS[3::-1]:
        poly = term + t * poly
    bell = jnp.exp2(-(u * u))
    tail = (t * poly) * bell
    return jnp.where(u >= 0, 1.0 / SLOPE - tail, tail), bell


def mix_kernel(
    n2, n2_top, n2_low, cot, cot_top, cot_low, mid, edge, vec, hid, we, ws,
    y_out, gmid_out, gwe_out, gws_out, ghid_out, gvec_out,
    nx, cx, nt, ct, wx, wt, e_scr, e_low, ga_scr, gc_scr, act_scr, ge_scr, branch, gn2,
):
    scenes, rows = n2.shape[0], n2.shape[1]
    ext = (rows + 4) * W
    gext = (rows + 2) * W
    own = rows * W
    top, low = edge[0], edge[1]

    def inside(value, there):
        return jnp.where(there > 0, value.astype(F32), 0.0).astype(BF16)

    for s in range(scenes):
        mine = n2[s].reshape(own, C)
        nx[s * ext : s * ext + 2 * W, 0:C] = inside(n2_top[s].reshape(2 * W, C), top)
        nx[s * ext + 2 * W : s * ext + 2 * W + own, 0:C] = mine
        nx[s * ext + 2 * W + own : (s + 1) * ext, 0:C] = inside(n2_low[s].reshape(2 * W, C), low)
        nx[s * ext : (s + 1) * ext, C:] = jnp.ones((ext, 64), BF16)
        for there, start in ((top, 0), (low, 2 * W + own)):

            @pl.when(there == 0)
            def _():
                spot = slice(s * ext + start, s * ext + start + 2 * W)
                nx[spot, C:] = jnp.zeros((2 * W, 64), BF16)

        nt[0:C, s * own : (s + 1) * own] = mine.T
        mine = cot[s].reshape(own, C)
        cx[s * gext : s * gext + W, :] = inside(cot_top[s].reshape(W, C), top)
        cx[s * gext + W : s * gext + W + own, :] = mine
        cx[s * gext + W + own : (s + 1) * gext, :] = inside(cot_low[s].reshape(W, C), low)
        ct[:, s * own : (s + 1) * own] = mine.T
    wx[0:C, :] = we[...]
    wx[C : C + 16, :] = jnp.concatenate(
        [hid[0:1, :], jnp.zeros((15, FF), F32)], axis=0
    ).astype(BF16)
    wx[C + 16 :, :] = jnp.zeros((48, FF), BF16)
    wt[...] = ws[...].T
    nt[C:, :] = jnp.ones((16, scenes * own), BF16)
    branch[...] = jnp.zeros_like(branch)
    gn2[...] = jnp.zeros_like(gn2)

    def chunk(step, carry):
        cols = pl.ds(pl.multiple_of(step * CH, CH), CH)
        wcol = we[:, cols]
        wrow = ws[cols, :]
        wx_col = wx[:, cols]
        wt_col = wt[:, cols]

        def expand(at, size):
            part = mm(nx[pl.ds(at, size), :], wx_col).astype(BF16)
            e_low[pl.ds(at, size), :] = part
            e_scr[pl.ds(at, size), :] = part.astype(F32)

        def activ_grad(at, size):
            ga_scr[pl.ds(at, size), :] = mm(cx[pl.ds(at, size), :], wt_col)

        col = lax.broadcasted_iota(jnp.int32, (8, CH), 0)
        first, last = col == 0, col == 7

        def right(value):
            moved = pltpu.roll(value, 1, axis=0)
            return jnp.concatenate([jnp.where(first, 0.0, moved[0:8]), moved[8:]], axis=0)

        def left(value):
            moved = pltpu.roll(value, W - 1, axis=0)
            return jnp.concatenate([moved[: W - 8], jnp.where(last, 0.0, moved[W - 8 :])], axis=0)

        def fold(value):
            value = value[0:32] + value[32:64]
            value = value[0:16] + value[16:32]
            return (value[0:8] + value[8:16]).astype(F32)

        taps = [hid[1 + k : 2 + k, cols] * SHRINK_IN for k in range(9)]
        low_taps = [hid[1 + k : 2 + k, cols].astype(BF16) for k in range(9)]
        conv_bias = hid[10:11, cols] * SHRINK_IN

        for s in range(scenes):

            def forward_row(r):
                at = pl.multiple_of(s * ext + r * W, W)
                lines = [e_scr[pl.ds(at + a * W, W), :] for a in range(3)]
                sums = [
                    lines[0] * taps[b] + lines[1] * taps[3 + b] + lines[2] * taps[6 + b]
                    for b in range(3)
                ]
                u = conv_bias + right(sums[0]) + sums[1] + left(sums[2])
                cdf, bell = gelu_parts(u)
                gat = pl.multiple_of(s * gext + r * W, W)
                gc = ga_scr[pl.ds(gat, W), :] * (cdf + u * bell)
                act_scr[pl.ds(gat, W), :] = (u * cdf).astype(BF16)
                gc_scr[0, pl.ds(gat, W), :] = left(gc).astype(BF16)
                gc_scr[1, pl.ds(gat, W), :] = gc.astype(BF16)
                gc_scr[2, pl.ds(gat, W), :] = right(gc).astype(BF16)

            def forward(i, carry):
                r = i * AHEAD
                for j in range(AHEAD):
                    forward_row(r + j)
                expand(pl.multiple_of(s * ext + (r + AHEAD + 2) * W, W), AHEAD * W)
                activ_grad(pl.multiple_of(s * gext + (r + AHEAD) * W, W), AHEAD * W)
                return carry

            expand(s * ext, (AHEAD + 2) * W)
            activ_grad(s * gext, AHEAD * W)
            lax.fori_loop(0, (rows + 2) // AHEAD, forward, 0)

        def backward(s, r, carry):
            line = e_low[pl.ds(pl.multiple_of(s * ext + (r + 2) * W, W), W), :]
            grads = list(carry)
            total = None
            for a in range(3):
                gat = pl.multiple_of(s * gext + (r + 2 - a) * W, W)
                for b in range(3):
                    g = gc_scr[b, pl.ds(gat, W), :]
                    term = g * low_taps[3 * a + b]
                    total = term if total is None else total + term
                    grads[3 * a + b] = grads[3 * a + b] + fold(g * line)
                    if a == 1 and b == 1:
                        grads[9] = grads[9] + fold(g)
            ge_scr[pl.ds(pl.multiple_of(s * own + r * W, W), W), :] = total
            return tuple(grads)

        sums = tuple(jnp.zeros((8, CH), F32) for _ in range(10))
        for s in range(scenes):
            sums = lax.fori_loop(0, rows, functools.partial(backward, s), sums)
        for k in range(10):
            ghid_out[1 + k : 2 + k, cols] = row_sum(sums[k]) * SLOPE

        ge = ge_scr[...]
        grads = mm(nt[...], ge)
        gwe_out[:, cols] = grads[0:C, :] * SLOPE
        ghid_out[0:1, cols] = grads[C : C + 1, :] * SLOPE
        gn2[...] += mm_nt(ge, wcol)
        gws = None
        for s in range(scenes):
            at = slice(s * own, (s + 1) * own)
            act = act_scr[s * gext + W : s * gext + W + own, :]
            branch[at, :] += mm(act, wrow)
            term = mm(ct[:, at], act)
            gws = term if gws is None else gws + term
        gws_out[:, cols] = gws * ACT_SCALE
        return carry

    lax.fori_loop(0, FF // CH, chunk, 0)

    size = 4 * W
    per = own // size
    gain = vec[V_GAIN2 : V_GAIN2 + 1, :]

    def finish(i, carry):
        at = pl.multiple_of(i * size, size)
        s = i // per
        line = (i % per) * 4
        middle = mid[pl.ds(at, size), :]
        y_out[pl.ds(at, size), :] = (
            middle + branch[pl.ds(at, size), :] * ACT_SCALE + vec[V_SHRINK : V_SHRINK + 1, :]
        ).astype(BF16)
        grad = gn2[pl.ds(at, size), :] * SLOPE
        unit, rstd = norm_parts(middle)
        direct = cot[s, pl.ds(line, 4)].reshape(size, C).astype(F32)
        gmid_out[pl.ds(at, size), :] = direct + norm_back(grad, unit, rstd, gain)
        return (
            carry[0] + row_sum(grad * unit),
            carry[1] + row_sum(grad),
            carry[2] + row_sum(direct),
        )

    zero = jnp.zeros((1, C), F32)
    sums = lax.fori_loop(0, scenes * per, finish, (zero, zero, zero))
    for i in range(3):
        gvec_out[i : i + 1, :] = sums[i]


def mix(n2, n2_top, n2_low, cot, cot_top, cot_low, mid, edge, vec, hid, we, ws):
    scenes, rows = n2.shape[0], n2.shape[1]
    tokens = scenes * rows * W
    ext = scenes * (rows + 4) * W
    gext = scenes * (rows + 2) * W
    return pl.pallas_call(
        mix_kernel,
        name="mix",
        in_specs=[VM] * 7 + [pl.BlockSpec(memory_space=pltpu.SMEM)] + [VM] * 4,
        out_specs=[VM] * 6,
        out_shape=(
            shape_of((tokens, C), BF16),
            shape_of((tokens, C), F32),
            shape_of((C, FF), F32),
            shape_of((C, FF), F32),
            shape_of((16, FF), F32),
            shape_of((8, C), F32),
        ),
        scratch_shapes=[
            pltpu.VMEM((ext + AHEAD * W, C + 64), BF16),
            pltpu.VMEM((gext + AHEAD * W, C), BF16),
            pltpu.VMEM((C + 16, tokens), BF16),
            pltpu.VMEM((C, tokens), BF16),
            pltpu.VMEM((C + 64, FF), BF16),
            pltpu.VMEM((C, FF), BF16),
            pltpu.VMEM((ext + AHEAD * W, CH), F32),
            pltpu.VMEM((ext + AHEAD * W, CH), BF16),
            pltpu.VMEM((gext + AHEAD * W, CH), F32),
            pltpu.VMEM((3, gext, CH), BF16),
            pltpu.VMEM((gext, CH), BF16),
            pltpu.VMEM((tokens, CH), BF16),
            pltpu.VMEM((tokens, C), F32),
            pltpu.VMEM((tokens, C), F32),
        ],
        compiler_params=params("mix"),
    )(n2, n2_top, n2_low, cot, cot_top, cot_low, mid, edge, vec, hid, we, ws)


QTB = 256


def attend_back_kernel(
    q_ref, inv_ref, mixed_ref, gmid_ref, p_ref, key_ref, vt_ref, rn_ref, wk, wv, wo,
    dq_out, grn_out, gwk_out, gwv_out, gwo_out, gvec_out, kh, dkt, dvt,
):
    scene, step = pl.program_id(0), pl.program_id(1)
    keys = rn_ref.shape[0] * rn_ref.shape[2]

    @pl.when(jnp.logical_and(scene == 0, step == 0))
    def _():
        for ref in (gwk_out, gwv_out, gwo_out, gvec_out):
            ref[...] = jnp.zeros_like(ref)

    @pl.when(step == 0)
    def _():
        for h in range(HEADS):
            kh[h] = key_ref[0, :, h * HD : (h + 1) * HD]
        dkt[...] = jnp.zeros_like(dkt)
        dvt[...] = jnp.zeros_like(dvt)

    gatt = gmid_ref[...].astype(BF16)
    gvec_out[8:9, :] += row_sum(gatt.astype(F32))
    mixed = mixed_ref[...]
    gwo_out[...] += mm_tn(mixed, gatt)
    inv = jnp.concatenate(
        [jnp.broadcast_to(inv_ref[:, h : h + 1], (QTB, HD)) for h in range(HEADS)], axis=1
    )
    scaled = (mm_nt(gatt, wo[...]) * inv).astype(BF16)
    prod = scaled.astype(F32) * mixed.astype(F32)
    q_t = q_ref[...].T
    g_t = scaled.T
    dqs = []
    for h in range(HEADS):
        cols = slice(h * HD, (h + 1) * HD)
        inner = jnp.sum(prod[:, cols], axis=-1, keepdims=True)
        probs = p_ref[0, h]
        gprobs = mm(scaled[:, cols], vt_ref[0, cols, :])
        gscores = (probs.astype(F32) * (gprobs - inner)).astype(BF16)
        dqs.append(mm(gscores, kh[h]))
        dkt[cols, :] += mm(q_t[cols, :], gscores)
        dvt[cols, :] += mm(g_t[cols, :], probs)
    dq_out[...] = (jnp.concatenate(dqs, axis=1) * (1.0 / math.sqrt(HD))).astype(BF16)

    @pl.when(step == pl.num_programs(1) - 1)
    def _():
        rn = rn_ref[:, 0].reshape(keys, C)
        dk = dkt[...].astype(BF16)
        dv = dvt[...].astype(BF16)
        gvec_out[0:8, :] += mm_nt(jnp.ones((8, keys), BF16), dv)
        gwk_out[...] += mm(dk, rn)
        gwv_out[...] += mm(dv, rn)
        grn = (mm(wk[...], dk) + mm(wv[...], dv)).astype(BF16)
        grn_out[...] = grn.T.reshape(grn_out.shape)


def attend_back(q, inv, mixed, gmid, p, key, vt, rn_all, wk, wv, wo):
    tokens = q.shape[0]
    bands, scenes, per_band, _ = rn_all.shape
    keys = bands * per_band
    steps = tokens // scenes // QTB
    tile = pl.BlockSpec((QTB, C), lambda s, i: (s * steps + i, 0))
    return pl.pallas_call(
        attend_back_kernel,
        name="attend_back",
        grid=(scenes, steps),
        in_specs=[
            tile,
            pl.BlockSpec((QTB, 128), lambda s, i: (s * steps + i, 0)),
            tile,
            tile,
            pl.BlockSpec((1, HEADS, QTB, keys), lambda s, i: (s, 0, i, 0)),
            pl.BlockSpec((1, keys, C), lambda s, i: (s, 0, 0)),
            pl.BlockSpec((1, C, keys), lambda s, i: (s, 0, 0)),
            pl.BlockSpec((bands, 1, per_band, C), lambda s, i: (0, s, 0, 0)),
            full((C, C)),
            full((C, C)),
            full((C, C)),
        ],
        out_specs=[
            tile,
            pl.BlockSpec((bands, 1, per_band, C), lambda s, i: (0, s, 0, 0)),
            full((C, C)),
            full((C, C)),
            full((C, C)),
            full((16, C)),
        ],
        out_shape=(
            shape_of((tokens, C), BF16),
            shape_of(rn_all.shape, BF16),
            shape_of((C, C), F32),
            shape_of((C, C), F32),
            shape_of((C, C), F32),
            shape_of((16, C), F32),
        ),
        scratch_shapes=[
            pltpu.VMEM((HEADS, keys, HD), BF16),
            pltpu.VMEM((C, keys), F32),
            pltpu.VMEM((C, keys), F32),
        ],
        compiler_params=params("attend_back"),
    )(q, inv, mixed, gmid, p, key, vt, rn_all, wk, wv, wo)


def flip(value, by):
    return value + by * (1 - 2 * value)


def remote(src, dst, send, recv, where):
    return pltpu.make_async_remote_copy(
        src_ref=src,
        dst_ref=dst,
        send_sem=send,
        recv_sem=recv,
        device_id=where,
        device_id_type=pl.DeviceIdType.MESH,
    )


def greet(places):
    barrier = pltpu.get_barrier_semaphore()
    count = 0
    for place, there in places:
        if there is None:
            pl.semaphore_signal(
                barrier, inc=1, device_id=place, device_id_type=pl.DeviceIdType.MESH
            )
            count = count + 1
        else:

            @pl.when(there)
            def _():
                pl.semaphore_signal(
                    barrier, inc=1, device_id=place, device_id_type=pl.DeviceIdType.MESH
                )

            count = count + there.astype(jnp.int32)
    pl.semaphore_wait(barrier, count)


def comm_params(name, number):
    return pltpu.CompilerParams(
        collective_id=number, has_side_effects=True, vmem_limit_bytes=ROOM[name] * 1024 * 1024
    )


class Place:
    def __init__(self):
        dp, space = lax.axis_index("dp"), lax.axis_index("space")
        self.z, self.x = dp // 2, dp % 2
        self.y, self.c = space // 2, space % 2
        self.line = lax.axis_size("dp") // 2

    def block(self, z, x, y, c):
        return ((z * 2 + x) * 2 + y) * 2 + c

    def device(self, z, x, y, c):
        return {"dp": z * 2 + x, "space": y * 2 + c}

    def spot(self, da, db, c):
        return (
            flip(self.x, da * (1 - c) + db * c),
            flip(self.y, db * (1 - c) + da * c),
        )

    def partners(self):
        ax, ay = self.spot(1, 0, self.c)
        bx, by = self.spot(0, 1, self.c)
        return (
            self.device(self.z, ax, ay, self.c),
            self.device(self.z, bx, by, self.c),
            self.device(self.z, self.x, self.y, 1 - self.c),
            self.device(self.z + 1, self.x, self.y, self.c),
            self.device(self.z - 1, self.x, self.y, self.c),
        )

    def meet(self):
        first, second, sibling, up, down = self.partners()
        greet(
            [
                (first, None),
                (second, None),
                (sibling, None),
                (up, self.z < self.line - 1),
                (down, self.z > 0),
            ]
        )


DMA = pltpu.SemaphoreType.DMA
SPAN = 208
PART = 144
BOTH = (pl.ds(0, PART), pl.ds(PART, SPAN - PART))


def compact(block):
    half = BLOCK_ROWS // 2
    tail = jnp.concatenate([block[:half, 256:], block[half:, 256:]], axis=1)
    spare = jnp.zeros((2 * SPAN - 2 * BLOCK_ROWS - half, 128), block.dtype)
    rows = jnp.concatenate([block[:, 0:128], block[:, 128:256], tail, spare], axis=0)
    return jnp.concatenate([rows[:SPAN], rows[SPAN:]], axis=1)


def restore(block):
    half = BLOCK_ROWS // 2
    rows = jnp.concatenate([block[:, 0:128], block[:, 128:256]], axis=0)
    tail = rows[2 * BLOCK_ROWS : 2 * BLOCK_ROWS + half]
    return jnp.concatenate(
        [
            rows[:BLOCK_ROWS],
            rows[BLOCK_ROWS : 2 * BLOCK_ROWS],
            jnp.concatenate([tail[:, 0:64], tail[:, 64:128]], axis=0),
        ],
        axis=1,
    )


PLANE = [(da, db) for da in range(2) for db in range(2)]


def gather_kernel(own_ref, out, own, p_z, p_a, p_b, p_c, q_z, q_a, q_b, q_c, recv):
    at = Place()
    line = at.line
    first, second, sibling, up, down = at.partners()
    own[...] = compact(own_ref[...].astype(F32)).astype(BF16)
    at.meet()
    can_up, can_down = at.z < line - 1, at.z > 0

    def index_of(z, da, db, c):
        x, y = at.spot(da, db, at.c)
        return at.block(z, x, y, c)

    def push(part, index, src, sem, where):
        remote(src, out.at[index, BOTH[part]], sem, recv.at[index, part], where).start()

    def landed(part, index):
        remote(
            out.at[index, BOTH[part]], out.at[index, BOTH[part]], p_a.at[0], recv.at[index, part], sibling
        ).wait_recv()

    def here(part, index, is_own):
        return own.at[BOTH[part]] if is_own else out.at[index, BOTH[part]]

    def along_z(part, z, k, index, src, way, sems):
        if way >= 0:

            @pl.when(can_up)
            def _():
                push(part, index, src, sems.at[0, k, z], up)

        if way <= 0:

            @pl.when(can_down)
            def _():
                push(part, index, src, sems.at[1, k, z], down)

    def first_order(z, da, db, way, is_own=False):
        index = index_of(z, da, db, at.c)
        if not is_own:
            landed(0, index)
        src = here(0, index, is_own)
        if da == 0 and db == 0:
            along_z(0, z, 0, index, src, way, p_z)
            push(0, index, src, p_a.at[z], first)
        if db == 0:
            push(0, index, src, p_b.at[da, z], second)
        push(0, index, src, p_c.at[2 * da + db, z], sibling)

    def second_order(z, da, db, way, is_own=False):
        index = index_of(z, da, db, at.c)
        if not is_own:
            landed(1, index)
        src = here(1, index, is_own)
        if way == 0:
            if da == 0 and db == 0:
                push(1, index, src, q_a, first)
            if db == 0:
                push(1, index, src, q_b.at[da], second)
        along_z(1, z, 2 * da + db, index, src, way, q_z)
        push(1, index, src, q_c.at[2 * da + db, z], sibling)

    def hop(d, order, places):
        for z in range(line):
            if z >= d:

                @pl.when(at.z == z)
                def _():
                    for da, db in places:
                        order(z - d, da, db, 1)

            if z + d < line:

                @pl.when(at.z == z)
                def _():
                    for da, db in places:
                        order(z + d, da, db, -1)

    def flat_hops(da, db):
        first_order(at.z, da, db, 0)
        for d in range(1, line):
            hop(d, lambda z, da, db, way: first_order(z, da, db, way), [(da, db)])

    second_order(at.z, 0, 0, 0, True)
    first_order(at.z, 0, 0, 0, True)
    mine = index_of(at.z, 0, 0, at.c)
    out[mine] = own[...]
    second_order(at.z, 1, 0, 0)
    hop(1, first_order, [(0, 0)])
    second_order(at.z, 0, 1, 0)
    second_order(at.z, 1, 1, 0)
    hop(2, first_order, [(0, 0)])
    hop(1, second_order, PLANE)
    hop(3, first_order, [(0, 0)])
    flat_hops(1, 0)
    hop(2, second_order, PLANE)
    flat_hops(0, 1)
    flat_hops(1, 1)
    hop(3, second_order, PLANE)
    for z in range(line):
        for da, db in PLANE:
            for part in range(2):
                landed(part, index_of(z, da, db, 1 - at.c))

    def sent(part, sem, where):
        remote(own.at[BOTH[part]], out.at[mine, BOTH[part]], sem, recv.at[mine, part], where).wait_send()

    sent(1, q_a, first)
    for z in range(line):
        for k in range(4):
            sent(0, p_c.at[k, z], sibling)
            sent(1, q_c.at[k, z], sibling)
        sent(0, p_a.at[z], first)
        for da in range(2):
            sent(0, p_b.at[da, z], second)

        @pl.when(jnp.logical_and(can_up, z <= at.z))
        def _():
            sent(0, p_z.at[0, 0, z], up)
            for k in range(4):
                sent(1, q_z.at[0, k, z], up)

        @pl.when(jnp.logical_and(can_down, z >= at.z))
        def _():
            sent(0, p_z.at[1, 0, z], down)
            for k in range(4):
                sent(1, q_z.at[1, k, z], down)

    for da in range(2):
        sent(1, q_b.at[da], second)


def gather_blocks(own):
    return pl.pallas_call(
        gather_kernel,
        name="gather",
        out_shape=shape_of((BLOCKS, SPAN, 256), BF16),
        in_specs=[VM],
        out_specs=VM,
        scratch_shapes=[
            pltpu.VMEM((SPAN, 256), BF16),
            DMA((2, 1, 4)), DMA((4,)), DMA((2, 4)), DMA((4, 4)),
            DMA((2, 4, 4)), DMA, DMA((2,)), DMA((4, 4)),
            DMA((BLOCKS, 2)),
        ],
        compiler_params=comm_params("gather", 1),
    )(own)


def scatter_kernel(
    parts, out,
    rc, acc, ra, acc2, rb, acc3, rz, sz,
    qc, qacc, qrz, qsz, qplane, qra, qacc2, qrb,
    c_out, a_out, b_out, z_out, qc_out, qz_out, qa_out, qb_out,
    c_in, a_in, b_in, z_in, qc_in, qz_in, qa_in, qb_in,
):
    at = Place()
    line = at.line
    first, second, sibling, up, down = at.partners()
    at.meet()
    slots = [(da, db, z) for da in (1, 0) for db in (1, 0) for z in range(line)]

    def add(*terms):
        if len(terms) == 2:
            return terms[0] + terms[1]
        total = terms[0].astype(F32)
        for term in terms[1:]:
            total = total + term.astype(F32)
        return total.astype(BF16)

    def source(k, c):
        da, db, z = slots[k]
        x, y = at.spot(da, db, c)
        return at.block(z, x, y, c)

    def c_copy(k):
        src = parts.at[source(k, 1 - at.c), BOTH[0]]
        return remote(src, rc.at[k], c_out.at[k], c_in.at[k], sibling)

    def qc_copy(k):
        src = parts.at[source(k, 1 - at.c), BOTH[1]]
        return remote(src, qc.at[k], qc_out.at[k], qc_in.at[k], sibling)

    def a_copy(j):
        return remote(acc.at[j], ra.at[j], a_out.at[j], a_in.at[j], first)

    def b_copy(j):
        return remote(acc2.at[j], rb.at[j], b_out.at[j], b_in.at[j], second)

    def z_copy(way, z):
        return remote(
            sz.at[way, z], rz.at[way, z], z_out.at[way, z], z_in.at[way, z], (up, down)[way]
        )

    def qz_copy(way, k, src=None):
        src = qsz.at[way, k] if src is None else src
        return remote(src, qrz.at[way, k], qz_out.at[way, k], qz_in.at[way, k], (up, down)[way])

    def qa_copy(j):
        return remote(qplane.at[j], qra.at[j], qa_out.at[j], qa_in.at[j], first)

    def qb_copy():
        return remote(qacc2.at[0], qrb, qb_out, qb_in, second)

    count = 4 * line
    for k in range(count):
        qc_copy(k).start()
        c_copy(k).start()
    for k in range(count):
        da, db, z = slots[k]
        qc_copy(k).wait_recv()
        mine = source(k, at.c)
        qacc[k] = add(parts[mine, BOTH[1]], qc[k])
        if z > 0:

            @pl.when(at.z == 0)
            def _():
                qz_copy(0, k, qacc.at[k]).start()

        if z < line - 1:

            @pl.when(at.z == line - 1)
            def _():
                qz_copy(1, k, qacc.at[k]).start()

        c_copy(k).wait_recv()
        acc[k] = add(parts[mine, BOTH[0]], rc[k])
        if da:
            a_copy(k).start()

    def q_hop(d):
        for k in range(count):
            z = slots[k][2]
            if z >= d:

                @pl.when(at.z == d)
                def _():
                    qz_copy(0, k).wait_recv()
                    if z > d:
                        qsz[0, k] = add(qacc[k], qrz[0, k])
                        qz_copy(0, k).start()

            if z <= line - 1 - d:

                @pl.when(at.z == line - 1 - d)
                def _():
                    qz_copy(1, k).wait_recv()
                    if z < line - 1 - d:
                        qsz[1, k] = add(qacc[k], qrz[1, k])
                        qz_copy(1, k).start()

    def p_hop(d):
        for z in reversed(range(d, line)):

            @pl.when(at.z == d)
            def _():
                if d > 0:
                    z_copy(0, z).wait_recv()
                if z > d:
                    sz[0, z] = add(acc3[z], rz[0, z]) if d > 0 else acc3[z]
                    z_copy(0, z).start()

        for z in range(line - d):

            @pl.when(at.z == line - 1 - d)
            def _():
                if d > 0:
                    z_copy(1, z).wait_recv()
                if z < line - 1 - d:
                    sz[1, z] = add(acc3[z], rz[1, z]) if d > 0 else acc3[z]
                    z_copy(1, z).start()

    def inflows(z):
        return [way for way, there in ((0, z > 0), (1, z < line - 1)) if there]

    for j in range(line):
        a_copy(j).wait_recv()
        acc2[j] = add(acc[2 * line + j], ra[j])
        b_copy(j).start()
    q_hop(1)
    for j in range(line, 2 * line):
        a_copy(j).wait_recv()
        acc2[j] = add(acc[2 * line + j], ra[j])
    q_hop(2)
    for z in range(line):
        b_copy(z).wait_recv()
        acc3[z] = add(acc2[line + z], rb[z])
    p_hop(0)
    q_hop(3)
    for z in range(line):

        @pl.when(at.z == z)
        def _():
            for j in range(4):
                k = j * line + z
                qplane[j] = add(qacc[k], *[qrz[way, k] for way in inflows(z)])

    qa_copy(0).start()
    qa_copy(1).start()
    p_hop(1)
    for j in range(2):
        qa_copy(j).wait_recv()
        qacc2[j] = add(qplane[2 + j], qra[j])
        if j == 0:
            qb_copy().start()
    p_hop(2)
    qb_copy().wait_recv()
    q_total = qacc2[1].astype(F32) + qrb[...].astype(F32)
    p_hop(3)
    for z in range(line):

        @pl.when(at.z == z)
        def _():
            total = acc3[z].astype(F32)
            for way in inflows(z):
                total = total + rz[way, z].astype(F32)
            out[...] = restore(jnp.concatenate([total, q_total], axis=0))

    for k in range(count):
        c_copy(k).wait_send()
        qc_copy(k).wait_send()
        z = slots[k][2]

        @pl.when(at.z < z)
        def _():
            qz_copy(0, k).wait_send()

        @pl.when(at.z > z)
        def _():
            qz_copy(1, k).wait_send()

    for j in range(2 * line):
        a_copy(j).wait_send()
    for z in range(line):
        b_copy(z).wait_send()

        @pl.when(at.z < z)
        def _():
            z_copy(0, z).wait_send()

        @pl.when(at.z > z)
        def _():
            z_copy(1, z).wait_send()

    qa_copy(0).wait_send()
    qa_copy(1).wait_send()
    qb_copy().wait_send()


def scatter_blocks(parts):
    room = lambda *n: pltpu.VMEM(n + (PART, 256), BF16)
    less = lambda *n: pltpu.VMEM(n + (SPAN - PART, 256), BF16)
    sems = lambda: [
        DMA((16,)), DMA((8,)), DMA((4,)), DMA((2, 4)), DMA((16,)), DMA((2, 16)), DMA((2,)), DMA,
    ]
    return pl.pallas_call(
        scatter_kernel,
        name="scatter",
        out_shape=shape_of((BLOCK_ROWS, C), F32),
        in_specs=[VM],
        out_specs=VM,
        scratch_shapes=[
            room(16), room(16), room(8), room(8), room(4), room(4), room(2, 4), room(2, 4),
            less(16), less(16), less(2, 16), less(2, 16), less(4), less(2), less(2), less(),
        ]
        + sems()
        + sems(),
        compiler_params=comm_params("scatter", 2),
    )(parts)


def bands_of():
    band = lax.axis_index("space")
    pair, core = band // 2, band % 2
    return band, pair * 2 + 1 - core, (1 - pair) * 2 + core


def swap_kernel(width, value, above, below, up_sem, down_sem, up_in, down_in, ready):
    band = lax.axis_index("space")
    rows = value.shape[1]
    ends = lax.axis_size("space") - 1
    down = remote(
        value.at[:, pl.ds(rows - width, width)], above, down_sem, down_in, {"space": band + 1}
    )
    up = remote(value.at[:, pl.ds(0, width)], below, up_sem, up_in, {"space": band - 1})

    @pl.when(band < ends)
    def _():
        down.start()

    @pl.when(band > 0)
    def _():
        up.start()

    def finish():
        @pl.when(band < ends)
        def _():
            down.wait_send()
            up.wait_recv()

        @pl.when(band > 0)
        def _():
            up.wait_send()
            down.wait_recv()

    return finish


def bands_meet(others):
    band = lax.axis_index("space")
    ends = lax.axis_size("space") - 1
    greet(
        [({"space": o}, None) for o in others]
        + [({"space": band + 1}, band < ends), ({"space": band - 1}, band > 0)]
    )


def share_kernel(
    rn, cot, rn_all, above, below, send, recv, own_sem, up_sem, down_sem, up_in, down_in
):
    band, sibling, across = bands_of()
    bands_meet((sibling, across))
    to_sibling = remote(rn, rn_all.at[band], send.at[0], recv.at[band], {"space": sibling})
    to_across = remote(rn, rn_all.at[band], send.at[1], recv.at[band], {"space": across})
    to_across.start()
    to_sibling.start()
    own = pltpu.make_async_copy(rn, rn_all.at[band], own_sem)
    own.start()
    finish = swap_kernel(1, cot, above, below, up_sem, down_sem, up_in, down_in, None)

    def landed(index):
        remote(rn, rn_all.at[index], send.at[0], recv.at[index], {"space": sibling}).wait_recv()

    landed(across)
    onward = remote(
        rn_all.at[across], rn_all.at[across], send.at[2], recv.at[across], {"space": sibling}
    )
    onward.start()
    landed(sibling)
    landed(across + sibling - band)
    own.wait()
    to_across.wait_send()
    to_sibling.wait_send()
    onward.wait_send()
    finish()


def share(rn, cot):
    bands = lax.axis_size("space")
    dma = pltpu.SemaphoreType.DMA
    edge = (cot.shape[0], 1) + cot.shape[2:]
    return pl.pallas_call(
        share_kernel,
        name="share",
        out_shape=(
            shape_of((bands,) + rn.shape, rn.dtype),
            shape_of(edge, cot.dtype),
            shape_of(edge, cot.dtype),
        ),
        in_specs=[VM, ANY],
        out_specs=(ANY, ANY, ANY),
        scratch_shapes=[dma((3,)), dma((bands,)), dma, dma, dma, dma, dma],
        compiler_params=comm_params("share", 3),
    )(rn, cot)


def halo_kernel(value, above, below, up_sem, down_sem, up_in, down_in):
    bands_meet(())
    swap_kernel(2, value, above, below, up_sem, down_sem, up_in, down_in, None)()


def halo(value):
    dma = pltpu.SemaphoreType.DMA
    edge = (value.shape[0], 2) + value.shape[2:]
    return pl.pallas_call(
        halo_kernel,
        name="halo",
        out_shape=(shape_of(edge, value.dtype), shape_of(edge, value.dtype)),
        in_specs=[ANY],
        out_specs=(ANY, ANY),
        scratch_shapes=[dma, dma, dma, dma],
        compiler_params=comm_params("halo", 4),
    )(value)


CHUNKS = 4


def tail_kernel(
    parts, x_ref, dq_ref, red_ref, vec, wq, wr,
    gx_out, gwq_out, gwr_out, gvec_out,
    rc, acc, rb, grn_scr, gn_scr, unit_scr, rstd_scr, pieces_scr, scr, gscr,
    c_sem, c_in, b_sem, b_in,
):
    band, sibling, across = bands_of()
    greet([({"space": sibling}, None), ({"space": across}, None)])
    far = across + sibling - band
    size = rc.shape[1] // CHUNKS
    chunks = [pl.ds(j * size, size) for j in range(CHUNKS)]

    def copy_first(j):
        src, dst = parts.at[far, chunks[j]], rc.at[0, chunks[j]]
        return remote(src, dst, c_sem.at[0, j], c_in.at[0, j], {"space": sibling})

    def copy_second(j):
        src, dst = parts.at[sibling, chunks[j]], rc.at[1, chunks[j]]
        return remote(src, dst, c_sem.at[1, j], c_in.at[1, j], {"space": sibling})

    def copy_onward(j):
        src, dst = acc.at[chunks[j]], rb.at[chunks[j]]
        return remote(src, dst, b_sem.at[j], b_in.at[j], {"space": across})

    for j in range(CHUNKS):
        copy_first(j).start()
    for j in range(CHUNKS):
        copy_second(j).start()
    tiles = x_ref.shape[0] // TILE
    gain = vec[V_GAIN1 : V_GAIN1 + 1, :]
    for ref in (gwq_out, gwr_out, gvec_out):
        ref[...] = jnp.zeros_like(ref)
    for j in range(CHUNKS):
        copy_first(j).wait_recv()
        acc[chunks[j], :] = parts[across, chunks[j]] + rc[0, chunks[j]]
        copy_onward(j).start()

    def before(i, carry):
        rows = pl.ds(pl.multiple_of(i * TILE, TILE), TILE)
        unit, rstd = norm_parts(x_ref[rows, :].astype(F32))
        unit_scr[rows, :] = unit
        rstd_scr[rows, :] = jnp.broadcast_to(rstd, (TILE, 128))
        normed = (unit * gain + vec[V_SHIFT1 : V_SHIFT1 + 1, :]).astype(BF16)
        split_tiles(scr, normed.astype(F32))
        pieces = patch_pieces(scr)
        spot = pl.ds(pl.multiple_of(i * RTILE, RTILE), RTILE)
        for k in range(4):
            pieces_scr[k, spot, :] = pieces[k].astype(BF16)
        dq = dq_ref[rows, :]
        gwq_out[...] += mm_tn(normed, dq)
        gn_scr[rows, :] = mm_nt(dq, wq[...])
        gvec_out[0:1, :] += row_sum(dq.astype(F32))
        return carry

    lax.fori_loop(0, tiles, before, 0)
    def after(i, carry):
        rows = pl.ds(pl.multiple_of(i * TILE, TILE), TILE)
        spot = pl.ds(pl.multiple_of(i * RTILE, RTILE), RTILE)
        runit, rrstd = norm_parts(red_ref[spot, :])
        grn = grn_scr[spot, :]
        gred = norm_back(grn, runit, rrstd, vec[V_RGAIN : V_RGAIN + 1, :]).astype(BF16)
        back = {}
        for k in range(4):
            at = slice(k * C, (k + 1) * C)
            gwr_out[at, :] += mm_tn(pieces_scr[k, spot, :], gred)
            back[k] = mm_nt(gred, wr[at, :]).reshape(TILE // (2 * W), 1, W // 2, C)
        for b in range(2):
            cols = jnp.concatenate([back[b], back[2 + b]], axis=1).reshape(TILE // 2, C)
            places = pl.ds(b, TILE // 2, stride=2)
            gscr[0, places, :] = cols[:, 0:128]
            gscr[1, places, :] = cols[:, 128:256]
            gscr[2, places, :] = jnp.concatenate(
                [cols[:, 256:320], jnp.zeros((TILE // 2, 64), F32)], axis=1
            )
        placed = jnp.concatenate([gscr[0], gscr[1], gscr[2][:, 0:64]], axis=1)
        gnormed = gn_scr[rows, :] + placed
        unit = unit_scr[rows, :]
        gx_out[rows, :] = norm_back(gnormed, unit, rstd_scr[rows, 0:1], gain)
        gvec_out[1:2, :] += row_sum(gred.astype(F32))
        gvec_out[2:3, :] += row_sum(grn * runit)
        gvec_out[3:4, :] += row_sum(grn)
        gvec_out[4:5, :] += row_sum(gnormed * unit)
        gvec_out[5:6, :] += row_sum(gnormed)
        return carry

    for j in range(CHUNKS):
        copy_second(j).wait_recv()
        copy_onward(j).wait_recv()
        own = parts[band, chunks[j]].astype(F32)
        grn_scr[chunks[j], :] = own + (
            rc[1, chunks[j]].astype(F32) + rb[chunks[j], :].astype(F32)
        )
        lax.fori_loop(j * tiles // CHUNKS, (j + 1) * tiles // CHUNKS, after, 0)
    for j in range(CHUNKS):
        copy_first(j).wait_send()
        copy_second(j).wait_send()
        copy_onward(j).wait_send()


def tail(parts, x, dq, red, vec, wq, wr):
    one = parts.shape[1:]
    tokens = x.shape[0]
    return pl.pallas_call(
        tail_kernel,
        name="tail",
        out_shape=(
            shape_of((tokens, C), F32),
            shape_of((C, C), F32),
            shape_of((4 * C, C), F32),
            shape_of((8, C), F32),
        ),
        in_specs=[VM] * 7,
        out_specs=(VM,) * 4,
        scratch_shapes=[
            pltpu.VMEM((2,) + one, BF16),
            pltpu.VMEM(one, BF16),
            pltpu.VMEM(one, BF16),
            pltpu.VMEM(one, F32),
            pltpu.VMEM((tokens, C), F32),
            pltpu.VMEM((tokens, C), F32),
            pltpu.VMEM((tokens, 128), F32),
            pltpu.VMEM((4,) + one, BF16),
            pltpu.VMEM((3, TILE, 128), F32),
            pltpu.VMEM((3, TILE, 128), F32),
            DMA((2, CHUNKS)),
            DMA((2, CHUNKS)),
            DMA((CHUNKS,)),
            DMA((CHUNKS,)),
        ],
        compiler_params=comm_params("tail", 5),
    )(parts, x, dq, red, vec, wq, wr)


def blocks_fit(size):
    return (
        lax.axis_size("dp") == 8 and lax.axis_size("space") == 4 and size == BLOCK_ROWS * C
    )


def gather_flat(shard):
    if blocks_fit(shard.shape[0]):
        return gather_blocks(shard.reshape(BLOCK_ROWS, C))
    flat = lax.all_gather(shard, ("dp", "space"), axis=0, tiled=True)
    want = ROWS * C
    flat = flat[:want] if flat.shape[0] >= want else jnp.pad(flat, (0, want - flat.shape[0]))
    blocks = jax.vmap(compact)(flat.reshape(BLOCKS, BLOCK_ROWS, C))
    return blocks


def scatter_grads(blocks, size):
    if blocks_fit(size):
        return scatter_blocks(blocks).reshape(size)
    flat = jax.vmap(restore)(blocks).reshape(-1)
    want = size * lax.axis_size("dp") * lax.axis_size("space")
    flat = flat[:want] if flat.shape[0] >= want else jnp.pad(flat, (0, want - flat.shape[0]))
    own = lax.psum_scatter(flat, ("dp", "space"), scatter_dimension=0, tiled=True)
    return own.astype(F32)


def on_device(scenes, shard, cotangent):
    count, rows, breadth = scenes.shape[0], scenes.shape[1], scenes.shape[2]
    tokens = count * rows * breadth
    bands = lax.axis_size("space")
    per_band = rows * breadth // 4
    band = lax.axis_index("space")
    edge = jnp.stack([band > 0, band < bands - 1]).astype(F32)
    wq, wr, wk, wv, wo, we, ws, vec, hid = unpack(gather_flat(shard))
    x = scenes.reshape(tokens, C)
    q, red, rn = front(x, vec, wq, wr)
    rn_all, cot_top, cot_low = share(rn, cotangent)
    rn_all = rn_all.reshape(bands, count, per_band, C)
    mixed, inv, mid, n2, p, key, vt = attend(x, q, rn_all, vec, wk, wv, wo)
    n2 = n2.reshape(scenes.shape)
    n2_top, n2_low = halo(n2)
    y, gmid, gwe, gws, ghid, gvec2 = mix(
        n2, n2_top, n2_low, cotangent, cot_top, cot_low, mid, edge, vec, hid, we, ws
    )
    dq, grn_all, gwk, gwv, gwo, gvec1 = attend_back(
        q, inv, mixed, gmid, p, key, vt, rn_all, wk, wv, wo
    )
    parts = grn_all.reshape(bands, count * per_band, C)
    gnorm, gwq, gwr, gvec0 = tail(parts, x, dq, red, vec, wq, wr)
    blocks, gx = pack(
        gwq, gwr, gwk, gwv, gwo, gwe, gws, gvec0, gvec1, gvec2, ghid, gmid, gnorm
    )
    grads = scatter_grads(blocks, shard.shape[0])
    return y.reshape(scenes.shape), gx.reshape(scenes.shape), grads


def solution(mesh):
    band = P("dp", "space", None, None)
    flat = P(("dp", "space"))
    return jax.shard_map(
        on_device,
        mesh=mesh,
        in_specs=(band, flat, band),
        out_specs=(band, band, flat),
        check_vma=False,
    )
```

```python
import functools
import math

import jax
import jax.numpy as jnp
from jax import lax
from jax.experimental import pallas as pl
from jax.experimental.pallas import tpu as pltpu
from jax.sharding import PartitionSpec as P

C = 320
HEADS = 5
HD = 64
FF = 1280
W = 64
EPSILON = 1e-06
F32 = jnp.float32
BF16 = jnp.bfloat16

ROWS = 5184
USED_ROWS = 5175
BLOCKS = 32
BLOCK_ROWS = ROWS // BLOCKS
R_QUERY = 0
R_REDUCE = 321
R_KEYVAL = 1604
R_OUTPUT = 2245
R_EXPAND = 2570
R_HIDDEN = 3850
R_SHRINK = 3894
VECTOR_ROWS = (320, 1601, 1602, 1603, 2244, 2565, 2566, 2567, 2568, 2569, 5174)
(
    V_QUERY,
    V_REDUCE,
    V_RGAIN,
    V_RSHIFT,
    V_VALUE,
    V_OUTPUT,
    V_GAIN1,
    V_SHIFT1,
    V_GAIN2,
    V_SHIFT2,
    V_SHRINK,
) = range(11)
HIDDEN_ROWS = 11

ROOM = dict(
    unpack=30, front=10, attend=34, mix=32, attend_back=26, tail=15, pack=32,
    gather=8, scatter=18, halo=2,
)


def params(name):
    return pltpu.CompilerParams(vmem_limit_bytes=ROOM[name] * 1024 * 1024)


ANY = pl.BlockSpec(memory_space=pl.ANY)
VM = pl.BlockSpec(memory_space=pltpu.VMEM)


def shape_of(dims, kind):
    return jax.ShapeDtypeStruct(dims, kind)


def mm(left, right):
    return jnp.dot(left, right, preferred_element_type=F32)


def mm_tn(left, right):
    return lax.dot_general(left, right, (((0,), (0,)), ((), ())), preferred_element_type=F32)


def mm_nt(left, right):
    return lax.dot_general(left, right, (((1,), (1,)), ((), ())), preferred_element_type=F32)


def mm_tt(left, right):
    return lax.dot_general(left, right, (((0,), (1,)), ((), ())), preferred_element_type=F32)


def norm_parts(values):
    center = values - jnp.mean(values, axis=-1, keepdims=True)
    rstd = lax.rsqrt(jnp.mean(center * center, axis=-1, keepdims=True) + EPSILON)
    return center * rstd, rstd


def norm_back(grad, unit, rstd, gain):
    scaled = grad * gain
    first = jnp.mean(scaled, axis=-1, keepdims=True)
    second = jnp.mean(scaled * unit, axis=-1, keepdims=True)
    return rstd * (scaled - first - unit * second)


def row_sum(values):
    return jnp.sum(values, axis=0, keepdims=True)


def full(dims):
    return pl.BlockSpec(dims, lambda *_: (0,) * len(dims))


def unpack_kernel(g_ref, wq, wr, wk, wv, wo, we, ws, vec, hid, rows, tiles):
    for i in range(BLOCKS):
        at = i * BLOCK_ROWS
        block = restore(g_ref[i].astype(F32))
        rows[at : at + BLOCK_ROWS, :] = block
        tiles[0, at : at + BLOCK_ROWS, :] = block[:, 0:128]
        tiles[1, at : at + BLOCK_ROWS, :] = block[:, 128:256]
        tiles[2, at : at + BLOCK_ROWS, 0:64] = block[:, 256:320]

    def strided(start, count, step):
        parts = [tiles[t, pl.ds(start, count, stride=step), :] for t in range(3)]
        return jnp.concatenate([parts[0], parts[1], parts[2][:, 0:64]], axis=1)

    wq[...] = rows[R_QUERY : R_QUERY + C, :].astype(BF16)
    wr[...] = rows[R_REDUCE : R_REDUCE + 4 * C, :].astype(BF16)
    wk[...] = strided(R_KEYVAL, C, 2).astype(BF16)
    wv[...] = strided(R_KEYVAL + 1, C, 2).astype(BF16)
    wo[...] = rows[R_OUTPUT : R_OUTPUT + C, :].astype(BF16)
    ws[...] = rows[R_SHRINK : R_SHRINK + FF, :].astype(BF16)
    we[...] = jnp.concatenate([strided(R_EXPAND + j, C, 4) for j in range(4)], axis=1).astype(BF16)
    hid[0:HIDDEN_ROWS, :] = jnp.concatenate(
        [strided(R_HIDDEN + j, HIDDEN_ROWS, 4) for j in range(4)], axis=1
    )
    for i, row in enumerate(VECTOR_ROWS):
        vec[i : i + 1, :] = rows[row : row + 1, :]


def unpack(blocks):
    return pl.pallas_call(
        unpack_kernel,
        name="unpack",
        out_shape=(
            shape_of((C, C), BF16),
            shape_of((4 * C, C), BF16),
            shape_of((C, C), BF16),
            shape_of((C, C), BF16),
            shape_of((C, C), BF16),
            shape_of((C, FF), BF16),
            shape_of((FF, C), BF16),
            shape_of((16, C), F32),
            shape_of((16, FF), F32),
        ),
        scratch_shapes=[pltpu.VMEM((ROWS, C), F32), pltpu.VMEM((3, ROWS, 128), F32)],
        compiler_params=params("unpack"),
    )(blocks)


def pack_kernel(
    gwq, gwr, gwk, gwv, gwo, gwe, gws, gvec0, gvec1, gvec2, ghid, gmid, gnorm, out, gx, tiles
):
    gx[...] = gmid[...] + gnorm[...]

    def put(start, value):
        count = value.shape[0]
        tiles[0, start : start + count, :] = value[:, 0:128]
        tiles[1, start : start + count, :] = value[:, 128:256]
        tiles[2, start : start + count, 0:64] = value[:, 256:320]

    def put_strided(start, step, value):
        count = value.shape[0]
        tiles[0, pl.ds(start, count, stride=step), :] = value[:, 0:128]
        tiles[1, pl.ds(start, count, stride=step), :] = value[:, 128:256]
        tail = jnp.concatenate([value[:, 256:320], jnp.zeros((count, 64), F32)], axis=1)
        tiles[2, pl.ds(start, count, stride=step), :] = tail

    put(R_QUERY, gwq[...])
    put(R_REDUCE, gwr[...])
    put_strided(R_KEYVAL, 2, gwk[...].T)
    put_strided(R_KEYVAL + 1, 2, gwv[...].T)
    put(R_OUTPUT, gwo[...])
    put(R_SHRINK, gws[...].T)
    for j in range(4):
        put_strided(R_EXPAND + j, 4, gwe[:, C * j : C * j + C])
        put_strided(R_HIDDEN + j, 4, ghid[0:HIDDEN_ROWS, C * j : C * j + C])
    for source, names in (
        (gvec0, (V_QUERY, V_REDUCE, V_RGAIN, V_RSHIFT, V_GAIN1, V_SHIFT1)),
        (gvec2, (V_GAIN2, V_SHIFT2, V_SHRINK)),
    ):
        for i, name in enumerate(names):
            put(VECTOR_ROWS[name], source[i : i + 1, :])
    put(VECTOR_ROWS[V_VALUE], gvec1[0:1, :])
    put(VECTOR_ROWS[V_OUTPUT], gvec1[8:9, :])
    put(USED_ROWS, jnp.zeros((ROWS - USED_ROWS, C), F32))
    half = BLOCK_ROWS // 2
    spare = jnp.zeros((2 * SPAN - 2 * BLOCK_ROWS - half, 128), F32)
    for i in range(BLOCKS):
        at = i * BLOCK_ROWS
        tail = jnp.concatenate(
            [
                tiles[2, at : at + half, 0:64],
                tiles[2, at + half : at + BLOCK_ROWS, 0:64],
            ],
            axis=1,
        )
        rows = [tiles[0, at : at + BLOCK_ROWS, :], tiles[1, at : at + BLOCK_ROWS, :], tail, spare]
        rows = jnp.concatenate(rows, axis=0)
        out[i] = jnp.concatenate([rows[:SPAN], rows[SPAN:]], axis=1).astype(BF16)


def pack(*pieces):
    return pl.pallas_call(
        pack_kernel,
        name="pack",
        out_shape=(shape_of((BLOCKS, SPAN, 256), BF16), shape_of(pieces[-1].shape, F32)),
        scratch_shapes=[pltpu.VMEM((3, ROWS, 128), F32)],
        compiler_params=params("pack"),
    )(*pieces)


TILE = 8 * W
RTILE = TILE // 4


def split_tiles(scr, value):
    scr[0, :, :] = value[:, 0:128]
    scr[1, :, :] = value[:, 128:256]
    scr[2, :, 0:64] = value[:, 256:320]


def patch_pieces(scr):
    pieces = {}
    for b in range(2):
        parts = [scr[t, pl.ds(b, TILE // 2, stride=2), :] for t in range(3)]
        cols = jnp.concatenate([parts[0], parts[1], parts[2][:, 0:64]], axis=1)
        cols = cols.reshape(TILE // (2 * W), 2, W // 2, C)
        for a in range(2):
            pieces[2 * a + b] = cols[:, a].reshape(RTILE, C)
    return pieces


QT = 512


def attend_kernel(
    x_ref, q_ref, rn_ref, vec, wk, wv, wo,
    mixed_out, inv_out, mid_out, n2_out, p_out, key_out, vt_out, kt, vones,
):
    keys = rn_ref.shape[0] * rn_ref.shape[2]

    @pl.when(pl.program_id(1) == 0)
    def _():
        rn = rn_ref[:, 0].reshape(keys, C)
        key = mm(rn, wk[...]).astype(BF16)
        value = (mm(rn, wv[...]) + vec[V_VALUE : V_VALUE + 1, :]).astype(BF16)
        key_out[0] = key
        vt_out[0] = value.T
        kt[...] = key.T
        for h in range(HEADS):
            vones[h, :, 0:HD] = value[:, h * HD : (h + 1) * HD]
            vones[h, :, HD:] = jnp.ones((keys, HD), BF16)

    lane = lax.broadcasted_iota(jnp.int32, (QT, 128), 1)
    invs = jnp.zeros((QT, 128), F32)
    outs = []
    for h in range(HEADS):
        scores = mm(q_ref[:, h * HD : (h + 1) * HD], kt[h * HD : (h + 1) * HD, :])
        top = jnp.max(scores, axis=-1, keepdims=True)
        probs = jnp.exp(scores - top).astype(BF16)
        p_out[0, h] = probs
        both = mm(probs, vones[h])
        inv = 1.0 / both[:, HD:]
        outs.append(both[:, 0:HD] * inv)
        invs = jnp.where(lane == h, inv[:, 0:1], invs)
    inv_out[...] = invs
    mixed = jnp.concatenate(outs, axis=1).astype(BF16)
    mixed_out[...] = mixed
    middle = x_ref[...].astype(F32) + mm(mixed, wo[...]) + vec[V_OUTPUT : V_OUTPUT + 1, :]
    mid_out[...] = middle
    unit, _ = norm_parts(middle)
    n2_out[...] = (unit * vec[V_GAIN2 : V_GAIN2 + 1, :] + vec[V_SHIFT2 : V_SHIFT2 + 1, :]).astype(
        BF16
    )


def attend(x, q, rn_all, vec, wk, wv, wo):
    tokens = x.shape[0]
    bands, scenes, per_band, _ = rn_all.shape
    keys = bands * per_band
    per_scene = tokens // scenes
    steps = per_scene // QT
    tile = pl.BlockSpec((QT, C), lambda s, i: (s * steps + i, 0))
    return pl.pallas_call(
        attend_kernel,
        name="attend",
        grid=(scenes, steps),
        in_specs=[
            tile,
            tile,
            pl.BlockSpec((bands, 1, per_band, C), lambda s, i: (0, s, 0, 0)),
            full((16, C)),
            full((C, C)),
            full((C, C)),
            full((C, C)),
        ],
        out_specs=[
            tile,
            pl.BlockSpec((QT, 128), lambda s, i: (s * steps + i, 0)),
            tile,
            tile,
            pl.BlockSpec((1, HEADS, QT, keys), lambda s, i: (s, 0, i, 0)),
            pl.BlockSpec((1, keys, C), lambda s, i: (s, 0, 0)),
            pl.BlockSpec((1, C, keys), lambda s, i: (s, 0, 0)),
        ],
        out_shape=(
            shape_of((tokens, C), BF16),
            shape_of((tokens, 128), F32),
            shape_of((tokens, C), F32),
            shape_of((tokens, C), BF16),
            shape_of((scenes, HEADS, per_scene, keys), BF16),
            shape_of((scenes, keys, C), BF16),
            shape_of((scenes, C, keys), BF16),
        ),
        scratch_shapes=[pltpu.VMEM((C, keys), BF16), pltpu.VMEM((HEADS, keys, 2 * HD), BF16)],
        compiler_params=params("attend"),
    )(x, q, rn_all, vec, wk, wv, wo)


CH = 256
AHEAD = 2


SHRINK_IN = math.sqrt(0.5 * math.log2(math.e))
SLOPE = 1.0 / (math.sqrt(2.0 * math.pi) * SHRINK_IN)
ACT_SCALE = SLOPE / SHRINK_IN
ERF_RATE = 0.3275911 * math.sqrt(0.5) / SHRINK_IN
ERF_TERMS = [
    0.5 * k / SLOPE
    for k in (0.254829592, -0.284496736, 1.421413741, -1.453152027, 1.061405429)
]


def gelu_parts(u):
    size = jnp.abs(u)
    t = 1.0 / (1.0 + ERF_RATE * size)
    poly = ERF_TERMS[4]
    for term in ERF_TERMS[3::-1]:
        poly = term + t * poly
    bell = jnp.exp2(-(u * u))
    tail = (t * poly) * bell
    return jnp.where(u >= 0, 1.0 / SLOPE - tail, tail), bell


def mix_kernel(
    n2, n2_top, n2_low, cot, cot_top, cot_low, mid, edge, vec, hid, we, ws,
    y_out, gmid_out, gwe_out, gws_out, ghid_out, gvec_out,
    nx, cx, nt, ct, wx, wt, e_scr, e_low, ga_scr, gc_scr, act_scr, ge_scr, branch, gn2,
):
    scenes, rows = n2.shape[0], n2.shape[1]
    ext = (rows + 4) * W
    gext = (rows + 2) * W
    own = rows * W
    top, low = edge[0], edge[1]

    def inside(value, there):
        return jnp.where(there > 0, value.astype(F32), 0.0).astype(BF16)

    for s in range(scenes):
        mine = n2[s].reshape(own, C)
        nx[s * ext : s * ext + 2 * W, 0:C] = inside(n2_top[s].reshape(2 * W, C), top)
        nx[s * ext + 2 * W : s * ext + 2 * W + own, 0:C] = mine
        nx[s * ext + 2 * W + own : (s + 1) * ext, 0:C] = inside(n2_low[s].reshape(2 * W, C), low)
        nx[s * ext : (s + 1) * ext, C:] = jnp.ones((ext, 64), BF16)
        for there, start in ((top, 0), (low, 2 * W + own)):

            @pl.when(there == 0)
            def _():
                spot = slice(s * ext + start, s * ext + start + 2 * W)
                nx[spot, C:] = jnp.zeros((2 * W, 64), BF16)

        nt[0:C, s * own : (s + 1) * own] = mine.T
        mine = cot[s].reshape(own, C)
        cx[s * gext : s * gext + W, :] = inside(cot_top[s].reshape(W, C), top)
        cx[s * gext + W : s * gext + W + own, :] = mine
        cx[s * gext + W + own : (s + 1) * gext, :] = inside(cot_low[s].reshape(W, C), low)
        ct[:, s * own : (s + 1) * own] = mine.T
    wx[0:C, :] = we[...]
    wx[C : C + 16, :] = jnp.concatenate(
        [hid[0:1, :], jnp.zeros((15, FF), F32)], axis=0
    ).astype(BF16)
    wx[C + 16 :, :] = jnp.zeros((48, FF), BF16)
    wt[...] = ws[...].T
    nt[C:, :] = jnp.ones((16, scenes * own), BF16)
    branch[...] = jnp.zeros_like(branch)
    gn2[...] = jnp.zeros_like(gn2)

    def chunk(step, carry):
        cols = pl.ds(pl.multiple_of(step * CH, CH), CH)
        wcol = we[:, cols]
        wrow = ws[cols, :]
        wx_col = wx[:, cols]
        wt_col = wt[:, cols]

        def expand(at, size):
            part = mm(nx[pl.ds(at, size), :], wx_col).astype(BF16)
            e_low[pl.ds(at, size), :] = part
            e_scr[pl.ds(at, size), :] = part.astype(F32)

        def activ_grad(at, size):
            ga_scr[pl.ds(at, size), :] = mm(cx[pl.ds(at, size), :], wt_col)

        col = lax.broadcasted_iota(jnp.int32, (8, CH), 0)
        first, last = col == 0, col == 7

        def right(value):
            moved = pltpu.roll(value, 1, axis=0)
            return jnp.concatenate([jnp.where(first, 0.0, moved[0:8]), moved[8:]], axis=0)

        def left(value):
            moved = pltpu.roll(value, W - 1, axis=0)
            return jnp.concatenate([moved[: W - 8], jnp.where(last, 0.0, moved[W - 8 :])], axis=0)

        def fold(value):
            value = value[0:32] + value[32:64]
            value = value[0:16] + value[16:32]
            return (value[0:8] + value[8:16]).astype(F32)

        taps = [hid[1 + k : 2 + k, cols] * SHRINK_IN for k in range(9)]
        low_taps = [hid[1 + k : 2 + k, cols].astype(BF16) for k in range(9)]
        conv_bias = hid[10:11, cols] * SHRINK_IN

        for s in range(scenes):

            def forward_row(r):
                at = pl.multiple_of(s * ext + r * W, W)
                lines = [e_scr[pl.ds(at + a * W, W), :] for a in range(3)]
                sums = [
                    lines[0] * taps[b] + lines[1] * taps[3 + b] + lines[2] * taps[6 + b]
                    for b in range(3)
                ]
                u = conv_bias + right(sums[0]) + sums[1] + left(sums[2])
                cdf, bell = gelu_parts(u)
                gat = pl.multiple_of(s * gext + r * W, W)
                gc = ga_scr[pl.ds(gat, W), :] * (cdf + u * bell)
                act_scr[pl.ds(gat, W), :] = (u * cdf).astype(BF16)
                gc_scr[0, pl.ds(gat, W), :] = left(gc).astype(BF16)
                gc_scr[1, pl.ds(gat, W), :] = gc.astype(BF16)
                gc_scr[2, pl.ds(gat, W), :] = right(gc).astype(BF16)

            def forward(i, carry):
                r = i * AHEAD
                for j in range(AHEAD):
                    forward_row(r + j)
                expand(pl.multiple_of(s * ext + (r + AHEAD + 2) * W, W), AHEAD * W)
                activ_grad(pl.multiple_of(s * gext + (r + AHEAD) * W, W), AHEAD * W)
                return carry

            expand(s * ext, (AHEAD + 2) * W)
            activ_grad(s * gext, AHEAD * W)
            lax.fori_loop(0, (rows + 2) // AHEAD, forward, 0)

        def backward(s, r, carry):
            line = e_low[pl.ds(pl.multiple_of(s * ext + (r + 2) * W, W), W), :]
            grads = list(carry)
            total = None
            for a in range(3):
                gat = pl.multiple_of(s * gext + (r + 2 - a) * W, W)
                for b in range(3):
                    g = gc_scr[b, pl.ds(gat, W), :]
                    term = g * low_taps[3 * a + b]
                    total = term if total is None else total + term
                    grads[3 * a + b] = grads[3 * a + b] + fold(g * line)
                    if a == 1 and b == 1:
                        grads[9] = grads[9] + fold(g)
            ge_scr[pl.ds(pl.multiple_of(s * own + r * W, W), W), :] = total
            return tuple(grads)

        sums = tuple(jnp.zeros((8, CH), F32) for _ in range(10))
        for s in range(scenes):
            sums = lax.fori_loop(0, rows, functools.partial(backward, s), sums)
        for k in range(10):
            ghid_out[1 + k : 2 + k, cols] = row_sum(sums[k]) * SLOPE

        ge = ge_scr[...]
        grads = mm(nt[...], ge)
        gwe_out[:, cols] = grads[0:C, :] * SLOPE
        ghid_out[0:1, cols] = grads[C : C + 1, :] * SLOPE
        gn2[...] += mm_nt(ge, wcol)
        gws = None
        for s in range(scenes):
            at = slice(s * own, (s + 1) * own)
            act = act_scr[s * gext + W : s * gext + W + own, :]
            branch[at, :] += mm(act, wrow)
            term = mm(ct[:, at], act)
            gws = term if gws is None else gws + term
        gws_out[:, cols] = gws * ACT_SCALE
        return carry

    lax.fori_loop(0, FF // CH, chunk, 0)

    size = 4 * W
    per = own // size
    gain = vec[V_GAIN2 : V_GAIN2 + 1, :]

    def finish(i, carry):
        at = pl.multiple_of(i * size, size)
        s = i // per
        line = (i % per) * 4
        middle = mid[pl.ds(at, size), :]
        y_out[pl.ds(at, size), :] = (
            middle + branch[pl.ds(at, size), :] * ACT_SCALE + vec[V_SHRINK : V_SHRINK + 1, :]
        ).astype(BF16)
        grad = gn2[pl.ds(at, size), :] * SLOPE
        unit, rstd = norm_parts(middle)
        direct = cot[s, pl.ds(line, 4)].reshape(size, C).astype(F32)
        gmid_out[pl.ds(at, size), :] = direct + norm_back(grad, unit, rstd, gain)
        return (
            carry[0] + row_sum(grad * unit),
            carry[1] + row_sum(grad),
            carry[2] + row_sum(direct),
        )

    zero = jnp.zeros((1, C), F32)
    sums = lax.fori_loop(0, scenes * per, finish, (zero, zero, zero))
    for i in range(3):
        gvec_out[i : i + 1, :] = sums[i]


def mix(n2, n2_top, n2_low, cot, cot_top, cot_low, mid, edge, vec, hid, we, ws):
    scenes, rows = n2.shape[0], n2.shape[1]
    tokens = scenes * rows * W
    ext = scenes * (rows + 4) * W
    gext = scenes * (rows + 2) * W
    return pl.pallas_call(
        mix_kernel,
        name="mix",
        in_specs=[VM] * 7 + [pl.BlockSpec(memory_space=pltpu.SMEM)] + [VM] * 4,
        out_specs=[VM] * 6,
        out_shape=(
            shape_of((tokens, C), BF16),
            shape_of((tokens, C), F32),
            shape_of((C, FF), F32),
            shape_of((C, FF), F32),
            shape_of((16, FF), F32),
            shape_of((8, C), F32),
        ),
        scratch_shapes=[
            pltpu.VMEM((ext + AHEAD * W, C + 64), BF16),
            pltpu.VMEM((gext + AHEAD * W, C), BF16),
            pltpu.VMEM((C + 16, tokens), BF16),
            pltpu.VMEM((C, tokens), BF16),
            pltpu.VMEM((C + 64, FF), BF16),
            pltpu.VMEM((C, FF), BF16),
            pltpu.VMEM((ext + AHEAD * W, CH), F32),
            pltpu.VMEM((ext + AHEAD * W, CH), BF16),
            pltpu.VMEM((gext + AHEAD * W, CH), F32),
            pltpu.VMEM((3, gext, CH), BF16),
            pltpu.VMEM((gext, CH), BF16),
            pltpu.VMEM((tokens, CH), BF16),
            pltpu.VMEM((tokens, C), F32),
            pltpu.VMEM((tokens, C), F32),
        ],
        compiler_params=params("mix"),
    )(n2, n2_top, n2_low, cot, cot_top, cot_low, mid, edge, vec, hid, we, ws)


QTB = 256


def attend_back_kernel(
    q_ref, inv_ref, mixed_ref, gmid_ref, p_ref, key_ref, vt_ref, rn_ref, wk, wv, wo,
    dq_out, grn_out, gwk_out, gwv_out, gwo_out, gvec_out, kh, dkt, dvt,
):
    scene, step = pl.program_id(0), pl.program_id(1)
    keys = rn_ref.shape[0] * rn_ref.shape[2]

    @pl.when(jnp.logical_and(scene == 0, step == 0))
    def _():
        for ref in (gwk_out, gwv_out, gwo_out, gvec_out):
            ref[...] = jnp.zeros_like(ref)

    @pl.when(step == 0)
    def _():
        for h in range(HEADS):
            kh[h] = key_ref[0, :, h * HD : (h + 1) * HD]
        dkt[...] = jnp.zeros_like(dkt)
        dvt[...] = jnp.zeros_like(dvt)

    gatt = gmid_ref[...].astype(BF16)
    gvec_out[8:9, :] += row_sum(gatt.astype(F32))
    mixed = mixed_ref[...]
    gwo_out[...] += mm_tn(mixed, gatt)
    inv = jnp.concatenate(
        [jnp.broadcast_to(inv_ref[:, h : h + 1], (QTB, HD)) for h in range(HEADS)], axis=1
    )
    scaled = (mm_nt(gatt, wo[...]) * inv).astype(BF16)
    prod = scaled.astype(F32) * mixed.astype(F32)
    q_t = q_ref[...].T
    g_t = scaled.T
    dqs = []
    for h in range(HEADS):
        cols = slice(h * HD, (h + 1) * HD)
        inner = jnp.sum(prod[:, cols], axis=-1, keepdims=True)
        probs = p_ref[0, h]
        gprobs = mm(scaled[:, cols], vt_ref[0, cols, :])
        gscores = (probs.astype(F32) * (gprobs - inner)).astype(BF16)
        dqs.append(mm(gscores, kh[h]))
        dkt[cols, :] += mm(q_t[cols, :], gscores)
        dvt[cols, :] += mm(g_t[cols, :], probs)
    dq_out[...] = (jnp.concatenate(dqs, axis=1) * (1.0 / math.sqrt(HD))).astype(BF16)

    @pl.when(step == pl.num_programs(1) - 1)
    def _():
        rn = rn_ref[:, 0].reshape(keys, C)
        dk = dkt[...].astype(BF16)
        dv = dvt[...].astype(BF16)
        gvec_out[0:8, :] += mm_nt(jnp.ones((8, keys), BF16), dv)
        gwk_out[...] += mm(dk, rn)
        gwv_out[...] += mm(dv, rn)
        grn = (mm(wk[...], dk) + mm(wv[...], dv)).astype(BF16)
        grn_out[...] = grn.T.reshape(grn_out.shape)


def attend_back(q, inv, mixed, gmid, p, key, vt, rn_all, wk, wv, wo):
    tokens = q.shape[0]
    bands, scenes, per_band, _ = rn_all.shape
    keys = bands * per_band
    steps = tokens // scenes // QTB
    tile = pl.BlockSpec((QTB, C), lambda s, i: (s * steps + i, 0))
    return pl.pallas_call(
        attend_back_kernel,
        name="attend_back",
        grid=(scenes, steps),
        in_specs=[
            tile,
            pl.BlockSpec((QTB, 128), lambda s, i: (s * steps + i, 0)),
            tile,
            tile,
            pl.BlockSpec((1, HEADS, QTB, keys), lambda s, i: (s, 0, i, 0)),
            pl.BlockSpec((1, keys, C), lambda s, i: (s, 0, 0)),
            pl.BlockSpec((1, C, keys), lambda s, i: (s, 0, 0)),
            pl.BlockSpec((bands, 1, per_band, C), lambda s, i: (0, s, 0, 0)),
            full((C, C)),
            full((C, C)),
            full((C, C)),
        ],
        out_specs=[
            tile,
            pl.BlockSpec((bands, 1, per_band, C), lambda s, i: (0, s, 0, 0)),
            full((C, C)),
            full((C, C)),
            full((C, C)),
            full((16, C)),
        ],
        out_shape=(
            shape_of((tokens, C), BF16),
            shape_of(rn_all.shape, BF16),
            shape_of((C, C), F32),
            shape_of((C, C), F32),
            shape_of((C, C), F32),
            shape_of((16, C), F32),
        ),
        scratch_shapes=[
            pltpu.VMEM((HEADS, keys, HD), BF16),
            pltpu.VMEM((C, keys), F32),
            pltpu.VMEM((C, keys), F32),
        ],
        compiler_params=params("attend_back"),
    )(q, inv, mixed, gmid, p, key, vt, rn_all, wk, wv, wo)


def flip(value, by):
    return value + by * (1 - 2 * value)


def remote(src, dst, send, recv, where):
    return pltpu.make_async_remote_copy(
        src_ref=src,
        dst_ref=dst,
        send_sem=send,
        recv_sem=recv,
        device_id=where,
        device_id_type=pl.DeviceIdType.MESH,
    )


def greet(places):
    barrier = pltpu.get_barrier_semaphore()
    count = 0
    for place, there in places:
        if there is None:
            pl.semaphore_signal(
                barrier, inc=1, device_id=place, device_id_type=pl.DeviceIdType.MESH
            )
            count = count + 1
        else:

            @pl.when(there)
            def _():
                pl.semaphore_signal(
                    barrier, inc=1, device_id=place, device_id_type=pl.DeviceIdType.MESH
                )

            count = count + there.astype(jnp.int32)
    pl.semaphore_wait(barrier, count)


def comm_params(name, number):
    return pltpu.CompilerParams(
        collective_id=number, has_side_effects=True, vmem_limit_bytes=ROOM[name] * 1024 * 1024
    )


class Place:
    def __init__(self):
        dp, space = lax.axis_index("dp"), lax.axis_index("space")
        self.z, self.x = dp // 2, dp % 2
        self.y, self.c = space // 2, space % 2
        self.line = lax.axis_size("dp") // 2

    def block(self, z, x, y, c):
        return ((z * 2 + x) * 2 + y) * 2 + c

    def device(self, z, x, y, c):
        return {"dp": z * 2 + x, "space": y * 2 + c}

    def spot(self, da, db, c):
        return (
            flip(self.x, da * (1 - c) + db * c),
            flip(self.y, db * (1 - c) + da * c),
        )

    def partners(self):
        ax, ay = self.spot(1, 0, self.c)
        bx, by = self.spot(0, 1, self.c)
        return (
            self.device(self.z, ax, ay, self.c),
            self.device(self.z, bx, by, self.c),
            self.device(self.z, self.x, self.y, 1 - self.c),
            self.device(self.z + 1, self.x, self.y, self.c),
            self.device(self.z - 1, self.x, self.y, self.c),
        )

    def meet(self):
        first, second, sibling, up, down = self.partners()
        greet(
            [
                (first, None),
                (second, None),
                (sibling, None),
                (up, self.z < self.line - 1),
                (down, self.z > 0),
            ]
        )


DMA = pltpu.SemaphoreType.DMA
SPAN = 208
PART = 144
BOTH = (pl.ds(0, PART), pl.ds(PART, SPAN - PART))


def compact(block):
    half = BLOCK_ROWS // 2
    tail = jnp.concatenate([block[:half, 256:], block[half:, 256:]], axis=1)
    spare = jnp.zeros((2 * SPAN - 2 * BLOCK_ROWS - half, 128), block.dtype)
    rows = jnp.concatenate([block[:, 0:128], block[:, 128:256], tail, spare], axis=0)
    return jnp.concatenate([rows[:SPAN], rows[SPAN:]], axis=1)


def restore(block):
    half = BLOCK_ROWS // 2
    rows = jnp.concatenate([block[:, 0:128], block[:, 128:256]], axis=0)
    tail = rows[2 * BLOCK_ROWS : 2 * BLOCK_ROWS + half]
    return jnp.concatenate(
        [
            rows[:BLOCK_ROWS],
            rows[BLOCK_ROWS : 2 * BLOCK_ROWS],
            jnp.concatenate([tail[:, 0:64], tail[:, 64:128]], axis=0),
        ],
        axis=1,
    )


PLANE = [(da, db) for da in range(2) for db in range(2)]


def gather_kernel(own_ref, out, own, p_z, p_a, p_b, p_c, q_z, q_a, q_b, q_c, recv):
    at = Place()
    line = at.line
    first, second, sibling, up, down = at.partners()
    own[...] = compact(own_ref[...].astype(F32)).astype(BF16)
    at.meet()
    can_up, can_down = at.z < line - 1, at.z > 0

    def index_of(z, da, db, c):
        x, y = at.spot(da, db, at.c)
        return at.block(z, x, y, c)

    def push(part, index, src, sem, where):
        remote(src, out.at[index, BOTH[part]], sem, recv.at[index, part], where).start()

    def landed(part, index):
        remote(
            out.at[index, BOTH[part]], out.at[index, BOTH[part]], p_a.at[0], recv.at[index, part], sibling
        ).wait_recv()

    def here(part, index, is_own):
        return own.at[BOTH[part]] if is_own else out.at[index, BOTH[part]]

    def along_z(part, z, k, index, src, way, sems):
        if way >= 0:

            @pl.when(can_up)
            def _():
                push(part, index, src, sems.at[0, k, z], up)

        if way <= 0:

            @pl.when(can_down)
            def _():
                push(part, index, src, sems.at[1, k, z], down)

    def first_order(z, da, db, way, is_own=False):
        index = index_of(z, da, db, at.c)
        if not is_own:
            landed(0, index)
        src = here(0, index, is_own)
        if da == 0 and db == 0:
            along_z(0, z, 0, index, src, way, p_z)
            push(0, index, src, p_a.at[z], first)
        if db == 0:
            push(0, index, src, p_b.at[da, z], second)
        push(0, index, src, p_c.at[2 * da + db, z], sibling)

    def second_order(z, da, db, way, is_own=False):
        index = index_of(z, da, db, at.c)
        if not is_own:
            landed(1, index)
        src = here(1, index, is_own)
        if way == 0:
            if da == 0 and db == 0:
                push(1, index, src, q_a, first)
            if db == 0:
                push(1, index, src, q_b.at[da], second)
        along_z(1, z, 2 * da + db, index, src, way, q_z)
        push(1, index, src, q_c.at[2 * da + db, z], sibling)

    def hop(d, order, places):
        for z in range(line):
            if z >= d:

                @pl.when(at.z == z)
                def _():
                    for da, db in places:
                        order(z - d, da, db, 1)

            if z + d < line:

                @pl.when(at.z == z)
                def _():
                    for da, db in places:
                        order(z + d, da, db, -1)

    def flat_hops(da, db):
        first_order(at.z, da, db, 0)
        for d in range(1, line):
            hop(d, lambda z, da, db, way: first_order(z, da, db, way), [(da, db)])

    second_order(at.z, 0, 0, 0, True)
    first_order(at.z, 0, 0, 0, True)
    mine = index_of(at.z, 0, 0, at.c)
    out[mine] = own[...]
    second_order(at.z, 1, 0, 0)
    hop(1, first_order, [(0, 0)])
    second_order(at.z, 0, 1, 0)
    second_order(at.z, 1, 1, 0)
    hop(2, first_order, [(0, 0)])
    hop(1, second_order, PLANE)
    hop(3, first_order, [(0, 0)])
    flat_hops(1, 0)
    hop(2, second_order, PLANE)
    flat_hops(0, 1)
    flat_hops(1, 1)
    hop(3, second_order, PLANE)
    for z in range(line):
        for da, db in PLANE:
            for part in range(2):
                landed(part, index_of(z, da, db, 1 - at.c))

    def sent(part, sem, where):
        remote(own.at[BOTH[part]], out.at[mine, BOTH[part]], sem, recv.at[mine, part], where).wait_send()

    sent(1, q_a, first)
    for z in range(line):
        for k in range(4):
            sent(0, p_c.at[k, z], sibling)
            sent(1, q_c.at[k, z], sibling)
        sent(0, p_a.at[z], first)
        for da in range(2):
            sent(0, p_b.at[da, z], second)

        @pl.when(jnp.logical_and(can_up, z <= at.z))
        def _():
            sent(0, p_z.at[0, 0, z], up)
            for k in range(4):
                sent(1, q_z.at[0, k, z], up)

        @pl.when(jnp.logical_and(can_down, z >= at.z))
        def _():
            sent(0, p_z.at[1, 0, z], down)
            for k in range(4):
                sent(1, q_z.at[1, k, z], down)

    for da in range(2):
        sent(1, q_b.at[da], second)


def gather_blocks(own):
    return pl.pallas_call(
        gather_kernel,
        name="gather",
        out_shape=shape_of((BLOCKS, SPAN, 256), BF16),
        in_specs=[VM],
        out_specs=VM,
        scratch_shapes=[
            pltpu.VMEM((SPAN, 256), BF16),
            DMA((2, 1, 4)), DMA((4,)), DMA((2, 4)), DMA((4, 4)),
            DMA((2, 4, 4)), DMA, DMA((2,)), DMA((4, 4)),
            DMA((BLOCKS, 2)),
        ],
        compiler_params=comm_params("gather", 1),
    )(own)


def scatter_kernel(
    parts, out,
    rc, acc, ra, acc2, rb, acc3, rz, sz,
    qc, qacc, qrz, qsz, qplane, qra, qacc2, qrb,
    c_out, a_out, b_out, z_out, qc_out, qz_out, qa_out, qb_out,
    c_in, a_in, b_in, z_in, qc_in, qz_in, qa_in, qb_in,
):
    at = Place()
    line = at.line
    first, second, sibling, up, down = at.partners()
    at.meet()
    slots = [(da, db, z) for da in (1, 0) for db in (1, 0) for z in range(line)]

    def add(*terms):
        if len(terms) == 2:
            return terms[0] + terms[1]
        total = terms[0].astype(F32)
        for term in terms[1:]:
            total = total + term.astype(F32)
        return total.astype(BF16)

    def source(k, c):
        da, db, z = slots[k]
        x, y = at.spot(da, db, c)
        return at.block(z, x, y, c)

    def c_copy(k):
        src = parts.at[source(k, 1 - at.c), BOTH[0]]
        return remote(src, rc.at[k], c_out.at[k], c_in.at[k], sibling)

    def qc_copy(k):
        src = parts.at[source(k, 1 - at.c), BOTH[1]]
        return remote(src, qc.at[k], qc_out.at[k], qc_in.at[k], sibling)

    def a_copy(j):
        return remote(acc.at[j], ra.at[j], a_out.at[j], a_in.at[j], first)

    def b_copy(j):
        return remote(acc2.at[j], rb.at[j], b_out.at[j], b_in.at[j], second)

    def z_copy(way, z):
        return remote(
            sz.at[way, z], rz.at[way, z], z_out.at[way, z], z_in.at[way, z], (up, down)[way]
        )

    def qz_copy(way, k, src=None):
        src = qsz.at[way, k] if src is None else src
        return remote(src, qrz.at[way, k], qz_out.at[way, k], qz_in.at[way, k], (up, down)[way])

    def qa_copy(j):
        return remote(qplane.at[j], qra.at[j], qa_out.at[j], qa_in.at[j], first)

    def qb_copy():
        return remote(qacc2.at[0], qrb, qb_out, qb_in, second)

    count = 4 * line
    for k in range(count):
        qc_copy(k).start()
        c_copy(k).start()
    for k in range(count):
        da, db, z = slots[k]
        qc_copy(k).wait_recv()
        mine = source(k, at.c)
        qacc[k] = add(parts[mine, BOTH[1]], qc[k])
        if z > 0:

            @pl.when(at.z == 0)
            def _():
                qz_copy(0, k, qacc.at[k]).start()

        if z < line - 1:

            @pl.when(at.z == line - 1)
            def _():
                qz_copy(1, k, qacc.at[k]).start()

        c_copy(k).wait_recv()
        acc[k] = add(parts[mine, BOTH[0]], rc[k])
        if da:
            a_copy(k).start()

    def q_hop(d):
        for k in range(count):
            z = slots[k][2]
            if z >= d:

                @pl.when(at.z == d)
                def _():
                    qz_copy(0, k).wait_recv()
                    if z > d:
                        qsz[0, k] = add(qacc[k], qrz[0, k])
                        qz_copy(0, k).start()

            if z <= line - 1 - d:

                @pl.when(at.z == line - 1 - d)
                def _():
                    qz_copy(1, k).wait_recv()
                    if z < line - 1 - d:
                        qsz[1, k] = add(qacc[k], qrz[1, k])
                        qz_copy(1, k).start()

    def p_hop(d):
        for z in reversed(range(d, line)):

            @pl.when(at.z == d)
            def _():
                if d > 0:
                    z_copy(0, z).wait_recv()
                if z > d:
                    sz[0, z] = add(acc3[z], rz[0, z]) if d > 0 else acc3[z]
                    z_copy(0, z).start()

        for z in range(line - d):

            @pl.when(at.z == line - 1 - d)
            def _():
                if d > 0:
                    z_copy(1, z).wait_recv()
                if z < line - 1 - d:
                    sz[1, z] = add(acc3[z], rz[1, z]) if d > 0 else acc3[z]
                    z_copy(1, z).start()

    def inflows(z):
        return [way for way, there in ((0, z > 0), (1, z < line - 1)) if there]

    for j in range(line):
        a_copy(j).wait_recv()
        acc2[j] = add(acc[2 * line + j], ra[j])
        b_copy(j).start()
    q_hop(1)
    for j in range(line, 2 * line):
        a_copy(j).wait_recv()
        acc2[j] = add(acc[2 * line + j], ra[j])
    q_hop(2)
    for z in range(line):
        b_copy(z).wait_recv()
        acc3[z] = add(acc2[line + z], rb[z])
    p_hop(0)
    q_hop(3)
    for z in range(line):

        @pl.when(at.z == z)
        def _():
            for j in range(4):
                k = j * line + z
                qplane[j] = add(qacc[k], *[qrz[way, k] for way in inflows(z)])

    qa_copy(0).start()
    qa_copy(1).start()
    p_hop(1)
    for j in range(2):
        qa_copy(j).wait_recv()
        qacc2[j] = add(qplane[2 + j], qra[j])
        if j == 0:
            qb_copy().start()
    p_hop(2)
    qb_copy().wait_recv()
    q_total = qacc2[1].astype(F32) + qrb[...].astype(F32)
    p_hop(3)
    for z in range(line):

        @pl.when(at.z == z)
        def _():
            total = acc3[z].astype(F32)
            for way in inflows(z):
                total = total + rz[way, z].astype(F32)
            out[...] = restore(jnp.concatenate([total, q_total], axis=0))

    for k in range(count):
        c_copy(k).wait_send()
        qc_copy(k).wait_send()
        z = slots[k][2]

        @pl.when(at.z < z)
        def _():
            qz_copy(0, k).wait_send()

        @pl.when(at.z > z)
        def _():
            qz_copy(1, k).wait_send()

    for j in range(2 * line):
        a_copy(j).wait_send()
    for z in range(line):
        b_copy(z).wait_send()

        @pl.when(at.z < z)
        def _():
            z_copy(0, z).wait_send()

        @pl.when(at.z > z)
        def _():
            z_copy(1, z).wait_send()

    qa_copy(0).wait_send()
    qa_copy(1).wait_send()
    qb_copy().wait_send()


def scatter_blocks(parts):
    room = lambda *n: pltpu.VMEM(n + (PART, 256), BF16)
    less = lambda *n: pltpu.VMEM(n + (SPAN - PART, 256), BF16)
    sems = lambda: [
        DMA((16,)), DMA((8,)), DMA((4,)), DMA((2, 4)), DMA((16,)), DMA((2, 16)), DMA((2,)), DMA,
    ]
    return pl.pallas_call(
        scatter_kernel,
        name="scatter",
        out_shape=shape_of((BLOCK_ROWS, C), F32),
        in_specs=[VM],
        out_specs=VM,
        scratch_shapes=[
            room(16), room(16), room(8), room(8), room(4), room(4), room(2, 4), room(2, 4),
            less(16), less(16), less(2, 16), less(2, 16), less(4), less(2), less(2), less(),
        ]
        + sems()
        + sems(),
        compiler_params=comm_params("scatter", 2),
    )(parts)


def bands_of():
    band = lax.axis_index("space")
    pair, core = band // 2, band % 2
    return band, pair * 2 + 1 - core, (1 - pair) * 2 + core


def swap_kernel(width, value, above, below, up_sem, down_sem, up_in, down_in):
    band = lax.axis_index("space")
    rows = value.shape[1]
    ends = lax.axis_size("space") - 1
    down = remote(
        value.at[:, pl.ds(rows - width, width)], above, down_sem, down_in, {"space": band + 1}
    )
    up = remote(value.at[:, pl.ds(0, width)], below, up_sem, up_in, {"space": band - 1})

    @pl.when(band < ends)
    def _():
        down.start()

    @pl.when(band > 0)
    def _():
        up.start()

    def finish():
        @pl.when(band < ends)
        def _():
            down.wait_send()
            up.wait_recv()

        @pl.when(band > 0)
        def _():
            up.wait_send()
            down.wait_recv()

    return finish


def bands_meet(others):
    band = lax.axis_index("space")
    ends = lax.axis_size("space") - 1
    greet(
        [({"space": o}, None) for o in others]
        + [({"space": band + 1}, band < ends), ({"space": band - 1}, band > 0)]
    )


def front_kernel(
    x_ref, cot, vec, wq, wr, q_out, red_out, rn_all, above, below,
    normed_scr, scr, send, recv, up_sem, down_sem, up_in, down_in,
):
    band, sibling, across = bands_of()
    far = across + sibling - band
    bands_meet((sibling, across))
    finish = swap_kernel(1, cot, above, below, up_sem, down_sem, up_in, down_in)
    tiles = x_ref.shape[0] // TILE

    def spot_of(i):
        return pl.ds(pl.multiple_of(i * RTILE, RTILE), RTILE)

    def rows_of(i):
        return pl.ds(pl.multiple_of(i * TILE, TILE), TILE)

    def carry_on(index, way, i):
        tile = rn_all.at[index, spot_of(i)]
        where = {"space": across if way == 0 else sibling}
        return remote(tile, tile, send.at[way, i], recv.at[index, i], where)

    def reduce(i, carry):
        unit, _ = norm_parts(x_ref[rows_of(i), :].astype(F32))
        normed = unit * vec[V_GAIN1 : V_GAIN1 + 1, :] + vec[V_SHIFT1 : V_SHIFT1 + 1, :]
        normed = normed.astype(BF16)
        normed_scr[rows_of(i), :] = normed
        split_tiles(scr, normed.astype(F32))
        pieces = patch_pieces(scr)
        reduced = vec[V_REDUCE : V_REDUCE + 1, :]
        for k in range(4):
            reduced = reduced + mm(pieces[k].astype(BF16), wr[k * C : (k + 1) * C, :])
        red_out[spot_of(i), :] = reduced
        unit, _ = norm_parts(reduced)
        rnorm = unit * vec[V_RGAIN : V_RGAIN + 1, :] + vec[V_RSHIFT : V_RSHIFT + 1, :]
        rn_all[band, spot_of(i)] = rnorm.astype(BF16)
        carry_on(band, 0, i).start()
        carry_on(band, 1, i).start()
        return carry

    def query(i, carry):
        queries = (mm(normed_scr[rows_of(i), :], wq[...]) + vec[V_QUERY : V_QUERY + 1, :]).astype(
            BF16
        )
        q_out[rows_of(i), :] = queries * jnp.asarray(1.0 / math.sqrt(HD), BF16)
        carry_on(across, 2, i).wait_recv()
        carry_on(across, 2, i).start()
        return carry

    def close(i, carry):
        carry_on(sibling, 1, i).wait_recv()
        carry_on(far, 1, i).wait_recv()
        carry_on(band, 0, i).wait_send()
        carry_on(band, 1, i).wait_send()
        carry_on(across, 2, i).wait_send()
        return carry

    lax.fori_loop(0, tiles, reduce, 0)
    lax.fori_loop(0, tiles, query, 0)
    lax.fori_loop(0, tiles, close, 0)
    finish()


def front(x, cot, vec, wq, wr):
    tokens = x.shape[0]
    tiles = tokens // TILE
    bands = lax.axis_size("space")
    edge = (cot.shape[0], 1) + cot.shape[2:]
    return pl.pallas_call(
        front_kernel,
        name="front",
        out_shape=(
            shape_of((tokens, C), BF16),
            shape_of((tokens // 4, C), F32),
            shape_of((bands, tokens // 4, C), BF16),
            shape_of(edge, cot.dtype),
            shape_of(edge, cot.dtype),
        ),
        in_specs=[VM, ANY, VM, VM, VM],
        out_specs=(VM, VM, VM, ANY, ANY),
        scratch_shapes=[
            pltpu.VMEM((tokens, C), BF16),
            pltpu.VMEM((3, TILE, 128), F32),
            DMA((3, tiles)),
            DMA((bands, tiles)),
            DMA,
            DMA,
            DMA,
            DMA,
        ],
        compiler_params=comm_params("front", 3),
    )(x, cot, vec, wq, wr)


def halo_kernel(value, above, below, up_sem, down_sem, up_in, down_in):
    bands_meet(())
    swap_kernel(2, value, above, below, up_sem, down_sem, up_in, down_in)()


def halo(value):
    dma = pltpu.SemaphoreType.DMA
    edge = (value.shape[0], 2) + value.shape[2:]
    return pl.pallas_call(
        halo_kernel,
        name="halo",
        out_shape=(shape_of(edge, value.dtype), shape_of(edge, value.dtype)),
        in_specs=[ANY],
        out_specs=(ANY, ANY),
        scratch_shapes=[dma, dma, dma, dma],
        compiler_params=comm_params("halo", 4),
    )(value)


CHUNKS = 4


def tail_kernel(
    parts, x_ref, dq_ref, red_ref, vec, wq, wr,
    gx_out, gwq_out, gwr_out, gvec_out,
    rc, acc, rb, grn_scr, gn_scr, unit_scr, rstd_scr, pieces_scr, scr, gscr,
    c_sem, c_in, b_sem, b_in,
):
    band, sibling, across = bands_of()
    greet([({"space": sibling}, None), ({"space": across}, None)])
    far = across + sibling - band
    size = rc.shape[1] // CHUNKS
    chunks = [pl.ds(j * size, size) for j in range(CHUNKS)]

    def copy_first(j):
        src, dst = parts.at[far, chunks[j]], rc.at[0, chunks[j]]
        return remote(src, dst, c_sem.at[0, j], c_in.at[0, j], {"space": sibling})

    def copy_second(j):
        src, dst = parts.at[sibling, chunks[j]], rc.at[1, chunks[j]]
        return remote(src, dst, c_sem.at[1, j], c_in.at[1, j], {"space": sibling})

    def copy_onward(j):
        src, dst = acc.at[chunks[j]], rb.at[chunks[j]]
        return remote(src, dst, b_sem.at[j], b_in.at[j], {"space": across})

    for j in range(CHUNKS):
        copy_first(j).start()
    for j in range(CHUNKS):
        copy_second(j).start()
    tiles = x_ref.shape[0] // TILE
    gain = vec[V_GAIN1 : V_GAIN1 + 1, :]
    for ref in (gwq_out, gwr_out, gvec_out):
        ref[...] = jnp.zeros_like(ref)
    for j in range(CHUNKS):
        copy_first(j).wait_recv()
        acc[chunks[j], :] = parts[across, chunks[j]] + rc[0, chunks[j]]
        copy_onward(j).start()

    def before(i, carry):
        rows = pl.ds(pl.multiple_of(i * TILE, TILE), TILE)
        unit, rstd = norm_parts(x_ref[rows, :].astype(F32))
        unit_scr[rows, :] = unit
        rstd_scr[rows, :] = jnp.broadcast_to(rstd, (TILE, 128))
        normed = (unit * gain + vec[V_SHIFT1 : V_SHIFT1 + 1, :]).astype(BF16)
        split_tiles(scr, normed.astype(F32))
        pieces = patch_pieces(scr)
        spot = pl.ds(pl.multiple_of(i * RTILE, RTILE), RTILE)
        for k in range(4):
            pieces_scr[k, spot, :] = pieces[k].astype(BF16)
        dq = dq_ref[rows, :]
        gwq_out[...] += mm_tn(normed, dq)
        gn_scr[rows, :] = mm_nt(dq, wq[...])
        gvec_out[0:1, :] += row_sum(dq.astype(F32))
        return carry

    lax.fori_loop(0, tiles, before, 0)
    def after(i, carry):
        rows = pl.ds(pl.multiple_of(i * TILE, TILE), TILE)
        spot = pl.ds(pl.multiple_of(i * RTILE, RTILE), RTILE)
        runit, rrstd = norm_parts(red_ref[spot, :])
        grn = grn_scr[spot, :]
        gred = norm_back(grn, runit, rrstd, vec[V_RGAIN : V_RGAIN + 1, :]).astype(BF16)
        back = {}
        for k in range(4):
            at = slice(k * C, (k + 1) * C)
            gwr_out[at, :] += mm_tn(pieces_scr[k, spot, :], gred)
            back[k] = mm_nt(gred, wr[at, :]).reshape(TILE // (2 * W), 1, W // 2, C)
        for b in range(2):
            cols = jnp.concatenate([back[b], back[2 + b]], axis=1).reshape(TILE // 2, C)
            places = pl.ds(b, TILE // 2, stride=2)
            gscr[0, places, :] = cols[:, 0:128]
            gscr[1, places, :] = cols[:, 128:256]
            gscr[2, places, :] = jnp.concatenate(
                [cols[:, 256:320], jnp.zeros((TILE // 2, 64), F32)], axis=1
            )
        placed = jnp.concatenate([gscr[0], gscr[1], gscr[2][:, 0:64]], axis=1)
        gnormed = gn_scr[rows, :] + placed
        unit = unit_scr[rows, :]
        gx_out[rows, :] = norm_back(gnormed, unit, rstd_scr[rows, 0:1], gain)
        gvec_out[1:2, :] += row_sum(gred.astype(F32))
        gvec_out[2:3, :] += row_sum(grn * runit)
        gvec_out[3:4, :] += row_sum(grn)
        gvec_out[4:5, :] += row_sum(gnormed * unit)
        gvec_out[5:6, :] += row_sum(gnormed)
        return carry

    for j in range(CHUNKS):
        copy_second(j).wait_recv()
        copy_onward(j).wait_recv()
        own = parts[band, chunks[j]].astype(F32)
        grn_scr[chunks[j], :] = own + (
            rc[1, chunks[j]].astype(F32) + rb[chunks[j], :].astype(F32)
        )
        lax.fori_loop(j * tiles // CHUNKS, (j + 1) * tiles // CHUNKS, after, 0)
    for j in range(CHUNKS):
        copy_first(j).wait_send()
        copy_second(j).wait_send()
        copy_onward(j).wait_send()


def tail(parts, x, dq, red, vec, wq, wr):
    one = parts.shape[1:]
    tokens = x.shape[0]
    return pl.pallas_call(
        tail_kernel,
        name="tail",
        out_shape=(
            shape_of((tokens, C), F32),
            shape_of((C, C), F32),
            shape_of((4 * C, C), F32),
            shape_of((8, C), F32),
        ),
        in_specs=[VM] * 7,
        out_specs=(VM,) * 4,
        scratch_shapes=[
            pltpu.VMEM((2,) + one, BF16),
            pltpu.VMEM(one, BF16),
            pltpu.VMEM(one, BF16),
            pltpu.VMEM(one, F32),
            pltpu.VMEM((tokens, C), F32),
            pltpu.VMEM((tokens, C), F32),
            pltpu.VMEM((tokens, 128), F32),
            pltpu.VMEM((4,) + one, BF16),
            pltpu.VMEM((3, TILE, 128), F32),
            pltpu.VMEM((3, TILE, 128), F32),
            DMA((2, CHUNKS)),
            DMA((2, CHUNKS)),
            DMA((CHUNKS,)),
            DMA((CHUNKS,)),
        ],
        compiler_params=comm_params("tail", 5),
    )(parts, x, dq, red, vec, wq, wr)


def blocks_fit(size):
    return (
        lax.axis_size("dp") == 8 and lax.axis_size("space") == 4 and size == BLOCK_ROWS * C
    )


def gather_flat(shard):
    if blocks_fit(shard.shape[0]):
        return gather_blocks(shard.reshape(BLOCK_ROWS, C))
    flat = lax.all_gather(shard, ("dp", "space"), axis=0, tiled=True)
    want = ROWS * C
    flat = flat[:want] if flat.shape[0] >= want else jnp.pad(flat, (0, want - flat.shape[0]))
    blocks = jax.vmap(compact)(flat.reshape(BLOCKS, BLOCK_ROWS, C))
    return blocks


def scatter_grads(blocks, size):
    if blocks_fit(size):
        return scatter_blocks(blocks).reshape(size)
    flat = jax.vmap(restore)(blocks).reshape(-1)
    want = size * lax.axis_size("dp") * lax.axis_size("space")
    flat = flat[:want] if flat.shape[0] >= want else jnp.pad(flat, (0, want - flat.shape[0]))
    own = lax.psum_scatter(flat, ("dp", "space"), scatter_dimension=0, tiled=True)
    return own.astype(F32)


def on_device(scenes, shard, cotangent):
    count, rows, breadth = scenes.shape[0], scenes.shape[1], scenes.shape[2]
    tokens = count * rows * breadth
    bands = lax.axis_size("space")
    per_band = rows * breadth // 4
    band = lax.axis_index("space")
    edge = jnp.stack([band > 0, band < bands - 1]).astype(F32)
    wq, wr, wk, wv, wo, we, ws, vec, hid = unpack(gather_flat(shard))
    x = scenes.reshape(tokens, C)
    q, red, rn_all, cot_top, cot_low = front(x, cotangent, vec, wq, wr)
    rn_all = rn_all.reshape(bands, count, per_band, C)
    mixed, inv, mid, n2, p, key, vt = attend(x, q, rn_all, vec, wk, wv, wo)
    n2 = n2.reshape(scenes.shape)
    n2_top, n2_low = halo(n2)
    y, gmid, gwe, gws, ghid, gvec2 = mix(
        n2, n2_top, n2_low, cotangent, cot_top, cot_low, mid, edge, vec, hid, we, ws
    )
    dq, grn_all, gwk, gwv, gwo, gvec1 = attend_back(
        q, inv, mixed, gmid, p, key, vt, rn_all, wk, wv, wo
    )
    parts = grn_all.reshape(bands, count * per_band, C)
    gnorm, gwq, gwr, gvec0 = tail(parts, x, dq, red, vec, wq, wr)
    blocks, gx = pack(
        gwq, gwr, gwk, gwv, gwo, gwe, gws, gvec0, gvec1, gvec2, ghid, gmid, gnorm
    )
    grads = scatter_grads(blocks, shard.shape[0])
    return y.reshape(scenes.shape), gx.reshape(scenes.shape), grads


def solution(mesh):
    band = P("dp", "space", None, None)
    flat = P(("dp", "space"))
    return jax.shard_map(
        on_device,
        mesh=mesh,
        in_specs=(band, flat, band),
        out_specs=(band, band, flat),
        check_vma=False,
    )
```
